32 devices in a mesh: rows: 16 (over z, x, core), cols: 2 (over y).
Axes of the slice: x: 2, y: 2, z: 4, core: 2. Of those that a mesh axis runs over, the one named last changes fastest.
Arguments:
- cells: bfloat16 [2048, 768], P('rows', 'cols'), may hold values from -6 to 6
- feat_mask: int32 [2048, 4], P('rows'), may hold values from 0 to 1, as said below
- train_rows: int32 [1], replicated, may hold values from 512 to 1536
- cotangent: bfloat16 [2048, 768], P('rows', 'cols'), may hold values from -6 to 6
- proj_weights: float32 [6, 192, 192], replicated, may hold values from -0.625 to 0.625
- feat_out_w: float32 [192, 192], replicated, may hold values from -0.75 to 0.75
- item_out_w: float32 [192, 192], replicated, may hold values from -2 to 2
- mlp_in: float32 [192, 384], replicated, may hold values from -0.4375 to 0.4375
- mlp_out: float32 [384, 192], replicated, may hold values from -0.3125 to 0.3125
- norm_gains: float32 [3, 192], replicated, may hold values from 0.5 to 1.5
- norm_shifts: float32 [3, 192], replicated, may hold values from -1.8 to 1.8
- bases_small: float32 [18, 192, 192], replicated, may hold values from -1 to 1, as said below
- bases_big: float32 [2, 384, 384], replicated, may hold values from -1 to 1, as said below
- owner_rows: int32 [2304], replicated, may hold values from 0 to 2303, each once
- bank_first: float32 [2304, 192], P('rows'), may hold values from -0.0010000406 to 0.0010000406
- bank_second: float32 [2304, 192], P('rows'), may hold values from 1.1859668e-07 to 4.746122e-07
- norm_first: float32 [2, 3, 192], replicated, may hold values from -0.0010000406 to 0.0010000406
- norm_second: float32 [2, 3, 192], replicated, may hold values from 1.1859668e-07 to 4.746122e-07
Outputs:
- layer_out: bfloat16 [2048, 768], P('rows', 'cols')
- cells_grad: float32 [2048, 768], P('rows', 'cols')
- square_grads: float32 [8, 192, 192], replicated
- mlp_in_grad: float32 [192, 384], replicated
- mlp_out_grad: float32 [384, 192], replicated
- norm_grads: float32 [2, 3, 192], replicated
- clip_norm: float32 [1], replicated
- bank_first_new: float32 [2304, 192], P('rows')
- bank_second_new: float32 [2304, 192], P('rows')
- square_new: float32 [8, 192, 192], replicated
- mlp_in_new: float32 [192, 384], replicated
- mlp_out_new: float32 [384, 192], replicated
- square_low: bfloat16 [8, 192, 192], replicated
- mlp_in_low: bfloat16 [192, 384], replicated
- mlp_out_low: bfloat16 [384, 192], replicated
- norm_new: float32 [2, 3, 192], replicated
- norm_first_new: float32 [2, 3, 192], replicated
- norm_second_new: float32 [2, 3, 192], replicated
The draws below stay inside these ranges and needn't reach their ends.
Inputs may be any that keep to these rules, and one draw needn't show every extreme that they name: `feat_mask`: every row has at least one 1. rows 0 to train_rows - 1 are the training rows. `owner_rows`: each number once. `bases_small`: each matrix is orthogonal. `bases_big`: each matrix is orthogonal.
All inputs are finite; a program needn't handle non-finite values.
Results may differ from the reference program's by a relative error of at most 0.02.
The reference program's roundings to bfloat16 on the way count: a program that leaves them out, or rounds other values in their place, can miss the bound.
Values may be sent and summed in bfloat16 or wider, within the bound.
A program may use at most 192 MiB of HBM per device.

```python
import math
import jax
import jax.numpy as jnp
from jax import lax

D = 192
HEADS = 6
FF = 384
STEP = 10
C = 4
ROWS = 2048
NBANK = 2304


def draw_feat_mask(key, part):
    key_one, key_two = jax.random.split(key)
    levels = jax.random.randint(key_one, (ROWS, C), 0, 4)
    forced = jax.random.randint(key_two, (ROWS, 1), 0, C)
    column = jnp.arange(C, dtype=jnp.int32)[None, :]
    return jnp.where(column == forced, 1, jnp.where(levels > 0, 1, 0)).astype(jnp.int32)


def rotation_stack(key, stack_count, side_width):
    key_one, key_two, key_three = jax.random.split(key, 3)
    row_order = jax.vmap(lambda subkey: jax.random.permutation(subkey, side_width))(jax.random.split(key_one, stack_count))
    col_order = jax.vmap(lambda subkey: jax.random.permutation(subkey, side_width))(jax.random.split(key_two, stack_count))
    angle_table = jax.random.uniform(key_three, (stack_count, side_width // 2), jnp.float32, -math.pi, math.pi)
    row_pair = row_order // 2
    angles_row = jnp.take_along_axis(angle_table, row_pair, axis=1)[:, :, None]
    paired = row_pair[:, :, None] == (col_order // 2)[:, None, :]
    diagonal = row_order[:, :, None] == col_order[:, None, :]
    sign_factor = jnp.where(row_order % 2 == 0, -1.0, 1.0)[:, :, None]
    entries = jnp.where(diagonal, jnp.cos(angles_row), sign_factor * jnp.sin(angles_row))
    return jnp.where(paired, entries, 0.0).astype(jnp.float32)


def draw_bases_small(key, part):
    return rotation_stack(key, 18, D)


def draw_bases_big(key, part):
    return rotation_stack(key, 2, FF)


def block_scale(stream_key, dims, cuts, smallest, largest):
    def one(dim, blocks):
        heights = jax.random.uniform(jax.random.fold_in(jax.random.fold_in(stream_key, 6), dim), (blocks,), jnp.float32, smallest / len(cuts), largest / len(cuts))
        return jnp.repeat(jnp.exp(heights), dims[dim] // blocks).reshape((-1,) + (1,) * (len(dims) - dim - 1))

    factor_of = one(*cuts[0])
    for cut in cuts[1:]:
        factor_of = factor_of * one(*cut)
    return factor_of


def noise(key, dims, scale, limit, pieces=(), held_as=jnp.bfloat16):
    result = jax.random.normal(key, dims, jnp.float32) * scale
    if len(pieces) > 0:
        result = block_scale(key, dims, pieces, -0.22, 0.18) * result
    return jnp.clip(result, min=-limit, max=limit).astype(held_as)


def setup_inputs(seed: int = 0) -> dict:
    arg_keys = jax.random.split(jax.random.key(seed), 19)
    return {
        "cells": noise(arg_keys[0], (ROWS, C * D), 1.0, 6.0, ((0, 16), (1, 2))),
        "feat_mask": draw_feat_mask(jax.random.fold_in(arg_keys[18], 71), 0),
        "train_rows": jax.random.randint(arg_keys[2], (1,), ROWS // 4, 3 * ROWS // 4 + 1).astype(jnp.int32),
        "cotangent": noise(arg_keys[3], (ROWS, C * D), 1.0, 6.0, ((0, 16), (1, 2))),
        "proj_weights": noise(arg_keys[4], (6, D, D), (D / 2) ** -0.5, 0.625, (), jnp.float32),
        "feat_out_w": noise(arg_keys[5], (D, D), (D / 3) ** -0.5, 0.75, (), jnp.float32),
        "item_out_w": noise(arg_keys[6], (D, D), (100 * D / ROWS) ** -0.5, 2.0, (), jnp.float32),
        "mlp_in": noise(arg_keys[7], (D, FF), D ** -0.5, 0.4375, (), jnp.float32),
        "mlp_out": noise(arg_keys[8], (FF, D), FF ** -0.5, 0.3125, (), jnp.float32),
        "norm_gains": jnp.clip(1.0 + 0.1 * jax.random.normal(arg_keys[9], (3, D), jnp.float32), 0.5, 1.5),
        "norm_shifts": noise(arg_keys[10], (3, D), 0.3, 1.8, (), jnp.float32),
        "bases_small": draw_bases_small(jax.random.fold_in(arg_keys[18], 71), 0),
        "bases_big": draw_bases_big(jax.random.fold_in(arg_keys[18], 71), 0),
        "owner_rows": jax.random.permutation(arg_keys[13], NBANK).astype(jnp.int32),
        "bank_first": noise(arg_keys[14], (NBANK, D), (0.111 / (8 * D * D + 2 * D * FF + 6 * D) ** 0.5), 0.0010000406, ((0, 16),), jnp.float32),
        "bank_second": jnp.clip(jnp.exp(math.log(4.7461219310207525e-07) - 1.3867695 * jax.random.uniform(arg_keys[15], (NBANK, D), jnp.float32) ** block_scale(arg_keys[15], (NBANK, D), ((0, 16),), -0.2, 0.2)), 1.1859668092029096e-07, 4.7461219310207525e-07),
        "norm_first": noise(arg_keys[16], (2, 3, D), (0.111 / (8 * D * D + 2 * D * FF + 6 * D) ** 0.5), 0.0010000406, (), jnp.float32),
        "norm_second": jnp.clip(jnp.exp(jax.random.uniform(arg_keys[17], (2, 3, D), jnp.float32, math.log(1.1859668092029096e-07), math.log(4.7461219310207525e-07))), 1.1859668092029096e-07, 4.7461219310207525e-07),
    }


@jax.custom_vjp
def low(v):
    return lax.optimization_barrier(v.astype(jnp.bfloat16)).astype(jnp.float32)

@jax.custom_vjp
def low_back(v):
    return v

def low_keep(v):
    return (low(v), None)

def low_pass(kept, grad):
    return (grad,)

def back_keep(v):
    return (v, None)

def back_low(kept, grad):
    return (low(grad),)
low.defvjp(low_keep, low_pass)
low_back.defvjp(back_keep, back_low)
HIGHEST = lax.Precision.HIGHEST
NEGATIVE = -1e+30
CLIP_NORM = 1.0
BETA_ONE = 0.9
BETA_TWO = 0.95
EPSILON = 1e-08
LEARN_RATE = 1.0

def round_both(value):
    return low(low_back(value))

def layer_norm(hidden, gain_row, shift_row):
    center = lax.optimization_barrier(jnp.mean(hidden, axis=-1, keepdims=True))
    centered = hidden - center
    spread = lax.optimization_barrier(jnp.mean(centered * centered, axis=-1, keepdims=True))
    return centered * lax.rsqrt(spread + 1e-05) * gain_row + shift_row

def linear(hidden, weight):
    return jnp.dot(hidden, weight, precision=HIGHEST, preferred_element_type=jnp.float32)

def feature_attention(feat_in, weights_qkv, weight_out, feat_open):
    row_total = feat_in.shape[0] // C
    head_dim = D // HEADS
    scaling = head_dim ** (-0.5)
    projected = round_both(linear(feat_in, weights_qkv)).reshape(row_total, C, 3, HEADS, head_dim)
    queries = projected[:, :, 0]
    key_rows = projected[:, :, 1]
    value_rows = projected[:, :, 2]
    scores = low_back(jnp.einsum('rqhe,rkhe->rhqk', queries, key_rows, precision=HIGHEST) * scaling)
    scores = jnp.where(feat_open[:, None, None, :], scores, NEGATIVE)
    attend = low(jax.nn.softmax(scores, axis=-1))
    mixed = jnp.einsum('rhqk,rkhe->rqhe', attend, value_rows, precision=HIGHEST)
    mixed = round_both(mixed.reshape(row_total * C, D))
    return round_both(linear(mixed, weight_out))

def item_block(queries, key_rows, value_rows, item_open):
    scaling = (D // HEADS) ** (-0.5)
    scores = low_back(jnp.einsum('qhe,khe->hqk', queries, key_rows, precision=HIGHEST) * scaling)
    scores = jnp.where(item_open[None, None, :], scores, NEGATIVE)
    attend = low(jax.nn.softmax(scores, axis=-1))
    return jnp.einsum('hqk,khe->qhe', attend, value_rows, precision=HIGHEST)

def item_attention(queries, key_rows, value_rows, item_open):
    row_total = queries.shape[0]
    block_size = math.gcd(row_total, 1024)
    block_count = row_total // block_size
    head_dim = D // HEADS
    query_blocks = jnp.transpose(queries, (1, 0, 2, 3)).reshape(C * block_count, block_size, HEADS, head_dim)
    key_cols = jnp.transpose(key_rows, (1, 0, 2, 3))
    value_cols = jnp.transpose(value_rows, (1, 0, 2, 3))
    column_ids = (jnp.arange(C * block_count, dtype=jnp.int32) // block_count).astype(jnp.int32)
    block_check = jax.checkpoint(item_block)

    def one_block(packed):
        query_block, column_id = packed
        return block_check(query_block, key_cols[column_id], value_cols[column_id], item_open)
    outputs = lax.map(one_block, (query_blocks, column_ids))
    return jnp.transpose(outputs.reshape(C, row_total, HEADS, head_dim), (1, 0, 2, 3))

def forward(inputs, proj_weights, feat_out_w, item_out_w, mlp_in, mlp_out, norm_gains, norm_shifts, feat_open, item_open):
    row_total = inputs.shape[0]
    head_dim = D // HEADS
    flat = inputs.reshape(row_total * C, D)
    proj_low = low(proj_weights)
    feat_qkv = jnp.concatenate([proj_low[0], proj_low[1], proj_low[2]], axis=1)
    item_qkv = jnp.concatenate([proj_low[3], proj_low[4], proj_low[5]], axis=1)
    feat_branch = feature_attention(low_back(flat), feat_qkv, low(feat_out_w), feat_open)
    first_out = layer_norm(flat + feat_branch, norm_gains[0], norm_shifts[0])
    first_low = low(first_out)
    projected = round_both(linear(first_low, item_qkv)).reshape(row_total, C, 3, HEADS, head_dim)
    item_full = item_attention(projected[:, :, 0], projected[:, :, 1], projected[:, :, 2], item_open)
    item_mixed = round_both(item_full.reshape(row_total * C, D))
    item_branch = low_back(linear(item_mixed, low(item_out_w)))
    second_out = layer_norm(first_out + item_branch, norm_gains[1], norm_shifts[1])
    hidden_pre = low_back(linear(low(second_out), low(mlp_in)))
    hidden_low = low(jax.nn.gelu(hidden_pre, approximate=False))
    mlp_branch = low_back(linear(hidden_low, low(mlp_out)))
    third_out = layer_norm(second_out + mlp_branch, norm_gains[2], norm_shifts[2])
    return third_out.reshape(row_total, C * D)

def clip_all(gradients):
    total_sq = jnp.sum(gradients[0] * gradients[0])
    for extra in gradients[1:]:
        total_sq = total_sq + jnp.sum(extra * extra)
    grad_norm = jnp.sqrt(total_sq)
    factor = jnp.minimum(1.0, CLIP_NORM / grad_norm)
    return ([gradient * factor for gradient in gradients], grad_norm)

def rotate_bank(square_grad, in_grad, out_grad, bases_small, bases_big):
    model_width = in_grad.shape[0]
    left_bases = bases_small[0:8]
    right_bases = bases_small[8:16]
    rot_square = jnp.matmul(jnp.swapaxes(left_bases, 1, 2), jnp.matmul(square_grad, right_bases, precision=HIGHEST), precision=HIGHEST)
    rot_in = jnp.dot(bases_small[16].T, jnp.dot(in_grad, bases_big[0], precision=HIGHEST), precision=HIGHEST)
    rot_out = jnp.dot(bases_big[1].T, jnp.dot(out_grad, bases_small[17], precision=HIGHEST), precision=HIGHEST)
    return jnp.concatenate([rot_square.reshape(8 * model_width, model_width), rot_in.T, rot_out], axis=0)

def rotate_back(step_bank, bases_small, bases_big):
    model_width = step_bank.shape[1]
    ff_width = (step_bank.shape[0] - 8 * model_width) // 2
    step_square = step_bank[:8 * model_width].reshape(8, model_width, model_width)
    step_in = step_bank[8 * model_width:8 * model_width + ff_width].T
    step_out = step_bank[8 * model_width + ff_width:]
    up_square = jnp.matmul(bases_small[0:8], jnp.matmul(step_square, jnp.swapaxes(bases_small[8:16], 1, 2), precision=HIGHEST), precision=HIGHEST)
    up_in = jnp.dot(bases_small[16], jnp.dot(step_in, bases_big[0].T, precision=HIGHEST), precision=HIGHEST)
    up_out = jnp.dot(bases_big[1], jnp.dot(step_out, bases_small[17].T, precision=HIGHEST), precision=HIGHEST)
    return (up_square, up_in, up_out)

def adam_rows(gradient, first_old, second_old, step_float):
    first_new = BETA_ONE * first_old + (1.0 - BETA_ONE) * gradient
    second_new = BETA_TWO * second_old + (1.0 - BETA_TWO) * gradient * gradient
    first_hat = first_new / (1.0 - jnp.power(BETA_ONE, step_float))
    second_hat = second_new / (1.0 - jnp.power(BETA_TWO, step_float))
    return (first_new, second_new, first_hat / (jnp.sqrt(second_hat) + EPSILON))

def trusted(weight, update, over_axes):
    scaling = jnp.sqrt(lax.optimization_barrier(jnp.mean(weight * weight, axis=over_axes, keepdims=True)) + 1e-06)
    return weight - LEARN_RATE * scaling * update

def reference(cells, feat_mask, train_rows, cotangent, proj_weights, feat_out_w, item_out_w, mlp_in, mlp_out, norm_gains, norm_shifts, bases_small, bases_big, owner_rows, bank_first, bank_second, norm_first, norm_second):
    inputs = cells.astype(jnp.float32)
    feat_open = feat_mask > 0
    item_open = jnp.arange(ROWS, dtype=jnp.int32) < train_rows[0]

    def layer(inputs, proj_weights, feat_out_w, item_out_w, mlp_in, mlp_out, norm_gains, norm_shifts):
        return forward(inputs, proj_weights, feat_out_w, item_out_w, mlp_in, mlp_out, norm_gains, norm_shifts, feat_open, item_open)
    layer_out, pullback = jax.vjp(layer, inputs, proj_weights, feat_out_w, item_out_w, mlp_in, mlp_out, norm_gains, norm_shifts)
    cells_grad, proj_grad, feat_out_grad, item_out_grad, in_grad, out_grad, gain_grad, shift_grad = pullback(cotangent.astype(jnp.float32))
    square_grad = jnp.concatenate([proj_grad, feat_out_grad[None], item_out_grad[None]], axis=0)
    norm_grad = jnp.stack([gain_grad, shift_grad])
    clipped, grad_norm = clip_all([square_grad, in_grad, out_grad, norm_grad])
    square_clip, in_clip, out_clip, norm_clip = clipped
    rot_bank = rotate_bank(square_clip, in_clip, out_clip, bases_small, bases_big)
    step_float = jnp.asarray(STEP, jnp.float32)
    first_new, second_new, slot_steps = adam_rows(jnp.take(rot_bank, owner_rows.astype(jnp.int32), axis=0), bank_first, bank_second, step_float)
    full_steps = jnp.take(slot_steps, jnp.argsort(owner_rows).astype(jnp.int32), axis=0)
    up_square, up_in, up_out = rotate_back(full_steps, bases_small, bases_big)
    square_old = jnp.concatenate([proj_weights, feat_out_w[None], item_out_w[None]], axis=0)
    square_new = trusted(square_old, up_square, (1, 2))
    in_new = trusted(mlp_in, up_in, (0, 1))
    out_new = trusted(mlp_out, up_out, (0, 1))
    norm_old = jnp.stack([norm_gains, norm_shifts])
    norm_first_new, norm_second_new, norm_steps = adam_rows(norm_clip, norm_first, norm_second, step_float)
    norm_new = trusted(norm_old, norm_steps, (2,))
    return (layer_out.astype(jnp.bfloat16), cells_grad, square_clip, in_clip, out_clip, norm_clip, grad_norm.reshape(1), first_new, second_new, square_new, in_new, out_new, square_new.astype(jnp.bfloat16), in_new.astype(jnp.bfloat16), out_new.astype(jnp.bfloat16), norm_new, norm_first_new, norm_second_new)
```

```python
import functools
import math

import jax
import jax.numpy as jnp
from jax import lax
from jax.experimental import pallas as pl
from jax.experimental.pallas import tpu as pltpu
from jax.sharding import PartitionSpec as P

HEADS = 6
STEP = 10


HIGHEST = lax.Precision.HIGHEST
NEGATIVE = -1e30
CLIP_NORM = 1.0
BETA_ONE = 0.9
BETA_TWO = 0.95
EPSILON = 1e-08
LEARN_RATE = 1.0


def layer_norm(hidden, gain_row, shift_row):
    center = jnp.mean(hidden, axis=-1, keepdims=True)
    centered = hidden - center
    spread = jnp.mean(centered * centered, axis=-1, keepdims=True)
    return centered * lax.rsqrt(spread + 1e-05) * gain_row + shift_row


def gelu_exact(hidden):
    return jax.nn.gelu(hidden, approximate=False)


def product(left_side, right_side):
    return jnp.dot(left_side, right_side, preferred_element_type=jnp.float32)


def product_left(left_side, right_side):
    return lax.dot_general(
        left_side, right_side, (((0,), (0,)), ((), ())), preferred_element_type=jnp.float32
    )


def product_right(left_side, right_side):
    return lax.dot_general(
        left_side, right_side, (((1,), (1,)), ((), ())), preferred_element_type=jnp.float32
    )


def feature_forward(queries, key_rows, value_rows, key_open):
    scaling = queries.shape[-1] ** (-0.5)
    scores = (
        jnp.einsum("nqhe,nkhe->nhqk", queries, key_rows, preferred_element_type=jnp.float32)
        * scaling
    )
    scores = jnp.where(key_open[:, None, None, :], scores, NEGATIVE)
    attend = jax.nn.softmax(scores, axis=-1)
    attend_low = attend.astype(jnp.bfloat16)
    mixed = jnp.einsum(
        "nhqk,nkhe->nqhe", attend_low, value_rows, preferred_element_type=jnp.float32
    )
    return (attend, attend_low, mixed.astype(jnp.bfloat16))


def feature_backward(queries, key_rows, value_rows, attend, attend_low, mixed_grad):
    scaling = queries.shape[-1] ** (-0.5)
    value_dots = jnp.einsum(
        "nqhe,nkhe->nhqk", mixed_grad, value_rows, preferred_element_type=jnp.float32
    )
    row_delta = jnp.sum(attend * value_dots, axis=-1, keepdims=True)
    score_grad = (attend * (value_dots - row_delta)).astype(jnp.bfloat16)
    query_grad = (
        jnp.einsum("nhqk,nkhe->nqhe", score_grad, key_rows, preferred_element_type=jnp.float32)
        * scaling
    )
    key_grad = (
        jnp.einsum("nhqk,nqhe->nkhe", score_grad, queries, preferred_element_type=jnp.float32)
        * scaling
    )
    value_grad = jnp.einsum(
        "nhqk,nqhe->nkhe", attend_low, mixed_grad, preferred_element_type=jnp.float32
    )
    return (
        query_grad.astype(jnp.bfloat16),
        key_grad.astype(jnp.bfloat16),
        value_grad.astype(jnp.bfloat16),
    )


def key_blocks_of(key_rows, value_rows):
    key_total = key_rows.shape[0]
    block_size = math.gcd(key_total, 1024)
    block_count = key_total // block_size
    tail_shape = key_rows.shape[1:]
    starts = jnp.arange(block_count, dtype=jnp.int32) * block_size
    return (
        key_rows.reshape((block_count, block_size) + tail_shape),
        value_rows.reshape((block_count, block_size) + tail_shape),
        starts,
    )


def block_scores(queries, key_block, start_row, train_count):
    scaling = queries.shape[-1] ** (-0.5)
    scores = (
        jnp.einsum("qche,kche->chqk", queries, key_block, preferred_element_type=jnp.float32)
        * scaling
    )
    open_keys = start_row + jnp.arange(key_block.shape[0], dtype=jnp.int32) < train_count
    return jnp.where(open_keys[None, None, None, :], scores, NEGATIVE)


def item_forward(queries, key_rows, value_rows, train_count):
    key_split, value_split, starts = key_blocks_of(key_rows, value_rows)
    stat_shape = (queries.shape[1], queries.shape[2], queries.shape[0])

    def max_pass(carried, packed):
        running_max, running_sum = carried
        key_block, start_row = packed
        scores = block_scores(queries, key_block, start_row, train_count)
        new_max = jnp.maximum(running_max, jnp.max(scores, axis=-1))
        running_sum = running_sum * jnp.exp(running_max - new_max) + jnp.sum(
            jnp.exp(scores - new_max[..., None]), axis=-1
        )
        return ((new_max, running_sum), None)

    start_max = jnp.full(stat_shape, NEGATIVE, jnp.float32)
    (row_max, row_sum), _ = lax.scan(
        max_pass, (start_max, jnp.zeros(stat_shape, jnp.float32)), (key_split, starts)
    )
    log_total = row_max + jnp.log(row_sum)

    def value_pass(carried, packed):
        key_block, value_block, start_row = packed
        attend = jnp.exp(
            block_scores(queries, key_block, start_row, train_count) - log_total[..., None]
        )
        added = jnp.einsum(
            "chqk,kche->qche",
            attend.astype(jnp.bfloat16),
            value_block,
            preferred_element_type=jnp.float32,
        )
        return (carried + added, None)

    item_full, _ = lax.scan(
        value_pass, jnp.zeros(queries.shape, jnp.float32), (key_split, value_split, starts)
    )
    return (log_total, item_full)


def delta_of(mixed_grad, item_full):
    return jnp.transpose(jnp.sum(mixed_grad.astype(jnp.float32) * item_full, axis=-1), (1, 2, 0))


def item_backward(queries, key_rows, value_rows, train_count, log_total, mixed_grad, item_full):
    key_split, value_split, starts = key_blocks_of(key_rows, value_rows)
    scaling = queries.shape[-1] ** (-0.5)
    row_delta = delta_of(mixed_grad, item_full)

    def back_pass(carried, packed):
        key_block, value_block, start_row = packed
        attend = jnp.exp(
            block_scores(queries, key_block, start_row, train_count) - log_total[..., None]
        )
        value_dots = jnp.einsum(
            "qche,kche->chqk", mixed_grad, value_block, preferred_element_type=jnp.float32
        )
        score_grad = (attend * (value_dots - row_delta[..., None])).astype(jnp.bfloat16)
        carried = carried + jnp.einsum(
            "chqk,kche->qche", score_grad, key_block, preferred_element_type=jnp.float32
        )
        key_grad = (
            jnp.einsum("chqk,qche->kche", score_grad, queries, preferred_element_type=jnp.float32)
            * scaling
        )
        value_grad = jnp.einsum(
            "chqk,qche->kche",
            attend.astype(jnp.bfloat16),
            mixed_grad,
            preferred_element_type=jnp.float32,
        )
        return (carried, (key_grad, value_grad))

    query_sum, (key_grads, value_grads) = lax.scan(
        back_pass, jnp.zeros(queries.shape, jnp.float32), (key_split, value_split, starts)
    )
    key_total = key_rows.shape[0]
    flat_width = queries.shape[1] * queries.shape[2] * queries.shape[3]
    return (
        query_sum * scaling,
        key_grads.reshape(key_total, flat_width),
        value_grads.reshape(key_total, flat_width),
    )


def clip_all(gradients):
    total_sq = jnp.sum(gradients[0] * gradients[0])
    for extra in gradients[1:]:
        total_sq = total_sq + jnp.sum(extra * extra)
    grad_norm = jnp.sqrt(total_sq)
    factor = jnp.minimum(1.0, CLIP_NORM / grad_norm)
    return ([gradient * factor for gradient in gradients], grad_norm)


def rotate_bank(square_grad, in_grad, out_grad, bases_small, bases_big):
    model_width = in_grad.shape[0]
    left_bases = bases_small[0:8]
    right_bases = bases_small[8:16]
    rot_square = jnp.matmul(
        jnp.swapaxes(left_bases, 1, 2),
        jnp.matmul(square_grad, right_bases, precision=HIGHEST),
        precision=HIGHEST,
    )
    rot_in = jnp.dot(
        bases_small[16].T, jnp.dot(in_grad, bases_big[0], precision=HIGHEST), precision=HIGHEST
    )
    rot_out = jnp.dot(
        bases_big[1].T, jnp.dot(out_grad, bases_small[17], precision=HIGHEST), precision=HIGHEST
    )
    return jnp.concatenate(
        [rot_square.reshape(8 * model_width, model_width), rot_in.T, rot_out], axis=0
    )


def rotate_back(step_bank, bases_small, bases_big):
    model_width = step_bank.shape[1]
    ff_width = (step_bank.shape[0] - 8 * model_width) // 2
    step_square = step_bank[: 8 * model_width].reshape(8, model_width, model_width)
    step_in = step_bank[8 * model_width : 8 * model_width + ff_width].T
    step_out = step_bank[8 * model_width + ff_width :]
    up_square = jnp.matmul(
        bases_small[0:8],
        jnp.matmul(step_square, jnp.swapaxes(bases_small[8:16], 1, 2), precision=HIGHEST),
        precision=HIGHEST,
    )
    up_in = jnp.dot(
        bases_small[16], jnp.dot(step_in, bases_big[0].T, precision=HIGHEST), precision=HIGHEST
    )
    up_out = jnp.dot(
        bases_big[1], jnp.dot(step_out, bases_small[17].T, precision=HIGHEST), precision=HIGHEST
    )
    return (up_square, up_in, up_out)


def adam_rows(gradient, first_old, second_old, step_float):
    first_new = BETA_ONE * first_old + (1.0 - BETA_ONE) * gradient
    second_new = BETA_TWO * second_old + (1.0 - BETA_TWO) * gradient * gradient
    first_hat = first_new / (1.0 - jnp.power(BETA_ONE, step_float))
    second_hat = second_new / (1.0 - jnp.power(BETA_TWO, step_float))
    return (first_new, second_new, first_hat / (jnp.sqrt(second_hat) + EPSILON))


def trusted(weight, update, over_axes):
    scaling = jnp.sqrt(jnp.mean(weight * weight, axis=over_axes, keepdims=True) + 1e-06)
    return weight - LEARN_RATE * scaling * update


def per_device(
    cells,
    feat_mask,
    train_rows,
    cotangent,
    proj_weights,
    feat_out_w,
    item_out_w,
    mlp_in,
    mlp_out,
    norm_gains,
    norm_shifts,
    bases_small,
    bases_big,
    owner_rows,
    bank_first,
    bank_second,
    norm_first,
    norm_second,
):
    rows_dev, width_dev = cells.shape
    model_width = proj_weights.shape[-1]
    head_count = HEADS
    head_dim = model_width // head_count
    cols_dev = width_dev // model_width
    col_count = lax.axis_size("cols")
    all_cols = cols_dev * col_count
    half_rows = rows_dev // col_count
    cell_count = rows_dev * cols_dev
    proj_low = proj_weights.astype(jnp.bfloat16)
    feat_qkv = jnp.concatenate([proj_low[0], proj_low[1], proj_low[2]], axis=1)
    item_qkv = jnp.concatenate([proj_low[3], proj_low[4], proj_low[5]], axis=1)
    feat_out_low = feat_out_w.astype(jnp.bfloat16)
    item_out_low = item_out_w.astype(jnp.bfloat16)
    mlp_in_cast = mlp_in.astype(jnp.bfloat16)
    mlp_out_cast = mlp_out.astype(jnp.bfloat16)
    train_count = train_rows[0]
    column_cells = lax.all_to_all(cells, "cols", split_axis=0, concat_axis=1, tiled=True)
    column_flat = column_cells.reshape(half_rows * all_cols, model_width)
    row_mask = (
        lax.dynamic_slice_in_dim(feat_mask, lax.axis_index("cols") * half_rows, half_rows, 0) > 0
    )
    feat_proj = (
        product(column_flat, feat_qkv)
        .astype(jnp.bfloat16)
        .reshape(half_rows, all_cols, 3, head_count, head_dim)
    )
    feat_query = feat_proj[:, :, 0]
    feat_key = feat_proj[:, :, 1]
    feat_value = feat_proj[:, :, 2]
    feat_attend, feat_attend_low, feat_mixed = feature_forward(
        feat_query, feat_key, feat_value, row_mask
    )
    feat_mixed_flat = feat_mixed.reshape(half_rows * all_cols, model_width)
    feat_branch = (
        product(feat_mixed_flat, feat_out_low)
        .astype(jnp.bfloat16)
        .reshape(half_rows, all_cols * model_width)
    )
    feat_back = lax.all_to_all(feat_branch, "cols", split_axis=1, concat_axis=0, tiled=True)
    inputs_flat = cells.astype(jnp.float32).reshape(cell_count, model_width)
    first_sum = inputs_flat + feat_back.astype(jnp.float32).reshape(cell_count, model_width)
    first_out, first_pull = jax.vjp(layer_norm, first_sum, norm_gains[0], norm_shifts[0])
    first_low = first_out.astype(jnp.bfloat16)
    item_proj = product(first_low, item_qkv).astype(jnp.bfloat16)
    item_query = item_proj[:, :model_width].reshape(rows_dev, cols_dev, head_count, head_dim)
    item_key = item_proj[:, model_width : 2 * model_width].reshape(rows_dev, width_dev)
    item_value = item_proj[:, 2 * model_width :].reshape(rows_dev, width_dev)
    key_rows, value_rows = (
        lax.all_gather(item_key, "rows", axis=0, tiled=True),
        lax.all_gather(item_value, "rows", axis=0, tiled=True),
    )
    key_total = key_rows.shape[0]
    key_rows = key_rows.reshape(key_total, cols_dev, head_count, head_dim)
    value_rows = value_rows.reshape(key_total, cols_dev, head_count, head_dim)
    log_total, item_full = item_forward(item_query, key_rows, value_rows, train_count)
    item_low = item_full.astype(jnp.bfloat16).reshape(cell_count, model_width)
    item_branch = product(item_low, item_out_low)
    second_sum = first_out + item_branch
    second_out, second_pull = jax.vjp(layer_norm, second_sum, norm_gains[1], norm_shifts[1])
    second_low = second_out.astype(jnp.bfloat16)
    hidden_pre = product(second_low, mlp_in_cast)
    hidden_act, gelu_pull = jax.vjp(gelu_exact, hidden_pre)
    hidden_low = hidden_act.astype(jnp.bfloat16)
    mlp_branch = product(hidden_low, mlp_out_cast)
    third_sum = second_out + mlp_branch
    third_out, third_pull = jax.vjp(layer_norm, third_sum, norm_gains[2], norm_shifts[2])
    layer_out = third_out.astype(jnp.bfloat16).reshape(rows_dev, width_dev)
    third_grad, gain_three, shift_three = third_pull(
        cotangent.astype(jnp.float32).reshape(cell_count, model_width)
    )
    branch_low = third_grad.astype(jnp.bfloat16)
    mlp_out_grad = product_left(hidden_low, branch_low)
    hidden_grad = product_right(branch_low, mlp_out_cast)
    (pre_grad,) = gelu_pull(hidden_grad)
    pre_low = pre_grad.astype(jnp.bfloat16)
    mlp_in_grad = product_left(second_low, pre_low)
    second_grad = third_grad + product_right(pre_low, mlp_in_cast)
    second_in_grad, gain_two, shift_two = second_pull(second_grad)
    item_branch_low = second_in_grad.astype(jnp.bfloat16)
    item_out_grad = product_left(item_low, item_branch_low)
    item_mixed_grad = (
        product_right(item_branch_low, item_out_low)
        .astype(jnp.bfloat16)
        .reshape(rows_dev, cols_dev, head_count, head_dim)
    )
    key_again, value_again = (
        lax.all_gather(item_key, "rows", axis=0, tiled=True),
        lax.all_gather(item_value, "rows", axis=0, tiled=True),
    )
    key_rows = key_again.reshape(key_total, cols_dev, head_count, head_dim)
    value_rows = value_again.reshape(key_total, cols_dev, head_count, head_dim)
    query_sum, key_grads, value_grads = item_backward(
        item_query, key_rows, value_rows, train_count, log_total, item_mixed_grad, item_full
    )
    key_sum, value_sum = (
        lax.psum_scatter(key_grads, "rows", scatter_dimension=0, tiled=True),
        lax.psum_scatter(value_grads, "rows", scatter_dimension=0, tiled=True),
    )
    item_grad_low = jnp.concatenate(
        [
            query_sum.astype(jnp.bfloat16).reshape(cell_count, model_width),
            key_sum.astype(jnp.bfloat16).reshape(cell_count, model_width),
            value_sum.astype(jnp.bfloat16).reshape(cell_count, model_width),
        ],
        axis=1,
    )
    item_qkv_grad = product_left(first_low, item_grad_low)
    first_grad = second_in_grad + product_right(item_grad_low, item_qkv)
    first_in_grad, gain_one, shift_one = first_pull(first_grad)
    feat_branch_grad = first_in_grad.astype(jnp.bfloat16).reshape(rows_dev, width_dev)
    column_grad = lax.all_to_all(
        feat_branch_grad, "cols", split_axis=0, concat_axis=1, tiled=True
    ).reshape(half_rows * all_cols, model_width)
    feat_out_grad = product_left(feat_mixed_flat, column_grad)
    feat_mixed_grad = (
        product_right(column_grad, feat_out_low)
        .astype(jnp.bfloat16)
        .reshape(half_rows, all_cols, head_count, head_dim)
    )
    feat_query_grad, feat_key_grad, feat_value_grad = feature_backward(
        feat_query, feat_key, feat_value, feat_attend, feat_attend_low, feat_mixed_grad
    )
    feat_grad_low = jnp.concatenate(
        [
            feat_query_grad.reshape(half_rows * all_cols, model_width),
            feat_key_grad.reshape(half_rows * all_cols, model_width),
            feat_value_grad.reshape(half_rows * all_cols, model_width),
        ],
        axis=1,
    )
    feat_qkv_grad = product_left(column_flat, feat_grad_low)
    column_in_grad = (
        product_right(feat_grad_low, feat_qkv)
        .astype(jnp.bfloat16)
        .reshape(half_rows, all_cols * model_width)
    )
    row_in_grad = lax.all_to_all(column_in_grad, "cols", split_axis=1, concat_axis=0, tiled=True)
    cells_grad = first_in_grad.reshape(rows_dev, width_dev) + row_in_grad.astype(jnp.float32)
    proj_grad = jnp.stack(
        [
            feat_qkv_grad[:, :model_width],
            feat_qkv_grad[:, model_width : 2 * model_width],
            feat_qkv_grad[:, 2 * model_width :],
            item_qkv_grad[:, :model_width],
            item_qkv_grad[:, model_width : 2 * model_width],
            item_qkv_grad[:, 2 * model_width :],
        ]
    )
    norm_grad = jnp.stack(
        [
            jnp.stack([gain_one, gain_two, gain_three]),
            jnp.stack([shift_one, shift_two, shift_three]),
        ]
    )
    proj_total, feat_total, item_total, in_total, out_total, norm_total = lax.psum(
        (proj_grad, feat_out_grad, item_out_grad, mlp_in_grad, mlp_out_grad, norm_grad),
        ("rows", "cols"),
    )
    square_grad = jnp.concatenate([proj_total, feat_total[None], item_total[None]], axis=0)
    clipped, grad_norm = clip_all([square_grad, in_total, out_total, norm_total])
    square_clip, in_clip, out_clip, norm_clip = clipped
    rot_bank = rotate_bank(square_clip, in_clip, out_clip, bases_small, bases_big)
    step_float = jnp.asarray(STEP, jnp.float32)
    slot_count = bank_first.shape[0]
    my_slots = lax.dynamic_slice_in_dim(
        owner_rows, lax.axis_index("rows") * slot_count, slot_count, 0
    )
    first_new, second_new, slot_steps = adam_rows(
        jnp.take(rot_bank, my_slots, axis=0), bank_first, bank_second, step_float
    )
    all_steps = lax.all_gather(slot_steps, "rows", axis=0, tiled=True)
    full_steps = jnp.take(all_steps, jnp.argsort(owner_rows), axis=0)
    up_square, up_in, up_out = rotate_back(full_steps, bases_small, bases_big)
    square_old = jnp.concatenate([proj_weights, feat_out_w[None], item_out_w[None]], axis=0)
    square_new = trusted(square_old, up_square, (1, 2))
    in_new = trusted(mlp_in, up_in, (0, 1))
    out_new = trusted(mlp_out, up_out, (0, 1))
    norm_old = jnp.stack([norm_gains, norm_shifts])
    norm_first_new, norm_second_new, norm_steps = adam_rows(
        norm_clip, norm_first, norm_second, step_float
    )
    norm_new = trusted(norm_old, norm_steps, (2,))
    return (
        layer_out,
        cells_grad,
        square_clip,
        in_clip,
        out_clip,
        norm_clip,
        grad_norm.reshape(1),
        first_new,
        second_new,
        square_new,
        in_new,
        out_new,
        square_new.astype(jnp.bfloat16),
        in_new.astype(jnp.bfloat16),
        out_new.astype(jnp.bfloat16),
        norm_new,
        norm_first_new,
        norm_second_new,
    )


F32 = jnp.float32
BF16 = jnp.bfloat16
MESH = pl.DeviceIdType.MESH
VMEM_BYTES = 56 * 1024 * 1024
LANES = 128
KEY_BLOCK = 256
QUERY_BLOCK = 256


def dot_nn(left, right):
    return jnp.dot(left, right, preferred_element_type=F32)


def dot_nt(left, right):
    return lax.dot_general(left, right, (((1,), (1,)), ((), ())), preferred_element_type=F32)


def dot_tn(left, right):
    return lax.dot_general(left, right, (((0,), (0,)), ((), ())), preferred_element_type=F32)


def split_two(value):
    high = value.astype(BF16)
    return high, (value - high.astype(F32)).astype(BF16)


def dot_fine(dot, left, right):
    left_high, left_low = split_two(left)
    right_high, right_low = split_two(right)
    return dot(left_high, right_high) + (dot(left_high, right_low) + dot(left_low, right_high))


def stack_columns(packed, width):
    count = packed.shape[1] // width
    return jnp.concatenate([packed[:, n * width : (n + 1) * width] for n in range(count)], axis=0)


def pack_columns(stacked, rows):
    count = stacked.shape[0] // rows
    return jnp.concatenate([stacked[n * rows : (n + 1) * rows] for n in range(count)], axis=1)


def norm_parts(hidden):
    width = hidden.shape[1]
    center = jnp.sum(hidden, axis=1, keepdims=True) * (1.0 / width)
    centered = hidden - center
    spread = jnp.sum(centered * centered, axis=1, keepdims=True) * (1.0 / width)
    root = lax.rsqrt(spread + 1e-05)
    return centered * root, root


def norm_back(unit, root, gain, incoming):
    width = unit.shape[1]
    scaled = incoming * gain
    mean_one = jnp.sum(scaled, axis=1, keepdims=True) * (1.0 / width)
    mean_two = jnp.sum(scaled * unit, axis=1, keepdims=True) * (1.0 / width)
    gain_grad = jnp.sum(incoming * unit, axis=0, keepdims=True)
    shift_grad = jnp.sum(incoming, axis=0, keepdims=True)
    return root * (scaled - mean_one - unit * mean_two), gain_grad, shift_grad


def head_table(width, head_dim):
    feature = lax.broadcasted_iota(jnp.int32, (width, LANES), 0)
    head = lax.broadcasted_iota(jnp.int32, (width, LANES), 1)
    inside = (feature >= head * head_dim) & (feature < (head + 1) * head_dim)
    return jnp.where(inside, 1.0, 0.0).astype(BF16)


def spread_table(width, head_dim):
    head = lax.broadcasted_iota(jnp.int32, (LANES, width), 0)
    feature = lax.broadcasted_iota(jnp.int32, (LANES, width), 1)
    inside = (feature >= head * head_dim) & (feature < (head + 1) * head_dim)
    return jnp.where(inside, 1.0, 0.0).astype(BF16)


def head_sums(value, table):
    high, low = split_two(value)
    return dot_nn(high, table) + dot_nn(low, table)


def head_mask(rows, width, head_dim, head, offset=0):
    feature = lax.broadcasted_iota(jnp.int32, (rows, width), 1)
    start = offset + head * head_dim
    return (feature >= start) & (feature < start + head_dim)


def tile_rows(value, count):
    return jnp.concatenate([value] * count, axis=0)


def column_open(mask_ref, own_first, cols_dev, slot):
    table = jnp.transpose(mask_ref[...].astype(F32))
    if slot < cols_dev:
        first, second = slot, slot + cols_dev
    else:
        first, second = slot, slot - cols_dev
    picked = jnp.where(own_first, table[:, first : first + 1], table[:, second : second + 1])
    return picked > 0.0


def feature_weights(queries, key_list, open_list, repeat, table, scaling):
    scores = []
    for keys, is_open in zip(key_list, open_list):
        raw = head_sums(queries * tile_rows(keys, repeat), table) * scaling
        scores.append(jnp.where(tile_rows(is_open, repeat), raw, NEGATIVE))
    top = scores[0]
    for extra in scores[1:]:
        top = jnp.maximum(top, extra)
    grown = [jnp.exp(score - top) for score in scores]
    total = grown[0]
    for extra in grown[1:]:
        total = total + extra
    return [part / total for part in grown]


def flip(value, pattern, bits):
    out = 0
    for bit in range(bits):
        step = 1 << bit
        digit = (value // step) % 2
        out = out + step * ((1 - digit) if (pattern >> bit) & 1 else digit)
    return out


class RowGather:
    def __init__(self, pieces, send_sem, recv_sem, rows_count):
        self.pieces, self.send_sem, self.recv_sem = pieces, send_sem, recv_sem
        self.deep = rows_count // 4
        self.bits = self.deep.bit_length() - 1
        me = lax.axis_index("rows")
        self.core, self.side, self.depth = me % 2, (me // 2) % 2, me // 4
        self.sent = []

    @staticmethod
    def slots(rows_count):
        return rows_count - 1

    def place(self, depth, side, core):
        return (depth * 2 + side) * 2 + core

    def neighbours(self):
        found = [
            self.place(flip(self.depth, k, self.bits), self.side, self.core)
            for k in range(1, self.deep)
        ]
        found.append(self.place(self.depth, 1 - self.side, self.core))
        found.append(self.place(self.depth, self.side, 1 - self.core))
        return found

    def copies(self, shard, target, slot):
        return [
            pltpu.make_async_remote_copy(
                src_ref=piece(shard),
                dst_ref=piece(shard),
                send_sem=self.send_sem.at[n, slot],
                recv_sem=self.recv_sem.at[n, slot],
                device_id={"rows": target},
                device_id_type=MESH,
            )
            for n, piece in enumerate(self.pieces)
        ]

    def push(self, shard, target, slot):
        for copy in self.copies(shard, target, slot):
            copy.start()
            self.sent.append(copy)

    def arrive(self, shard, source, slot):
        for copy in self.copies(shard, source, slot):
            copy.wait_recv()

    def start(self):
        own = self.place(self.depth, self.side, self.core)
        for k in range(1, self.deep):
            self.push(own, self.place(flip(self.depth, k, self.bits), self.side, self.core), k - 1)
        self.push(own, self.place(self.depth, 1 - self.side, self.core), self.deep - 1)
        self.push(own, self.place(self.depth, self.side, 1 - self.core), 2 * self.deep - 1)

    def along_depth(self, k):
        source = flip(self.depth, k, self.bits)
        shard = self.place(source, self.side, self.core)
        self.arrive(shard, shard, k - 1)
        self.push(shard, self.place(self.depth, 1 - self.side, self.core), self.deep - 1 + k)
        self.push(shard, self.place(self.depth, self.side, 1 - self.core), 2 * self.deep - 1 + k)

    def across_side(self, k):
        source = flip(self.depth, k, self.bits)
        shard = self.place(source, 1 - self.side, self.core)
        self.arrive(shard, self.place(self.depth, 1 - self.side, self.core), self.deep - 1 + k)
        self.push(
            shard, self.place(self.depth, self.side, 1 - self.core), 3 * self.deep - 1 + k
        )

    def steps(self):
        found = [functools.partial(self.across_side, 0)]
        for k in range(1, self.deep):
            found.append(functools.partial(self.along_depth, k))
            found.append(functools.partial(self.across_side, k))
        return found

    def finish(self):
        other = self.place(self.depth, self.side, 1 - self.core)
        for k in range(self.deep):
            source = flip(self.depth, k, self.bits)
            self.arrive(self.place(source, self.side, 1 - self.core), other, 2 * self.deep - 1 + k)
            self.arrive(
                self.place(source, 1 - self.side, 1 - self.core), other, 3 * self.deep - 1 + k
            )
        for copy in self.sent:
            copy.wait_send()


def meet(targets):
    barrier = pltpu.get_barrier_semaphore()
    for target in targets:
        pl.semaphore_signal(barrier, inc=1, device_id=target, device_id_type=MESH)
    pl.semaphore_wait(barrier, len(targets))


def swap_copy(source, landing, send_sem, recv_sem):
    return pltpu.make_async_remote_copy(
        src_ref=source,
        dst_ref=landing,
        send_sem=send_sem,
        recv_sem=recv_sem,
        device_id={"cols": 1 - lax.axis_index("cols")},
        device_id_type=MESH,
    )


def first_kernel(
    rows_count,
    cells_ref,
    mask_ref,
    proj_ref,
    feat_out_ref,
    gains_ref,
    shifts_ref,
    peer_ref,
    first_sum_ref,
    mixed_ref,
    gathered_ref,
    swap_send,
    swap_recv,
    send_sem,
    recv_sem,
):
    rows_dev, width_dev = cells_ref.shape
    width = feat_out_ref.shape[0]
    cols_dev = width_dev // width
    head_dim = width // HEADS
    scaling = head_dim ** (-0.5)

    def shard_view(shard):
        return gathered_ref.at[pl.ds(pl.multiple_of(shard * rows_dev, rows_dev), rows_dev), :]

    gather = RowGather([shard_view], send_sem, recv_sem, rows_count)
    meet(
        [{"rows": row} for row in gather.neighbours()]
        + [{"cols": 1 - lax.axis_index("cols")}]
    )
    swap = swap_copy(cells_ref, peer_ref, swap_send, swap_recv)
    swap.start()
    query_w, key_w, value_w = [proj_ref[n].astype(BF16) for n in range(3)]
    own = stack_columns(cells_ref[...].astype(F32), width)
    own_low = own.astype(BF16)
    queries = dot_nn(own_low, query_w).astype(BF16).astype(F32)
    table = head_table(width, head_dim)
    wide = spread_table(width, head_dim)
    own_keys = dot_nn(own_low, key_w).astype(BF16).astype(F32)
    own_values = dot_nn(own_low, value_w).astype(BF16).astype(F32)
    swap.wait()
    peer_low = stack_columns(peer_ref[...].astype(F32), width).astype(BF16)
    peer_keys = dot_nn(peer_low, key_w).astype(BF16).astype(F32)
    peer_values = dot_nn(peer_low, value_w).astype(BF16).astype(F32)
    all_keys = jnp.concatenate([own_keys, peer_keys], axis=0)
    all_values = jnp.concatenate([own_values, peer_values], axis=0)
    slots = all_keys.shape[0] // rows_dev
    own_first = lax.axis_index("cols") == 0
    key_list = [all_keys[n * rows_dev : (n + 1) * rows_dev] for n in range(slots)]
    value_list = [all_values[n * rows_dev : (n + 1) * rows_dev] for n in range(slots)]
    open_list = [column_open(mask_ref, own_first, cols_dev, n) for n in range(slots)]
    weights = feature_weights(queries, key_list, open_list, cols_dev, table, scaling)
    mixed = None
    for weight, values in zip(weights, value_list):
        added = dot_nn(weight.astype(BF16), wide) * tile_rows(values, cols_dev)
        mixed = added if mixed is None else mixed + added
    mixed_low = mixed.astype(BF16)
    mixed_ref[...] = mixed_low
    branch = dot_nn(mixed_low, feat_out_ref[...].astype(BF16)).astype(BF16).astype(F32)
    first_sum = own + branch
    first_sum_ref[...] = first_sum
    unit, _ = norm_parts(first_sum)
    first_out = unit * gains_ref[0:1, :] + shifts_ref[0:1, :]
    packed = pack_columns(first_out, rows_dev).astype(BF16)
    me = lax.axis_index("rows")
    gathered_ref[pl.ds(pl.multiple_of(me * rows_dev, rows_dev), rows_dev), :] = packed
    gather.start()
    for step in gather.steps():
        step()
    gather.finish()


def window_of(column, width, width_dev):
    start = (column * width) // LANES * LANES
    offset = column * width - start
    size = -(-(offset + width) // LANES) * LANES
    return start, offset, min(size, width_dev - start)


def padded_weight(weight, offset, size):
    width = weight.shape[1]
    parts = []
    if offset:
        parts.append(jnp.zeros((offset, width), F32))
    parts.append(weight)
    if size - offset - weight.shape[0]:
        parts.append(jnp.zeros((size - offset - weight.shape[0], width), F32))
    return (jnp.concatenate(parts, axis=0) if len(parts) > 1 else weight).astype(BF16)


def head_blocks(value, head_dim, offset=0, size=None):
    rows, width = value.shape
    if size is not None and size != width:
        parts = []
        if offset:
            parts.append(jnp.zeros((rows, offset), F32))
        parts.append(value)
        if size - offset - width:
            parts.append(jnp.zeros((rows, size - offset - width), F32))
        value = jnp.concatenate(parts, axis=1)
        width = size
    blocks = [
        jnp.where(head_mask(rows, width, head_dim, head, offset), value, 0.0).astype(BF16)
        for head in range(HEADS)
    ]
    return jnp.concatenate(blocks, axis=0)


def gather_heads(value, rows, head_dim, offset=0, width=None):
    total = None
    for head in range(HEADS):
        block = value[head * rows : (head + 1) * rows]
        kept = jnp.where(head_mask(rows, value.shape[1], head_dim, head, offset), block, 0.0)
        total = kept if total is None else total + kept
    if width is not None and width != total.shape[1]:
        total = total[:, offset : offset + width]
    return total


def second_kernel(
    train_ref,
    gathered_ref,
    first_sum_ref,
    proj_ref,
    item_out_ref,
    mlp_in_ref,
    mlp_out_ref,
    gains_ref,
    shifts_ref,
    cotangent_ref,
    layer_ref,
    mixed_grad_ref,
    stats_ref,
    stats_wide_ref,
    second_grad_ref,
    keys_ref,
    values_ref,
    weight_grads_ref,
    norm_grads_ref,
    blocks_ref,
    top_ref,
    sum_ref,
    total_ref,
):
    rows_dev, width_dev = cotangent_ref.shape
    width = item_out_ref.shape[0]
    cols_dev = width_dev // width
    head_dim = width // HEADS
    scaling = head_dim ** (-0.5)
    key_total = keys_ref.shape[1]
    train_count = train_ref[0]
    block_count = (train_count + KEY_BLOCK - 1) // KEY_BLOCK
    table = head_table(width, head_dim)

    unit_one, _ = norm_parts(first_sum_ref[...])
    first_out = unit_one * gains_ref[0:1, :] + shifts_ref[0:1, :]
    first_low = first_out.astype(BF16)
    queries = dot_nn(first_low, proj_ref[3].astype(BF16)).astype(BF16).astype(F32)

    item_full = []
    lane = lax.broadcasted_iota(jnp.int32, (rows_dev, LANES), 1)
    stats = []
    for column in range(cols_dev):
        start, offset, size = window_of(column, width, width_dev)
        key_w = padded_weight(proj_ref[4], offset, size)
        value_w = padded_weight(proj_ref[5], offset, size)
        blocks_ref[...] = head_blocks(
            queries[column * rows_dev : (column + 1) * rows_dev], head_dim
        )
        top_ref[...] = jnp.full(top_ref.shape, NEGATIVE, F32)
        sum_ref[...] = jnp.zeros(sum_ref.shape, F32)
        total_ref[...] = jnp.zeros(total_ref.shape, F32)

        @pl.loop(0, key_total // KEY_BLOCK)
        def _(step):
            span = pl.ds(pl.multiple_of(step * KEY_BLOCK, KEY_BLOCK), KEY_BLOCK)
            hidden = gathered_ref[span, start : start + size]
            keys_ref[column, span, :] = dot_nn(hidden, key_w).astype(BF16)
            values_ref[column, span, :] = dot_nn(hidden, value_w).astype(BF16)

        @pl.loop(0, block_count)
        def _(step):
            span = pl.ds(pl.multiple_of(step * KEY_BLOCK, KEY_BLOCK), KEY_BLOCK)
            scores = dot_nt(blocks_ref[...], keys_ref[column, span, :]) * scaling
            key_row = step * KEY_BLOCK + lax.broadcasted_iota(jnp.int32, (1, KEY_BLOCK), 1)
            scores = jnp.where(key_row < train_count, scores, NEGATIVE)
            top_old = top_ref[...]
            top_new = jnp.maximum(top_old, jnp.max(scores, axis=1, keepdims=True))
            grown = jnp.exp(scores - top_new)
            fade = jnp.exp(top_old - top_new)
            top_ref[...] = top_new
            sum_ref[...] = sum_ref[...] * fade + jnp.sum(grown, axis=1, keepdims=True)
            total_ref[...] = total_ref[...] * fade + dot_nn(
                grown.astype(BF16), values_ref[column, span, :]
            )

        item_full.append(
            gather_heads(total_ref[...] / sum_ref[...], rows_dev, head_dim)
        )
        log_total = top_ref[...] + jnp.log(sum_ref[...])
        stat = jnp.zeros((rows_dev, LANES), F32)
        for head in range(HEADS):
            stat = jnp.where(
                lane == head, log_total[head * rows_dev : (head + 1) * rows_dev], stat
            )
        stats.append(stat)

    full = jnp.concatenate(item_full, axis=0)
    item_low = full.astype(BF16)
    item_out_w = item_out_ref[...].astype(BF16)
    mlp_in_w = mlp_in_ref[...].astype(BF16)
    mlp_out_w = mlp_out_ref[...].astype(BF16)
    unit_two, root_two = norm_parts(first_out + dot_nn(item_low, item_out_w))
    second_out = unit_two * gains_ref[1:2, :] + shifts_ref[1:2, :]
    second_low = second_out.astype(BF16)
    hidden_pre = dot_nn(second_low, mlp_in_w)
    normal = 0.5 + 0.5 * lax.erf(hidden_pre * (0.5**0.5))
    hidden_low = (hidden_pre * normal).astype(BF16)
    unit_three, root_three = norm_parts(second_out + dot_nt(hidden_low, mlp_out_w))
    third_out = unit_three * gains_ref[2:3, :] + shifts_ref[2:3, :]
    layer_ref[...] = pack_columns(third_out, rows_dev).astype(BF16)

    incoming = stack_columns(cotangent_ref[...].astype(F32), width)
    third_grad, gain_three, shift_three = norm_back(
        unit_three, root_three, gains_ref[2:3, :], incoming
    )
    branch_low = third_grad.astype(BF16)
    ff_width = mlp_in_w.shape[1]
    weight_grads_ref[width + ff_width : width + 2 * ff_width, :] = dot_tn(hidden_low, branch_low)
    density = jnp.exp(-0.5 * hidden_pre * hidden_pre) * (1.0 / math.sqrt(2.0 * math.pi))
    pre_low = (dot_nn(branch_low, mlp_out_w) * (normal + hidden_pre * density)).astype(BF16)
    weight_grads_ref[width : width + ff_width, :] = dot_tn(pre_low, second_low)
    second_grad, gain_two, shift_two = norm_back(
        unit_two, root_two, gains_ref[1:2, :], third_grad + dot_nt(pre_low, mlp_in_w)
    )
    second_grad_ref[...] = second_grad
    second_grad_low = second_grad.astype(BF16)
    weight_grads_ref[0:width, :] = dot_tn(item_low, second_grad_low)
    mixed_grad = dot_nt(second_grad_low, item_out_w).astype(BF16)
    mixed_grad_wide = mixed_grad.astype(F32)
    mixed_grad_ref[...] = pack_columns(mixed_grad_wide, rows_dev).astype(BF16)
    delta = head_sums(mixed_grad_wide * full, table)
    norm_grads_ref[...] = jnp.concatenate(
        [jnp.zeros_like(gain_two), gain_two, gain_three, jnp.zeros_like(gain_two), shift_two, shift_three]
        + [jnp.zeros_like(gain_two)] * (norm_grads_ref.shape[0] - 6),
        axis=0,
    )
    for column in range(cols_dev):
        stat = stats[column]
        part = delta[column * rows_dev : (column + 1) * rows_dev]
        for head in range(HEADS):
            stat = jnp.where(lane == 8 + head, part[:, head : head + 1], stat)
        stats_wide_ref[column] = stat
        stats_ref[16 * column : 16 * (column + 1), :] = jnp.transpose(stat)[0:16, :]


def third_kernel(
    rows_count,
    train_ref,
    cells_ref,
    peer_ref,
    mask_ref,
    proj_ref,
    feat_out_ref,
    gains_ref,
    shifts_ref,
    first_sum_ref,
    feat_mixed_ref,
    gathered_ref,
    keys_ref,
    values_ref,
    mixed_grad_ref,
    stats_ref,
    stats_wide_ref,
    second_grad_ref,
    cells_grad_ref,
    weight_grads_ref,
    norm_grads_ref,
    grads_ref,
    all_stats_ref,
    blocks_ref,
    grad_blocks_ref,
    total_ref,
    value_total_ref,
    branch_ref,
    peer_branch_ref,
    swap_send,
    swap_recv,
    send_sem,
    recv_sem,
):
    rows_dev, width_dev = cells_ref.shape
    width = feat_out_ref.shape[0]
    cols_dev = width_dev // width
    head_dim = width // HEADS
    scaling = head_dim ** (-0.5)
    key_total = keys_ref.shape[1]
    query_total = gathered_ref.shape[0]
    train_count = train_ref[0]
    me = lax.axis_index("rows")

    def grads_view(shard):
        return grads_ref.at[pl.ds(pl.multiple_of(shard * rows_dev, rows_dev), rows_dev), :]

    def stats_view(shard):
        return all_stats_ref.at[:, pl.ds(pl.multiple_of(shard * rows_dev, rows_dev), rows_dev)]

    gather = RowGather([grads_view, stats_view], send_sem, recv_sem, rows_count)
    own_rows = pl.ds(pl.multiple_of(me * rows_dev, rows_dev), rows_dev)
    grads_ref[own_rows, :] = mixed_grad_ref[...]
    all_stats_ref[:, own_rows] = stats_ref[...]
    meet(
        [{"rows": row} for row in gather.neighbours()]
        + [{"cols": 1 - lax.axis_index("cols")}]
    )
    gather.start()

    unit_one, root_one = norm_parts(first_sum_ref[...])
    first_out = unit_one * gains_ref[0:1, :] + shifts_ref[0:1, :]
    first_low = first_out.astype(BF16)
    item_w = [proj_ref[3 + n].astype(BF16) for n in range(3)]
    queries, own_keys, own_values = [
        dot_nn(first_low, weight).astype(BF16).astype(F32) for weight in item_w
    ]
    own_grad = stack_columns(mixed_grad_ref[...].astype(F32), width)

    pending = gather.steps()

    def forward_some(count):
        for _ in range(min(count, len(pending))):
            pending.pop(0)()

    query_grads = []
    for column in range(cols_dev):
        rows_here = slice(column * rows_dev, (column + 1) * rows_dev)
        blocks_ref[...] = head_blocks(queries[rows_here], head_dim)
        grad_blocks_ref[:, 0:width] = head_blocks(own_grad[rows_here], head_dim)
        stat = stats_wide_ref[column]
        log_total = jnp.concatenate([stat[:, h : h + 1] for h in range(HEADS)], axis=0)
        delta = jnp.concatenate([stat[:, 8 + h : 9 + h] for h in range(HEADS)], axis=0)
        total_ref[...] = jnp.zeros(total_ref.shape, F32)
        half = key_total // KEY_BLOCK // 2
        for first, last in ((0, half), (half, key_total // KEY_BLOCK)):

            @pl.loop(first, last)
            def _(step):
                span = pl.ds(pl.multiple_of(step * KEY_BLOCK, KEY_BLOCK), KEY_BLOCK)
                keys = keys_ref[column, span, :]
                scores = dot_nt(blocks_ref[...], keys) * scaling
                key_row = step * KEY_BLOCK + lax.broadcasted_iota(jnp.int32, (1, KEY_BLOCK), 1)
                scores = jnp.where(key_row < train_count, scores, NEGATIVE)
                attend = jnp.exp(scores - log_total)
                dots = dot_nt(grad_blocks_ref[:, 0:width], values_ref[column, span, :])
                score_grad = (attend * (dots - delta)).astype(BF16)
                total_ref[...] += dot_nn(score_grad, keys)

            forward_some(2)
        query_grads.append(gather_heads(total_ref[...], rows_dev, head_dim) * scaling)
    forward_some(len(pending))
    gather.finish()

    key_grads, value_grads = [], []
    own_row = me * rows_dev + lax.broadcasted_iota(jnp.int32, (rows_dev, 1), 0)
    own_open = tile_rows(own_row, HEADS) < train_count
    for column in range(cols_dev):
        rows_here = slice(column * rows_dev, (column + 1) * rows_dev)
        start, offset, size = window_of(column, width, width_dev)
        query_w = padded_weight(proj_ref[3], offset, size)
        blocks_ref[...] = head_blocks(own_keys[rows_here], head_dim)
        grad_blocks_ref[:, 0:size] = head_blocks(own_values[rows_here], head_dim, offset, size)
        total_ref[...] = jnp.zeros(total_ref.shape, F32)
        value_total_ref[:, 0:size] = jnp.zeros((value_total_ref.shape[0], size), F32)

        @pl.loop(0, query_total // QUERY_BLOCK)
        def _(step):
            span = pl.ds(pl.multiple_of(step * QUERY_BLOCK, QUERY_BLOCK), QUERY_BLOCK)
            block = dot_nn(gathered_ref[span, start : start + size], query_w).astype(BF16)
            grads = grads_ref[span, start : start + size]
            scores = dot_nt(blocks_ref[...], block) * scaling
            dots = dot_nt(grad_blocks_ref[:, 0:size], grads)
            attends, score_grads = [], []
            for head in range(HEADS):
                part = slice(head * rows_dev, (head + 1) * rows_dev)
                log_total = all_stats_ref[16 * column + head : 16 * column + head + 1, span]
                delta = all_stats_ref[16 * column + 8 + head : 16 * column + 9 + head, span]
                attend = jnp.exp(
                    jnp.where(own_open[part], scores[part], NEGATIVE) - log_total
                )
                attends.append(attend.astype(BF16))
                score_grads.append((attend * (dots[part] - delta)).astype(BF16))
            total_ref[...] += dot_nn(jnp.concatenate(score_grads, axis=0), block)
            value_total_ref[:, 0:size] += dot_nn(jnp.concatenate(attends, axis=0), grads)

        key_grads.append(gather_heads(total_ref[...], rows_dev, head_dim) * scaling)
        value_grads.append(
            gather_heads(value_total_ref[:, 0:size], rows_dev, head_dim, offset, width)
        )
    item_grads = [
        jnp.concatenate(parts, axis=0).astype(BF16)
        for parts in (query_grads, key_grads, value_grads)
    ]
    first_grad = second_grad_ref[...]
    for n in range(3):
        first_grad = first_grad + dot_nt(item_grads[n], item_w[n])
    first_in_grad, gain_one, shift_one = norm_back(
        unit_one, root_one, gains_ref[0:1, :], first_grad
    )
    norm_grads_ref[...] = jnp.concatenate([gain_one, shift_one] + [jnp.zeros_like(gain_one)] * 6, axis=0)
    branch_ref[...] = pack_columns(first_in_grad, rows_dev).astype(BF16)
    swap = swap_copy(branch_ref, peer_branch_ref, swap_send, swap_recv)
    swap.start()
    for n in range(3):
        weight_grads_ref[(3 + n) * width : (4 + n) * width, :] = dot_tn(first_low, item_grads[n])

    feat_w = [proj_ref[n].astype(BF16) for n in range(3)]
    own_low = stack_columns(cells_ref[...].astype(F32), width).astype(BF16)
    all_low = jnp.concatenate(
        [own_low, stack_columns(peer_ref[...].astype(F32), width).astype(BF16)], axis=0
    )
    feat_query, feat_key, feat_value = [
        dot_nn(all_low, weight).astype(BF16).astype(F32) for weight in feat_w
    ]
    slots = all_low.shape[0] // rows_dev
    own_first = lax.axis_index("cols") == 0
    feat_table = head_table(width, head_dim)
    wide = spread_table(width, head_dim)
    key_list = [feat_key[n * rows_dev : (n + 1) * rows_dev] for n in range(slots)]
    value_list = [feat_value[n * rows_dev : (n + 1) * rows_dev] for n in range(slots)]
    open_list = [column_open(mask_ref, own_first, cols_dev, n) for n in range(slots)]
    weights = feature_weights(feat_query, key_list, open_list, slots, feat_table, scaling)
    own_branch = first_in_grad.astype(BF16)
    weight_grads_ref[6 * width : 7 * width, :] = dot_tn(feat_mixed_ref[...], own_branch)
    swap.wait()
    peer_branch = stack_columns(peer_branch_ref[...].astype(F32), width).astype(BF16)
    all_branch = jnp.concatenate([own_branch, peer_branch], axis=0)
    feat_grad = dot_nt(all_branch, feat_out_ref[...].astype(BF16)).astype(BF16).astype(F32)
    dots = [head_sums(feat_grad * tile_rows(values, slots), feat_table) for values in value_list]
    row_delta = None
    for weight, dot in zip(weights, dots):
        added = weight * dot
        row_delta = added if row_delta is None else row_delta + added
    score_grads = [
        (weight * (dot - row_delta)).astype(BF16) for weight, dot in zip(weights, dots)
    ]
    own_count = cols_dev * rows_dev
    query_grad = None
    for score_grad, keys in zip(score_grads, key_list):
        added = dot_nn(score_grad[:own_count], wide) * tile_rows(keys, cols_dev)
        query_grad = added if query_grad is None else query_grad + added
    key_parts, value_parts = [], []
    for column in range(cols_dev):
        key_products = dot_nn(score_grads[column], wide) * feat_query
        value_products = dot_nn(weights[column].astype(BF16), wide) * feat_grad
        key_sum = key_products[:rows_dev]
        value_sum = value_products[:rows_dev]
        for n in range(1, slots):
            key_sum = key_sum + key_products[n * rows_dev : (n + 1) * rows_dev]
            value_sum = value_sum + value_products[n * rows_dev : (n + 1) * rows_dev]
        key_parts.append(key_sum)
        value_parts.append(value_sum)
    feat_grads = [
        (query_grad * scaling).astype(BF16),
        (jnp.concatenate(key_parts, axis=0) * scaling).astype(BF16),
        jnp.concatenate(value_parts, axis=0).astype(BF16),
    ]
    inner = None
    for n in range(3):
        weight_grads_ref[n * width : (n + 1) * width, :] = dot_tn(own_low, feat_grads[n])
        added = dot_nt(feat_grads[n], feat_w[n])
        inner = added if inner is None else inner + added
    cells_grad_ref[...] = pack_columns(first_in_grad + inner.astype(BF16).astype(F32), rows_dev)


def sum_kernel(
    rows_count,
    cols_count,
    block,
    late_ref,
    early_ref,
    late_norm_ref,
    early_norm_ref,
    total_ref,
    low_ref,
    other_ref,
    half_ref,
    parts_ref,
    result_ref,
    core_send,
    core_recv,
    part_send,
    part_recv,
    back_send,
    back_recv,
):
    chips = rows_count // 2 * cols_count
    row, col = lax.axis_index("rows"), lax.axis_index("cols")
    core = row % 2
    chip = (row // 2) * cols_count + col
    half_rows = chips * block
    width = late_ref.shape[1]

    def device(number):
        return {"rows": (number // cols_count) * 2 + core, "cols": number % cols_count}

    twin = {"rows": row + 1 - 2 * core}
    meet([device((chip + k) % chips) for k in range(1, chips)] + [twin])

    late, early = late_ref.shape[0], early_ref.shape[0]
    low_ref[0:late, :] = late_ref[...].astype(BF16)
    low_ref[late : late + early, :] = early_ref[...].astype(BF16)
    norms = early_norm_ref[...]
    zero = jnp.zeros((1, width), F32)
    zeros = [zero] * (norms.shape[0] - 4)
    mine = jnp.concatenate(
        [late_norm_ref[0:1, :], zero, zero, late_norm_ref[1:2, :]] + zeros, axis=0
    )
    low_ref[late + early : late + early + norms.shape[0], :] = (norms + mine).astype(BF16)
    rest = low_ref.shape[0] - late - early - norms.shape[0]
    if rest:
        low_ref[late + early + norms.shape[0] :, :] = jnp.zeros((rest, width), BF16)

    def half_of(which):
        return pl.ds(pl.multiple_of(which * half_rows, block), half_rows)

    exchange = pltpu.make_async_remote_copy(
        src_ref=low_ref.at[half_of(1 - core), :],
        dst_ref=other_ref,
        send_sem=core_send.at[0],
        recv_sem=core_recv.at[0],
        device_id=twin,
        device_id_type=MESH,
    )
    exchange.start()
    exchange.wait()
    half_ref[...] = (
        low_ref[half_of(core), :].astype(F32) + other_ref[...].astype(F32)
    ).astype(BF16)

    def block_of(number):
        return pl.ds(pl.multiple_of(number * block, block), block)

    copies = []
    for k in range(1, chips):
        target = (chip + k) % chips
        copy = pltpu.make_async_remote_copy(
            src_ref=half_ref.at[block_of(target), :],
            dst_ref=parts_ref.at[k - 1],
            send_sem=part_send.at[k - 1],
            recv_sem=part_recv.at[k - 1],
            device_id=device(target),
            device_id_type=MESH,
        )
        copy.start()
        copies.append(copy)
    total = half_ref[block_of(chip), :].astype(F32)
    for k in range(1, chips):
        copies[k - 1].wait_recv()
        total = total + parts_ref[k - 1].astype(F32)
    for copy in copies:
        copy.wait_send()
    mine_rows = pl.ds(pl.multiple_of(core * half_rows + chip * block, block), block)
    result_ref[mine_rows, :] = total.astype(BF16)
    copies = []
    for k in range(1, chips):
        copy = pltpu.make_async_remote_copy(
            src_ref=result_ref.at[mine_rows, :],
            dst_ref=result_ref.at[mine_rows, :],
            send_sem=back_send.at[k - 1],
            recv_sem=back_recv.at[k - 1],
            device_id=device((chip + k) % chips),
            device_id_type=MESH,
        )
        copy.start()
        copies.append(copy)
    for k in range(1, chips):
        source = (chip + chips - k) % chips
        rows_there = pl.ds(pl.multiple_of(core * half_rows + source * block, block), block)
        pltpu.make_async_remote_copy(
            src_ref=result_ref.at[rows_there, :],
            dst_ref=result_ref.at[rows_there, :],
            send_sem=back_send.at[k - 1],
            recv_sem=back_recv.at[k - 1],
            device_id=device((chip + k) % chips),
            device_id_type=MESH,
        ).wait_recv()
    for copy in copies:
        copy.wait_send()
    back = pltpu.make_async_remote_copy(
        src_ref=result_ref.at[half_of(core), :],
        dst_ref=result_ref.at[half_of(core), :],
        send_sem=core_send.at[1],
        recv_sem=core_recv.at[1],
        device_id=twin,
        device_id_type=MESH,
    )
    back.start()
    pltpu.make_async_remote_copy(
        src_ref=result_ref.at[half_of(1 - core), :],
        dst_ref=result_ref.at[half_of(1 - core), :],
        send_sem=core_send.at[1],
        recv_sem=core_recv.at[1],
        device_id=twin,
        device_id_type=MESH,
    ).wait_recv()
    back.wait_send()
    total_ref[...] = result_ref[...].astype(F32)


def moment_rule(gradient, first_old, second_old):
    first_new = BETA_ONE * first_old + (1.0 - BETA_ONE) * gradient
    second_new = BETA_TWO * second_old + (1.0 - BETA_TWO) * gradient * gradient
    first_hat = first_new * (1.0 / (1.0 - BETA_ONE**STEP))
    second_hat = second_new * (1.0 / (1.0 - BETA_TWO**STEP))
    return first_new, second_new, first_hat / (jnp.sqrt(second_hat) + EPSILON)


def root_mean(value):
    count = value.shape[0] * value.shape[1]
    square = jnp.sum(jnp.sum(value * value, axis=1, keepdims=True), axis=0, keepdims=True)
    return jnp.sqrt(square * (1.0 / count) + 1e-06)


def update_kernel(
    owner_ref,
    total_ref,
    small_ref,
    big_ref,
    first_ref,
    second_ref,
    all_first_ref,
    all_second_ref,
    proj_ref,
    feat_out_ref,
    item_out_ref,
    mlp_in_ref,
    mlp_out_ref,
    gains_ref,
    shifts_ref,
    norm_first_ref,
    norm_second_ref,
    square_grad_ref,
    in_grad_ref,
    out_grad_ref,
    norm_grad_ref,
    clip_ref,
    first_new_ref,
    second_new_ref,
    square_new_ref,
    in_new_ref,
    out_new_ref,
    square_low_ref,
    in_low_ref,
    out_low_ref,
    norm_new_ref,
    norm_first_new_ref,
    norm_second_new_ref,
    sorted_first_ref,
    sorted_second_ref,
    rotated_ref,
    own_ref,
):
    bank_rows, width = all_first_ref.shape
    ff_width = mlp_in_ref.shape[1]
    slots = first_ref.shape[0]
    squares = 8

    @pl.loop(0, bank_rows // 8)
    def _(step):
        for n in range(8):
            slot = step * 8 + n
            row = owner_ref[slot]
            sorted_first_ref[pl.ds(row, 1), :] = all_first_ref[pl.ds(slot, 1), :]
            sorted_second_ref[pl.ds(row, 1), :] = all_second_ref[pl.ds(slot, 1), :]

    everything = total_ref[...]
    square = jnp.sum(
        jnp.sum(everything * everything, axis=1, keepdims=True), axis=0, keepdims=True
    )
    grad_norm = jnp.sqrt(square)
    factor = jnp.minimum(1.0, CLIP_NORM / grad_norm)
    clip_ref[0] = grad_norm[0, 0]

    for n in range(squares):
        clipped = total_ref[n * width : (n + 1) * width, :] * factor
        square_grad_ref[n] = clipped
        turned = dot_fine(dot_nn, clipped, small_ref[8 + n])
        rotated_ref[n * width : (n + 1) * width, :] = dot_fine(dot_tn, small_ref[n], turned)
    start = squares * width
    clipped = total_ref[start : start + ff_width, :] * factor
    in_grad_ref[...] = jnp.transpose(clipped)
    turned = dot_fine(dot_nn, clipped, small_ref[16])
    rotated_ref[start : start + ff_width, :] = dot_fine(dot_tn, big_ref[0], turned)
    middle = start + ff_width
    clipped = total_ref[middle : middle + ff_width, :] * factor
    out_grad_ref[...] = jnp.transpose(clipped)
    turned = dot_fine(dot_nn, clipped, small_ref[17])
    rotated_ref[middle : middle + ff_width, :] = dot_fine(dot_tn, big_ref[1], turned)

    base = lax.axis_index("rows") * slots

    @pl.loop(0, slots // 8)
    def _(step):
        for n in range(8):
            row = owner_ref[base + step * 8 + n]
            own_ref[pl.ds(step * 8 + n, 1), :] = rotated_ref[pl.ds(row, 1), :]

    first_new, second_new, _ = moment_rule(own_ref[...], first_ref[...], second_ref[...])
    first_new_ref[...] = first_new
    second_new_ref[...] = second_new

    def step_of(first_row, count):
        rows = slice(first_row, first_row + count)
        return moment_rule(
            rotated_ref[rows, :], sorted_first_ref[rows, :], sorted_second_ref[rows, :]
        )[2]

    def old_square(n):
        if n < 6:
            return proj_ref[n]
        return feat_out_ref[...] if n == 6 else item_out_ref[...]

    for n in range(squares):
        turned = dot_fine(dot_nt, step_of(n * width, width), small_ref[8 + n])
        update = dot_fine(dot_nn, small_ref[n], turned)
        old = old_square(n)
        new = old - LEARN_RATE * root_mean(old) * update
        square_new_ref[n] = new
        square_low_ref[n] = new.astype(BF16)
    turned = dot_fine(dot_nn, big_ref[0], step_of(start, ff_width))
    update = dot_fine(dot_nt, small_ref[16], turned)
    new = mlp_in_ref[...] - LEARN_RATE * root_mean(mlp_in_ref[...]) * update
    in_new_ref[...] = new
    in_low_ref[...] = new.astype(BF16)
    turned = dot_fine(dot_nt, step_of(middle, ff_width), small_ref[17])
    update = dot_fine(dot_nn, big_ref[1], turned)
    new = mlp_out_ref[...] - LEARN_RATE * root_mean(mlp_out_ref[...]) * jnp.transpose(update)
    out_new_ref[...] = new
    out_low_ref[...] = new.astype(BF16)

    last = middle + ff_width
    clipped = total_ref[last : last + 8, :] * factor
    for n in range(3):
        both = jnp.concatenate([clipped[n : n + 1], clipped[3 + n : 4 + n]], axis=0)
        norm_grad_ref[n] = both
        first_new, second_new, change = moment_rule(both, norm_first_ref[n], norm_second_ref[n])
        norm_first_new_ref[n] = first_new
        norm_second_new_ref[n] = second_new
        old = jnp.concatenate([gains_ref[n : n + 1, :], shifts_ref[n : n + 1, :]], axis=0)
        size = jnp.sqrt(jnp.sum(old * old, axis=1, keepdims=True) * (1.0 / width) + 1e-06)
        norm_new_ref[n] = old - LEARN_RATE * size * change


def in_vmem():
    return pl.BlockSpec(memory_space=pltpu.VMEM)


def in_smem():
    return pl.BlockSpec(memory_space=pltpu.SMEM)


def fast_device(
    cells,
    feat_mask,
    train_rows,
    cotangent,
    proj_weights,
    feat_out_w,
    item_out_w,
    mlp_in,
    mlp_out,
    norm_gains,
    norm_shifts,
    bases_small,
    bases_big,
    owner_rows,
    bank_first,
    bank_second,
    norm_first,
    norm_second,
):
    rows_count, cols_count = lax.axis_size("rows"), lax.axis_size("cols")
    rows_dev, width_dev = cells.shape
    width = proj_weights.shape[-1]
    ff_width = mlp_in.shape[1]
    cols_dev = width_dev // width
    own_cells = rows_dev * cols_dev
    rows_all = rows_dev * rows_count
    key_total = rows_all // 4 * 3
    head_rows = HEADS * rows_dev
    slots = RowGather.slots(rows_count)
    dma = pltpu.SemaphoreType.DMA
    shape = jax.ShapeDtypeStruct

    mask_rows = feat_mask.T
    mlp_out_turned = mlp_out.T
    norm_first_turned = jnp.transpose(norm_first, (1, 0, 2))
    norm_second_turned = jnp.transpose(norm_second, (1, 0, 2))
    all_first = lax.all_gather(bank_first, "rows", axis=0, tiled=True)
    all_second = lax.all_gather(bank_second, "rows", axis=0, tiled=True)

    peer_cells, first_sum, feat_mixed, gathered = pl.pallas_call(
        functools.partial(first_kernel, rows_count),
        name="feature_forward",
        out_shape=(
            shape((rows_dev, width_dev), BF16),
            shape((own_cells, width), F32),
            shape((own_cells, width), BF16),
            shape((rows_all, width_dev), BF16),
        ),
        in_specs=[in_vmem()] * 6,
        out_specs=[in_vmem()] * 4,
        scratch_shapes=[dma, dma, dma((1, slots)), dma((1, slots))],
        compiler_params=pltpu.CompilerParams(
            collective_id=0, has_side_effects=True, vmem_limit_bytes=VMEM_BYTES
        ),
    )(cells, mask_rows, proj_weights, feat_out_w, norm_gains, norm_shifts)

    (
        layer_out,
        mixed_grad,
        stats,
        stats_wide,
        second_grad,
        keys,
        values,
        early_grads,
        early_norms,
    ) = pl.pallas_call(
        second_kernel,
        name="item_forward_mlp",
        out_shape=(
            shape((rows_dev, width_dev), BF16),
            shape((rows_dev, width_dev), BF16),
            shape((16 * cols_dev, rows_dev), F32),
            shape((cols_dev, rows_dev, LANES), F32),
            shape((own_cells, width), F32),
            shape((cols_dev, key_total, width), BF16),
            shape((cols_dev, key_total, width), BF16),
            shape((width + 2 * ff_width, width), F32),
            shape((16, width), F32),
        ),
        in_specs=[in_smem()] + [in_vmem()] * 9,
        out_specs=[in_vmem()] * 9,
        scratch_shapes=[
            pltpu.VMEM((head_rows, width), BF16),
            pltpu.VMEM((head_rows, 1), F32),
            pltpu.VMEM((head_rows, 1), F32),
            pltpu.VMEM((head_rows, width), F32),
        ],
        compiler_params=pltpu.CompilerParams(vmem_limit_bytes=VMEM_BYTES),
    )(
        train_rows,
        gathered,
        first_sum,
        proj_weights,
        item_out_w,
        mlp_in,
        mlp_out_turned,
        norm_gains,
        norm_shifts,
        cotangent,
    )

    cells_grad, late_grads, late_norms = pl.pallas_call(
        functools.partial(third_kernel, rows_count),
        name="attention_backward",
        out_shape=(
            shape((rows_dev, width_dev), F32),
            shape((7 * width, width), F32),
            shape((8, width), F32),
        ),
        in_specs=[in_smem()] + [in_vmem()] * 16,
        out_specs=[in_vmem()] * 3,
        scratch_shapes=[
            pltpu.VMEM((rows_all, width_dev), BF16),
            pltpu.VMEM((16 * cols_dev, rows_all), F32),
            pltpu.VMEM((head_rows, width), BF16),
            pltpu.VMEM((head_rows, 2 * LANES), BF16),
            pltpu.VMEM((head_rows, width), F32),
            pltpu.VMEM((head_rows, 2 * LANES), F32),
            pltpu.VMEM((rows_dev, width_dev), BF16),
            pltpu.VMEM((rows_dev, width_dev), BF16),
            dma,
            dma,
            dma((2, slots)),
            dma((2, slots)),
        ],
        compiler_params=pltpu.CompilerParams(
            collective_id=1, has_side_effects=True, vmem_limit_bytes=VMEM_BYTES
        ),
    )(
        train_rows,
        cells,
        peer_cells,
        mask_rows,
        proj_weights,
        feat_out_w,
        norm_gains,
        norm_shifts,
        first_sum,
        feat_mixed,
        gathered,
        keys,
        values,
        mixed_grad,
        stats,
        stats_wide,
        second_grad,
    )

    devices = rows_count * cols_count
    chips = devices // 2
    grad_rows = late_grads.shape[0] + early_grads.shape[0] + early_norms.shape[0]
    block = -(-grad_rows // (16 * devices)) * 16
    total = pl.pallas_call(
        functools.partial(sum_kernel, rows_count, cols_count, block),
        name="gradient_sum",
        out_shape=shape((devices * block, width), F32),
        in_specs=[in_vmem()] * 4,
        out_specs=in_vmem(),
        scratch_shapes=[
            pltpu.VMEM((devices * block, width), BF16),
            pltpu.VMEM((chips * block, width), BF16),
            pltpu.VMEM((chips * block, width), BF16),
            pltpu.VMEM((chips - 1, block, width), BF16),
            pltpu.VMEM((devices * block, width), BF16),
            dma((2,)),
            dma((2,)),
            dma((chips - 1,)),
            dma((chips - 1,)),
            dma((chips - 1,)),
            dma((chips - 1,)),
        ],
        compiler_params=pltpu.CompilerParams(
            collective_id=2, has_side_effects=True, vmem_limit_bytes=VMEM_BYTES
        ),
    )(late_grads, early_grads, late_norms, early_norms)

    slots_dev = bank_first.shape[0]
    bank_rows = owner_rows.shape[0]
    square = (8, width, width)
    (
        square_grads,
        in_grad,
        out_grad,
        norm_grads,
        clip_norm,
        first_new,
        second_new,
        square_new,
        in_new,
        out_new,
        square_low,
        in_low,
        out_low,
        norm_new,
        norm_first_new,
        norm_second_new,
    ) = pl.pallas_call(
        update_kernel,
        name="rotated_update",
        out_shape=(
            shape(square, F32),
            shape(mlp_in.shape, F32),
            shape(mlp_in.shape, F32),
            shape(norm_first_turned.shape, F32),
            shape((1,), F32),
            shape(bank_first.shape, F32),
            shape(bank_first.shape, F32),
            shape(square, F32),
            shape(mlp_in.shape, F32),
            shape(mlp_in.shape, F32),
            shape(square, BF16),
            shape(mlp_in.shape, BF16),
            shape(mlp_in.shape, BF16),
            shape(norm_first_turned.shape, F32),
            shape(norm_first_turned.shape, F32),
            shape(norm_first_turned.shape, F32),
        ),
        in_specs=[in_smem()] + [in_vmem()] * 16,
        out_specs=[in_vmem()] * 4 + [in_smem()] + [in_vmem()] * 11,
        scratch_shapes=[
            pltpu.VMEM((bank_rows, width), F32),
            pltpu.VMEM((bank_rows, width), F32),
            pltpu.VMEM((bank_rows, width), F32),
            pltpu.VMEM((slots_dev, width), F32),
        ],
        compiler_params=pltpu.CompilerParams(vmem_limit_bytes=VMEM_BYTES),
    )(
        owner_rows,
        total,
        bases_small,
        bases_big,
        bank_first,
        bank_second,
        all_first,
        all_second,
        proj_weights,
        feat_out_w,
        item_out_w,
        mlp_in,
        mlp_out_turned,
        norm_gains,
        norm_shifts,
        norm_first_turned,
        norm_second_turned,
    )
    return (
        layer_out,
        cells_grad,
        square_grads,
        in_grad,
        out_grad.T,
        jnp.transpose(norm_grads, (1, 0, 2)),
        clip_norm,
        first_new,
        second_new,
        square_new,
        in_new,
        out_new.T,
        square_low,
        in_low,
        out_low.T,
        jnp.transpose(norm_new, (1, 0, 2)),
        jnp.transpose(norm_first_new, (1, 0, 2)),
        jnp.transpose(norm_second_new, (1, 0, 2)),
    )


def solution(mesh):
    in_specs = (
        P("rows", "cols"),
        P("rows", None),
        P(),
        P("rows", "cols"),
        P(),
        P(),
        P(),
        P(),
        P(),
        P(),
        P(),
        P(),
        P(),
        P(),
        P("rows", None),
        P("rows", None),
        P(),
        P(),
    )
    out_specs = (
        P("rows", "cols"),
        P("rows", "cols"),
        P(),
        P(),
        P(),
        P(),
        P(),
        P("rows", None),
        P("rows", None),
        P(),
        P(),
        P(),
        P(),
        P(),
        P(),
        P(),
        P(),
        P(),
    )
    small = mesh.shape["rows"] == 16 and mesh.shape["cols"] == 2
    return jax.shard_map(
        fast_device if small else per_device, mesh=mesh, in_specs=in_specs, out_specs=out_specs, check_vma=False
    )
```

```python
import functools
import math

import jax
import jax.numpy as jnp
from jax import lax
from jax.experimental import pallas as pl
from jax.experimental.pallas import tpu as pltpu
from jax.sharding import PartitionSpec as P

HEADS = 6
STEP = 10


HIGHEST = lax.Precision.HIGHEST
NEGATIVE = -1e30
CLIP_NORM = 1.0
BETA_ONE = 0.9
BETA_TWO = 0.95
EPSILON = 1e-08
LEARN_RATE = 1.0


def layer_norm(hidden, gain_row, shift_row):
    center = jnp.mean(hidden, axis=-1, keepdims=True)
    centered = hidden - center
    spread = jnp.mean(centered * centered, axis=-1, keepdims=True)
    return centered * lax.rsqrt(spread + 1e-05) * gain_row + shift_row


def gelu_exact(hidden):
    return jax.nn.gelu(hidden, approximate=False)


def product(left_side, right_side):
    return jnp.dot(left_side, right_side, preferred_element_type=jnp.float32)


def product_left(left_side, right_side):
    return lax.dot_general(
        left_side, right_side, (((0,), (0,)), ((), ())), preferred_element_type=jnp.float32
    )


def product_right(left_side, right_side):
    return lax.dot_general(
        left_side, right_side, (((1,), (1,)), ((), ())), preferred_element_type=jnp.float32
    )


def feature_forward(queries, key_rows, value_rows, key_open):
    scaling = queries.shape[-1] ** (-0.5)
    scores = (
        jnp.einsum("nqhe,nkhe->nhqk", queries, key_rows, preferred_element_type=jnp.float32)
        * scaling
    )
    scores = jnp.where(key_open[:, None, None, :], scores, NEGATIVE)
    attend = jax.nn.softmax(scores, axis=-1)
    attend_low = attend.astype(jnp.bfloat16)
    mixed = jnp.einsum(
        "nhqk,nkhe->nqhe", attend_low, value_rows, preferred_element_type=jnp.float32
    )
    return (attend, attend_low, mixed.astype(jnp.bfloat16))


def feature_backward(queries, key_rows, value_rows, attend, attend_low, mixed_grad):
    scaling = queries.shape[-1] ** (-0.5)
    value_dots = jnp.einsum(
        "nqhe,nkhe->nhqk", mixed_grad, value_rows, preferred_element_type=jnp.float32
    )
    row_delta = jnp.sum(attend * value_dots, axis=-1, keepdims=True)
    score_grad = (attend * (value_dots - row_delta)).astype(jnp.bfloat16)
    query_grad = (
        jnp.einsum("nhqk,nkhe->nqhe", score_grad, key_rows, preferred_element_type=jnp.float32)
        * scaling
    )
    key_grad = (
        jnp.einsum("nhqk,nqhe->nkhe", score_grad, queries, preferred_element_type=jnp.float32)
        * scaling
    )
    value_grad = jnp.einsum(
        "nhqk,nqhe->nkhe", attend_low, mixed_grad, preferred_element_type=jnp.float32
    )
    return (
        query_grad.astype(jnp.bfloat16),
        key_grad.astype(jnp.bfloat16),
        value_grad.astype(jnp.bfloat16),
    )


def key_blocks_of(key_rows, value_rows):
    key_total = key_rows.shape[0]
    block_size = math.gcd(key_total, 1024)
    block_count = key_total // block_size
    tail_shape = key_rows.shape[1:]
    starts = jnp.arange(block_count, dtype=jnp.int32) * block_size
    return (
        key_rows.reshape((block_count, block_size) + tail_shape),
        value_rows.reshape((block_count, block_size) + tail_shape),
        starts,
    )


def block_scores(queries, key_block, start_row, train_count):
    scaling = queries.shape[-1] ** (-0.5)
    scores = (
        jnp.einsum("qche,kche->chqk", queries, key_block, preferred_element_type=jnp.float32)
        * scaling
    )
    open_keys = start_row + jnp.arange(key_block.shape[0], dtype=jnp.int32) < train_count
    return jnp.where(open_keys[None, None, None, :], scores, NEGATIVE)


def item_forward(queries, key_rows, value_rows, train_count):
    key_split, value_split, starts = key_blocks_of(key_rows, value_rows)
    stat_shape = (queries.shape[1], queries.shape[2], queries.shape[0])

    def max_pass(carried, packed):
        running_max, running_sum = carried
        key_block, start_row = packed
        scores = block_scores(queries, key_block, start_row, train_count)
        new_max = jnp.maximum(running_max, jnp.max(scores, axis=-1))
        running_sum = running_sum * jnp.exp(running_max - new_max) + jnp.sum(
            jnp.exp(scores - new_max[..., None]), axis=-1
        )
        return ((new_max, running_sum), None)

    start_max = jnp.full(stat_shape, NEGATIVE, jnp.float32)
    (row_max, row_sum), _ = lax.scan(
        max_pass, (start_max, jnp.zeros(stat_shape, jnp.float32)), (key_split, starts)
    )
    log_total = row_max + jnp.log(row_sum)

    def value_pass(carried, packed):
        key_block, value_block, start_row = packed
        attend = jnp.exp(
            block_scores(queries, key_block, start_row, train_count) - log_total[..., None]
        )
        added = jnp.einsum(
            "chqk,kche->qche",
            attend.astype(jnp.bfloat16),
            value_block,
            preferred_element_type=jnp.float32,
        )
        return (carried + added, None)

    item_full, _ = lax.scan(
        value_pass, jnp.zeros(queries.shape, jnp.float32), (key_split, value_split, starts)
    )
    return (log_total, item_full)


def delta_of(mixed_grad, item_full):
    return jnp.transpose(jnp.sum(mixed_grad.astype(jnp.float32) * item_full, axis=-1), (1, 2, 0))


def item_backward(queries, key_rows, value_rows, train_count, log_total, mixed_grad, item_full):
    key_split, value_split, starts = key_blocks_of(key_rows, value_rows)
    scaling = queries.shape[-1] ** (-0.5)
    row_delta = delta_of(mixed_grad, item_full)

    def back_pass(carried, packed):
        key_block, value_block, start_row = packed
        attend = jnp.exp(
            block_scores(queries, key_block, start_row, train_count) - log_total[..., None]
        )
        value_dots = jnp.einsum(
            "qche,kche->chqk", mixed_grad, value_block, preferred_element_type=jnp.float32
        )
        score_grad = (attend * (value_dots - row_delta[..., None])).astype(jnp.bfloat16)
        carried = carried + jnp.einsum(
            "chqk,kche->qche", score_grad, key_block, preferred_element_type=jnp.float32
        )
        key_grad = (
            jnp.einsum("chqk,qche->kche", score_grad, queries, preferred_element_type=jnp.float32)
            * scaling
        )
        value_grad = jnp.einsum(
            "chqk,qche->kche",
            attend.astype(jnp.bfloat16),
            mixed_grad,
            preferred_element_type=jnp.float32,
        )
        return (carried, (key_grad, value_grad))

    query_sum, (key_grads, value_grads) = lax.scan(
        back_pass, jnp.zeros(queries.shape, jnp.float32), (key_split, value_split, starts)
    )
    key_total = key_rows.shape[0]
    flat_width = queries.shape[1] * queries.shape[2] * queries.shape[3]
    return (
        query_sum * scaling,
        key_grads.reshape(key_total, flat_width),
        value_grads.reshape(key_total, flat_width),
    )


def clip_all(gradients):
    total_sq = jnp.sum(gradients[0] * gradients[0])
    for extra in gradients[1:]:
        total_sq = total_sq + jnp.sum(extra * extra)
    grad_norm = jnp.sqrt(total_sq)
    factor = jnp.minimum(1.0, CLIP_NORM / grad_norm)
    return ([gradient * factor for gradient in gradients], grad_norm)


def rotate_bank(square_grad, in_grad, out_grad, bases_small, bases_big):
    model_width = in_grad.shape[0]
    left_bases = bases_small[0:8]
    right_bases = bases_small[8:16]
    rot_square = jnp.matmul(
        jnp.swapaxes(left_bases, 1, 2),
        jnp.matmul(square_grad, right_bases, precision=HIGHEST),
        precision=HIGHEST,
    )
    rot_in = jnp.dot(
        bases_small[16].T, jnp.dot(in_grad, bases_big[0], precision=HIGHEST), precision=HIGHEST
    )
    rot_out = jnp.dot(
        bases_big[1].T, jnp.dot(out_grad, bases_small[17], precision=HIGHEST), precision=HIGHEST
    )
    return jnp.concatenate(
        [rot_square.reshape(8 * model_width, model_width), rot_in.T, rot_out], axis=0
    )


def rotate_back(step_bank, bases_small, bases_big):
    model_width = step_bank.shape[1]
    ff_width = (step_bank.shape[0] - 8 * model_width) // 2
    step_square = step_bank[: 8 * model_width].reshape(8, model_width, model_width)
    step_in = step_bank[8 * model_width : 8 * model_width + ff_width].T
    step_out = step_bank[8 * model_width + ff_width :]
    up_square = jnp.matmul(
        bases_small[0:8],
        jnp.matmul(step_square, jnp.swapaxes(bases_small[8:16], 1, 2), precision=HIGHEST),
        precision=HIGHEST,
    )
    up_in = jnp.dot(
        bases_small[16], jnp.dot(step_in, bases_big[0].T, precision=HIGHEST), precision=HIGHEST
    )
    up_out = jnp.dot(
        bases_big[1], jnp.dot(step_out, bases_small[17].T, precision=HIGHEST), precision=HIGHEST
    )
    return (up_square, up_in, up_out)


def adam_rows(gradient, first_old, second_old, step_float):
    first_new = BETA_ONE * first_old + (1.0 - BETA_ONE) * gradient
    second_new = BETA_TWO * second_old + (1.0 - BETA_TWO) * gradient * gradient
    first_hat = first_new / (1.0 - jnp.power(BETA_ONE, step_float))
    second_hat = second_new / (1.0 - jnp.power(BETA_TWO, step_float))
    return (first_new, second_new, first_hat / (jnp.sqrt(second_hat) + EPSILON))


def trusted(weight, update, over_axes):
    scaling = jnp.sqrt(jnp.mean(weight * weight, axis=over_axes, keepdims=True) + 1e-06)
    return weight - LEARN_RATE * scaling * update


def per_device(
    cells,
    feat_mask,
    train_rows,
    cotangent,
    proj_weights,
    feat_out_w,
    item_out_w,
    mlp_in,
    mlp_out,
    norm_gains,
    norm_shifts,
    bases_small,
    bases_big,
    owner_rows,
    bank_first,
    bank_second,
    norm_first,
    norm_second,
):
    rows_dev, width_dev = cells.shape
    model_width = proj_weights.shape[-1]
    head_count = HEADS
    head_dim = model_width // head_count
    cols_dev = width_dev // model_width
    col_count = lax.axis_size("cols")
    all_cols = cols_dev * col_count
    half_rows = rows_dev // col_count
    cell_count = rows_dev * cols_dev
    proj_low = proj_weights.astype(jnp.bfloat16)
    feat_qkv = jnp.concatenate([proj_low[0], proj_low[1], proj_low[2]], axis=1)
    item_qkv = jnp.concatenate([proj_low[3], proj_low[4], proj_low[5]], axis=1)
    feat_out_low = feat_out_w.astype(jnp.bfloat16)
    item_out_low = item_out_w.astype(jnp.bfloat16)
    mlp_in_cast = mlp_in.astype(jnp.bfloat16)
    mlp_out_cast = mlp_out.astype(jnp.bfloat16)
    train_count = train_rows[0]
    column_cells = lax.all_to_all(cells, "cols", split_axis=0, concat_axis=1, tiled=True)
    column_flat = column_cells.reshape(half_rows * all_cols, model_width)
    row_mask = (
        lax.dynamic_slice_in_dim(feat_mask, lax.axis_index("cols") * half_rows, half_rows, 0) > 0
    )
    feat_proj = (
        product(column_flat, feat_qkv)
        .astype(jnp.bfloat16)
        .reshape(half_rows, all_cols, 3, head_count, head_dim)
    )
    feat_query = feat_proj[:, :, 0]
    feat_key = feat_proj[:, :, 1]
    feat_value = feat_proj[:, :, 2]
    feat_attend, feat_attend_low, feat_mixed = feature_forward(
        feat_query, feat_key, feat_value, row_mask
    )
    feat_mixed_flat = feat_mixed.reshape(half_rows * all_cols, model_width)
    feat_branch = (
        product(feat_mixed_flat, feat_out_low)
        .astype(jnp.bfloat16)
        .reshape(half_rows, all_cols * model_width)
    )
    feat_back = lax.all_to_all(feat_branch, "cols", split_axis=1, concat_axis=0, tiled=True)
    inputs_flat = cells.astype(jnp.float32).reshape(cell_count, model_width)
    first_sum = inputs_flat + feat_back.astype(jnp.float32).reshape(cell_count, model_width)
    first_out, first_pull = jax.vjp(layer_norm, first_sum, norm_gains[0], norm_shifts[0])
    first_low = first_out.astype(jnp.bfloat16)
    item_proj = product(first_low, item_qkv).astype(jnp.bfloat16)
    item_query = item_proj[:, :model_width].reshape(rows_dev, cols_dev, head_count, head_dim)
    item_key = item_proj[:, model_width : 2 * model_width].reshape(rows_dev, width_dev)
    item_value = item_proj[:, 2 * model_width :].reshape(rows_dev, width_dev)
    key_rows, value_rows = (
        lax.all_gather(item_key, "rows", axis=0, tiled=True),
        lax.all_gather(item_value, "rows", axis=0, tiled=True),
    )
    key_total = key_rows.shape[0]
    key_rows = key_rows.reshape(key_total, cols_dev, head_count, head_dim)
    value_rows = value_rows.reshape(key_total, cols_dev, head_count, head_dim)
    log_total, item_full = item_forward(item_query, key_rows, value_rows, train_count)
    item_low = item_full.astype(jnp.bfloat16).reshape(cell_count, model_width)
    item_branch = product(item_low, item_out_low)
    second_sum = first_out + item_branch
    second_out, second_pull = jax.vjp(layer_norm, second_sum, norm_gains[1], norm_shifts[1])
    second_low = second_out.astype(jnp.bfloat16)
    hidden_pre = product(second_low, mlp_in_cast)
    hidden_act, gelu_pull = jax.vjp(gelu_exact, hidden_pre)
    hidden_low = hidden_act.astype(jnp.bfloat16)
    mlp_branch = product(hidden_low, mlp_out_cast)
    third_sum = second_out + mlp_branch
    third_out, third_pull = jax.vjp(layer_norm, third_sum, norm_gains[2], norm_shifts[2])
    layer_out = third_out.astype(jnp.bfloat16).reshape(rows_dev, width_dev)
    third_grad, gain_three, shift_three = third_pull(
        cotangent.astype(jnp.float32).reshape(cell_count, model_width)
    )
    branch_low = third_grad.astype(jnp.bfloat16)
    mlp_out_grad = product_left(hidden_low, branch_low)
    hidden_grad = product_right(branch_low, mlp_out_cast)
    (pre_grad,) = gelu_pull(hidden_grad)
    pre_low = pre_grad.astype(jnp.bfloat16)
    mlp_in_grad = product_left(second_low, pre_low)
    second_grad = third_grad + product_right(pre_low, mlp_in_cast)
    second_in_grad, gain_two, shift_two = second_pull(second_grad)
    item_branch_low = second_in_grad.astype(jnp.bfloat16)
    item_out_grad = product_left(item_low, item_branch_low)
    item_mixed_grad = (
        product_right(item_branch_low, item_out_low)
        .astype(jnp.bfloat16)
        .reshape(rows_dev, cols_dev, head_count, head_dim)
    )
    key_again, value_again = (
        lax.all_gather(item_key, "rows", axis=0, tiled=True),
        lax.all_gather(item_value, "rows", axis=0, tiled=True),
    )
    key_rows = key_again.reshape(key_total, cols_dev, head_count, head_dim)
    value_rows = value_again.reshape(key_total, cols_dev, head_count, head_dim)
    query_sum, key_grads, value_grads = item_backward(
        item_query, key_rows, value_rows, train_count, log_total, item_mixed_grad, item_full
    )
    key_sum, value_sum = (
        lax.psum_scatter(key_grads, "rows", scatter_dimension=0, tiled=True),
        lax.psum_scatter(value_grads, "rows", scatter_dimension=0, tiled=True),
    )
    item_grad_low = jnp.concatenate(
        [
            query_sum.astype(jnp.bfloat16).reshape(cell_count, model_width),
            key_sum.astype(jnp.bfloat16).reshape(cell_count, model_width),
            value_sum.astype(jnp.bfloat16).reshape(cell_count, model_width),
        ],
        axis=1,
    )
    item_qkv_grad = product_left(first_low, item_grad_low)
    first_grad = second_in_grad + product_right(item_grad_low, item_qkv)
    first_in_grad, gain_one, shift_one = first_pull(first_grad)
    feat_branch_grad = first_in_grad.astype(jnp.bfloat16).reshape(rows_dev, width_dev)
    column_grad = lax.all_to_all(
        feat_branch_grad, "cols", split_axis=0, concat_axis=1, tiled=True
    ).reshape(half_rows * all_cols, model_width)
    feat_out_grad = product_left(feat_mixed_flat, column_grad)
    feat_mixed_grad = (
        product_right(column_grad, feat_out_low)
        .astype(jnp.bfloat16)
        .reshape(half_rows, all_cols, head_count, head_dim)
    )
    feat_query_grad, feat_key_grad, feat_value_grad = feature_backward(
        feat_query, feat_key, feat_value, feat_attend, feat_attend_low, feat_mixed_grad
    )
    feat_grad_low = jnp.concatenate(
        [
            feat_query_grad.reshape(half_rows * all_cols, model_width),
            feat_key_grad.reshape(half_rows * all_cols, model_width),
            feat_value_grad.reshape(half_rows * all_cols, model_width),
        ],
        axis=1,
    )
    feat_qkv_grad = product_left(column_flat, feat_grad_low)
    column_in_grad = (
        product_right(feat_grad_low, feat_qkv)
        .astype(jnp.bfloat16)
        .reshape(half_rows, all_cols * model_width)
    )
    row_in_grad = lax.all_to_all(column_in_grad, "cols", split_axis=1, concat_axis=0, tiled=True)
    cells_grad = first_in_grad.reshape(rows_dev, width_dev) + row_in_grad.astype(jnp.float32)
    proj_grad = jnp.stack(
        [
            feat_qkv_grad[:, :model_width],
            feat_qkv_grad[:, model_width : 2 * model_width],
            feat_qkv_grad[:, 2 * model_width :],
            item_qkv_grad[:, :model_width],
            item_qkv_grad[:, model_width : 2 * model_width],
            item_qkv_grad[:, 2 * model_width :],
        ]
    )
    norm_grad = jnp.stack(
        [
            jnp.stack([gain_one, gain_two, gain_three]),
            jnp.stack([shift_one, shift_two, shift_three]),
        ]
    )
    proj_total, feat_total, item_total, in_total, out_total, norm_total = lax.psum(
        (proj_grad, feat_out_grad, item_out_grad, mlp_in_grad, mlp_out_grad, norm_grad),
        ("rows", "cols"),
    )
    square_grad = jnp.concatenate([proj_total, feat_total[None], item_total[None]], axis=0)
    clipped, grad_norm = clip_all([square_grad, in_total, out_total, norm_total])
    square_clip, in_clip, out_clip, norm_clip = clipped
    rot_bank = rotate_bank(square_clip, in_clip, out_clip, bases_small, bases_big)
    step_float = jnp.asarray(STEP, jnp.float32)
    slot_count = bank_first.shape[0]
    my_slots = lax.dynamic_slice_in_dim(
        owner_rows, lax.axis_index("rows") * slot_count, slot_count, 0
    )
    first_new, second_new, slot_steps = adam_rows(
        jnp.take(rot_bank, my_slots, axis=0), bank_first, bank_second, step_float
    )
    all_steps = lax.all_gather(slot_steps, "rows", axis=0, tiled=True)
    full_steps = jnp.take(all_steps, jnp.argsort(owner_rows), axis=0)
    up_square, up_in, up_out = rotate_back(full_steps, bases_small, bases_big)
    square_old = jnp.concatenate([proj_weights, feat_out_w[None], item_out_w[None]], axis=0)
    square_new = trusted(square_old, up_square, (1, 2))
    in_new = trusted(mlp_in, up_in, (0, 1))
    out_new = trusted(mlp_out, up_out, (0, 1))
    norm_old = jnp.stack([norm_gains, norm_shifts])
    norm_first_new, norm_second_new, norm_steps = adam_rows(
        norm_clip, norm_first, norm_second, step_float
    )
    norm_new = trusted(norm_old, norm_steps, (2,))
    return (
        layer_out,
        cells_grad,
        square_clip,
        in_clip,
        out_clip,
        norm_clip,
        grad_norm.reshape(1),
        first_new,
        second_new,
        square_new,
        in_new,
        out_new,
        square_new.astype(jnp.bfloat16),
        in_new.astype(jnp.bfloat16),
        out_new.astype(jnp.bfloat16),
        norm_new,
        norm_first_new,
        norm_second_new,
    )


F32 = jnp.float32
BF16 = jnp.bfloat16
MESH = pl.DeviceIdType.MESH
VMEM_BYTES = 56 * 1024 * 1024
LANES = 128


def dot_nn(left, right):
    return jnp.dot(left, right, preferred_element_type=F32)


def dot_nt(left, right):
    return lax.dot_general(left, right, (((1,), (1,)), ((), ())), preferred_element_type=F32)


def dot_tn(left, right):
    return lax.dot_general(left, right, (((0,), (0,)), ((), ())), preferred_element_type=F32)


def split_two(value):
    high = value.astype(BF16)
    return high, (value - high.astype(F32)).astype(BF16)


def dot_fine(dot, left, right):
    left_high, left_low = split_two(left)
    right_high, right_low = split_two(right)
    return dot(left_high, right_high) + (dot(left_high, right_low) + dot(left_low, right_high))


def stack_columns(packed, width):
    count = packed.shape[1] // width
    return jnp.concatenate([packed[:, n * width : (n + 1) * width] for n in range(count)], axis=0)


def pack_columns(stacked, rows):
    count = stacked.shape[0] // rows
    return jnp.concatenate([stacked[n * rows : (n + 1) * rows] for n in range(count)], axis=1)


def norm_parts(hidden):
    width = hidden.shape[1]
    center = jnp.sum(hidden, axis=1, keepdims=True) * (1.0 / width)
    centered = hidden - center
    spread = jnp.sum(centered * centered, axis=1, keepdims=True) * (1.0 / width)
    root = lax.rsqrt(spread + 1e-05)
    return centered * root, root


def norm_back(unit, root, gain, incoming):
    width = unit.shape[1]
    scaled = incoming * gain
    mean_one = jnp.sum(scaled, axis=1, keepdims=True) * (1.0 / width)
    mean_two = jnp.sum(scaled * unit, axis=1, keepdims=True) * (1.0 / width)
    gain_grad = jnp.sum(incoming * unit, axis=0, keepdims=True)
    shift_grad = jnp.sum(incoming, axis=0, keepdims=True)
    return root * (scaled - mean_one - unit * mean_two), gain_grad, shift_grad


def head_table(width, head_dim):
    feature = lax.broadcasted_iota(jnp.int32, (width, LANES), 0)
    head = lax.broadcasted_iota(jnp.int32, (width, LANES), 1)
    inside = (feature >= head * head_dim) & (feature < (head + 1) * head_dim)
    return jnp.where(inside, 1.0, 0.0).astype(BF16)


def spread_table(width, head_dim):
    head = lax.broadcasted_iota(jnp.int32, (LANES, width), 0)
    feature = lax.broadcasted_iota(jnp.int32, (LANES, width), 1)
    inside = (feature >= head * head_dim) & (feature < (head + 1) * head_dim)
    return jnp.where(inside, 1.0, 0.0).astype(BF16)


def head_sums(value, table):
    high, low = split_two(value)
    return dot_nn(high, table) + dot_nn(low, table)


def head_mask(rows, width, head_dim, head, offset=0):
    feature = lax.broadcasted_iota(jnp.int32, (rows, width), 1)
    start = offset + head * head_dim
    return (feature >= start) & (feature < start + head_dim)


def tile_rows(value, count):
    return jnp.concatenate([value] * count, axis=0)


def column_open(mask_ref, own_first, cols_dev, slot):
    table = jnp.transpose(mask_ref[...].astype(F32))
    if slot < cols_dev:
        first, second = slot, slot + cols_dev
    else:
        first, second = slot, slot - cols_dev
    picked = jnp.where(own_first, table[:, first : first + 1], table[:, second : second + 1])
    return picked > 0.0


def feature_weights(queries, key_list, open_list, repeat, table, scaling):
    scores = []
    for keys, is_open in zip(key_list, open_list):
        raw = head_sums(queries * tile_rows(keys, repeat), table) * scaling
        scores.append(jnp.where(tile_rows(is_open, repeat), raw, NEGATIVE))
    top = scores[0]
    for extra in scores[1:]:
        top = jnp.maximum(top, extra)
    grown = [jnp.exp(score - top) for score in scores]
    total = grown[0]
    for extra in grown[1:]:
        total = total + extra
    return [part / total for part in grown]


def flip(value, pattern, size):
    out, step = 0, 1
    while step < size:
        out = out + step * (((value // step) % 2 + (pattern // step) % 2) % 2)
        step *= 2
    return out


class RowGather:
    def __init__(self, pieces, send_sem, recv_sem, rows_count):
        self.pieces, self.send_sem, self.recv_sem = pieces, send_sem, recv_sem
        self.deep = rows_count // 4
        me = lax.axis_index("rows")
        self.core, self.side, self.depth = me % 2, (me // 2) % 2, me // 4

    @staticmethod
    def slots(rows_count):
        return rows_count - 1

    def place(self, depth, side, core):
        return (depth * 2 + side) * 2 + core

    def source(self, k):
        return flip(self.depth, k, self.deep)

    def side_peer(self):
        return self.place(self.depth, 1 - self.side, self.core)

    def core_peer(self):
        return self.place(self.depth, self.side, 1 - self.core)

    def copies(self, shard, target, slot):
        return [
            pltpu.make_async_remote_copy(
                src_ref=piece(shard),
                dst_ref=piece(shard),
                send_sem=self.send_sem.at[n, slot],
                recv_sem=self.recv_sem.at[n, slot],
                device_id={"rows": target},
                device_id_type=MESH,
            )
            for n, piece in enumerate(self.pieces)
        ]

    def push(self, shard, target, slot):
        for copy in self.copies(shard, target, slot):
            copy.start()

    def arrive(self, shard, source, slot):
        for copy in self.copies(shard, source, slot):
            copy.wait_recv()

    def start_depth(self):
        own = self.place(self.depth, self.side, self.core)
        for k in range(1, self.deep):
            self.push(own, self.place(self.source(k), self.side, self.core), k - 1)

    def start_near(self):
        own = self.place(self.depth, self.side, self.core)
        self.push(own, self.core_peer(), 2 * self.deep - 1)
        self.push(own, self.side_peer(), self.deep - 1)

    def along_depth(self, k):
        shard = self.place(self.source(k), self.side, self.core)
        self.arrive(shard, shard, k - 1)
        self.push(shard, self.side_peer(), self.deep - 1 + k)
        self.push(shard, self.core_peer(), 2 * self.deep - 1 + k)

    def across_side(self, k):
        shard = self.place(self.source(k), 1 - self.side, self.core)
        self.arrive(shard, self.side_peer(), self.deep - 1 + k)
        self.push(shard, self.core_peer(), 3 * self.deep - 1 + k)

    def from_core(self, k, other_side):
        side = self.side + other_side - 2 * self.side * other_side
        shard = self.place(self.source(k), side, 1 - self.core)
        self.arrive(shard, self.core_peer(), (2 + other_side) * self.deep - 1 + k)

    def run(self, use):
        self.across_side(0)

        @pl.loop(0, 2 * self.deep)
        def _(turn):
            k, other = turn // 2, turn % 2

            @pl.when((k + 1 < self.deep) & (other == 0))
            def _():
                self.along_depth(k + 1)

            @pl.when((k + 1 < self.deep) & (other == 1))
            def _():
                self.across_side(k + 1)

            self.from_core(k, other)
            use(self.source(k), self.side + other - 2 * self.side * other)

    def wait_sent(self):
        own = self.place(self.depth, self.side, self.core)

        @pl.loop(0, 4 * self.deep - 1)
        def _(slot):
            for copy in self.copies(own, self.core_peer(), slot):
                copy.wait_send()


class StagedSum:
    def __init__(self, stages, sizes, part_ref, total_ref, landing, sems, rows):
        self.stages, self.sizes = stages, sizes
        self.part_ref, self.total_ref, self.landing, self.sems = part_ref, total_ref, landing, sems
        row = lax.axis_index("rows")
        self.me = {"z": row // 4, "x": (row // 2) % 2, "k": row % 2, "y": lax.axis_index("cols")}
        self.spans, base, size = [], 0, rows
        for stage in stages:
            size = size // members(stage, sizes)
            self.spans.append((base, size))
            base = base + self.number(self.me, stage) * size
        self.base, self.size = base, size
        self.unit = size

    def number(self, place, stage):
        out, scale = 0, 1
        for axis in stage:
            out = out + place[axis] * scale
            scale *= self.sizes[axis]
        return out

    def partner(self, stage, pattern):
        place = dict(self.me)
        for axis in stage:
            place[axis] = flip(self.me[axis], pattern % self.sizes[axis], self.sizes[axis])
            pattern //= self.sizes[axis]
        return place

    def device(self, place):
        return {"rows": (place["z"] * 2 + place["x"]) * 2 + place["k"], "cols": place["y"]}

    def rows_at(self, base, size):
        return pl.ds(pl.multiple_of(base, self.unit), size)

    def scatter(self, s):
        stage, (base, size) = self.stages[s], self.spans[s]
        found = []
        for j in range(1, members(stage, self.sizes)):
            place = self.partner(stage, j)
            rows = self.rows_at(base + self.number(place, stage) * size, size)
            found.append(
                pltpu.make_async_remote_copy(
                    src_ref=self.part_ref.at[rows, :],
                    dst_ref=self.landing[s].at[j - 1],
                    send_sem=self.sems.at[0, s, j - 1],
                    recv_sem=self.sems.at[1, s, j - 1],
                    device_id=self.device(place),
                    device_id_type=MESH,
                )
            )
        return found

    def scatter_start(self, s):
        for copy in self.scatter(s):
            copy.start()

    def scatter_finish(self, s):
        stage, (base, size) = self.stages[s], self.spans[s]
        rows = self.rows_at(base + self.number(self.me, stage) * size, size)
        total = self.part_ref[rows, :].astype(F32)
        copies = self.scatter(s)
        for j, copy in enumerate(copies):
            copy.wait_recv()
            total = total + self.landing[s][j].astype(F32)
        for copy in copies:
            copy.wait_send()
        target = self.total_ref if s == len(self.stages) - 1 else self.part_ref
        target[rows, :] = total.astype(BF16)

    def gather(self, s, own):
        stage, (base, size) = self.stages[s], self.spans[s]
        found = []
        for j in range(1, members(stage, self.sizes)):
            place = self.partner(stage, j)
            holder = self.me if own else place
            rows = self.rows_at(base + self.number(holder, stage) * size, size)
            found.append(
                pltpu.make_async_remote_copy(
                    src_ref=self.total_ref.at[rows, :],
                    dst_ref=self.total_ref.at[rows, :],
                    send_sem=self.sems.at[2, s, j - 1],
                    recv_sem=self.sems.at[3, s, j - 1],
                    device_id=self.device(place),
                    device_id_type=MESH,
                )
            )
        return found

    def gather_start(self, s):
        for copy in self.gather(s, True):
            copy.start()

    def gather_finish(self, s):
        for copy in self.gather(s, False):
            copy.wait_recv()
        for copy in self.gather(s, True):
            copy.wait_send()


def members(stage, sizes):
    return math.prod(sizes[axis] for axis in stage)


def meet(targets):
    barrier = pltpu.get_barrier_semaphore()
    for target in targets:
        pl.semaphore_signal(barrier, inc=1, device_id=target, device_id_type=MESH)
    pl.semaphore_wait(barrier, len(targets))


def swap_copy(source, landing, send_sem, recv_sem):
    return pltpu.make_async_remote_copy(
        src_ref=source,
        dst_ref=landing,
        send_sem=send_sem,
        recv_sem=recv_sem,
        device_id={"cols": 1 - lax.axis_index("cols")},
        device_id_type=MESH,
    )


def window_of(column, width, width_dev):
    start = (column * width) // LANES * LANES
    offset = column * width - start
    size = -(-(offset + width) // LANES) * LANES
    return start, offset, min(size, width_dev - start)


def padded_weight(weight, offset, size):
    width = weight.shape[1]
    parts = []
    if offset:
        parts.append(jnp.zeros((offset, width), F32))
    parts.append(weight)
    if size - offset - weight.shape[0]:
        parts.append(jnp.zeros((size - offset - weight.shape[0], width), F32))
    return (jnp.concatenate(parts, axis=0) if len(parts) > 1 else weight).astype(BF16)


def head_blocks(value, head_dim, offset=0, size=None):
    rows, width = value.shape
    if size is not None and size != width:
        parts = []
        if offset:
            parts.append(jnp.zeros((rows, offset), F32))
        parts.append(value)
        if size - offset - width:
            parts.append(jnp.zeros((rows, size - offset - width), F32))
        value = jnp.concatenate(parts, axis=1)
        width = size
    blocks = [
        jnp.where(head_mask(rows, width, head_dim, head, offset), value, 0.0).astype(BF16)
        for head in range(HEADS)
    ]
    return jnp.concatenate(blocks, axis=0)


def gather_heads(value, rows, head_dim, offset=0, width=None):
    total = None
    for head in range(HEADS):
        block = value[head * rows : (head + 1) * rows]
        kept = jnp.where(head_mask(rows, value.shape[1], head_dim, head, offset), block, 0.0)
        total = kept if total is None else total + kept
    if width is not None and width != total.shape[1]:
        total = total[:, offset : offset + width]
    return total


STAGES = ("k", "xy", "z")


def layer_kernel(
    rows_count,
    cols_count,
    train_ref,
    owner_ref,
    cells_ref,
    mask_ref,
    cotangent_ref,
    proj_ref,
    feat_out_ref,
    item_out_ref,
    mlp_in_ref,
    mlp_out_ref,
    gains_ref,
    shifts_ref,
    bank_first_ref,
    bank_second_ref,
    layer_ref,
    cells_grad_ref,
    early_total_ref,
    late_total_ref,
    sorted_ref,
    peer_ref,
    gathered_ref,
    keys_ref,
    values_ref,
    grads_ref,
    all_stats_ref,
    banks_ref,
    blocks_ref,
    grad_blocks_ref,
    wide_blocks_ref,
    top_ref,
    sum_ref,
    total_ref,
    value_total_ref,
    item_w_ref,
    branch_ref,
    peer_branch_ref,
    early_ref,
    late_ref,
    early_land_k,
    early_land_xy,
    early_land_z,
    late_land_k,
    late_land_xy,
    late_land_z,
    swap_sem,
    gather_sem,
    grads_sem,
    banks_sem,
    early_sem,
    late_sem,
):
    rows_dev, width_dev = cells_ref.shape
    width = feat_out_ref.shape[0]
    cols_dev = width_dev // width
    head_dim = width // HEADS
    scaling = head_dim ** (-0.5)
    ff_width = mlp_in_ref.shape[1]
    key_total = keys_ref.shape[1]
    chip_rows = 2 * rows_dev
    bank_slots = bank_first_ref.shape[0]
    train_count = train_ref[0]
    me = lax.axis_index("rows")
    sizes = {"z": rows_count // 4, "x": 2, "k": 2, "y": cols_count}
    own_count = cols_dev * rows_dev

    def shard_of(ref, rows):
        return lambda shard: ref.at[pl.ds(pl.multiple_of(shard * rows, rows), rows), :]

    def stats_shard(shard):
        return all_stats_ref.at[:, pl.ds(pl.multiple_of(shard * rows_dev, rows_dev), rows_dev)]

    hidden_gather = RowGather(
        [shard_of(gathered_ref, rows_dev)], gather_sem.at[0], gather_sem.at[1], rows_count
    )
    grads_gather = RowGather(
        [shard_of(grads_ref, rows_dev), stats_shard], grads_sem.at[0], grads_sem.at[1], rows_count
    )
    banks_gather = RowGather(
        [shard_of(banks_ref, bank_slots)], banks_sem.at[0], banks_sem.at[1], rows_count
    )
    early_sum = StagedSum(
        STAGES,
        sizes,
        early_ref,
        early_total_ref,
        (early_land_k, early_land_xy, early_land_z),
        early_sem,
        early_ref.shape[0],
    )
    late_sum = StagedSum(
        STAGES,
        sizes,
        late_ref,
        late_total_ref,
        (late_land_k, late_land_xy, late_land_z),
        late_sem,
        late_ref.shape[0],
    )
    meet(
        [
            early_sum.device(early_sum.partner(stage, j))
            for stage in STAGES
            for j in range(1, members(stage, sizes))
        ]
    )

    swap = swap_copy(cells_ref, peer_ref, swap_sem.at[0], swap_sem.at[1])
    swap.start()
    banks_ref[pl.ds(pl.multiple_of(me * bank_slots, bank_slots), bank_slots), :] = jnp.concatenate(
        [bank_first_ref[...], bank_second_ref[...]], axis=1
    ).astype(BF16)
    banks_gather.start_depth()
    feat_w = [proj_ref[n].astype(BF16) for n in range(3)]
    own = stack_columns(cells_ref[...].astype(F32), width)
    own_low = own.astype(BF16)
    queries, own_keys, own_values = [
        dot_nn(own_low, weight).astype(BF16).astype(F32) for weight in feat_w
    ]
    table = head_table(width, head_dim)
    wide = spread_table(width, head_dim)
    swap.wait()
    peer_low = stack_columns(peer_ref[...].astype(F32), width).astype(BF16)
    peer_queries, peer_keys, peer_values = [
        dot_nn(peer_low, weight).astype(BF16).astype(F32) for weight in feat_w
    ]
    feat_query = jnp.concatenate([queries, peer_queries], axis=0)
    all_keys = jnp.concatenate([own_keys, peer_keys], axis=0)
    all_values = jnp.concatenate([own_values, peer_values], axis=0)
    slots = all_keys.shape[0] // rows_dev
    own_first = lax.axis_index("cols") == 0
    key_list = [all_keys[n * rows_dev : (n + 1) * rows_dev] for n in range(slots)]
    value_list = [all_values[n * rows_dev : (n + 1) * rows_dev] for n in range(slots)]
    open_list = [column_open(mask_ref, own_first, cols_dev, n) for n in range(slots)]
    weights = feature_weights(feat_query, key_list, open_list, slots, table, scaling)
    mixed = None
    for weight, column_values in zip(weights, value_list):
        added = dot_nn(weight[:own_count].astype(BF16), wide) * tile_rows(column_values, cols_dev)
        mixed = added if mixed is None else mixed + added
    feat_mixed = mixed.astype(BF16)
    feat_out_w = feat_out_ref[...].astype(BF16)
    first_sum = own + dot_nn(feat_mixed, feat_out_w).astype(BF16).astype(F32)
    unit_one, root_one = norm_parts(first_sum)
    first_out = unit_one * gains_ref[0:1, :] + shifts_ref[0:1, :]
    first_low = first_out.astype(BF16)
    own_rows = pl.ds(pl.multiple_of(me * rows_dev, rows_dev), rows_dev)
    gathered_ref[own_rows, :] = pack_columns(first_out, rows_dev).astype(BF16)
    hidden_gather.start_near()
    hidden_gather.start_depth()

    item_w = [proj_ref[3 + n].astype(BF16) for n in range(3)]
    queries, own_keys, own_values = [
        dot_nn(first_low, weight).astype(BF16).astype(F32) for weight in item_w
    ]
    windows = [window_of(column, width, width_dev) for column in range(cols_dev)]
    for column, (_, offset, size) in enumerate(windows):
        for n in range(3):
            item_w_ref[column, n, 0:size, :] = padded_weight(proj_ref[3 + n], offset, size)
        blocks_ref[column] = head_blocks(
            queries[column * rows_dev : (column + 1) * rows_dev], head_dim
        )
    top_ref[...] = jnp.full(top_ref.shape, NEGATIVE, F32)
    sum_ref[...] = jnp.zeros(sum_ref.shape, F32)
    total_ref[...] = jnp.zeros(total_ref.shape, F32)

    def chip_start(depth, side):
        return pl.multiple_of((depth * 2 + side) * chip_rows, chip_rows)

    def masked_scores(column, keys, start_row):
        key_row = start_row + lax.broadcasted_iota(jnp.int32, (1, chip_rows), 1)
        scores = dot_nt(blocks_ref[column], keys) * scaling
        return jnp.where(key_row < train_count, scores, NEGATIVE)

    def attend_chip(depth, side):
        @pl.when(depth * 4 * rows_dev < key_total)
        def _():
            start_row = chip_start(depth, side)
            span = pl.ds(start_row, chip_rows)
            for column, (start, _, size) in enumerate(windows):
                hidden = gathered_ref[span, start : start + size]
                keys = dot_nn(hidden, item_w_ref[column, 1, 0:size, :]).astype(BF16)
                values = dot_nn(hidden, item_w_ref[column, 2, 0:size, :]).astype(BF16)
                keys_ref[column, span, :] = keys
                values_ref[column, span, :] = values
                scores = masked_scores(column, keys, start_row)
                top_old = top_ref[column]
                top_new = jnp.maximum(top_old, jnp.max(scores, axis=1, keepdims=True))
                grown = jnp.exp(scores - top_new)
                fade = jnp.exp(top_old - top_new)
                top_ref[column] = top_new
                sum_ref[column] = sum_ref[column] * fade + jnp.sum(grown, axis=1, keepdims=True)
                total_ref[column] = total_ref[column] * fade + dot_nn(grown.astype(BF16), values)

    hidden_gather.run(attend_chip)
    banks_gather.start_near()

    item_full, log_totals = [], []
    for column in range(cols_dev):
        item_full.append(gather_heads(total_ref[column] / sum_ref[column], rows_dev, head_dim))
        log_totals.append(top_ref[column] + jnp.log(sum_ref[column]))

    full = jnp.concatenate(item_full, axis=0)
    item_low = full.astype(BF16)
    item_out_w = item_out_ref[...].astype(BF16)
    mlp_in_w = mlp_in_ref[...].astype(BF16)
    mlp_out_w = mlp_out_ref[...].astype(BF16)
    unit_two, root_two = norm_parts(first_out + dot_nn(item_low, item_out_w))
    second_out = unit_two * gains_ref[1:2, :] + shifts_ref[1:2, :]
    second_low = second_out.astype(BF16)
    hidden_pre = dot_nn(second_low, mlp_in_w)
    normal = 0.5 + 0.5 * lax.erf(hidden_pre * (0.5**0.5))
    hidden_low = (hidden_pre * normal).astype(BF16)
    unit_three, root_three = norm_parts(second_out + dot_nt(hidden_low, mlp_out_w))
    third_out = unit_three * gains_ref[2:3, :] + shifts_ref[2:3, :]
    layer_ref[...] = pack_columns(third_out, rows_dev).astype(BF16)
    incoming = stack_columns(cotangent_ref[...].astype(F32), width)
    third_grad, gain_three, shift_three = norm_back(
        unit_three, root_three, gains_ref[2:3, :], incoming
    )
    branch_low = third_grad.astype(BF16)
    density = jnp.exp(-0.5 * hidden_pre * hidden_pre) * (1.0 / math.sqrt(2.0 * math.pi))
    pre_low = (dot_nn(branch_low, mlp_out_w) * (normal + hidden_pre * density)).astype(BF16)
    second_grad, gain_two, shift_two = norm_back(
        unit_two, root_two, gains_ref[1:2, :], third_grad + dot_nt(pre_low, mlp_in_w)
    )
    second_grad_low = second_grad.astype(BF16)
    mixed_grad = dot_nt(second_grad_low, item_out_w).astype(BF16).astype(F32)
    delta_all = head_sums(mixed_grad * full, table)
    lane = lax.broadcasted_iota(jnp.int32, (rows_dev, LANES), 1)
    deltas = []
    for column in range(cols_dev):
        rows_here = slice(column * rows_dev, (column + 1) * rows_dev)
        part = delta_all[rows_here]
        stat = jnp.zeros((rows_dev, LANES), F32)
        for head in range(HEADS):
            head_rows = slice(head * rows_dev, (head + 1) * rows_dev)
            stat = jnp.where(lane == head, log_totals[column][head_rows], stat)
            stat = jnp.where(lane == 8 + head, part[:, head : head + 1], stat)
        deltas.append(jnp.concatenate([part[:, h : h + 1] for h in range(HEADS)], axis=0))
        all_stats_ref[16 * column : 16 * (column + 1), own_rows] = jnp.transpose(stat)[0:16, :]
    grads_ref[own_rows, :] = pack_columns(mixed_grad, rows_dev).astype(BF16)
    grads_gather.start_near()
    grads_gather.start_depth()

    early_ref[2 * width : 3 * width, :] = dot_tn(second_low, pre_low).astype(BF16)
    early_ref[3 * width : 4 * width, :] = dot_tn(branch_low, hidden_low).astype(BF16)
    item_out_grad = dot_tn(item_low, second_grad_low)

    for column in range(cols_dev):
        rows_here = slice(column * rows_dev, (column + 1) * rows_dev)
        grad_blocks_ref[column] = head_blocks(mixed_grad[rows_here], head_dim)
    total_ref[...] = jnp.zeros(total_ref.shape, F32)

    @pl.loop(0, key_total // chip_rows)
    def _(step):
        start_row = pl.multiple_of(step * chip_rows, chip_rows)
        span = pl.ds(start_row, chip_rows)
        for column in range(cols_dev):
            keys = keys_ref[column, span, :]
            attend = jnp.exp(masked_scores(column, keys, start_row) - log_totals[column])
            dots = dot_nt(grad_blocks_ref[column], values_ref[column, span, :])
            score_grad = (attend * (dots - deltas[column])).astype(BF16)
            total_ref[column] += dot_nn(score_grad, keys)

    query_grads = [
        gather_heads(total_ref[column], rows_dev, head_dim) * scaling for column in range(cols_dev)
    ]

    own_row = me * rows_dev + lax.broadcasted_iota(jnp.int32, (rows_dev, 1), 0)
    own_open = own_row < train_count
    for column, (_, offset, size) in enumerate(windows):
        rows_here = slice(column * rows_dev, (column + 1) * rows_dev)
        blocks_ref[column] = head_blocks(own_keys[rows_here], head_dim)
        wide_blocks_ref[column, :, 0:size] = head_blocks(
            own_values[rows_here], head_dim, offset, size
        )
    total_ref[...] = jnp.zeros(total_ref.shape, F32)
    value_total_ref[...] = jnp.zeros(value_total_ref.shape, F32)

    def answer_chip(depth, side):
        span = pl.ds(chip_start(depth, side), chip_rows)
        for column, (start, _, size) in enumerate(windows):
            hidden = gathered_ref[span, start : start + size]
            asked = dot_nn(hidden, item_w_ref[column, 0, 0:size, :]).astype(BF16)
            grads = grads_ref[span, start : start + size]
            scores = dot_nt(blocks_ref[column], asked) * scaling
            dots = dot_nt(wide_blocks_ref[column, :, 0:size], grads)
            attends, score_grads = [], []
            for head in range(HEADS):
                part = slice(head * rows_dev, (head + 1) * rows_dev)
                log_total = all_stats_ref[16 * column + head : 16 * column + head + 1, span]
                delta = all_stats_ref[16 * column + 8 + head : 16 * column + 9 + head, span]
                attend = jnp.exp(jnp.where(own_open, scores[part], NEGATIVE) - log_total)
                attends.append(attend.astype(BF16))
                score_grads.append((attend * (dots[part] - delta)).astype(BF16))
            total_ref[column] += dot_nn(jnp.concatenate(score_grads, axis=0), asked)
            value_total_ref[column, :, 0:size] += dot_nn(jnp.concatenate(attends, axis=0), grads)

    grads_gather.run(answer_chip)

    key_grads, value_grads = [], []
    for column, (_, offset, size) in enumerate(windows):
        key_grads.append(gather_heads(total_ref[column], rows_dev, head_dim) * scaling)
        value_grads.append(
            gather_heads(value_total_ref[column, :, 0:size], rows_dev, head_dim, offset, width)
        )
    item_grads = [
        jnp.concatenate(parts, axis=0).astype(BF16)
        for parts in (query_grads, key_grads, value_grads)
    ]
    first_grad = second_grad
    for n in range(3):
        first_grad = first_grad + dot_nt(item_grads[n], item_w[n])
    first_in_grad, gain_one, shift_one = norm_back(
        unit_one, root_one, gains_ref[0:1, :], first_grad
    )
    branch_ref[...] = pack_columns(first_in_grad, rows_dev).astype(BF16)
    swap = swap_copy(branch_ref, peer_branch_ref, swap_sem.at[2], swap_sem.at[3])
    swap.start()

    def side_by_side(left, right):
        return jnp.concatenate([left, right], axis=1).astype(BF16)

    early_ref[0:width, :] = side_by_side(
        dot_tn(first_low, item_grads[0]), dot_tn(first_low, item_grads[1])
    )
    early_ref[width : 2 * width, :] = side_by_side(
        dot_tn(first_low, item_grads[2]), item_out_grad
    )
    if early_ref.shape[0] > 4 * width:
        early_ref[4 * width :, :] = jnp.zeros((early_ref.shape[0] - 4 * width, 2 * width), BF16)
    early_sum.scatter_start(0)
    banks_gather.across_side(0)
    for k in range(1, rows_count // 4):
        banks_gather.along_depth(k)
    early_sum.scatter_finish(0)
    early_sum.scatter_start(1)
    for k in range(1, rows_count // 4):
        banks_gather.across_side(k)

    own_branch = first_in_grad.astype(BF16)
    feat_out_grad = dot_tn(feat_mixed, own_branch)
    swap.wait()
    peer_branch = stack_columns(peer_branch_ref[...].astype(F32), width).astype(BF16)
    all_branch = jnp.concatenate([own_branch, peer_branch], axis=0)
    feat_grad = dot_nt(all_branch, feat_out_w).astype(BF16).astype(F32)
    dots = [head_sums(feat_grad * tile_rows(part, slots), table) for part in value_list]
    row_delta = None
    for weight, dot in zip(weights, dots):
        added = weight * dot
        row_delta = added if row_delta is None else row_delta + added
    score_grads = [
        (weight * (dot - row_delta)).astype(BF16) for weight, dot in zip(weights, dots)
    ]
    early_sum.scatter_finish(1)
    early_sum.scatter_start(2)
    query_grad = None
    for score_grad, part in zip(score_grads, key_list):
        added = dot_nn(score_grad[:own_count], wide) * tile_rows(part, cols_dev)
        query_grad = added if query_grad is None else query_grad + added
    key_parts, value_parts = [], []
    for column in range(cols_dev):
        key_products = dot_nn(score_grads[column], wide) * feat_query
        value_products = dot_nn(weights[column].astype(BF16), wide) * feat_grad
        key_sum = key_products[:rows_dev]
        value_sum = value_products[:rows_dev]
        for n in range(1, slots):
            key_sum = key_sum + key_products[n * rows_dev : (n + 1) * rows_dev]
            value_sum = value_sum + value_products[n * rows_dev : (n + 1) * rows_dev]
        key_parts.append(key_sum)
        value_parts.append(value_sum)
    feat_grads = [
        (query_grad * scaling).astype(BF16),
        (jnp.concatenate(key_parts, axis=0) * scaling).astype(BF16),
        jnp.concatenate(value_parts, axis=0).astype(BF16),
    ]
    late_ref[0:width, :] = side_by_side(
        dot_tn(own_low, feat_grads[0]), dot_tn(own_low, feat_grads[1])
    )
    late_ref[width : 2 * width, :] = side_by_side(dot_tn(own_low, feat_grads[2]), feat_out_grad)
    pairs = [
        jnp.concatenate(pair, axis=1)
        for pair in ((gain_one, shift_one), (gain_two, shift_two), (gain_three, shift_three))
    ]
    rest = late_ref.shape[0] - 2 * width - len(pairs)
    late_ref[2 * width :, :] = jnp.concatenate(
        pairs + [jnp.zeros((rest, 2 * width), F32)], axis=0
    ).astype(BF16)
    late_sum.scatter_start(0)
    early_sum.scatter_finish(2)
    early_sum.gather_start(2)
    late_sum.scatter_finish(0)
    late_sum.scatter_start(1)
    inner = None
    for n in range(3):
        added = dot_nt(feat_grads[n], feat_w[n])
        inner = added if inner is None else inner + added
    cells_grad_ref[...] = pack_columns(first_in_grad + inner.astype(BF16).astype(F32), rows_dev)
    for k in range(rows_count // 4):
        banks_gather.from_core(k, 0)
        banks_gather.from_core(k, 1)
    sort_rows = sorted_ref.shape[0]
    sort_block = math.gcd(sort_rows, 256)
    owner = owner_ref[...]

    def sort_some(first, last):
        @pl.loop(first, last)
        def _(step):
            start = pl.multiple_of(step * sort_block, sort_block)
            row = start + lax.broadcasted_iota(jnp.int32, (sort_block, sort_rows), 0)
            chosen = jnp.where(owner == row, 1.0, 0.0).astype(BF16)
            sorted_ref[pl.ds(start, sort_block), :] = dot_nn(chosen, banks_ref[...]).astype(BF16)

    thirds = sort_rows // sort_block // 3
    early_sum.gather_finish(2)
    early_sum.gather_start(1)
    late_sum.scatter_finish(1)
    late_sum.scatter_start(2)
    sort_some(0, thirds)
    early_sum.gather_finish(1)
    early_sum.gather_start(0)
    late_sum.scatter_finish(2)
    late_sum.gather_start(2)
    sort_some(thirds, 2 * thirds)
    late_sum.gather_finish(2)
    late_sum.gather_start(1)
    early_sum.gather_finish(0)
    sort_some(2 * thirds, sort_rows // sort_block)
    late_sum.gather_finish(1)
    late_sum.gather_start(0)
    for gather in (hidden_gather, grads_gather, banks_gather):
        gather.wait_sent()
    late_sum.gather_finish(0)


def moment_rule(gradient, first_old, second_old):
    first_new = BETA_ONE * first_old + (1.0 - BETA_ONE) * gradient
    second_new = BETA_TWO * second_old + (1.0 - BETA_TWO) * gradient * gradient
    first_hat = first_new * (1.0 / (1.0 - BETA_ONE**STEP))
    second_hat = second_new * (1.0 / (1.0 - BETA_TWO**STEP))
    return first_new, second_new, first_hat / (jnp.sqrt(second_hat) + EPSILON)


def root_mean(value):
    count = value.shape[0] * value.shape[1]
    square = jnp.sum(jnp.sum(value * value, axis=1, keepdims=True), axis=0, keepdims=True)
    return jnp.sqrt(square * (1.0 / count) + 1e-06)


def update_kernel(
    owner_ref,
    layer_ref,
    cells_grad_ref,
    early_ref,
    late_ref,
    sorted_ref,
    small_ref,
    big_ref,
    first_ref,
    second_ref,
    proj_ref,
    feat_out_ref,
    item_out_ref,
    mlp_in_ref,
    mlp_out_ref,
    gains_ref,
    shifts_ref,
    norm_first_ref,
    norm_second_ref,
    layer_out_ref,
    cells_out_ref,
    square_grad_ref,
    in_grad_ref,
    out_grad_ref,
    norm_grad_ref,
    clip_ref,
    first_new_ref,
    second_new_ref,
    square_new_ref,
    in_new_ref,
    out_new_ref,
    square_low_ref,
    in_low_ref,
    out_low_ref,
    norm_new_ref,
    norm_first_new_ref,
    norm_second_new_ref,
    rotated_ref,
    own_ref,
):
    width, ff_width = mlp_in_ref.shape
    slots = first_ref.shape[0]
    layer_out_ref[...] = layer_ref[...]
    cells_out_ref[...] = cells_grad_ref[...]

    early = early_ref[...].astype(F32)
    late = late_ref[...].astype(F32)
    square = None
    for part in (early, late):
        added = jnp.sum(jnp.sum(part * part, axis=1, keepdims=True), axis=0, keepdims=True)
        square = added if square is None else square + added
    grad_norm = jnp.sqrt(square)
    factor = jnp.minimum(1.0, CLIP_NORM / grad_norm)
    clip_ref[0] = grad_norm[0, 0]
    early = early * factor
    late = late * factor
    squares = [
        part[row : row + width, lane : lane + width]
        for part, row, lane in (
            (late, 0, 0),
            (late, 0, width),
            (late, width, 0),
            (early, 0, 0),
            (early, 0, width),
            (early, width, 0),
            (late, width, width),
            (early, width, width),
        )
    ]
    for n, clipped in enumerate(squares):
        square_grad_ref[n] = clipped
        turned = dot_fine(dot_nn, clipped, small_ref[8 + n])
        rotated_ref[n * width : (n + 1) * width, :] = dot_fine(dot_tn, small_ref[n], turned)
    start = len(squares) * width
    middle = start + ff_width
    clipped = early[2 * width : 3 * width]
    in_grad_ref[...] = clipped
    turned = dot_fine(dot_tn, clipped, small_ref[16])
    rotated_ref[start:middle, :] = dot_fine(dot_tn, big_ref[0], turned)
    clipped = early[3 * width : 4 * width]
    out_grad_ref[...] = clipped
    turned = dot_fine(dot_tn, clipped, small_ref[17])
    rotated_ref[middle : middle + ff_width, :] = dot_fine(dot_tn, big_ref[1], turned)

    base = lax.axis_index("rows") * slots

    @pl.loop(0, slots // 8)
    def _(step):
        for n in range(8):
            row = owner_ref[base + step * 8 + n]
            own_ref[pl.ds(step * 8 + n, 1), :] = rotated_ref[pl.ds(row, 1), :]

    first_new, second_new, _ = moment_rule(own_ref[...], first_ref[...], second_ref[...])
    first_new_ref[...] = first_new
    second_new_ref[...] = second_new

    def step_of(first_row, count):
        rows = slice(first_row, first_row + count)
        banks = sorted_ref[rows, :].astype(F32)
        return moment_rule(rotated_ref[rows, :], banks[:, :width], banks[:, width:])[2]

    for n in range(len(squares)):
        turned = dot_fine(dot_nt, step_of(n * width, width), small_ref[8 + n])
        update = dot_fine(dot_nn, small_ref[n], turned)
        old = proj_ref[n] if n < 6 else (feat_out_ref if n == 6 else item_out_ref)[...]
        new = old - LEARN_RATE * root_mean(old) * update
        square_new_ref[n] = new
        square_low_ref[n] = new.astype(BF16)
    turned = dot_fine(dot_nn, big_ref[0], step_of(start, ff_width))
    update = dot_fine(dot_nt, small_ref[16], turned)
    new = mlp_in_ref[...] - LEARN_RATE * root_mean(mlp_in_ref[...]) * update
    in_new_ref[...] = new
    in_low_ref[...] = new.astype(BF16)
    turned = dot_fine(dot_nn, big_ref[1], step_of(middle, ff_width))
    update = dot_fine(dot_nt, small_ref[17], turned)
    new = mlp_out_ref[...] - LEARN_RATE * root_mean(mlp_out_ref[...]) * update
    out_new_ref[...] = new
    out_low_ref[...] = new.astype(BF16)

    for n in range(3):
        pair = late[2 * width + n : 2 * width + n + 1]
        both = jnp.concatenate([pair[:, :width], pair[:, width:]], axis=0)
        norm_grad_ref[n] = both
        first_new, second_new, change = moment_rule(both, norm_first_ref[n], norm_second_ref[n])
        norm_first_new_ref[n] = first_new
        norm_second_new_ref[n] = second_new
        old = jnp.concatenate([gains_ref[n : n + 1, :], shifts_ref[n : n + 1, :]], axis=0)
        size = jnp.sqrt(jnp.sum(old * old, axis=1, keepdims=True) * (1.0 / width) + 1e-06)
        norm_new_ref[n] = old - LEARN_RATE * size * change


def in_vmem():
    return pl.BlockSpec(memory_space=pltpu.VMEM)


def in_smem():
    return pl.BlockSpec(memory_space=pltpu.SMEM)


def fast_device(
    cells,
    feat_mask,
    train_rows,
    cotangent,
    proj_weights,
    feat_out_w,
    item_out_w,
    mlp_in,
    mlp_out,
    norm_gains,
    norm_shifts,
    bases_small,
    bases_big,
    owner_rows,
    bank_first,
    bank_second,
    norm_first,
    norm_second,
):
    rows_count, cols_count = lax.axis_size("rows"), lax.axis_size("cols")
    rows_dev, width_dev = cells.shape
    width = proj_weights.shape[-1]
    cols_dev = width_dev // width
    rows_all = rows_dev * rows_count
    key_total = rows_all // 4 * 3
    head_rows = HEADS * rows_dev
    slots = RowGather.slots(rows_count)
    dma = pltpu.SemaphoreType.DMA
    shape = jax.ShapeDtypeStruct
    devices = rows_count * cols_count
    sizes = {"z": rows_count // 4, "x": 2, "k": 2, "y": cols_count}

    mask_rows = feat_mask.T
    mlp_out_turned = mlp_out.T
    norm_first_turned = jnp.transpose(norm_first, (1, 0, 2))
    norm_second_turned = jnp.transpose(norm_second, (1, 0, 2))
    bank_rows = owner_rows.shape[0]

    def block_rows(rows):
        return -(-rows // (16 * devices)) * 16 * devices

    def landings(rows):
        found = []
        for stage in STAGES:
            count = members(stage, sizes)
            rows //= count
            found.append(pltpu.VMEM((count - 1, rows, 2 * width), BF16))
        return found

    early_rows = block_rows(4 * width)
    late_rows = block_rows(2 * width + 3)
    widest = max(members(stage, sizes) for stage in STAGES) - 1
    layer_part, cells_part, early_total, late_total, sorted_banks = pl.pallas_call(
        functools.partial(layer_kernel, rows_count, cols_count),
        name="layer_and_gradients",
        out_shape=(
            shape((rows_dev, width_dev), BF16),
            shape((rows_dev, width_dev), F32),
            shape((early_rows, 2 * width), BF16),
            shape((late_rows, 2 * width), BF16),
            shape((bank_rows, 2 * width), BF16),
        ),
        in_specs=[in_smem()] + [in_vmem()] * 13,
        out_specs=[in_vmem()] * 5,
        scratch_shapes=[
            pltpu.VMEM((rows_dev, width_dev), BF16),
            pltpu.VMEM((rows_all, width_dev), BF16),
            pltpu.VMEM((cols_dev, key_total, width), BF16),
            pltpu.VMEM((cols_dev, key_total, width), BF16),
            pltpu.VMEM((rows_all, width_dev), BF16),
            pltpu.VMEM((16 * cols_dev, rows_all), F32),
            pltpu.VMEM((bank_rows, 2 * width), BF16),
            pltpu.VMEM((cols_dev, head_rows, width), BF16),
            pltpu.VMEM((cols_dev, head_rows, width), BF16),
            pltpu.VMEM((cols_dev, head_rows, 2 * LANES), BF16),
            pltpu.VMEM((cols_dev, head_rows, 1), F32),
            pltpu.VMEM((cols_dev, head_rows, 1), F32),
            pltpu.VMEM((cols_dev, head_rows, width), F32),
            pltpu.VMEM((cols_dev, head_rows, 2 * LANES), F32),
            pltpu.VMEM((cols_dev, 3, 2 * LANES, width), BF16),
            pltpu.VMEM((rows_dev, width_dev), BF16),
            pltpu.VMEM((rows_dev, width_dev), BF16),
            pltpu.VMEM((early_rows, 2 * width), BF16),
            pltpu.VMEM((late_rows, 2 * width), BF16),
        ]
        + landings(early_rows)
        + landings(late_rows)
        + [
            dma((4,)),
            dma((2, 1, slots)),
            dma((2, 2, slots)),
            dma((2, 1, slots)),
            dma((4, len(STAGES), widest)),
            dma((4, len(STAGES), widest)),
        ],
        compiler_params=pltpu.CompilerParams(
            collective_id=0, has_side_effects=True, vmem_limit_bytes=VMEM_BYTES
        ),
    )(
        train_rows,
        owner_rows.reshape(1, bank_rows),
        cells,
        mask_rows,
        cotangent,
        proj_weights,
        feat_out_w,
        item_out_w,
        mlp_in,
        mlp_out_turned,
        norm_gains,
        norm_shifts,
        bank_first,
        bank_second,
    )

    slots_dev = bank_first.shape[0]
    square = (8, width, width)
    (
        layer_out,
        cells_grad,
        square_grads,
        in_grad,
        out_grad,
        norm_grads,
        clip_norm,
        first_new,
        second_new,
        square_new,
        in_new,
        out_new,
        square_low,
        in_low,
        out_low,
        norm_new,
        norm_first_new,
        norm_second_new,
    ) = pl.pallas_call(
        update_kernel,
        name="rotated_update",
        out_shape=(
            shape(layer_part.shape, BF16),
            shape(cells_part.shape, F32),
            shape(square, F32),
            shape(mlp_in.shape, F32),
            shape(mlp_in.shape, F32),
            shape(norm_first_turned.shape, F32),
            shape((1,), F32),
            shape(bank_first.shape, F32),
            shape(bank_first.shape, F32),
            shape(square, F32),
            shape(mlp_in.shape, F32),
            shape(mlp_in.shape, F32),
            shape(square, BF16),
            shape(mlp_in.shape, BF16),
            shape(mlp_in.shape, BF16),
            shape(norm_first_turned.shape, F32),
            shape(norm_first_turned.shape, F32),
            shape(norm_first_turned.shape, F32),
        ),
        in_specs=[in_smem()] + [in_vmem()] * 18,
        out_specs=[in_vmem()] * 6 + [in_smem()] + [in_vmem()] * 11,
        scratch_shapes=[
            pltpu.VMEM((bank_rows, width), F32),
            pltpu.VMEM((slots_dev, width), F32),
        ],
        compiler_params=pltpu.CompilerParams(vmem_limit_bytes=VMEM_BYTES),
    )(
        owner_rows,
        layer_part,
        cells_part,
        early_total,
        late_total,
        sorted_banks,
        bases_small,
        bases_big,
        bank_first,
        bank_second,
        proj_weights,
        feat_out_w,
        item_out_w,
        mlp_in,
        mlp_out_turned,
        norm_gains,
        norm_shifts,
        norm_first_turned,
        norm_second_turned,
    )
    return (
        layer_out,
        cells_grad,
        square_grads,
        in_grad,
        out_grad.T,
        jnp.transpose(norm_grads, (1, 0, 2)),
        clip_norm,
        first_new,
        second_new,
        square_new,
        in_new,
        out_new.T,
        square_low,
        in_low,
        out_low.T,
        jnp.transpose(norm_new, (1, 0, 2)),
        jnp.transpose(norm_first_new, (1, 0, 2)),
        jnp.transpose(norm_second_new, (1, 0, 2)),
    )


def solution(mesh):
    in_specs = (
        P("rows", "cols"),
        P("rows", None),
        P(),
        P("rows", "cols"),
        P(),
        P(),
        P(),
        P(),
        P(),
        P(),
        P(),
        P(),
        P(),
        P(),
        P("rows", None),
        P("rows", None),
        P(),
        P(),
    )
    out_specs = (
        P("rows", "cols"),
        P("rows", "cols"),
        P(),
        P(),
        P(),
        P(),
        P(),
        P("rows", None),
        P("rows", None),
        P(),
        P(),
        P(),
        P(),
        P(),
        P(),
        P(),
        P(),
        P(),
    )
    small = mesh.shape["rows"] == 16 and mesh.shape["cols"] == 2
    return jax.shard_map(
        fast_device if small else per_device, mesh=mesh, in_specs=in_specs, out_specs=out_specs, check_vma=False
    )
```

```python
import functools
import math

import jax
import jax.numpy as jnp
from jax import lax
from jax.experimental import pallas as pl
from jax.experimental.pallas import tpu as pltpu
from jax.sharding import PartitionSpec as P

HEADS = 6
STEP = 10


HIGHEST = lax.Precision.HIGHEST
NEGATIVE = -1e30
CLIP_NORM = 1.0
BETA_ONE = 0.9
BETA_TWO = 0.95
EPSILON = 1e-08
LEARN_RATE = 1.0


def layer_norm(hidden, gain_row, shift_row):
    center = jnp.mean(hidden, axis=-1, keepdims=True)
    centered = hidden - center
    spread = jnp.mean(centered * centered, axis=-1, keepdims=True)
    return centered * lax.rsqrt(spread + 1e-05) * gain_row + shift_row


def gelu_exact(hidden):
    return jax.nn.gelu(hidden, approximate=False)


def product(left_side, right_side):
    return jnp.dot(left_side, right_side, preferred_element_type=jnp.float32)


def product_left(left_side, right_side):
    return lax.dot_general(
        left_side, right_side, (((0,), (0,)), ((), ())), preferred_element_type=jnp.float32
    )


def product_right(left_side, right_side):
    return lax.dot_general(
        left_side, right_side, (((1,), (1,)), ((), ())), preferred_element_type=jnp.float32
    )


def feature_forward(queries, key_rows, value_rows, key_open):
    scaling = queries.shape[-1] ** (-0.5)
    scores = (
        jnp.einsum("nqhe,nkhe->nhqk", queries, key_rows, preferred_element_type=jnp.float32)
        * scaling
    )
    scores = jnp.where(key_open[:, None, None, :], scores, NEGATIVE)
    attend = jax.nn.softmax(scores, axis=-1)
    attend_low = attend.astype(jnp.bfloat16)
    mixed = jnp.einsum(
        "nhqk,nkhe->nqhe", attend_low, value_rows, preferred_element_type=jnp.float32
    )
    return (attend, attend_low, mixed.astype(jnp.bfloat16))


def feature_backward(queries, key_rows, value_rows, attend, attend_low, mixed_grad):
    scaling = queries.shape[-1] ** (-0.5)
    value_dots = jnp.einsum(
        "nqhe,nkhe->nhqk", mixed_grad, value_rows, preferred_element_type=jnp.float32
    )
    row_delta = jnp.sum(attend * value_dots, axis=-1, keepdims=True)
    score_grad = (attend * (value_dots - row_delta)).astype(jnp.bfloat16)
    query_grad = (
        jnp.einsum("nhqk,nkhe->nqhe", score_grad, key_rows, preferred_element_type=jnp.float32)
        * scaling
    )
    key_grad = (
        jnp.einsum("nhqk,nqhe->nkhe", score_grad, queries, preferred_element_type=jnp.float32)
        * scaling
    )
    value_grad = jnp.einsum(
        "nhqk,nqhe->nkhe", attend_low, mixed_grad, preferred_element_type=jnp.float32
    )
    return (
        query_grad.astype(jnp.bfloat16),
        key_grad.astype(jnp.bfloat16),
        value_grad.astype(jnp.bfloat16),
    )


def key_blocks_of(key_rows, value_rows):
    key_total = key_rows.shape[0]
    block_size = math.gcd(key_total, 1024)
    block_count = key_total // block_size
    tail_shape = key_rows.shape[1:]
    starts = jnp.arange(block_count, dtype=jnp.int32) * block_size
    return (
        key_rows.reshape((block_count, block_size) + tail_shape),
        value_rows.reshape((block_count, block_size) + tail_shape),
        starts,
    )


def block_scores(queries, key_block, start_row, train_count):
    scaling = queries.shape[-1] ** (-0.5)
    scores = (
        jnp.einsum("qche,kche->chqk", queries, key_block, preferred_element_type=jnp.float32)
        * scaling
    )
    open_keys = start_row + jnp.arange(key_block.shape[0], dtype=jnp.int32) < train_count
    return jnp.where(open_keys[None, None, None, :], scores, NEGATIVE)


def item_forward(queries, key_rows, value_rows, train_count):
    key_split, value_split, starts = key_blocks_of(key_rows, value_rows)
    stat_shape = (queries.shape[1], queries.shape[2], queries.shape[0])

    def max_pass(carried, packed):
        running_max, running_sum = carried
        key_block, start_row = packed
        scores = block_scores(queries, key_block, start_row, train_count)
        new_max = jnp.maximum(running_max, jnp.max(scores, axis=-1))
        running_sum = running_sum * jnp.exp(running_max - new_max) + jnp.sum(
            jnp.exp(scores - new_max[..., None]), axis=-1
        )
        return ((new_max, running_sum), None)

    start_max = jnp.full(stat_shape, NEGATIVE, jnp.float32)
    (row_max, row_sum), _ = lax.scan(
        max_pass, (start_max, jnp.zeros(stat_shape, jnp.float32)), (key_split, starts)
    )
    log_total = row_max + jnp.log(row_sum)

    def value_pass(carried, packed):
        key_block, value_block, start_row = packed
        attend = jnp.exp(
            block_scores(queries, key_block, start_row, train_count) - log_total[..., None]
        )
        added = jnp.einsum(
            "chqk,kche->qche",
            attend.astype(jnp.bfloat16),
            value_block,
            preferred_element_type=jnp.float32,
        )
        return (carried + added, None)

    item_full, _ = lax.scan(
        value_pass, jnp.zeros(queries.shape, jnp.float32), (key_split, value_split, starts)
    )
    return (log_total, item_full)


def delta_of(mixed_grad, item_full):
    return jnp.transpose(jnp.sum(mixed_grad.astype(jnp.float32) * item_full, axis=-1), (1, 2, 0))


def item_backward(queries, key_rows, value_rows, train_count, log_total, mixed_grad, item_full):
    key_split, value_split, starts = key_blocks_of(key_rows, value_rows)
    scaling = queries.shape[-1] ** (-0.5)
    row_delta = delta_of(mixed_grad, item_full)

    def back_pass(carried, packed):
        key_block, value_block, start_row = packed
        attend = jnp.exp(
            block_scores(queries, key_block, start_row, train_count) - log_total[..., None]
        )
        value_dots = jnp.einsum(
            "qche,kche->chqk", mixed_grad, value_block, preferred_element_type=jnp.float32
        )
        score_grad = (attend * (value_dots - row_delta[..., None])).astype(jnp.bfloat16)
        carried = carried + jnp.einsum(
            "chqk,kche->qche", score_grad, key_block, preferred_element_type=jnp.float32
        )
        key_grad = (
            jnp.einsum("chqk,qche->kche", score_grad, queries, preferred_element_type=jnp.float32)
            * scaling
        )
        value_grad = jnp.einsum(
            "chqk,qche->kche",
            attend.astype(jnp.bfloat16),
            mixed_grad,
            preferred_element_type=jnp.float32,
        )
        return (carried, (key_grad, value_grad))

    query_sum, (key_grads, value_grads) = lax.scan(
        back_pass, jnp.zeros(queries.shape, jnp.float32), (key_split, value_split, starts)
    )
    key_total = key_rows.shape[0]
    flat_width = queries.shape[1] * queries.shape[2] * queries.shape[3]
    return (
        query_sum * scaling,
        key_grads.reshape(key_total, flat_width),
        value_grads.reshape(key_total, flat_width),
    )


def clip_all(gradients):
    total_sq = jnp.sum(gradients[0] * gradients[0])
    for extra in gradients[1:]:
        total_sq = total_sq + jnp.sum(extra * extra)
    grad_norm = jnp.sqrt(total_sq)
    factor = jnp.minimum(1.0, CLIP_NORM / grad_norm)
    return ([gradient * factor for gradient in gradients], grad_norm)


def rotate_bank(square_grad, in_grad, out_grad, bases_small, bases_big):
    model_width = in_grad.shape[0]
    left_bases = bases_small[0:8]
    right_bases = bases_small[8:16]
    rot_square = jnp.matmul(
        jnp.swapaxes(left_bases, 1, 2),
        jnp.matmul(square_grad, right_bases, precision=HIGHEST),
        precision=HIGHEST,
    )
    rot_in = jnp.dot(
        bases_small[16].T, jnp.dot(in_grad, bases_big[0], precision=HIGHEST), precision=HIGHEST
    )
    rot_out = jnp.dot(
        bases_big[1].T, jnp.dot(out_grad, bases_small[17], precision=HIGHEST), precision=HIGHEST
    )
    return jnp.concatenate(
        [rot_square.reshape(8 * model_width, model_width), rot_in.T, rot_out], axis=0
    )


def rotate_back(step_bank, bases_small, bases_big):
    model_width = step_bank.shape[1]
    ff_width = (step_bank.shape[0] - 8 * model_width) // 2
    step_square = step_bank[: 8 * model_width].reshape(8, model_width, model_width)
    step_in = step_bank[8 * model_width : 8 * model_width + ff_width].T
    step_out = step_bank[8 * model_width + ff_width :]
    up_square = jnp.matmul(
        bases_small[0:8],
        jnp.matmul(step_square, jnp.swapaxes(bases_small[8:16], 1, 2), precision=HIGHEST),
        precision=HIGHEST,
    )
    up_in = jnp.dot(
        bases_small[16], jnp.dot(step_in, bases_big[0].T, precision=HIGHEST), precision=HIGHEST
    )
    up_out = jnp.dot(
        bases_big[1], jnp.dot(step_out, bases_small[17].T, precision=HIGHEST), precision=HIGHEST
    )
    return (up_square, up_in, up_out)


def adam_rows(gradient, first_old, second_old, step_float):
    first_new = BETA_ONE * first_old + (1.0 - BETA_ONE) * gradient
    second_new = BETA_TWO * second_old + (1.0 - BETA_TWO) * gradient * gradient
    first_hat = first_new / (1.0 - jnp.power(BETA_ONE, step_float))
    second_hat = second_new / (1.0 - jnp.power(BETA_TWO, step_float))
    return (first_new, second_new, first_hat / (jnp.sqrt(second_hat) + EPSILON))


def trusted(weight, update, over_axes):
    scaling = jnp.sqrt(jnp.mean(weight * weight, axis=over_axes, keepdims=True) + 1e-06)
    return weight - LEARN_RATE * scaling * update


def per_device(
    cells,
    feat_mask,
    train_rows,
    cotangent,
    proj_weights,
    feat_out_w,
    item_out_w,
    mlp_in,
    mlp_out,
    norm_gains,
    norm_shifts,
    bases_small,
    bases_big,
    owner_rows,
    bank_first,
    bank_second,
    norm_first,
    norm_second,
):
    rows_dev, width_dev = cells.shape
    model_width = proj_weights.shape[-1]
    head_count = HEADS
    head_dim = model_width // head_count
    cols_dev = width_dev // model_width
    col_count = lax.axis_size("cols")
    all_cols = cols_dev * col_count
    half_rows = rows_dev // col_count
    cell_count = rows_dev * cols_dev
    proj_low = proj_weights.astype(jnp.bfloat16)
    feat_qkv = jnp.concatenate([proj_low[0], proj_low[1], proj_low[2]], axis=1)
    item_qkv = jnp.concatenate([proj_low[3], proj_low[4], proj_low[5]], axis=1)
    feat_out_low = feat_out_w.astype(jnp.bfloat16)
    item_out_low = item_out_w.astype(jnp.bfloat16)
    mlp_in_cast = mlp_in.astype(jnp.bfloat16)
    mlp_out_cast = mlp_out.astype(jnp.bfloat16)
    train_count = train_rows[0]
    column_cells = lax.all_to_all(cells, "cols", split_axis=0, concat_axis=1, tiled=True)
    column_flat = column_cells.reshape(half_rows * all_cols, model_width)
    row_mask = (
        lax.dynamic_slice_in_dim(feat_mask, lax.axis_index("cols") * half_rows, half_rows, 0) > 0
    )
    feat_proj = (
        product(column_flat, feat_qkv)
        .astype(jnp.bfloat16)
        .reshape(half_rows, all_cols, 3, head_count, head_dim)
    )
    feat_query = feat_proj[:, :, 0]
    feat_key = feat_proj[:, :, 1]
    feat_value = feat_proj[:, :, 2]
    feat_attend, feat_attend_low, feat_mixed = feature_forward(
        feat_query, feat_key, feat_value, row_mask
    )
    feat_mixed_flat = feat_mixed.reshape(half_rows * all_cols, model_width)
    feat_branch = (
        product(feat_mixed_flat, feat_out_low)
        .astype(jnp.bfloat16)
        .reshape(half_rows, all_cols * model_width)
    )
    feat_back = lax.all_to_all(feat_branch, "cols", split_axis=1, concat_axis=0, tiled=True)
    inputs_flat = cells.astype(jnp.float32).reshape(cell_count, model_width)
    first_sum = inputs_flat + feat_back.astype(jnp.float32).reshape(cell_count, model_width)
    first_out, first_pull = jax.vjp(layer_norm, first_sum, norm_gains[0], norm_shifts[0])
    first_low = first_out.astype(jnp.bfloat16)
    item_proj = product(first_low, item_qkv).astype(jnp.bfloat16)
    item_query = item_proj[:, :model_width].reshape(rows_dev, cols_dev, head_count, head_dim)
    item_key = item_proj[:, model_width : 2 * model_width].reshape(rows_dev, width_dev)
    item_value = item_proj[:, 2 * model_width :].reshape(rows_dev, width_dev)
    key_rows, value_rows = (
        lax.all_gather(item_key, "rows", axis=0, tiled=True),
        lax.all_gather(item_value, "rows", axis=0, tiled=True),
    )
    key_total = key_rows.shape[0]
    key_rows = key_rows.reshape(key_total, cols_dev, head_count, head_dim)
    value_rows = value_rows.reshape(key_total, cols_dev, head_count, head_dim)
    log_total, item_full = item_forward(item_query, key_rows, value_rows, train_count)
    item_low = item_full.astype(jnp.bfloat16).reshape(cell_count, model_width)
    item_branch = product(item_low, item_out_low)
    second_sum = first_out + item_branch
    second_out, second_pull = jax.vjp(layer_norm, second_sum, norm_gains[1], norm_shifts[1])
    second_low = second_out.astype(jnp.bfloat16)
    hidden_pre = product(second_low, mlp_in_cast)
    hidden_act, gelu_pull = jax.vjp(gelu_exact, hidden_pre)
    hidden_low = hidden_act.astype(jnp.bfloat16)
    mlp_branch = product(hidden_low, mlp_out_cast)
    third_sum = second_out + mlp_branch
    third_out, third_pull = jax.vjp(layer_norm, third_sum, norm_gains[2], norm_shifts[2])
    layer_out = third_out.astype(jnp.bfloat16).reshape(rows_dev, width_dev)
    third_grad, gain_three, shift_three = third_pull(
        cotangent.astype(jnp.float32).reshape(cell_count, model_width)
    )
    branch_low = third_grad.astype(jnp.bfloat16)
    mlp_out_grad = product_left(hidden_low, branch_low)
    hidden_grad = product_right(branch_low, mlp_out_cast)
    (pre_grad,) = gelu_pull(hidden_grad)
    pre_low = pre_grad.astype(jnp.bfloat16)
    mlp_in_grad = product_left(second_low, pre_low)
    second_grad = third_grad + product_right(pre_low, mlp_in_cast)
    second_in_grad, gain_two, shift_two = second_pull(second_grad)
    item_branch_low = second_in_grad.astype(jnp.bfloat16)
    item_out_grad = product_left(item_low, item_branch_low)
    item_mixed_grad = (
        product_right(item_branch_low, item_out_low)
        .astype(jnp.bfloat16)
        .reshape(rows_dev, cols_dev, head_count, head_dim)
    )
    key_again, value_again = (
        lax.all_gather(item_key, "rows", axis=0, tiled=True),
        lax.all_gather(item_value, "rows", axis=0, tiled=True),
    )
    key_rows = key_again.reshape(key_total, cols_dev, head_count, head_dim)
    value_rows = value_again.reshape(key_total, cols_dev, head_count, head_dim)
    query_sum, key_grads, value_grads = item_backward(
        item_query, key_rows, value_rows, train_count, log_total, item_mixed_grad, item_full
    )
    key_sum, value_sum = (
        lax.psum_scatter(key_grads, "rows", scatter_dimension=0, tiled=True),
        lax.psum_scatter(value_grads, "rows", scatter_dimension=0, tiled=True),
    )
    item_grad_low = jnp.concatenate(
        [
            query_sum.astype(jnp.bfloat16).reshape(cell_count, model_width),
            key_sum.astype(jnp.bfloat16).reshape(cell_count, model_width),
            value_sum.astype(jnp.bfloat16).reshape(cell_count, model_width),
        ],
        axis=1,
    )
    item_qkv_grad = product_left(first_low, item_grad_low)
    first_grad = second_in_grad + product_right(item_grad_low, item_qkv)
    first_in_grad, gain_one, shift_one = first_pull(first_grad)
    feat_branch_grad = first_in_grad.astype(jnp.bfloat16).reshape(rows_dev, width_dev)
    column_grad = lax.all_to_all(
        feat_branch_grad, "cols", split_axis=0, concat_axis=1, tiled=True
    ).reshape(half_rows * all_cols, model_width)
    feat_out_grad = product_left(feat_mixed_flat, column_grad)
    feat_mixed_grad = (
        product_right(column_grad, feat_out_low)
        .astype(jnp.bfloat16)
        .reshape(half_rows, all_cols, head_count, head_dim)
    )
    feat_query_grad, feat_key_grad, feat_value_grad = feature_backward(
        feat_query, feat_key, feat_value, feat_attend, feat_attend_low, feat_mixed_grad
    )
    feat_grad_low = jnp.concatenate(
        [
            feat_query_grad.reshape(half_rows * all_cols, model_width),
            feat_key_grad.reshape(half_rows * all_cols, model_width),
            feat_value_grad.reshape(half_rows * all_cols, model_width),
        ],
        axis=1,
    )
    feat_qkv_grad = product_left(column_flat, feat_grad_low)
    column_in_grad = (
        product_right(feat_grad_low, feat_qkv)
        .astype(jnp.bfloat16)
        .reshape(half_rows, all_cols * model_width)
    )
    row_in_grad = lax.all_to_all(column_in_grad, "cols", split_axis=1, concat_axis=0, tiled=True)
    cells_grad = first_in_grad.reshape(rows_dev, width_dev) + row_in_grad.astype(jnp.float32)
    proj_grad = jnp.stack(
        [
            feat_qkv_grad[:, :model_width],
            feat_qkv_grad[:, model_width : 2 * model_width],
            feat_qkv_grad[:, 2 * model_width :],
            item_qkv_grad[:, :model_width],
            item_qkv_grad[:, model_width : 2 * model_width],
            item_qkv_grad[:, 2 * model_width :],
        ]
    )
    norm_grad = jnp.stack(
        [
            jnp.stack([gain_one, gain_two, gain_three]),
            jnp.stack([shift_one, shift_two, shift_three]),
        ]
    )
    proj_total, feat_total, item_total, in_total, out_total, norm_total = lax.psum(
        (proj_grad, feat_out_grad, item_out_grad, mlp_in_grad, mlp_out_grad, norm_grad),
        ("rows", "cols"),
    )
    square_grad = jnp.concatenate([proj_total, feat_total[None], item_total[None]], axis=0)
    clipped, grad_norm = clip_all([square_grad, in_total, out_total, norm_total])
    square_clip, in_clip, out_clip, norm_clip = clipped
    rot_bank = rotate_bank(square_clip, in_clip, out_clip, bases_small, bases_big)
    step_float = jnp.asarray(STEP, jnp.float32)
    slot_count = bank_first.shape[0]
    my_slots = lax.dynamic_slice_in_dim(
        owner_rows, lax.axis_index("rows") * slot_count, slot_count, 0
    )
    first_new, second_new, slot_steps = adam_rows(
        jnp.take(rot_bank, my_slots, axis=0), bank_first, bank_second, step_float
    )
    all_steps = lax.all_gather(slot_steps, "rows", axis=0, tiled=True)
    full_steps = jnp.take(all_steps, jnp.argsort(owner_rows), axis=0)
    up_square, up_in, up_out = rotate_back(full_steps, bases_small, bases_big)
    square_old = jnp.concatenate([proj_weights, feat_out_w[None], item_out_w[None]], axis=0)
    square_new = trusted(square_old, up_square, (1, 2))
    in_new = trusted(mlp_in, up_in, (0, 1))
    out_new = trusted(mlp_out, up_out, (0, 1))
    norm_old = jnp.stack([norm_gains, norm_shifts])
    norm_first_new, norm_second_new, norm_steps = adam_rows(
        norm_clip, norm_first, norm_second, step_float
    )
    norm_new = trusted(norm_old, norm_steps, (2,))
    return (
        layer_out,
        cells_grad,
        square_clip,
        in_clip,
        out_clip,
        norm_clip,
        grad_norm.reshape(1),
        first_new,
        second_new,
        square_new,
        in_new,
        out_new,
        square_new.astype(jnp.bfloat16),
        in_new.astype(jnp.bfloat16),
        out_new.astype(jnp.bfloat16),
        norm_new,
        norm_first_new,
        norm_second_new,
    )


F32 = jnp.float32
BF16 = jnp.bfloat16
MESH = pl.DeviceIdType.MESH
VMEM_BYTES = 56 * 1024 * 1024
LANES = 128


def dot_nn(left, right):
    return jnp.dot(left, right, preferred_element_type=F32)


def dot_nt(left, right):
    return lax.dot_general(left, right, (((1,), (1,)), ((), ())), preferred_element_type=F32)


def dot_tn(left, right):
    return lax.dot_general(left, right, (((0,), (0,)), ((), ())), preferred_element_type=F32)


def split_two(value):
    high = value.astype(BF16)
    return high, (value - high.astype(F32)).astype(BF16)


def dot_low(dot, left, right):
    return dot(left.astype(BF16), right.astype(BF16))


def stack_columns(packed, width):
    count = packed.shape[1] // width
    return jnp.concatenate([packed[:, n * width : (n + 1) * width] for n in range(count)], axis=0)


def pack_columns(stacked, rows):
    count = stacked.shape[0] // rows
    return jnp.concatenate([stacked[n * rows : (n + 1) * rows] for n in range(count)], axis=1)


def norm_parts(hidden):
    width = hidden.shape[1]
    center = jnp.sum(hidden, axis=1, keepdims=True) * (1.0 / width)
    centered = hidden - center
    spread = jnp.sum(centered * centered, axis=1, keepdims=True) * (1.0 / width)
    root = lax.rsqrt(spread + 1e-05)
    return centered * root, root


def norm_back(unit, root, gain, incoming):
    width = unit.shape[1]
    scaled = incoming * gain
    mean_one = jnp.sum(scaled, axis=1, keepdims=True) * (1.0 / width)
    mean_two = jnp.sum(scaled * unit, axis=1, keepdims=True) * (1.0 / width)
    gain_grad = jnp.sum(incoming * unit, axis=0, keepdims=True)
    shift_grad = jnp.sum(incoming, axis=0, keepdims=True)
    return root * (scaled - mean_one - unit * mean_two), gain_grad, shift_grad


def head_table(width, head_dim):
    feature = lax.broadcasted_iota(jnp.int32, (width, LANES), 0)
    head = lax.broadcasted_iota(jnp.int32, (width, LANES), 1)
    inside = (feature >= head * head_dim) & (feature < (head + 1) * head_dim)
    return jnp.where(inside, 1.0, 0.0).astype(BF16)


def spread_table(width, head_dim):
    head = lax.broadcasted_iota(jnp.int32, (LANES, width), 0)
    feature = lax.broadcasted_iota(jnp.int32, (LANES, width), 1)
    inside = (feature >= head * head_dim) & (feature < (head + 1) * head_dim)
    return jnp.where(inside, 1.0, 0.0).astype(BF16)


def head_rows_of(value, wide):
    high, low = split_two(value)
    return dot_nt(wide, high) + dot_nt(wide, low)


def head_sums(value, table):
    high, low = split_two(value)
    return dot_nn(high, table) + dot_nn(low, table)


def head_mask(rows, width, head_dim, head, offset=0):
    feature = lax.broadcasted_iota(jnp.int32, (rows, width), 1)
    start = offset + head * head_dim
    return (feature >= start) & (feature < start + head_dim)


def tile_rows(value, count):
    return jnp.concatenate([value] * count, axis=0)


def column_open(mask_ref, own_first, cols_dev, slot):
    table = jnp.transpose(mask_ref[...].astype(F32))
    if slot < cols_dev:
        first, second = slot, slot + cols_dev
    else:
        first, second = slot, slot - cols_dev
    picked = jnp.where(own_first, table[:, first : first + 1], table[:, second : second + 1])
    return picked > 0.0


def feature_weights(queries, key_list, open_list, repeat, table, scaling):
    scores = []
    for keys, is_open in zip(key_list, open_list):
        raw = head_sums(queries * tile_rows(keys, repeat), table) * scaling
        scores.append(jnp.where(tile_rows(is_open, repeat), raw, NEGATIVE))
    top = scores[0]
    for extra in scores[1:]:
        top = jnp.maximum(top, extra)
    grown = [jnp.exp(score - top) for score in scores]
    total = grown[0]
    for extra in grown[1:]:
        total = total + extra
    return [part / total for part in grown]


def flip(value, pattern, size):
    out, step = 0, 1
    while step < size:
        out = out + step * (((value // step) % 2 + (pattern // step) % 2) % 2)
        step *= 2
    return out


class RowGather:
    def __init__(self, pieces, send_sem, recv_sem, rows_count):
        self.pieces, self.send_sem, self.recv_sem = pieces, send_sem, recv_sem
        self.deep = rows_count // 4
        me = lax.axis_index("rows")
        self.core, self.side, self.depth = me % 2, (me // 2) % 2, me // 4

    @staticmethod
    def slots(rows_count):
        return rows_count - 1

    def place(self, depth, side, core):
        return (depth * 2 + side) * 2 + core

    def source(self, k):
        return flip(self.depth, k, self.deep)

    def side_peer(self):
        return self.place(self.depth, 1 - self.side, self.core)

    def core_peer(self):
        return self.place(self.depth, self.side, 1 - self.core)

    def copies(self, shard, target, slot):
        return [
            pltpu.make_async_remote_copy(
                src_ref=piece(shard),
                dst_ref=piece(shard),
                send_sem=self.send_sem.at[n, slot],
                recv_sem=self.recv_sem.at[n, slot],
                device_id={"rows": target},
                device_id_type=MESH,
            )
            for n, piece in enumerate(self.pieces)
        ]

    def push(self, shard, target, slot):
        for copy in self.copies(shard, target, slot):
            copy.start()

    def arrive(self, shard, source, slot):
        for copy in self.copies(shard, source, slot):
            copy.wait_recv()

    def start_depth(self):
        own = self.place(self.depth, self.side, self.core)
        for k in range(1, self.deep):
            self.push(own, self.place(self.source(k), self.side, self.core), k - 1)

    def start_near(self):
        own = self.place(self.depth, self.side, self.core)
        self.push(own, self.core_peer(), 2 * self.deep - 1)
        self.push(own, self.side_peer(), self.deep - 1)

    def along_depth(self, k):
        shard = self.place(self.source(k), self.side, self.core)
        self.arrive(shard, shard, k - 1)
        self.push(shard, self.side_peer(), self.deep - 1 + k)
        self.push(shard, self.core_peer(), 2 * self.deep - 1 + k)

    def across_side(self, k):
        shard = self.place(self.source(k), 1 - self.side, self.core)
        self.arrive(shard, self.side_peer(), self.deep - 1 + k)
        self.push(shard, self.core_peer(), 3 * self.deep - 1 + k)

    def from_core(self, k, other_side):
        side = self.side + other_side - 2 * self.side * other_side
        shard = self.place(self.source(k), side, 1 - self.core)
        self.arrive(shard, self.core_peer(), (2 + other_side) * self.deep - 1 + k)

    def run(self, use):
        self.across_side(0)

        @pl.loop(0, 2 * self.deep)
        def _(turn):
            k, other = turn // 2, turn % 2

            @pl.when((k + 1 < self.deep) & (other == 0))
            def _():
                self.along_depth(k + 1)

            @pl.when((k + 1 < self.deep) & (other == 1))
            def _():
                self.across_side(k + 1)

            self.from_core(k, other)
            use(self.source(k), self.side + other - 2 * self.side * other)

    def wait_sent(self):
        own = self.place(self.depth, self.side, self.core)

        @pl.loop(0, 4 * self.deep - 1)
        def _(slot):
            for copy in self.copies(own, self.core_peer(), slot):
                copy.wait_send()


class StagedSum:
    def __init__(self, stages, sizes, part_ref, total_ref, landing, sems):
        self.stages, self.sizes = stages, sizes
        self.part_ref, self.total_ref, self.landing, self.sems = part_ref, total_ref, landing, sems
        row = lax.axis_index("rows")
        self.me = {"z": row // 4, "x": (row // 2) % 2, "k": row % 2, "y": lax.axis_index("cols")}
        self.spans, base, size = [], 0, part_ref.shape[0]
        for stage in stages:
            size = size // members(stage, sizes)
            self.spans.append((base, size))
            base = base + self.number(self.me, stage) * size
        self.base, self.size = base, size
        self.unit = size

    def number(self, place, stage):
        out, scale = 0, 1
        for axis in stage:
            out = out + place[axis] * scale
            scale *= self.sizes[axis]
        return out

    def partner(self, stage, pattern):
        place = dict(self.me)
        for axis in stage:
            place[axis] = flip(self.me[axis], pattern % self.sizes[axis], self.sizes[axis])
            pattern //= self.sizes[axis]
        return place

    def device(self, place):
        return {"rows": (place["z"] * 2 + place["x"]) * 2 + place["k"], "cols": place["y"]}

    def rows_at(self, base, size):
        return pl.ds(pl.multiple_of(base, self.unit), size)

    def scatter(self, s):
        stage, (base, size) = self.stages[s], self.spans[s]
        found = []
        for j in range(1, members(stage, self.sizes)):
            place = self.partner(stage, j)
            rows = self.rows_at(base + self.number(place, stage) * size, size)
            found.append(
                pltpu.make_async_remote_copy(
                    src_ref=self.part_ref.at[rows, :],
                    dst_ref=self.landing[s].at[j - 1],
                    send_sem=self.sems.at[0, s, j - 1],
                    recv_sem=self.sems.at[1, s, j - 1],
                    device_id=self.device(place),
                    device_id_type=MESH,
                )
            )
        return found

    def scatter_start(self, s):
        for copy in self.scatter(s):
            copy.start()

    def scatter_finish(self, s):
        stage, (base, size) = self.stages[s], self.spans[s]
        rows = self.rows_at(base + self.number(self.me, stage) * size, size)
        total = self.part_ref[rows, :].astype(F32)
        copies = self.scatter(s)
        for j, copy in enumerate(copies):
            copy.wait_recv()
            total = total + self.landing[s][j].astype(F32)
        for copy in copies:
            copy.wait_send()
        target = self.total_ref if s == len(self.stages) - 1 else self.part_ref
        target[rows, :] = total.astype(BF16)

    def gather(self, s, own):
        stage, (base, size) = self.stages[s], self.spans[s]
        found = []
        for j in range(1, members(stage, self.sizes)):
            place = self.partner(stage, j)
            holder = self.me if own else place
            rows = self.rows_at(base + self.number(holder, stage) * size, size)
            found.append(
                pltpu.make_async_remote_copy(
                    src_ref=self.total_ref.at[rows, :],
                    dst_ref=self.total_ref.at[rows, :],
                    send_sem=self.sems.at[2, s, j - 1],
                    recv_sem=self.sems.at[3, s, j - 1],
                    device_id=self.device(place),
                    device_id_type=MESH,
                )
            )
        return found

    def gather_start(self, s):
        for copy in self.gather(s, True):
            copy.start()

    def gather_finish(self, s):
        for copy in self.gather(s, False):
            copy.wait_recv()
        for copy in self.gather(s, True):
            copy.wait_send()


class Mover:
    def __init__(self, sem):
        self.sem, self.count = sem, 0

    def start(self, source, target):
        copy = pltpu.make_async_copy(source, target, self.sem.at[self.count])
        copy.start()
        self.count += 1
        return copy


def put_tiles(ref, row, value):
    rows, lanes = value.shape
    if lanes % LANES:
        value = jnp.concatenate([value, jnp.zeros((rows, LANES - lanes % LANES), F32)], axis=1)
    for n in range(value.shape[1] // LANES):
        ref[row : row + rows, :] = value[:, n * LANES : (n + 1) * LANES].astype(ref.dtype)
        row += rows
    return row


def put_zeros(ref, row):
    if row < ref.shape[0]:
        ref[row:, :] = jnp.zeros((ref.shape[0] - row, ref.shape[1]), ref.dtype)


def take_tiles(ref, row, rows, lanes):
    count = -(-lanes // LANES)
    tiles = [ref[row + n * rows : row + (n + 1) * rows, :].astype(F32) for n in range(count)]
    value = jnp.concatenate(tiles, axis=1)
    return value if lanes % LANES == 0 else value[:, :lanes]


def members(stage, sizes):
    return math.prod(sizes[axis] for axis in stage)


def meet(targets):
    barrier = pltpu.get_barrier_semaphore()
    for target in targets:
        pl.semaphore_signal(barrier, inc=1, device_id=target, device_id_type=MESH)
    pl.semaphore_wait(barrier, len(targets))


def swap_copy(source, landing, send_sem, recv_sem):
    return pltpu.make_async_remote_copy(
        src_ref=source,
        dst_ref=landing,
        send_sem=send_sem,
        recv_sem=recv_sem,
        device_id={"cols": 1 - lax.axis_index("cols")},
        device_id_type=MESH,
    )


def window_of(column, width, width_dev):
    start = (column * width) // LANES * LANES
    offset = column * width - start
    size = -(-(offset + width) // LANES) * LANES
    return start, offset, min(size, width_dev - start)


def padded_weight(weight, offset, size):
    width = weight.shape[1]
    parts = []
    if offset:
        parts.append(jnp.zeros((offset, width), F32))
    parts.append(weight)
    if size - offset - weight.shape[0]:
        parts.append(jnp.zeros((size - offset - weight.shape[0], width), F32))
    return (jnp.concatenate(parts, axis=0) if len(parts) > 1 else weight).astype(BF16)


def padded_turned(weight, offset, size):
    width = weight.shape[0]
    parts = []
    if offset:
        parts.append(jnp.zeros((width, offset), F32))
    parts.append(jnp.transpose(weight))
    if size - offset - width:
        parts.append(jnp.zeros((width, size - offset - width), F32))
    return (jnp.concatenate(parts, axis=1) if len(parts) > 1 else parts[0]).astype(BF16)


def head_blocks(value, head_dim, offset=0, size=None):
    rows, width = value.shape
    if size is not None and size != width:
        parts = []
        if offset:
            parts.append(jnp.zeros((rows, offset), F32))
        parts.append(value)
        if size - offset - width:
            parts.append(jnp.zeros((rows, size - offset - width), F32))
        value = jnp.concatenate(parts, axis=1)
        width = size
    blocks = [
        jnp.where(head_mask(rows, width, head_dim, head, offset), value, 0.0).astype(BF16)
        for head in range(HEADS)
    ]
    return jnp.concatenate(blocks, axis=0)


def gather_heads_turned(value, rows, head_dim):
    blocks = [
        value[head * head_dim : (head + 1) * head_dim, head * rows : (head + 1) * rows]
        for head in range(HEADS)
    ]
    return jnp.transpose(jnp.concatenate(blocks, axis=0))


def gather_heads(value, rows, head_dim, offset=0, width=None):
    total = None
    for head in range(HEADS):
        block = value[head * rows : (head + 1) * rows]
        kept = jnp.where(head_mask(rows, value.shape[1], head_dim, head, offset), block, 0.0)
        total = kept if total is None else total + kept
    if width is not None and width != total.shape[1]:
        total = total[:, offset : offset + width]
    return total


STAGES = ("k", "xy", "z")


def layer_kernel(
    rows_count,
    cols_count,
    train_ref,
    owner_ref,
    cells_ref,
    mask_ref,
    gains_ref,
    shifts_ref,
    proj_in,
    feat_out_in,
    bank_first_in,
    bank_second_in,
    item_out_in,
    mlp_in_in,
    mlp_out_in,
    cotangent_in,
    layer_out,
    cells_grad_out,
    mlp_total_ref,
    item_total_ref,
    feat_total_ref,
    sorted_out,
    proj_ref,
    feat_out_ref,
    bank_first_ref,
    bank_second_ref,
    item_out_ref,
    mlp_in_ref,
    mlp_out_ref,
    cotangent_ref,
    layer_ref,
    cells_grad_ref,
    sorted_ref,
    peer_ref,
    gathered_ref,
    keys_ref,
    keys_turned_ref,
    values_ref,
    grads_ref,
    all_stats_ref,
    banks_ref,
    blocks_ref,
    grad_blocks_ref,
    wide_blocks_ref,
    top_ref,
    sum_ref,
    turned_ref,
    total_ref,
    value_total_ref,
    item_w_ref,
    item_turned_ref,
    branch_ref,
    peer_branch_ref,
    mlp_part_ref,
    item_part_ref,
    feat_part_ref,
    mlp_land_k,
    mlp_land_xy,
    mlp_land_z,
    item_land_k,
    item_land_xy,
    item_land_z,
    feat_land_k,
    feat_land_xy,
    feat_land_z,
    swap_sem,
    gather_sem,
    grads_sem,
    banks_sem,
    mlp_sem,
    item_sem,
    feat_sem,
    move_sem,
):
    mover = Mover(move_sem)
    proj_load = mover.start(proj_in, proj_ref)
    feat_out_load = mover.start(feat_out_in, feat_out_ref)
    bank_loads = [
        mover.start(bank_first_in, bank_first_ref),
        mover.start(bank_second_in, bank_second_ref),
    ]
    later_loads = [
        mover.start(source, target)
        for source, target in (
            (item_out_in, item_out_ref),
            (mlp_in_in, mlp_in_ref),
            (mlp_out_in, mlp_out_ref),
            (cotangent_in, cotangent_ref),
        )
    ]
    rows_dev, width_dev = cells_ref.shape
    width = feat_out_ref.shape[0]
    cols_dev = width_dev // width
    head_dim = width // HEADS
    scaling = head_dim ** (-0.5)
    ff_width = mlp_in_ref.shape[1]
    key_total = keys_ref.shape[1]
    chip_rows = 2 * rows_dev
    bank_slots = bank_first_ref.shape[0]
    train_count = train_ref[0]
    me = lax.axis_index("rows")
    sizes = {"z": rows_count // 4, "x": 2, "k": 2, "y": cols_count}
    own_count = cols_dev * rows_dev

    def shard_of(ref, rows):
        return lambda shard: ref.at[pl.ds(pl.multiple_of(shard * rows, rows), rows), :]

    def stats_shard(shard):
        return all_stats_ref.at[:, pl.ds(pl.multiple_of(shard * rows_dev, rows_dev), rows_dev)]

    hidden_gather = RowGather(
        [shard_of(gathered_ref, rows_dev)], gather_sem.at[0], gather_sem.at[1], rows_count
    )
    grads_gather = RowGather(
        [shard_of(grads_ref, rows_dev), stats_shard], grads_sem.at[0], grads_sem.at[1], rows_count
    )
    banks_gather = RowGather(
        [shard_of(banks_ref, bank_slots)], banks_sem.at[0], banks_sem.at[1], rows_count
    )
    mlp_sum = StagedSum(
        STAGES,
        sizes,
        mlp_part_ref,
        mlp_total_ref,
        (mlp_land_k, mlp_land_xy, mlp_land_z),
        mlp_sem,
    )
    item_sum = StagedSum(
        STAGES,
        sizes,
        item_part_ref,
        item_total_ref,
        (item_land_k, item_land_xy, item_land_z),
        item_sem,
    )
    feat_sum = StagedSum(
        STAGES,
        sizes,
        feat_part_ref,
        feat_total_ref,
        (feat_land_k, feat_land_xy, feat_land_z),
        feat_sem,
    )
    meet(
        [
            mlp_sum.device(mlp_sum.partner(stage, j))
            for stage in STAGES
            for j in range(1, members(stage, sizes))
        ]
    )

    swap = swap_copy(cells_ref, peer_ref, swap_sem.at[0], swap_sem.at[1])
    swap.start()
    for load in bank_loads:
        load.wait()
    banks_ref[pl.ds(pl.multiple_of(me * bank_slots, bank_slots), bank_slots), :] = jnp.concatenate(
        [bank_first_ref[...], bank_second_ref[...]], axis=1
    ).astype(BF16)
    banks_gather.start_near()
    banks_gather.start_depth()
    proj_load.wait()
    feat_w = [proj_ref[n].astype(BF16) for n in range(3)]
    own = stack_columns(cells_ref[...].astype(F32), width)
    own_low = own.astype(BF16)
    queries, own_keys, own_values = [
        dot_nn(own_low, weight).astype(BF16).astype(F32) for weight in feat_w
    ]
    table = head_table(width, head_dim)
    wide = spread_table(width, head_dim)
    swap.wait()
    peer_low = stack_columns(peer_ref[...].astype(F32), width).astype(BF16)
    peer_queries, peer_keys, peer_values = [
        dot_nn(peer_low, weight).astype(BF16).astype(F32) for weight in feat_w
    ]
    feat_query = jnp.concatenate([queries, peer_queries], axis=0)
    all_keys = jnp.concatenate([own_keys, peer_keys], axis=0)
    all_values = jnp.concatenate([own_values, peer_values], axis=0)
    slots = all_keys.shape[0] // rows_dev
    own_first = lax.axis_index("cols") == 0
    key_list = [all_keys[n * rows_dev : (n + 1) * rows_dev] for n in range(slots)]
    value_list = [all_values[n * rows_dev : (n + 1) * rows_dev] for n in range(slots)]
    open_list = [column_open(mask_ref, own_first, cols_dev, n) for n in range(slots)]
    weights = feature_weights(feat_query, key_list, open_list, slots, table, scaling)
    mixed = None
    for weight, column_values in zip(weights, value_list):
        added = dot_nn(weight[:own_count].astype(BF16), wide) * tile_rows(column_values, cols_dev)
        mixed = added if mixed is None else mixed + added
    feat_mixed = mixed.astype(BF16)
    feat_out_load.wait()
    feat_out_w = feat_out_ref[...].astype(BF16)
    first_sum = own + dot_nn(feat_mixed, feat_out_w).astype(BF16).astype(F32)
    unit_one, root_one = norm_parts(first_sum)
    first_out = unit_one * gains_ref[0:1, :] + shifts_ref[0:1, :]
    first_low = first_out.astype(BF16)
    own_rows = pl.ds(pl.multiple_of(me * rows_dev, rows_dev), rows_dev)
    gathered_ref[own_rows, :] = pack_columns(first_out, rows_dev).astype(BF16)
    hidden_gather.start_near()
    hidden_gather.start_depth()

    item_w = [proj_ref[3 + n].astype(BF16) for n in range(3)]
    queries, own_keys, own_values = [
        dot_nn(first_low, weight).astype(BF16).astype(F32) for weight in item_w
    ]
    windows = [window_of(column, width, width_dev) for column in range(cols_dev)]
    for column, (_, offset, size) in enumerate(windows):
        for n in range(3):
            item_w_ref[column, n, 0:size, :] = padded_weight(proj_ref[3 + n], offset, size)
        for n in range(2):
            item_turned_ref[column, n, :, 0:size] = padded_turned(proj_ref[4 + n], offset, size)
        blocks_ref[column] = head_blocks(
            queries[column * rows_dev : (column + 1) * rows_dev], head_dim
        )
    top_ref[...] = jnp.full(top_ref.shape, NEGATIVE, F32)
    sum_ref[...] = jnp.zeros(sum_ref.shape, F32)
    turned_ref[...] = jnp.zeros(turned_ref.shape, F32)
    to_log2 = scaling * math.log2(math.e)

    def chip_start(depth, side):
        return pl.multiple_of((depth * 2 + side) * chip_rows, chip_rows)

    def masked_scores(column, keys, start_row):
        raw = dot_nt(keys, blocks_ref[column]) * to_log2
        key_row = lax.broadcasted_iota(jnp.int32, raw.shape, 0)
        return jnp.where(key_row < train_count - start_row, raw, NEGATIVE)

    def attend_chip(depth, side):
        @pl.when(depth * 4 * rows_dev < key_total)
        def _():
            start_row = chip_start(depth, side)
            span = pl.ds(start_row, chip_rows)
            for column, (start, _, size) in enumerate(windows):
                hidden = gathered_ref[span, start : start + size]
                keys = dot_nn(hidden, item_w_ref[column, 1, 0:size, :]).astype(BF16)
                keys_ref[column, span, :] = keys
                values_ref[column, span, :] = dot_nn(
                    hidden, item_w_ref[column, 2, 0:size, :]
                ).astype(BF16)
                keys_turned_ref[column, :, span] = dot_nt(
                    item_turned_ref[column, 0, :, 0:size], hidden
                ).astype(BF16)
                values_turned = dot_nt(item_turned_ref[column, 1, :, 0:size], hidden).astype(BF16)
                scores = masked_scores(column, keys, start_row)
                top_old = top_ref[column]
                top_new = jnp.maximum(top_old, jnp.max(scores, axis=0, keepdims=True))
                grown = jnp.exp2(scores - top_new)
                fade = jnp.exp2(top_old - top_new)
                top_ref[column] = top_new
                sum_ref[column] = sum_ref[column] * fade + jnp.sum(grown, axis=0, keepdims=True)
                turned_ref[column] = turned_ref[column] * fade + dot_nn(
                    values_turned, grown.astype(BF16)
                )

    hidden_gather.run(attend_chip)
    for k in range(1, rows_count // 4):
        banks_gather.along_depth(k)

    item_full, log_totals = [], []
    for column in range(cols_dev):
        item_full.append(
            gather_heads_turned(turned_ref[column] / sum_ref[column], rows_dev, head_dim)
        )
        log_totals.append(top_ref[column] + jnp.log2(sum_ref[column]))

    full = jnp.concatenate(item_full, axis=0)
    item_low = full.astype(BF16)
    for load in later_loads:
        load.wait()
    item_out_w = item_out_ref[...].astype(BF16)
    mlp_in_w = mlp_in_ref[...].astype(BF16)
    mlp_out_w = mlp_out_ref[...].astype(BF16)
    unit_two, root_two = norm_parts(first_out + dot_nn(item_low, item_out_w))
    second_out = unit_two * gains_ref[1:2, :] + shifts_ref[1:2, :]
    second_low = second_out.astype(BF16)
    hidden_pre = dot_nn(second_low, mlp_in_w)
    normal = 0.5 + 0.5 * lax.erf(hidden_pre * (0.5**0.5))
    hidden_low = (hidden_pre * normal).astype(BF16)
    unit_three, root_three = norm_parts(second_out + dot_nt(hidden_low, mlp_out_w))
    third_out = unit_three * gains_ref[2:3, :] + shifts_ref[2:3, :]
    layer_ref[...] = pack_columns(third_out, rows_dev).astype(BF16)
    results = [mover.start(layer_ref, layer_out)]
    incoming = stack_columns(cotangent_ref[...].astype(F32), width)
    third_grad, gain_three, shift_three = norm_back(
        unit_three, root_three, gains_ref[2:3, :], incoming
    )
    branch_low = third_grad.astype(BF16)
    density = jnp.exp(-0.5 * hidden_pre * hidden_pre) * (1.0 / math.sqrt(2.0 * math.pi))
    pre_low = (dot_nn(branch_low, mlp_out_w) * (normal + hidden_pre * density)).astype(BF16)
    second_grad, gain_two, shift_two = norm_back(
        unit_two, root_two, gains_ref[1:2, :], third_grad + dot_nt(pre_low, mlp_in_w)
    )
    second_grad_low = second_grad.astype(BF16)
    mixed_grad = dot_nt(second_grad_low, item_out_w).astype(BF16).astype(F32)
    delta_all = head_rows_of(mixed_grad * full, wide)
    deltas = []
    spare = jnp.zeros((8 - HEADS, rows_dev), F32)
    for column in range(cols_dev):
        part = delta_all[0:8, column * rows_dev : (column + 1) * rows_dev]
        deltas.append(jnp.concatenate([part[h : h + 1] for h in range(HEADS)], axis=1))
        totals = [
            log_totals[column][:, head * rows_dev : (head + 1) * rows_dev]
            for head in range(HEADS)
        ]
        all_stats_ref[16 * column : 16 * column + 8, own_rows] = jnp.concatenate(
            totals + [spare], axis=0
        )
        all_stats_ref[16 * column + 8 : 16 * column + 16, own_rows] = part
    grads_ref[own_rows, :] = pack_columns(mixed_grad, rows_dev).astype(BF16)
    grads_gather.start_near()
    grads_gather.start_depth()

    row = put_tiles(mlp_part_ref, 0, dot_tn(second_low, pre_low))
    row = put_tiles(mlp_part_ref, row, dot_tn(branch_low, hidden_low))
    row = put_tiles(mlp_part_ref, row, dot_tn(item_low, second_grad_low))
    put_zeros(mlp_part_ref, row)
    mlp_sum.scatter_start(0)

    for column in range(cols_dev):
        rows_here = slice(column * rows_dev, (column + 1) * rows_dev)
        grad_blocks_ref[column] = head_blocks(mixed_grad[rows_here], head_dim)
    turned_ref[...] = jnp.zeros(turned_ref.shape, F32)

    @pl.loop(0, key_total // chip_rows)
    def _(step):
        start_row = pl.multiple_of(step * chip_rows, chip_rows)
        span = pl.ds(start_row, chip_rows)
        for column in range(cols_dev):
            keys = keys_ref[column, span, :]
            attend = jnp.exp2(masked_scores(column, keys, start_row) - log_totals[column])
            dots = dot_nt(values_ref[column, span, :], grad_blocks_ref[column])
            score_grad = (attend * (dots - deltas[column])).astype(BF16)
            turned_ref[column] += dot_nn(keys_turned_ref[column, :, span], score_grad)

    query_grads = [
        gather_heads_turned(turned_ref[column], rows_dev, head_dim) * scaling
        for column in range(cols_dev)
    ]
    mlp_sum.scatter_finish(0)
    mlp_sum.scatter_start(1)
    for k in range(rows_count // 4):
        banks_gather.across_side(k)

    for column, (_, offset, size) in enumerate(windows):
        rows_here = slice(column * rows_dev, (column + 1) * rows_dev)
        blocks_ref[column] = head_blocks(own_keys[rows_here], head_dim)
        wide_blocks_ref[column, :, 0:size] = head_blocks(
            own_values[rows_here], head_dim, offset, size
        )
    total_ref[...] = jnp.zeros(total_ref.shape, F32)
    value_total_ref[...] = jnp.zeros(value_total_ref.shape, F32)

    def answer_chip(depth, side):
        span = pl.ds(chip_start(depth, side), chip_rows)
        for column, (start, _, size) in enumerate(windows):
            hidden = gathered_ref[span, start : start + size]
            asked = dot_nn(hidden, item_w_ref[column, 0, 0:size, :]).astype(BF16)
            grads = grads_ref[span, start : start + size]
            scores = dot_nt(blocks_ref[column], asked) * to_log2
            dots = dot_nt(wide_blocks_ref[column, :, 0:size], grads)
            attends, score_grads = [], []
            for head in range(HEADS):
                part = slice(head * rows_dev, (head + 1) * rows_dev)
                log_total = all_stats_ref[16 * column + head : 16 * column + head + 1, span]
                delta = all_stats_ref[16 * column + 8 + head : 16 * column + 9 + head, span]
                attend = jnp.exp2(scores[part] - log_total)
                attends.append(attend.astype(BF16))
                score_grads.append((attend * (dots[part] - delta)).astype(BF16))
            total_ref[column] += dot_nn(jnp.concatenate(score_grads, axis=0), asked)
            value_total_ref[column, :, 0:size] += dot_nn(jnp.concatenate(attends, axis=0), grads)

    grads_gather.run(answer_chip)
    mlp_sum.scatter_finish(1)
    mlp_sum.scatter_start(2)

    own_row = me * rows_dev + lax.broadcasted_iota(jnp.int32, (rows_dev, width), 0)
    own_open = own_row < train_count
    key_grads, value_grads = [], []
    for column, (_, offset, size) in enumerate(windows):
        key_grad = gather_heads(total_ref[column], rows_dev, head_dim) * scaling
        value_grad = gather_heads(
            value_total_ref[column, :, 0:size], rows_dev, head_dim, offset, width
        )
        key_grads.append(jnp.where(own_open, key_grad, 0.0))
        value_grads.append(jnp.where(own_open, value_grad, 0.0))
    item_grads = [
        jnp.concatenate(parts, axis=0).astype(BF16)
        for parts in (query_grads, key_grads, value_grads)
    ]
    first_grad = second_grad
    for n in range(3):
        first_grad = first_grad + dot_nt(item_grads[n], item_w[n])
    first_in_grad, gain_one, shift_one = norm_back(
        unit_one, root_one, gains_ref[0:1, :], first_grad
    )
    branch_ref[...] = pack_columns(first_in_grad, rows_dev).astype(BF16)
    swap = swap_copy(branch_ref, peer_branch_ref, swap_sem.at[2], swap_sem.at[3])
    swap.start()

    own_branch = first_in_grad.astype(BF16)
    row = put_tiles(
        item_part_ref,
        0,
        jnp.concatenate([dot_tn(first_low, item_grads[n]) for n in range(2)], axis=1),
    )
    row = put_tiles(
        item_part_ref,
        row,
        jnp.concatenate(
            [dot_tn(first_low, item_grads[2]), dot_tn(feat_mixed, own_branch)], axis=1
        ),
    )
    pairs = [
        jnp.concatenate(pair, axis=1)
        for pair in ((gain_one, shift_one), (gain_two, shift_two), (gain_three, shift_three))
    ]
    row = put_tiles(
        item_part_ref, row, jnp.concatenate(pairs + [jnp.zeros((13, 2 * width), F32)], axis=0)
    )
    put_zeros(item_part_ref, row)
    item_sum.scatter_start(0)
    mlp_sum.scatter_finish(2)
    mlp_sum.gather_start(2)
    item_sum.scatter_finish(0)
    item_sum.scatter_start(1)

    swap.wait()
    peer_branch = stack_columns(peer_branch_ref[...].astype(F32), width).astype(BF16)
    all_branch = jnp.concatenate([own_branch, peer_branch], axis=0)
    feat_grad = dot_nt(all_branch, feat_out_w).astype(BF16).astype(F32)
    dots = [head_sums(feat_grad * tile_rows(part, slots), table) for part in value_list]
    row_delta = None
    for weight, dot in zip(weights, dots):
        added = weight * dot
        row_delta = added if row_delta is None else row_delta + added
    score_grads = [
        (weight * (dot - row_delta)).astype(BF16) for weight, dot in zip(weights, dots)
    ]
    mlp_sum.gather_finish(2)
    mlp_sum.gather_start(1)
    item_sum.scatter_finish(1)
    item_sum.scatter_start(2)
    query_grad = None
    for score_grad, part in zip(score_grads, key_list):
        added = dot_nn(score_grad[:own_count], wide) * tile_rows(part, cols_dev)
        query_grad = added if query_grad is None else query_grad + added
    key_parts, value_parts = [], []
    for column in range(cols_dev):
        key_products = dot_nn(score_grads[column], wide) * feat_query
        value_products = dot_nn(weights[column].astype(BF16), wide) * feat_grad
        key_sum = key_products[:rows_dev]
        value_sum = value_products[:rows_dev]
        for n in range(1, slots):
            key_sum = key_sum + key_products[n * rows_dev : (n + 1) * rows_dev]
            value_sum = value_sum + value_products[n * rows_dev : (n + 1) * rows_dev]
        key_parts.append(key_sum)
        value_parts.append(value_sum)
    feat_grads = [
        (query_grad * scaling).astype(BF16),
        (jnp.concatenate(key_parts, axis=0) * scaling).astype(BF16),
        jnp.concatenate(value_parts, axis=0).astype(BF16),
    ]
    row = put_tiles(
        feat_part_ref,
        0,
        jnp.concatenate([dot_tn(own_low, feat_grads[n]) for n in range(2)], axis=1),
    )
    row = put_tiles(feat_part_ref, row, dot_tn(own_low, feat_grads[2]))
    put_zeros(feat_part_ref, row)
    feat_sum.scatter_start(0)
    item_sum.scatter_finish(2)
    item_sum.gather_start(2)
    feat_sum.scatter_finish(0)
    feat_sum.scatter_start(1)
    inner = None
    for n in range(3):
        added = dot_nt(feat_grads[n], feat_w[n])
        inner = added if inner is None else inner + added
    cells_grad_ref[...] = pack_columns(first_in_grad + inner.astype(BF16).astype(F32), rows_dev)
    results.append(mover.start(cells_grad_ref, cells_grad_out))
    for k in range(rows_count // 4):
        banks_gather.from_core(k, 0)
        banks_gather.from_core(k, 1)
    sort_rows = sorted_ref.shape[0]
    sort_block = math.gcd(sort_rows, 256)
    owner = owner_ref[...].reshape(1, sort_rows)

    def sort_some(first, last):
        @pl.loop(first, last)
        def _(step):
            start = pl.multiple_of(step * sort_block, sort_block)
            row = start + lax.broadcasted_iota(jnp.int32, (sort_block, sort_rows), 0)
            chosen = jnp.where(owner == row, 1.0, 0.0).astype(BF16)
            sorted_ref[pl.ds(start, sort_block), :] = dot_nn(chosen, banks_ref[...]).astype(BF16)

    thirds = sort_rows // sort_block // 3
    mlp_sum.gather_finish(1)
    mlp_sum.gather_start(0)
    item_sum.gather_finish(2)
    item_sum.gather_start(1)
    feat_sum.scatter_finish(1)
    feat_sum.scatter_start(2)
    sort_some(0, thirds)
    item_sum.gather_finish(1)
    item_sum.gather_start(0)
    feat_sum.scatter_finish(2)
    feat_sum.gather_start(2)
    sort_some(thirds, 2 * thirds)
    feat_sum.gather_finish(2)
    feat_sum.gather_start(1)
    sort_some(2 * thirds, sort_rows // sort_block)
    results.append(mover.start(sorted_ref, sorted_out))
    mlp_sum.gather_finish(0)
    item_sum.gather_finish(0)
    feat_sum.gather_finish(1)
    feat_sum.gather_start(0)
    for gather in (hidden_gather, grads_gather, banks_gather):
        gather.wait_sent()
    for result in results:
        result.wait()
    feat_sum.gather_finish(0)


def moment_rule(gradient, first_old, second_old):
    first_new = BETA_ONE * first_old + (1.0 - BETA_ONE) * gradient
    second_new = BETA_TWO * second_old + (1.0 - BETA_TWO) * gradient * gradient
    first_hat = first_new * (1.0 / (1.0 - BETA_ONE**STEP))
    second_hat = second_new * (1.0 / (1.0 - BETA_TWO**STEP))
    return first_new, second_new, first_hat / (jnp.sqrt(second_hat) + EPSILON)


def root_mean(value):
    count = value.shape[0] * value.shape[1]
    square = jnp.sum(jnp.sum(value * value, axis=1, keepdims=True), axis=0, keepdims=True)
    return jnp.sqrt(square * (1.0 / count) + 1e-06)


def update_kernel(
    owner_ref,
    mlp_sum_ref,
    item_sum_ref,
    feat_sum_ref,
    gains_ref,
    shifts_ref,
    norm_first_ref,
    norm_second_ref,
    first_ref,
    second_ref,
    small_in,
    big_in,
    sorted_in,
    proj_in,
    feat_out_in,
    item_out_in,
    mlp_in_in,
    mlp_out_in,
    layer_in,
    cells_grad_in,
    layer_out,
    cells_grad_out,
    square_grad_out,
    in_grad_out,
    out_grad_out,
    norm_grad_ref,
    clip_ref,
    first_new_ref,
    second_new_ref,
    square_new_out,
    in_new_out,
    out_new_out,
    square_low_out,
    in_low_out,
    out_low_out,
    norm_new_ref,
    norm_first_new_ref,
    norm_second_new_ref,
    small_ref,
    big_ref,
    sorted_ref,
    olds_ref,
    mlp_in_ref,
    mlp_out_ref,
    square_grad_ref,
    in_grad_ref,
    out_grad_ref,
    square_new_ref,
    in_new_ref,
    out_new_ref,
    square_low_ref,
    in_low_ref,
    out_low_ref,
    rotated_ref,
    own_ref,
    move_sem,
):
    width, ff_width = mlp_in_ref.shape
    slots = first_ref.shape[0]
    squares = square_grad_ref.shape[0]
    mover = Mover(move_sem)
    small_loads = [
        (
            mover.start(small_in.at[n], small_ref.at[n]),
            mover.start(small_in.at[squares + n], small_ref.at[squares + n]),
        )
        for n in range(squares)
    ]
    last_loads = [
        mover.start(small_in.at[2 * squares], small_ref.at[2 * squares]),
        mover.start(small_in.at[2 * squares + 1], small_ref.at[2 * squares + 1]),
        mover.start(big_in, big_ref),
    ]
    sorted_load = mover.start(sorted_in, sorted_ref)
    old_loads = [
        mover.start(proj_in, olds_ref.at[0 : squares - 2]),
        mover.start(feat_out_in, olds_ref.at[squares - 2]),
        mover.start(item_out_in, olds_ref.at[squares - 1]),
    ]
    mlp_loads = [mover.start(mlp_in_in, mlp_in_ref), mover.start(mlp_out_in, mlp_out_ref)]
    results = [mover.start(layer_in, layer_out), mover.start(cells_grad_in, cells_grad_out)]

    square = None
    for part_ref in (mlp_sum_ref, item_sum_ref, feat_sum_ref):
        part = part_ref[...].astype(F32)
        added = jnp.sum(jnp.sum(part * part, axis=1, keepdims=True), axis=0, keepdims=True)
        square = added if square is None else square + added
    grad_norm = jnp.sqrt(square)
    factor = jnp.minimum(1.0, CLIP_NORM / grad_norm)
    clip_ref[0] = grad_norm[0, 0]
    both_width = 2 * width
    both_tiles = both_width // LANES * width
    feat_pair = take_tiles(feat_sum_ref, 0, width, both_width) * factor
    item_pair = take_tiles(item_sum_ref, 0, width, both_width) * factor
    mixed_pair = take_tiles(item_sum_ref, both_tiles, width, both_width) * factor
    parts = [
        feat_pair[:, :width],
        feat_pair[:, width:],
        take_tiles(feat_sum_ref, both_tiles, width, width) * factor,
        item_pair[:, :width],
        item_pair[:, width:],
        mixed_pair[:, :width],
        mixed_pair[:, width:],
        take_tiles(mlp_sum_ref, 2 * both_tiles, width, width) * factor,
    ]
    for n, clipped in enumerate(parts):
        square_grad_ref[n] = clipped
        for load in small_loads[n]:
            load.wait()
        turned = dot_low(dot_nn, clipped, small_ref[squares + n])
        rotated_ref[n * width : (n + 1) * width, :] = dot_low(dot_tn, small_ref[n], turned)
    results.append(mover.start(square_grad_ref, square_grad_out))
    start = squares * width
    middle = start + ff_width
    for load in last_loads:
        load.wait()
    clipped = take_tiles(mlp_sum_ref, 0, width, ff_width) * factor
    in_grad_ref[...] = clipped
    results.append(mover.start(in_grad_ref, in_grad_out))
    turned = dot_low(dot_tn, clipped, small_ref[2 * squares])
    rotated_ref[start:middle, :] = dot_low(dot_tn, big_ref[0], turned)
    clipped = take_tiles(mlp_sum_ref, both_tiles, width, ff_width) * factor
    out_grad_ref[...] = clipped
    results.append(mover.start(out_grad_ref, out_grad_out))
    turned = dot_low(dot_tn, clipped, small_ref[2 * squares + 1])
    rotated_ref[middle : middle + ff_width, :] = dot_low(dot_tn, big_ref[1], turned)

    def step_of(first_row, count):
        rows = slice(first_row, first_row + count)
        banks = sorted_ref[rows, :].astype(F32)
        return moment_rule(rotated_ref[rows, :], banks[:, :width], banks[:, width:])[2]

    sorted_load.wait()
    for load in old_loads:
        load.wait()
    for n in range(squares):
        turned = dot_low(dot_nt, step_of(n * width, width), small_ref[squares + n])
        update = dot_low(dot_nn, small_ref[n], turned)
        old = olds_ref[n]
        new = old - LEARN_RATE * root_mean(old) * update
        square_new_ref[n] = new
        square_low_ref[n] = new.astype(BF16)
        results.append(mover.start(square_new_ref.at[n], square_new_out.at[n]))
    results.append(mover.start(square_low_ref, square_low_out))
    for load in mlp_loads:
        load.wait()
    turned = dot_low(dot_nn, big_ref[0], step_of(start, ff_width))
    update = dot_low(dot_nt, small_ref[2 * squares], turned)
    new = mlp_in_ref[...] - LEARN_RATE * root_mean(mlp_in_ref[...]) * update
    in_new_ref[...] = new
    in_low_ref[...] = new.astype(BF16)
    results.append(mover.start(in_new_ref, in_new_out))
    results.append(mover.start(in_low_ref, in_low_out))
    turned = dot_low(dot_nn, big_ref[1], step_of(middle, ff_width))
    update = dot_low(dot_nt, small_ref[2 * squares + 1], turned)
    new = mlp_out_ref[...] - LEARN_RATE * root_mean(mlp_out_ref[...]) * update
    out_new_ref[...] = new
    out_low_ref[...] = new.astype(BF16)
    results.append(mover.start(out_new_ref, out_new_out))
    results.append(mover.start(out_low_ref, out_low_out))

    base = lax.axis_index("rows") * slots

    @pl.loop(0, slots // 8)
    def _(step):
        for n in range(8):
            row = owner_ref[base + step * 8 + n]
            own_ref[pl.ds(step * 8 + n, 1), :] = rotated_ref[pl.ds(row, 1), :]

    first_new, second_new, _ = moment_rule(own_ref[...], first_ref[...], second_ref[...])
    first_new_ref[...] = first_new
    second_new_ref[...] = second_new

    norm_pairs = take_tiles(item_sum_ref, 2 * both_tiles, 16, both_width) * factor
    for n in range(3):
        pair = norm_pairs[n : n + 1]
        both = jnp.concatenate([pair[:, :width], pair[:, width:]], axis=0)
        norm_grad_ref[n] = both
        first_new, second_new, change = moment_rule(both, norm_first_ref[n], norm_second_ref[n])
        norm_first_new_ref[n] = first_new
        norm_second_new_ref[n] = second_new
        old = jnp.concatenate([gains_ref[n : n + 1, :], shifts_ref[n : n + 1, :]], axis=0)
        size = jnp.sqrt(jnp.sum(old * old, axis=1, keepdims=True) * (1.0 / width) + 1e-06)
        norm_new_ref[n] = old - LEARN_RATE * size * change
    for result in results:
        result.wait()


def in_vmem():
    return pl.BlockSpec(memory_space=pltpu.VMEM)


def anywhere():
    return pl.BlockSpec(memory_space=pl.ANY)


def in_smem():
    return pl.BlockSpec(memory_space=pltpu.SMEM)


def fast_device(
    cells,
    feat_mask,
    train_rows,
    cotangent,
    proj_weights,
    feat_out_w,
    item_out_w,
    mlp_in,
    mlp_out,
    norm_gains,
    norm_shifts,
    bases_small,
    bases_big,
    owner_rows,
    bank_first,
    bank_second,
    norm_first,
    norm_second,
):
    rows_count, cols_count = lax.axis_size("rows"), lax.axis_size("cols")
    rows_dev, width_dev = cells.shape
    width = proj_weights.shape[-1]
    ff_width = mlp_in.shape[1]
    cols_dev = width_dev // width
    rows_all = rows_dev * rows_count
    key_total = rows_all // 4 * 3
    head_rows = HEADS * rows_dev
    slots = RowGather.slots(rows_count)
    dma = pltpu.SemaphoreType.DMA
    shape = jax.ShapeDtypeStruct
    devices = rows_count * cols_count
    sizes = {"z": rows_count // 4, "x": 2, "k": 2, "y": cols_count}

    mask_rows = feat_mask.T
    mlp_out_turned = mlp_out.T
    norm_first_turned = jnp.transpose(norm_first, (1, 0, 2))
    norm_second_turned = jnp.transpose(norm_second, (1, 0, 2))
    bank_rows = owner_rows.shape[0]

    def block_rows(rows):
        return -(-rows // (16 * devices)) * 16 * devices

    def landings(rows):
        found = []
        for stage in STAGES:
            count = members(stage, sizes)
            rows //= count
            found.append(pltpu.VMEM((count - 1, rows, LANES), BF16))
        return found

    both_tiles = 2 * width // LANES * width
    half_tiles = -(-width // LANES) * width
    sum_rows = [
        block_rows(2 * (ff_width // LANES) * width + half_tiles),
        block_rows(2 * both_tiles + 2 * width // LANES * 16),
        block_rows(both_tiles + half_tiles),
    ]
    widest = max(members(stage, sizes) for stage in STAGES) - 1
    layer_part, cells_part, mlp_total, item_total, feat_total, sorted_banks = pl.pallas_call(
        functools.partial(layer_kernel, rows_count, cols_count),
        name="layer_and_gradients",
        out_shape=(
            shape((rows_dev, width_dev), BF16),
            shape((rows_dev, width_dev), F32),
            *[shape((rows, LANES), BF16) for rows in sum_rows],
            shape((bank_rows, 2 * width), BF16),
        ),
        in_specs=[in_smem()] + [in_vmem()] * 5 + [anywhere()] * 8,
        out_specs=[anywhere()] * 2 + [in_vmem()] * 3 + [anywhere()],
        scratch_shapes=[
            pltpu.VMEM(proj_weights.shape, F32),
            pltpu.VMEM(feat_out_w.shape, F32),
            pltpu.VMEM(bank_first.shape, F32),
            pltpu.VMEM(bank_first.shape, F32),
            pltpu.VMEM(item_out_w.shape, F32),
            pltpu.VMEM(mlp_in.shape, F32),
            pltpu.VMEM(mlp_in.shape, F32),
            pltpu.VMEM((rows_dev, width_dev), BF16),
            pltpu.VMEM((rows_dev, width_dev), BF16),
            pltpu.VMEM((rows_dev, width_dev), F32),
            pltpu.VMEM((bank_rows, 2 * width), BF16),
            pltpu.VMEM((rows_dev, width_dev), BF16),
            pltpu.VMEM((rows_all, width_dev), BF16),
            pltpu.VMEM((cols_dev, key_total, width), BF16),
            pltpu.VMEM((cols_dev, width, key_total), BF16),
            pltpu.VMEM((cols_dev, key_total, width), BF16),
            pltpu.VMEM((rows_all, width_dev), BF16),
            pltpu.VMEM((16 * cols_dev, rows_all), F32),
            pltpu.VMEM((bank_rows, 2 * width), BF16),
            pltpu.VMEM((cols_dev, head_rows, width), BF16),
            pltpu.VMEM((cols_dev, head_rows, width), BF16),
            pltpu.VMEM((cols_dev, head_rows, 2 * LANES), BF16),
            pltpu.VMEM((cols_dev, 1, head_rows), F32),
            pltpu.VMEM((cols_dev, 1, head_rows), F32),
            pltpu.VMEM((cols_dev, width, head_rows), F32),
            pltpu.VMEM((cols_dev, head_rows, width), F32),
            pltpu.VMEM((cols_dev, head_rows, 2 * LANES), F32),
            pltpu.VMEM((cols_dev, 3, 2 * LANES, width), BF16),
            pltpu.VMEM((cols_dev, 2, width, 2 * LANES), BF16),
            pltpu.VMEM((rows_dev, width_dev), BF16),
            pltpu.VMEM((rows_dev, width_dev), BF16),
        ]
        + [pltpu.VMEM((rows, LANES), BF16) for rows in sum_rows]
        + [landing for rows in sum_rows for landing in landings(rows)]
        + [
            dma((4,)),
            dma((2, 1, slots)),
            dma((2, 2, slots)),
            dma((2, 1, slots)),
        ]
        + [dma((4, len(STAGES), widest))] * len(sum_rows)
        + [dma((11,))],
        compiler_params=pltpu.CompilerParams(
            collective_id=0, has_side_effects=True, vmem_limit_bytes=VMEM_BYTES
        ),
    )(
        train_rows,
        owner_rows,
        cells,
        mask_rows,
        norm_gains,
        norm_shifts,
        proj_weights,
        feat_out_w,
        bank_first,
        bank_second,
        item_out_w,
        mlp_in,
        mlp_out_turned,
        cotangent,
    )

    slots_dev = bank_first.shape[0]
    square = (8, width, width)
    (
        layer_out,
        cells_grad,
        square_grads,
        in_grad,
        out_grad,
        norm_grads,
        clip_norm,
        first_new,
        second_new,
        square_new,
        in_new,
        out_new,
        square_low,
        in_low,
        out_low,
        norm_new,
        norm_first_new,
        norm_second_new,
    ) = pl.pallas_call(
        update_kernel,
        name="rotated_update",
        out_shape=(
            shape(layer_part.shape, BF16),
            shape(cells_part.shape, F32),
            shape(square, F32),
            shape(mlp_in.shape, F32),
            shape(mlp_in.shape, F32),
            shape(norm_first_turned.shape, F32),
            shape((1,), F32),
            shape(bank_first.shape, F32),
            shape(bank_first.shape, F32),
            shape(square, F32),
            shape(mlp_in.shape, F32),
            shape(mlp_in.shape, F32),
            shape(square, BF16),
            shape(mlp_in.shape, BF16),
            shape(mlp_in.shape, BF16),
            shape(norm_first_turned.shape, F32),
            shape(norm_first_turned.shape, F32),
            shape(norm_first_turned.shape, F32),
        ),
        in_specs=[in_smem()] + [in_vmem()] * 9 + [anywhere()] * 10,
        out_specs=[anywhere()] * 5
        + [in_vmem(), in_smem(), in_vmem(), in_vmem()]
        + [anywhere()] * 6
        + [in_vmem()] * 3,
        scratch_shapes=[
            pltpu.VMEM(bases_small.shape, F32),
            pltpu.VMEM(bases_big.shape, F32),
            pltpu.VMEM(sorted_banks.shape, BF16),
            pltpu.VMEM(square, F32),
            pltpu.VMEM(mlp_in.shape, F32),
            pltpu.VMEM(mlp_in.shape, F32),
            pltpu.VMEM(square, F32),
            pltpu.VMEM(mlp_in.shape, F32),
            pltpu.VMEM(mlp_in.shape, F32),
            pltpu.VMEM(square, F32),
            pltpu.VMEM(mlp_in.shape, F32),
            pltpu.VMEM(mlp_in.shape, F32),
            pltpu.VMEM(square, BF16),
            pltpu.VMEM(mlp_in.shape, BF16),
            pltpu.VMEM(mlp_in.shape, BF16),
            pltpu.VMEM((bank_rows, width), F32),
            pltpu.VMEM((slots_dev, width), F32),
            dma((48,)),
        ],
        compiler_params=pltpu.CompilerParams(vmem_limit_bytes=VMEM_BYTES),
    )(
        owner_rows,
        mlp_total,
        item_total,
        feat_total,
        norm_gains,
        norm_shifts,
        norm_first_turned,
        norm_second_turned,
        bank_first,
        bank_second,
        bases_small,
        bases_big,
        sorted_banks,
        proj_weights,
        feat_out_w,
        item_out_w,
        mlp_in,
        mlp_out_turned,
        layer_part,
        cells_part,
    )
    return (
        layer_out,
        cells_grad,
        square_grads,
        in_grad,
        out_grad.T,
        jnp.transpose(norm_grads, (1, 0, 2)),
        clip_norm,
        first_new,
        second_new,
        square_new,
        in_new,
        out_new.T,
        square_low,
        in_low,
        out_low.T,
        jnp.transpose(norm_new, (1, 0, 2)),
        jnp.transpose(norm_first_new, (1, 0, 2)),
        jnp.transpose(norm_second_new, (1, 0, 2)),
    )


def solution(mesh):
    in_specs = (
        P("rows", "cols"),
        P("rows", None),
        P(),
        P("rows", "cols"),
        P(),
        P(),
        P(),
        P(),
        P(),
        P(),
        P(),
        P(),
        P(),
        P(),
        P("rows", None),
        P("rows", None),
        P(),
        P(),
    )
    out_specs = (
        P("rows", "cols"),
        P("rows", "cols"),
        P(),
        P(),
        P(),
        P(),
        P(),
        P("rows", None),
        P("rows", None),
        P(),
        P(),
        P(),
        P(),
        P(),
        P(),
        P(),
        P(),
        P(),
    )
    small = mesh.shape["rows"] == 16 and mesh.shape["cols"] == 2
    return jax.shard_map(
        fast_device if small else per_device, mesh=mesh, in_specs=in_specs, out_specs=out_specs, check_vma=False
    )
```

```python
import functools
import math

import jax
import jax.numpy as jnp
from jax import lax
from jax.experimental import pallas as pl
from jax.experimental.pallas import tpu as pltpu
from jax.sharding import PartitionSpec as P

HEADS = 6
STEP = 10


HIGHEST = lax.Precision.HIGHEST
NEGATIVE = -1e30
CLIP_NORM = 1.0
BETA_ONE = 0.9
BETA_TWO = 0.95
EPSILON = 1e-08
LEARN_RATE = 1.0


def layer_norm(hidden, gain_row, shift_row):
    center = jnp.mean(hidden, axis=-1, keepdims=True)
    centered = hidden - center
    spread = jnp.mean(centered * centered, axis=-1, keepdims=True)
    return centered * lax.rsqrt(spread + 1e-05) * gain_row + shift_row


def gelu_exact(hidden):
    return jax.nn.gelu(hidden, approximate=False)


def product(left_side, right_side):
    return jnp.dot(left_side, right_side, preferred_element_type=jnp.float32)


def product_left(left_side, right_side):
    return lax.dot_general(
        left_side, right_side, (((0,), (0,)), ((), ())), preferred_element_type=jnp.float32
    )


def product_right(left_side, right_side):
    return lax.dot_general(
        left_side, right_side, (((1,), (1,)), ((), ())), preferred_element_type=jnp.float32
    )


def feature_forward(queries, key_rows, value_rows, key_open):
    scaling = queries.shape[-1] ** (-0.5)
    scores = (
        jnp.einsum("nqhe,nkhe->nhqk", queries, key_rows, preferred_element_type=jnp.float32)
        * scaling
    )
    scores = jnp.where(key_open[:, None, None, :], scores, NEGATIVE)
    attend = jax.nn.softmax(scores, axis=-1)
    attend_low = attend.astype(jnp.bfloat16)
    mixed = jnp.einsum(
        "nhqk,nkhe->nqhe", attend_low, value_rows, preferred_element_type=jnp.float32
    )
    return (attend, attend_low, mixed.astype(jnp.bfloat16))


def feature_backward(queries, key_rows, value_rows, attend, attend_low, mixed_grad):
    scaling = queries.shape[-1] ** (-0.5)
    value_dots = jnp.einsum(
        "nqhe,nkhe->nhqk", mixed_grad, value_rows, preferred_element_type=jnp.float32
    )
    row_delta = jnp.sum(attend * value_dots, axis=-1, keepdims=True)
    score_grad = (attend * (value_dots - row_delta)).astype(jnp.bfloat16)
    query_grad = (
        jnp.einsum("nhqk,nkhe->nqhe", score_grad, key_rows, preferred_element_type=jnp.float32)
        * scaling
    )
    key_grad = (
        jnp.einsum("nhqk,nqhe->nkhe", score_grad, queries, preferred_element_type=jnp.float32)
        * scaling
    )
    value_grad = jnp.einsum(
        "nhqk,nqhe->nkhe", attend_low, mixed_grad, preferred_element_type=jnp.float32
    )
    return (
        query_grad.astype(jnp.bfloat16),
        key_grad.astype(jnp.bfloat16),
        value_grad.astype(jnp.bfloat16),
    )


def key_blocks_of(key_rows, value_rows):
    key_total = key_rows.shape[0]
    block_size = math.gcd(key_total, 1024)
    block_count = key_total // block_size
    tail_shape = key_rows.shape[1:]
    starts = jnp.arange(block_count, dtype=jnp.int32) * block_size
    return (
        key_rows.reshape((block_count, block_size) + tail_shape),
        value_rows.reshape((block_count, block_size) + tail_shape),
        starts,
    )


def block_scores(queries, key_block, start_row, train_count):
    scaling = queries.shape[-1] ** (-0.5)
    scores = (
        jnp.einsum("qche,kche->chqk", queries, key_block, preferred_element_type=jnp.float32)
        * scaling
    )
    open_keys = start_row + jnp.arange(key_block.shape[0], dtype=jnp.int32) < train_count
    return jnp.where(open_keys[None, None, None, :], scores, NEGATIVE)


def item_forward(queries, key_rows, value_rows, train_count):
    key_split, value_split, starts = key_blocks_of(key_rows, value_rows)
    stat_shape = (queries.shape[1], queries.shape[2], queries.shape[0])

    def max_pass(carried, packed):
        running_max, running_sum = carried
        key_block, start_row = packed
        scores = block_scores(queries, key_block, start_row, train_count)
        new_max = jnp.maximum(running_max, jnp.max(scores, axis=-1))
        running_sum = running_sum * jnp.exp(running_max - new_max) + jnp.sum(
            jnp.exp(scores - new_max[..., None]), axis=-1
        )
        return ((new_max, running_sum), None)

    start_max = jnp.full(stat_shape, NEGATIVE, jnp.float32)
    (row_max, row_sum), _ = lax.scan(
        max_pass, (start_max, jnp.zeros(stat_shape, jnp.float32)), (key_split, starts)
    )
    log_total = row_max + jnp.log(row_sum)

    def value_pass(carried, packed):
        key_block, value_block, start_row = packed
        attend = jnp.exp(
            block_scores(queries, key_block, start_row, train_count) - log_total[..., None]
        )
        added = jnp.einsum(
            "chqk,kche->qche",
            attend.astype(jnp.bfloat16),
            value_block,
            preferred_element_type=jnp.float32,
        )
        return (carried + added, None)

    item_full, _ = lax.scan(
        value_pass, jnp.zeros(queries.shape, jnp.float32), (key_split, value_split, starts)
    )
    return (log_total, item_full)


def delta_of(mixed_grad, item_full):
    return jnp.transpose(jnp.sum(mixed_grad.astype(jnp.float32) * item_full, axis=-1), (1, 2, 0))


def item_backward(queries, key_rows, value_rows, train_count, log_total, mixed_grad, item_full):
    key_split, value_split, starts = key_blocks_of(key_rows, value_rows)
    scaling = queries.shape[-1] ** (-0.5)
    row_delta = delta_of(mixed_grad, item_full)

    def back_pass(carried, packed):
        key_block, value_block, start_row = packed
        attend = jnp.exp(
            block_scores(queries, key_block, start_row, train_count) - log_total[..., None]
        )
        value_dots = jnp.einsum(
            "qche,kche->chqk", mixed_grad, value_block, preferred_element_type=jnp.float32
        )
        score_grad = (attend * (value_dots - row_delta[..., None])).astype(jnp.bfloat16)
        carried = carried + jnp.einsum(
            "chqk,kche->qche", score_grad, key_block, preferred_element_type=jnp.float32
        )
        key_grad = (
            jnp.einsum("chqk,qche->kche", score_grad, queries, preferred_element_type=jnp.float32)
            * scaling
        )
        value_grad = jnp.einsum(
            "chqk,qche->kche",
            attend.astype(jnp.bfloat16),
            mixed_grad,
            preferred_element_type=jnp.float32,
        )
        return (carried, (key_grad, value_grad))

    query_sum, (key_grads, value_grads) = lax.scan(
        back_pass, jnp.zeros(queries.shape, jnp.float32), (key_split, value_split, starts)
    )
    key_total = key_rows.shape[0]
    flat_width = queries.shape[1] * queries.shape[2] * queries.shape[3]
    return (
        query_sum * scaling,
        key_grads.reshape(key_total, flat_width),
        value_grads.reshape(key_total, flat_width),
    )


def clip_all(gradients):
    total_sq = jnp.sum(gradients[0] * gradients[0])
    for extra in gradients[1:]:
        total_sq = total_sq + jnp.sum(extra * extra)
    grad_norm = jnp.sqrt(total_sq)
    factor = jnp.minimum(1.0, CLIP_NORM / grad_norm)
    return ([gradient * factor for gradient in gradients], grad_norm)


def rotate_bank(square_grad, in_grad, out_grad, bases_small, bases_big):
    model_width = in_grad.shape[0]
    left_bases = bases_small[0:8]
    right_bases = bases_small[8:16]
    rot_square = jnp.matmul(
        jnp.swapaxes(left_bases, 1, 2),
        jnp.matmul(square_grad, right_bases, precision=HIGHEST),
        precision=HIGHEST,
    )
    rot_in = jnp.dot(
        bases_small[16].T, jnp.dot(in_grad, bases_big[0], precision=HIGHEST), precision=HIGHEST
    )
    rot_out = jnp.dot(
        bases_big[1].T, jnp.dot(out_grad, bases_small[17], precision=HIGHEST), precision=HIGHEST
    )
    return jnp.concatenate(
        [rot_square.reshape(8 * model_width, model_width), rot_in.T, rot_out], axis=0
    )


def rotate_back(step_bank, bases_small, bases_big):
    model_width = step_bank.shape[1]
    ff_width = (step_bank.shape[0] - 8 * model_width) // 2
    step_square = step_bank[: 8 * model_width].reshape(8, model_width, model_width)
    step_in = step_bank[8 * model_width : 8 * model_width + ff_width].T
    step_out = step_bank[8 * model_width + ff_width :]
    up_square = jnp.matmul(
        bases_small[0:8],
        jnp.matmul(step_square, jnp.swapaxes(bases_small[8:16], 1, 2), precision=HIGHEST),
        precision=HIGHEST,
    )
    up_in = jnp.dot(
        bases_small[16], jnp.dot(step_in, bases_big[0].T, precision=HIGHEST), precision=HIGHEST
    )
    up_out = jnp.dot(
        bases_big[1], jnp.dot(step_out, bases_small[17].T, precision=HIGHEST), precision=HIGHEST
    )
    return (up_square, up_in, up_out)


def adam_rows(gradient, first_old, second_old, step_float):
    first_new = BETA_ONE * first_old + (1.0 - BETA_ONE) * gradient
    second_new = BETA_TWO * second_old + (1.0 - BETA_TWO) * gradient * gradient
    first_hat = first_new / (1.0 - jnp.power(BETA_ONE, step_float))
    second_hat = second_new / (1.0 - jnp.power(BETA_TWO, step_float))
    return (first_new, second_new, first_hat / (jnp.sqrt(second_hat) + EPSILON))


def trusted(weight, update, over_axes):
    scaling = jnp.sqrt(jnp.mean(weight * weight, axis=over_axes, keepdims=True) + 1e-06)
    return weight - LEARN_RATE * scaling * update


def per_device(
    cells,
    feat_mask,
    train_rows,
    cotangent,
    proj_weights,
    feat_out_w,
    item_out_w,
    mlp_in,
    mlp_out,
    norm_gains,
    norm_shifts,
    bases_small,
    bases_big,
    owner_rows,
    bank_first,
    bank_second,
    norm_first,
    norm_second,
):
    rows_dev, width_dev = cells.shape
    model_width = proj_weights.shape[-1]
    head_count = HEADS
    head_dim = model_width // head_count
    cols_dev = width_dev // model_width
    col_count = lax.axis_size("cols")
    all_cols = cols_dev * col_count
    half_rows = rows_dev // col_count
    cell_count = rows_dev * cols_dev
    proj_low = proj_weights.astype(jnp.bfloat16)
    feat_qkv = jnp.concatenate([proj_low[0], proj_low[1], proj_low[2]], axis=1)
    item_qkv = jnp.concatenate([proj_low[3], proj_low[4], proj_low[5]], axis=1)
    feat_out_low = feat_out_w.astype(jnp.bfloat16)
    item_out_low = item_out_w.astype(jnp.bfloat16)
    mlp_in_cast = mlp_in.astype(jnp.bfloat16)
    mlp_out_cast = mlp_out.astype(jnp.bfloat16)
    train_count = train_rows[0]
    column_cells = lax.all_to_all(cells, "cols", split_axis=0, concat_axis=1, tiled=True)
    column_flat = column_cells.reshape(half_rows * all_cols, model_width)
    row_mask = (
        lax.dynamic_slice_in_dim(feat_mask, lax.axis_index("cols") * half_rows, half_rows, 0) > 0
    )
    feat_proj = (
        product(column_flat, feat_qkv)
        .astype(jnp.bfloat16)
        .reshape(half_rows, all_cols, 3, head_count, head_dim)
    )
    feat_query = feat_proj[:, :, 0]
    feat_key = feat_proj[:, :, 1]
    feat_value = feat_proj[:, :, 2]
    feat_attend, feat_attend_low, feat_mixed = feature_forward(
        feat_query, feat_key, feat_value, row_mask
    )
    feat_mixed_flat = feat_mixed.reshape(half_rows * all_cols, model_width)
    feat_branch = (
        product(feat_mixed_flat, feat_out_low)
        .astype(jnp.bfloat16)
        .reshape(half_rows, all_cols * model_width)
    )
    feat_back = lax.all_to_all(feat_branch, "cols", split_axis=1, concat_axis=0, tiled=True)
    inputs_flat = cells.astype(jnp.float32).reshape(cell_count, model_width)
    first_sum = inputs_flat + feat_back.astype(jnp.float32).reshape(cell_count, model_width)
    first_out, first_pull = jax.vjp(layer_norm, first_sum, norm_gains[0], norm_shifts[0])
    first_low = first_out.astype(jnp.bfloat16)
    item_proj = product(first_low, item_qkv).astype(jnp.bfloat16)
    item_query = item_proj[:, :model_width].reshape(rows_dev, cols_dev, head_count, head_dim)
    item_key = item_proj[:, model_width : 2 * model_width].reshape(rows_dev, width_dev)
    item_value = item_proj[:, 2 * model_width :].reshape(rows_dev, width_dev)
    key_rows, value_rows = (
        lax.all_gather(item_key, "rows", axis=0, tiled=True),
        lax.all_gather(item_value, "rows", axis=0, tiled=True),
    )
    key_total = key_rows.shape[0]
    key_rows = key_rows.reshape(key_total, cols_dev, head_count, head_dim)
    value_rows = value_rows.reshape(key_total, cols_dev, head_count, head_dim)
    log_total, item_full = item_forward(item_query, key_rows, value_rows, train_count)
    item_low = item_full.astype(jnp.bfloat16).reshape(cell_count, model_width)
    item_branch = product(item_low, item_out_low)
    second_sum = first_out + item_branch
    second_out, second_pull = jax.vjp(layer_norm, second_sum, norm_gains[1], norm_shifts[1])
    second_low = second_out.astype(jnp.bfloat16)
    hidden_pre = product(second_low, mlp_in_cast)
    hidden_act, gelu_pull = jax.vjp(gelu_exact, hidden_pre)
    hidden_low = hidden_act.astype(jnp.bfloat16)
    mlp_branch = product(hidden_low, mlp_out_cast)
    third_sum = second_out + mlp_branch
    third_out, third_pull = jax.vjp(layer_norm, third_sum, norm_gains[2], norm_shifts[2])
    layer_out = third_out.astype(jnp.bfloat16).reshape(rows_dev, width_dev)
    third_grad, gain_three, shift_three = third_pull(
        cotangent.astype(jnp.float32).reshape(cell_count, model_width)
    )
    branch_low = third_grad.astype(jnp.bfloat16)
    mlp_out_grad = product_left(hidden_low, branch_low)
    hidden_grad = product_right(branch_low, mlp_out_cast)
    (pre_grad,) = gelu_pull(hidden_grad)
    pre_low = pre_grad.astype(jnp.bfloat16)
    mlp_in_grad = product_left(second_low, pre_low)
    second_grad = third_grad + product_right(pre_low, mlp_in_cast)
    second_in_grad, gain_two, shift_two = second_pull(second_grad)
    item_branch_low = second_in_grad.astype(jnp.bfloat16)
    item_out_grad = product_left(item_low, item_branch_low)
    item_mixed_grad = (
        product_right(item_branch_low, item_out_low)
        .astype(jnp.bfloat16)
        .reshape(rows_dev, cols_dev, head_count, head_dim)
    )
    key_again, value_again = (
        lax.all_gather(item_key, "rows", axis=0, tiled=True),
        lax.all_gather(item_value, "rows", axis=0, tiled=True),
    )
    key_rows = key_again.reshape(key_total, cols_dev, head_count, head_dim)
    value_rows = value_again.reshape(key_total, cols_dev, head_count, head_dim)
    query_sum, key_grads, value_grads = item_backward(
        item_query, key_rows, value_rows, train_count, log_total, item_mixed_grad, item_full
    )
    key_sum, value_sum = (
        lax.psum_scatter(key_grads, "rows", scatter_dimension=0, tiled=True),
        lax.psum_scatter(value_grads, "rows", scatter_dimension=0, tiled=True),
    )
    item_grad_low = jnp.concatenate(
        [
            query_sum.astype(jnp.bfloat16).reshape(cell_count, model_width),
            key_sum.astype(jnp.bfloat16).reshape(cell_count, model_width),
            value_sum.astype(jnp.bfloat16).reshape(cell_count, model_width),
        ],
        axis=1,
    )
    item_qkv_grad = product_left(first_low, item_grad_low)
    first_grad = second_in_grad + product_right(item_grad_low, item_qkv)
    first_in_grad, gain_one, shift_one = first_pull(first_grad)
    feat_branch_grad = first_in_grad.astype(jnp.bfloat16).reshape(rows_dev, width_dev)
    column_grad = lax.all_to_all(
        feat_branch_grad, "cols", split_axis=0, concat_axis=1, tiled=True
    ).reshape(half_rows * all_cols, model_width)
    feat_out_grad = product_left(feat_mixed_flat, column_grad)
    feat_mixed_grad = (
        product_right(column_grad, feat_out_low)
        .astype(jnp.bfloat16)
        .reshape(half_rows, all_cols, head_count, head_dim)
    )
    feat_query_grad, feat_key_grad, feat_value_grad = feature_backward(
        feat_query, feat_key, feat_value, feat_attend, feat_attend_low, feat_mixed_grad
    )
    feat_grad_low = jnp.concatenate(
        [
            feat_query_grad.reshape(half_rows * all_cols, model_width),
            feat_key_grad.reshape(half_rows * all_cols, model_width),
            feat_value_grad.reshape(half_rows * all_cols, model_width),
        ],
        axis=1,
    )
    feat_qkv_grad = product_left(column_flat, feat_grad_low)
    column_in_grad = (
        product_right(feat_grad_low, feat_qkv)
        .astype(jnp.bfloat16)
        .reshape(half_rows, all_cols * model_width)
    )
    row_in_grad = lax.all_to_all(column_in_grad, "cols", split_axis=1, concat_axis=0, tiled=True)
    cells_grad = first_in_grad.reshape(rows_dev, width_dev) + row_in_grad.astype(jnp.float32)
    proj_grad = jnp.stack(
        [
            feat_qkv_grad[:, :model_width],
            feat_qkv_grad[:, model_width : 2 * model_width],
            feat_qkv_grad[:, 2 * model_width :],
            item_qkv_grad[:, :model_width],
            item_qkv_grad[:, model_width : 2 * model_width],
            item_qkv_grad[:, 2 * model_width :],
        ]
    )
    norm_grad = jnp.stack(
        [
            jnp.stack([gain_one, gain_two, gain_three]),
            jnp.stack([shift_one, shift_two, shift_three]),
        ]
    )
    proj_total, feat_total, item_total, in_total, out_total, norm_total = lax.psum(
        (proj_grad, feat_out_grad, item_out_grad, mlp_in_grad, mlp_out_grad, norm_grad),
        ("rows", "cols"),
    )
    square_grad = jnp.concatenate([proj_total, feat_total[None], item_total[None]], axis=0)
    clipped, grad_norm = clip_all([square_grad, in_total, out_total, norm_total])
    square_clip, in_clip, out_clip, norm_clip = clipped
    rot_bank = rotate_bank(square_clip, in_clip, out_clip, bases_small, bases_big)
    step_float = jnp.asarray(STEP, jnp.float32)
    slot_count = bank_first.shape[0]
    my_slots = lax.dynamic_slice_in_dim(
        owner_rows, lax.axis_index("rows") * slot_count, slot_count, 0
    )
    first_new, second_new, slot_steps = adam_rows(
        jnp.take(rot_bank, my_slots, axis=0), bank_first, bank_second, step_float
    )
    all_steps = lax.all_gather(slot_steps, "rows", axis=0, tiled=True)
    full_steps = jnp.take(all_steps, jnp.argsort(owner_rows), axis=0)
    up_square, up_in, up_out = rotate_back(full_steps, bases_small, bases_big)
    square_old = jnp.concatenate([proj_weights, feat_out_w[None], item_out_w[None]], axis=0)
    square_new = trusted(square_old, up_square, (1, 2))
    in_new = trusted(mlp_in, up_in, (0, 1))
    out_new = trusted(mlp_out, up_out, (0, 1))
    norm_old = jnp.stack([norm_gains, norm_shifts])
    norm_first_new, norm_second_new, norm_steps = adam_rows(
        norm_clip, norm_first, norm_second, step_float
    )
    norm_new = trusted(norm_old, norm_steps, (2,))
    return (
        layer_out,
        cells_grad,
        square_clip,
        in_clip,
        out_clip,
        norm_clip,
        grad_norm.reshape(1),
        first_new,
        second_new,
        square_new,
        in_new,
        out_new,
        square_new.astype(jnp.bfloat16),
        in_new.astype(jnp.bfloat16),
        out_new.astype(jnp.bfloat16),
        norm_new,
        norm_first_new,
        norm_second_new,
    )


F32 = jnp.float32
BF16 = jnp.bfloat16
MESH = pl.DeviceIdType.MESH
VMEM_BYTES = 56 * 1024 * 1024
LANES = 128


def dot_nn(left, right):
    return jnp.dot(left, right, preferred_element_type=F32)


def dot_nt(left, right):
    return lax.dot_general(left, right, (((1,), (1,)), ((), ())), preferred_element_type=F32)


def dot_tn(left, right):
    return lax.dot_general(left, right, (((0,), (0,)), ((), ())), preferred_element_type=F32)


def split_two(value):
    high = value.astype(BF16)
    return high, (value - high.astype(F32)).astype(BF16)


def dot_low(dot, left, right):
    return dot(left.astype(BF16), right.astype(BF16))


def stack_columns(packed, width):
    count = packed.shape[1] // width
    return jnp.concatenate([packed[:, n * width : (n + 1) * width] for n in range(count)], axis=0)


def pack_columns(stacked, rows):
    count = stacked.shape[0] // rows
    return jnp.concatenate([stacked[n * rows : (n + 1) * rows] for n in range(count)], axis=1)


def norm_parts(hidden):
    width = hidden.shape[1]
    center = jnp.sum(hidden, axis=1, keepdims=True) * (1.0 / width)
    centered = hidden - center
    spread = jnp.sum(centered * centered, axis=1, keepdims=True) * (1.0 / width)
    root = lax.rsqrt(spread + 1e-05)
    return centered * root, root


def norm_back(unit, root, gain, incoming):
    width = unit.shape[1]
    scaled = incoming * gain
    mean_one = jnp.sum(scaled, axis=1, keepdims=True) * (1.0 / width)
    mean_two = jnp.sum(scaled * unit, axis=1, keepdims=True) * (1.0 / width)
    gain_grad = jnp.sum(incoming * unit, axis=0, keepdims=True)
    shift_grad = jnp.sum(incoming, axis=0, keepdims=True)
    return root * (scaled - mean_one - unit * mean_two), gain_grad, shift_grad


def head_table(width, head_dim):
    feature = lax.broadcasted_iota(jnp.int32, (width, LANES), 0)
    head = lax.broadcasted_iota(jnp.int32, (width, LANES), 1)
    inside = (feature >= head * head_dim) & (feature < (head + 1) * head_dim)
    return jnp.where(inside, 1.0, 0.0).astype(BF16)


def spread_table(width, head_dim):
    head = lax.broadcasted_iota(jnp.int32, (LANES, width), 0)
    feature = lax.broadcasted_iota(jnp.int32, (LANES, width), 1)
    inside = (feature >= head * head_dim) & (feature < (head + 1) * head_dim)
    return jnp.where(inside, 1.0, 0.0).astype(BF16)


def head_rows_of(value, wide):
    high, low = split_two(value)
    return dot_nt(wide, high) + dot_nt(wide, low)


def head_sums(value, table):
    high, low = split_two(value)
    return dot_nn(high, table) + dot_nn(low, table)


def head_mask(rows, width, head_dim, head):
    feature = lax.broadcasted_iota(jnp.int32, (rows, width), 1)
    return (feature >= head * head_dim) & (feature < (head + 1) * head_dim)


def tile_rows(value, count):
    return jnp.concatenate([value] * count, axis=0)


def feature_weights(queries, key_list, open_list, repeat, table, scaling):
    scores = []
    for keys, is_open in zip(key_list, open_list):
        raw = head_sums(queries * tile_rows(keys, repeat), table) * scaling
        scores.append(jnp.where(tile_rows(is_open, repeat), raw, NEGATIVE))
    top = scores[0]
    for extra in scores[1:]:
        top = jnp.maximum(top, extra)
    grown = [jnp.exp(score - top) for score in scores]
    total = grown[0]
    for extra in grown[1:]:
        total = total + extra
    return [part / total for part in grown]


def flip(value, pattern, size):
    out, step = 0, 1
    while step < size:
        out = out + step * (((value // step) % 2 + (pattern // step) % 2) % 2)
        step *= 2
    return out


class RowGather:
    def __init__(self, pieces, send_sem, recv_sem, rows_count):
        self.pieces, self.send_sem, self.recv_sem = pieces, send_sem, recv_sem
        self.deep = rows_count // 4
        me = lax.axis_index("rows")
        self.core, self.side, self.depth = me % 2, (me // 2) % 2, me // 4

    @staticmethod
    def slots(rows_count):
        return rows_count - 1

    def place(self, depth, side, core):
        return (depth * 2 + side) * 2 + core

    def source(self, k):
        return flip(self.depth, k, self.deep)

    def side_peer(self):
        return self.place(self.depth, 1 - self.side, self.core)

    def core_peer(self):
        return self.place(self.depth, self.side, 1 - self.core)

    def copies(self, shard, target, slot):
        return [
            pltpu.make_async_remote_copy(
                src_ref=piece(shard),
                dst_ref=piece(shard),
                send_sem=self.send_sem.at[n, slot],
                recv_sem=self.recv_sem.at[n, slot],
                device_id={"rows": target},
                device_id_type=MESH,
            )
            for n, piece in enumerate(self.pieces)
        ]

    def push(self, shard, target, slot):
        for copy in self.copies(shard, target, slot):
            copy.start()

    def arrive(self, shard, source, slot):
        for copy in self.copies(shard, source, slot):
            copy.wait_recv()

    def start_depth(self):
        own = self.place(self.depth, self.side, self.core)
        for k in range(1, self.deep):
            self.push(own, self.place(self.source(k), self.side, self.core), k - 1)

    def start_near(self):
        own = self.place(self.depth, self.side, self.core)
        self.push(own, self.core_peer(), 2 * self.deep - 1)
        self.push(own, self.side_peer(), self.deep - 1)

    def along_depth(self, k):
        shard = self.place(self.source(k), self.side, self.core)
        self.arrive(shard, shard, k - 1)
        self.push(shard, self.side_peer(), self.deep - 1 + k)
        self.push(shard, self.core_peer(), 2 * self.deep - 1 + k)

    def across_side(self, k):
        shard = self.place(self.source(k), 1 - self.side, self.core)
        self.arrive(shard, self.side_peer(), self.deep - 1 + k)
        self.push(shard, self.core_peer(), 3 * self.deep - 1 + k)

    def from_core(self, k, other_side):
        side = self.side + other_side - 2 * self.side * other_side
        shard = self.place(self.source(k), side, 1 - self.core)
        self.arrive(shard, self.core_peer(), (2 + other_side) * self.deep - 1 + k)

    def forward(self, k):
        self.across_side(k)

        @pl.when(k + 1 < self.deep)
        def _():
            self.along_depth(k + 1)

    def run(self, use, forwarded):
        @pl.loop(0, 2 * self.deep)
        def _(turn):
            k, other = turn // 2, turn % 2
            if forwarded:

                @pl.when((other == 0) & (k > 0) & (k + forwarded - 1 < self.deep))
                def _():
                    self.forward(k + forwarded - 1)

            else:

                @pl.when((turn == 1) | ((other == 0) & (k > 0)))
                def _():
                    self.forward(k)

            self.from_core(k, other)
            use(self.source(k), self.side + other - 2 * self.side * other)

    def wait_sent(self):
        own = self.place(self.depth, self.side, self.core)

        @pl.loop(0, 4 * self.deep - 1)
        def _(slot):
            for copy in self.copies(own, self.core_peer(), slot):
                copy.wait_send()


class DepthGather:
    def __init__(self, pieces, send_sem, recv_sem, rows_count):
        self.pieces, self.send_sem, self.recv_sem = pieces, send_sem, recv_sem
        self.deep = rows_count // 4
        me = lax.axis_index("rows")
        self.core, self.side, self.depth = me % 2, (me // 2) % 2, me // 4

    @staticmethod
    def slots(rows_count):
        return rows_count // 2 - 1

    def row(self, depth, core):
        return (depth * 2 + self.side) * 2 + core

    def source(self, k):
        return flip(self.depth, k, self.deep)

    def copies(self, shard, target, slot):
        return [
            pltpu.make_async_remote_copy(
                src_ref=piece(shard),
                dst_ref=piece(shard),
                send_sem=self.send_sem.at[n, slot],
                recv_sem=self.recv_sem.at[n, slot],
                device_id={"rows": target},
                device_id_type=MESH,
            )
            for n, piece in enumerate(self.pieces)
        ]

    def start(self):
        own = self.depth * 2 + self.core
        for copy in self.copies(own, self.row(self.depth, 1 - self.core), self.deep - 1):
            copy.start()
        for k in range(1, self.deep):
            for copy in self.copies(own, self.row(self.source(k), self.core), k - 1):
                copy.start()

    def forward(self, k):
        shard = self.source(k) * 2 + self.core
        for copy in self.copies(shard, self.row(self.source(k), self.core), k - 1):
            copy.wait_recv()
        twin = self.row(self.depth, 1 - self.core)
        for copy in self.copies(shard, twin, self.deep - 1 + k):
            copy.start()

    def run(self, use, forwarded):
        twin = self.row(self.depth, 1 - self.core)

        @pl.loop(0, 2 * self.deep)
        def _(turn):
            k, other = turn // 2, turn % 2

            @pl.when((other == 0) & (k > forwarded))
            def _():
                self.forward(k)

            @pl.when(other == 1)
            def _():
                shard = self.source(k) * 2 + 1 - self.core
                for copy in self.copies(shard, twin, self.deep - 1 + k):
                    copy.wait_recv()

            use(self.source(k), self.core + other - 2 * self.core * other)

    def wait_sent(self):
        own = self.depth * 2 + self.core

        @pl.loop(0, 2 * self.deep - 1)
        def _(slot):
            for copy in self.copies(own, self.row(self.depth, 1 - self.core), slot):
                copy.wait_send()


class Quad:
    def __init__(self):
        row = lax.axis_index("rows")
        self.side, self.col = (row // 2) % 2, lax.axis_index("cols")
        self.row = row
        self.own = self.side * 2 + self.col

    def device(self, pattern):
        side_flip, col_flip = pattern % 2, pattern // 2
        side = self.side + side_flip - 2 * self.side * side_flip
        col = self.col + col_flip - 2 * self.col * col_flip
        return {"rows": self.row + 2 * (side - self.side), "cols": col}

    def number(self, pattern):
        side_flip, col_flip = pattern % 2, pattern // 2
        side = self.side + side_flip - 2 * self.side * side_flip
        return side * 2 + self.col + col_flip - 2 * self.col * col_flip

    def spread(self, source, landing, sem):
        return [
            pltpu.make_async_remote_copy(
                src_ref=source,
                dst_ref=landing.at[self.own],
                send_sem=sem.at[0, pattern - 1],
                recv_sem=sem.at[1, pattern - 1],
                device_id=self.device(pattern),
                device_id_type=MESH,
            )
            for pattern in range(1, 4)
        ]

    def across(self, source, landing, sem):
        return pltpu.make_async_remote_copy(
            src_ref=source,
            dst_ref=landing,
            send_sem=sem.at[0],
            recv_sem=sem.at[1],
            device_id=self.device(1),
            device_id_type=MESH,
        )

    def pick(self, packed, width, other):
        left, right = packed[:, :width], packed[:, width:]
        return jnp.where(self.side == other, left, right)

    def joined(self, own, other):
        return jnp.concatenate(
            [jnp.where(self.side == 0, own, other), jnp.where(self.side == 0, other, own)], axis=1
        )

    def columns(self, landing, width):
        found = []
        for col_flip in range(2):
            col = self.col + col_flip - 2 * self.col * col_flip
            blocks = [landing[side * 2 + col].astype(F32) for side in range(2)]
            for other in range(2):
                found.append(
                    jnp.concatenate([self.pick(block, width, other) for block in blocks], axis=0)
                )
        return found


class StagedSum:
    def __init__(self, stages, sizes, part_ref, total_ref, landing, sems):
        self.stages, self.sizes = stages, sizes
        self.part_ref, self.total_ref, self.landing, self.sems = part_ref, total_ref, landing, sems
        row = lax.axis_index("rows")
        self.me = {"z": row // 4, "x": (row // 2) % 2, "k": row % 2, "y": lax.axis_index("cols")}
        self.spans, base, size = [], 0, part_ref.shape[0]
        for stage in stages[:-1]:
            size = size // members(stage, sizes)
            self.spans.append((base, size))
            base = base + self.number(self.me, stage) * size
        self.base, self.size = base, size
        self.unit = size

    def number(self, place, stage):
        out, scale = 0, 1
        for axis in stage:
            out = out + place[axis] * scale
            scale *= self.sizes[axis]
        return out

    def partner(self, stage, pattern):
        place = dict(self.me)
        for axis in stage:
            place[axis] = flip(self.me[axis], pattern % self.sizes[axis], self.sizes[axis])
            pattern //= self.sizes[axis]
        return place

    def device(self, place):
        return {"rows": (place["z"] * 2 + place["x"]) * 2 + place["k"], "cols": place["y"]}

    def rows_at(self, base, size):
        return pl.ds(pl.multiple_of(base, self.unit), size)

    def scatter(self, s):
        stage, (base, size) = self.stages[s], self.spans[s]
        found = []
        for j in range(1, members(stage, self.sizes)):
            place = self.partner(stage, j)
            rows = self.rows_at(base + self.number(place, stage) * size, size)
            found.append(
                pltpu.make_async_remote_copy(
                    src_ref=self.part_ref.at[rows, :],
                    dst_ref=self.landing[s].at[j - 1],
                    send_sem=self.sems.at[0, s, j - 1],
                    recv_sem=self.sems.at[1, s, j - 1],
                    device_id=self.device(place),
                    device_id_type=MESH,
                )
            )
        return found

    def scatter_start(self, s):
        for copy in self.scatter(s):
            copy.start()

    def scatter_finish(self, s):
        stage, (base, size) = self.stages[s], self.spans[s]
        rows = self.rows_at(base + self.number(self.me, stage) * size, size)
        total = self.part_ref[rows, :].astype(F32)
        copies = self.scatter(s)
        for j, copy in enumerate(copies):
            copy.wait_recv()
            total = total + self.landing[s][j].astype(F32)
        for copy in copies:
            copy.wait_send()
        self.part_ref[rows, :] = total.astype(BF16)

    def share(self):
        last = len(self.stages) - 1
        stage, landing = self.stages[last], self.landing[last]
        rows = self.rows_at(self.base, self.size)
        own = self.number(self.me, stage)
        found = []
        for j in range(1, members(stage, self.sizes)):
            found.append(
                pltpu.make_async_remote_copy(
                    src_ref=self.part_ref.at[rows, :],
                    dst_ref=landing.at[own],
                    send_sem=self.sems.at[0, last, j - 1],
                    recv_sem=self.sems.at[1, last, j - 1],
                    device_id=self.device(self.partner(stage, j)),
                    device_id_type=MESH,
                )
            )
        return found

    def share_start(self):
        for copy in self.share():
            copy.start()
        own = self.number(self.me, self.stages[-1])
        self.landing[-1][own] = self.part_ref[self.rows_at(self.base, self.size), :]

    def share_finish(self):
        copies = self.share()
        for copy in copies:
            copy.wait_recv()
        total = self.landing[-1][0].astype(F32)
        for n in range(1, members(self.stages[-1], self.sizes)):
            total = total + self.landing[-1][n].astype(F32)
        for copy in copies:
            copy.wait_send()
        self.total_ref[self.rows_at(self.base, self.size), :] = total.astype(BF16)

    def gather(self, s, own):
        stage, (base, size) = self.stages[s], self.spans[s]
        found = []
        for j in range(1, members(stage, self.sizes)):
            place = self.partner(stage, j)
            holder = self.me if own else place
            rows = self.rows_at(base + self.number(holder, stage) * size, size)
            found.append(
                pltpu.make_async_remote_copy(
                    src_ref=self.total_ref.at[rows, :],
                    dst_ref=self.total_ref.at[rows, :],
                    send_sem=self.sems.at[2, s, j - 1],
                    recv_sem=self.sems.at[3, s, j - 1],
                    device_id=self.device(place),
                    device_id_type=MESH,
                )
            )
        return found

    def gather_start(self, s):
        for copy in self.gather(s, True):
            copy.start()

    def gather_finish(self, s):
        for copy in self.gather(s, False):
            copy.wait_recv()
        for copy in self.gather(s, True):
            copy.wait_send()


class Mover:
    def __init__(self, sem):
        self.sem, self.count = sem, 0

    def start(self, source, target):
        copy = pltpu.make_async_copy(source, target, self.sem.at[self.count])
        copy.start()
        self.count += 1
        return copy


def put_tiles(ref, row, value):
    rows, lanes = value.shape
    if lanes % LANES:
        value = jnp.concatenate([value, jnp.zeros((rows, LANES - lanes % LANES), F32)], axis=1)
    for n in range(value.shape[1] // LANES):
        ref[row : row + rows, :] = value[:, n * LANES : (n + 1) * LANES].astype(ref.dtype)
        row += rows
    return row


def put_zeros(ref, row):
    if row < ref.shape[0]:
        ref[row:, :] = jnp.zeros((ref.shape[0] - row, ref.shape[1]), ref.dtype)


def take_tiles(ref, row, rows, lanes):
    count = -(-lanes // LANES)
    tiles = [ref[row + n * rows : row + (n + 1) * rows, :].astype(F32) for n in range(count)]
    value = jnp.concatenate(tiles, axis=1)
    return value if lanes % LANES == 0 else value[:, :lanes]


def members(stage, sizes):
    return math.prod(sizes[axis] for axis in stage)


def meet(targets):
    barrier = pltpu.get_barrier_semaphore()
    for target in targets:
        pl.semaphore_signal(barrier, inc=1, device_id=target, device_id_type=MESH)
    pl.semaphore_wait(barrier, len(targets))


def head_blocks(value, head_dim):
    rows, width = value.shape
    blocks = [
        jnp.where(head_mask(rows, width, head_dim, head), value, 0.0).astype(BF16)
        for head in range(HEADS)
    ]
    return jnp.concatenate(blocks, axis=0)


def gather_heads_turned(value, rows, head_dim):
    blocks = [
        value[head * head_dim : (head + 1) * head_dim, head * rows : (head + 1) * rows]
        for head in range(HEADS)
    ]
    return jnp.transpose(jnp.concatenate(blocks, axis=0))


def gather_heads(value, rows, head_dim):
    total = None
    for head in range(HEADS):
        block = value[head * rows : (head + 1) * rows]
        kept = jnp.where(head_mask(rows, value.shape[1], head_dim, head), block, 0.0)
        total = kept if total is None else total + kept
    return total


STAGES = ("k", "xy", "z")


def layer_kernel(
    rows_count,
    cols_count,
    train_ref,
    owner_ref,
    cells_ref,
    mask_ref,
    gains_ref,
    shifts_ref,
    proj_in,
    feat_out_in,
    bank_first_in,
    bank_second_in,
    item_out_in,
    mlp_in_in,
    mlp_out_in,
    cotangent_in,
    layer_out,
    cells_grad_out,
    mlp_total_ref,
    item_total_ref,
    feat_total_ref,
    sorted_out,
    proj_ref,
    feat_out_ref,
    bank_first_ref,
    bank_second_ref,
    item_out_ref,
    mlp_in_ref,
    mlp_out_ref,
    cotangent_ref,
    layer_ref,
    cells_grad_ref,
    sorted_ref,
    quad_ref,
    masks_ref,
    half_ref,
    cotangent_half_ref,
    layer_half_ref,
    layer_land_ref,
    grad_half_ref,
    grad_land_ref,
    gathered_ref,
    keys_ref,
    keys_turned_ref,
    values_ref,
    grads_ref,
    all_stats_ref,
    banks_ref,
    blocks_ref,
    grad_blocks_ref,
    top_ref,
    sum_ref,
    turned_ref,
    total_ref,
    value_total_ref,
    branch_ref,
    quad_branch_ref,
    mlp_part_ref,
    item_part_ref,
    feat_part_ref,
    mlp_land_k,
    mlp_land_xy,
    mlp_land_z,
    item_land_k,
    item_land_xy,
    item_land_z,
    feat_land_k,
    feat_land_xy,
    feat_land_z,
    quad_sem,
    side_sem,
    gather_sem,
    grads_sem,
    banks_sem,
    mlp_sem,
    item_sem,
    feat_sem,
    move_sem,
):
    mover = Mover(move_sem)
    proj_load = mover.start(proj_in, proj_ref)
    feat_out_load = mover.start(feat_out_in, feat_out_ref)
    cotangent_load = mover.start(cotangent_in, cotangent_ref)
    bank_loads = [
        mover.start(bank_first_in, bank_first_ref),
        mover.start(bank_second_in, bank_second_ref),
    ]
    later_loads = [
        mover.start(source, target)
        for source, target in (
            (item_out_in, item_out_ref),
            (mlp_in_in, mlp_in_ref),
            (mlp_out_in, mlp_out_ref),
        )
    ]
    rows_dev = cells_ref.shape[0]
    width = feat_out_ref.shape[0]
    head_dim = width // HEADS
    scaling = head_dim ** (-0.5)
    to_log2 = scaling * math.log2(math.e)
    key_total = keys_ref.shape[0]
    block_rows = 2 * rows_dev
    bank_slots = bank_first_ref.shape[0]
    train_count = train_ref[0]
    me = lax.axis_index("rows")
    quad = Quad()
    sizes = {"z": rows_count // 4, "x": 2, "k": 2, "y": cols_count}

    def shard_of(ref, rows):
        return lambda shard: ref.at[pl.ds(pl.multiple_of(shard * rows, rows), rows), :]

    def stats_shard(shard):
        return all_stats_ref.at[:, block_span(shard)]

    def block_span(shard):
        return pl.ds(pl.multiple_of(shard * block_rows, block_rows), block_rows)

    hidden_gather = DepthGather(
        [shard_of(gathered_ref, rows_dev)], gather_sem.at[0], gather_sem.at[1], rows_count
    )
    grads_gather = DepthGather(
        [shard_of(grads_ref, rows_dev), stats_shard], grads_sem.at[0], grads_sem.at[1], rows_count
    )
    banks_gather = RowGather(
        [shard_of(banks_ref, bank_slots)], banks_sem.at[0], banks_sem.at[1], rows_count
    )
    mlp_sum = StagedSum(
        STAGES,
        sizes,
        mlp_part_ref,
        mlp_total_ref,
        (mlp_land_k, mlp_land_xy, mlp_land_z),
        mlp_sem,
    )
    item_sum = StagedSum(
        STAGES,
        sizes,
        item_part_ref,
        item_total_ref,
        (item_land_k, item_land_xy, item_land_z),
        item_sem,
    )
    feat_sum = StagedSum(
        STAGES,
        sizes,
        feat_part_ref,
        feat_total_ref,
        (feat_land_k, feat_land_xy, feat_land_z),
        feat_sem,
    )
    depth, core = hidden_gather.depth, hidden_gather.core
    own_shard = depth * 2 + core
    own_rows = pl.ds(pl.multiple_of(own_shard * rows_dev, rows_dev), rows_dev)
    meet(
        [
            mlp_sum.device(mlp_sum.partner(stage, j))
            for stage in STAGES
            for j in range(1, members(stage, sizes))
        ]
    )

    cell_copies = quad.spread(cells_ref, quad_ref, quad_sem.at[0])
    for copy in cell_copies:
        copy.start()
    mask_copy = quad.across(mask_ref, masks_ref.at[quad.side], side_sem.at[0])
    mask_copy.start()
    quad_ref[quad.own] = cells_ref[...]
    masks_ref[quad.side] = mask_ref[...]
    for load in bank_loads:
        load.wait()
    banks_ref[pl.ds(pl.multiple_of(me * bank_slots, bank_slots), bank_slots), :] = jnp.concatenate(
        [bank_first_ref[...], bank_second_ref[...]], axis=1
    ).astype(BF16)
    cotangent_load.wait()
    cotangent = cotangent_ref[...].astype(F32)
    half_ref[...] = quad.pick(cotangent, width, 1).astype(BF16)
    cotangent_copy = quad.across(half_ref, cotangent_half_ref, side_sem.at[1])

    table = head_table(width, head_dim)
    wide = spread_table(width, head_dim)
    proj_load.wait()
    feat_w = [proj_ref[n].astype(BF16) for n in range(3)]
    for copy in cell_copies:
        copy.wait()
    mask_copy.wait()
    cotangent_copy.start()
    banks_gather.start_near()
    banks_gather.start_depth()
    columns = quad.columns(quad_ref, width)
    own = columns[0]
    own_low = own.astype(BF16)
    all_low = jnp.concatenate(columns, axis=0).astype(BF16)
    own_query = dot_nn(own_low, feat_w[0]).astype(BF16).astype(F32)
    feat_keys = dot_nn(all_low, feat_w[1]).astype(BF16).astype(F32)
    feat_values = dot_nn(all_low, feat_w[2]).astype(BF16).astype(F32)
    slots = len(columns)
    key_list = [feat_keys[n * block_rows : (n + 1) * block_rows] for n in range(slots)]
    value_list = [feat_values[n * block_rows : (n + 1) * block_rows] for n in range(slots)]
    mask_blocks = []
    for side in range(2):
        rows = [
            masks_ref[
                side,
                pl.ds(
                    2 * (quad.col + col_flip - 2 * quad.col * col_flip)
                    + quad.side
                    + other
                    - 2 * quad.side * other,
                    1,
                ),
                :,
            ]
            for col_flip in range(2)
            for other in range(2)
        ]
        rows.append(jnp.zeros((8 - slots, rows_dev), jnp.int32))
        mask_blocks.append(jnp.transpose(jnp.concatenate(rows, axis=0).astype(F32)))
    masks = jnp.concatenate(mask_blocks, axis=0)
    open_list = [masks[:, n : n + 1] > 0.0 for n in range(slots)]
    own_weights = feature_weights(own_query, key_list, open_list, 1, table, scaling)
    mixed = None
    for weight, column_values in zip(own_weights, value_list):
        added = dot_nn(weight.astype(BF16), wide) * column_values
        mixed = added if mixed is None else mixed + added
    feat_mixed = mixed.astype(BF16)
    feat_out_load.wait()
    feat_out_w = feat_out_ref[...].astype(BF16)
    first_sum = own + dot_nn(feat_mixed, feat_out_w).astype(BF16).astype(F32)
    unit_one, root_one = norm_parts(first_sum)
    first_out = unit_one * gains_ref[0:1, :] + shifts_ref[0:1, :]
    first_low = first_out.astype(BF16)
    gathered_ref[own_rows, :] = pack_columns(first_out, rows_dev).astype(BF16)
    hidden_gather.start()

    item_w = [proj_ref[3 + n].astype(BF16) for n in range(3)]
    turned_w = [jnp.transpose(proj_ref[4 + n]).astype(BF16) for n in range(2)]
    queries, own_keys, own_values = [
        dot_nn(first_low, weight).astype(BF16).astype(F32) for weight in item_w
    ]
    blocks_ref[...] = head_blocks(queries, head_dim)
    top_ref[...] = jnp.full(top_ref.shape, NEGATIVE, F32)
    sum_ref[...] = jnp.zeros(sum_ref.shape, F32)
    turned_ref[...] = jnp.zeros(turned_ref.shape, F32)

    def hidden_of(shard):
        rows = pl.ds(pl.multiple_of(shard * rows_dev, rows_dev), rows_dev)
        return stack_columns(gathered_ref[rows, :].astype(F32), width).astype(BF16)

    def open_rows(shape, shard_depth, shard_core):
        row = lax.broadcasted_iota(jnp.int32, shape, 0)
        row = row + jnp.where(row >= rows_dev, rows_dev, 0)
        return row < train_count - (shard_depth * 4 + shard_core) * rows_dev

    def masked_scores(keys, shard_depth, shard_core):
        raw = dot_nt(keys, blocks_ref[...]) * to_log2
        return jnp.where(open_rows(raw.shape, shard_depth, shard_core), raw, NEGATIVE)

    def attend(shard_depth, shard_core):
        @pl.when(shard_depth * 2 * block_rows < key_total)
        def _():
            shard = shard_depth * 2 + shard_core
            span = block_span(shard)
            hidden = hidden_of(shard)
            keys = dot_nn(hidden, item_w[1]).astype(BF16)
            keys_ref[span, :] = keys
            values_ref[span, :] = dot_nn(hidden, item_w[2]).astype(BF16)
            keys_turned_ref[:, span] = dot_nt(turned_w[0], hidden).astype(BF16)
            values_turned = dot_nt(turned_w[1], hidden).astype(BF16)
            scores = masked_scores(keys, shard_depth, shard_core)
            top_old = top_ref[...]
            top_new = jnp.maximum(top_old, jnp.max(scores, axis=0, keepdims=True))
            grown = jnp.exp2(scores - top_new)
            fade = jnp.exp2(top_old - top_new)
            top_ref[...] = top_new
            sum_ref[...] = sum_ref[...] * fade + jnp.sum(grown, axis=0, keepdims=True)
            turned_ref[...] = turned_ref[...] * fade + dot_nn(values_turned, grown.astype(BF16))

    hidden_gather.run(attend, 0)
    for k in range(1, rows_count // 4):
        banks_gather.along_depth(k)
    full = gather_heads_turned(turned_ref[...] / sum_ref[...], block_rows, head_dim)
    log_total = top_ref[...] + jnp.log2(sum_ref[...])

    item_low = full.astype(BF16)
    for load in later_loads:
        load.wait()
    item_out_w = item_out_ref[...].astype(BF16)
    mlp_in_w = mlp_in_ref[...].astype(BF16)
    mlp_out_w = mlp_out_ref[...].astype(BF16)
    unit_two, root_two = norm_parts(first_out + dot_nn(item_low, item_out_w))
    second_out = unit_two * gains_ref[1:2, :] + shifts_ref[1:2, :]
    second_low = second_out.astype(BF16)
    hidden_pre = dot_nn(second_low, mlp_in_w)
    normal = 0.5 + 0.5 * lax.erf(hidden_pre * (0.5**0.5))
    hidden_low = (hidden_pre * normal).astype(BF16)
    unit_three, root_three = norm_parts(second_out + dot_nt(hidden_low, mlp_out_w))
    third_out = unit_three * gains_ref[2:3, :] + shifts_ref[2:3, :]
    cotangent_copy.wait()
    own_part = quad.pick(cotangent, width, 0)
    other_part = cotangent_half_ref[...].astype(F32)
    incoming = jnp.concatenate(
        [
            jnp.where(quad.side == 0, own_part, other_part),
            jnp.where(quad.side == 0, other_part, own_part),
        ],
        axis=0,
    )
    third_grad, gain_three, shift_three = norm_back(
        unit_three, root_three, gains_ref[2:3, :], incoming
    )
    branch_low = third_grad.astype(BF16)
    density = jnp.exp(-0.5 * hidden_pre * hidden_pre) * (1.0 / math.sqrt(2.0 * math.pi))
    pre_low = (dot_nn(branch_low, mlp_out_w) * (normal + hidden_pre * density)).astype(BF16)
    second_grad, gain_two, shift_two = norm_back(
        unit_two, root_two, gains_ref[1:2, :], third_grad + dot_nt(pre_low, mlp_in_w)
    )
    second_grad_low = second_grad.astype(BF16)
    mixed_grad = dot_nt(second_grad_low, item_out_w).astype(BF16).astype(F32)
    part = head_rows_of(mixed_grad * full, wide)[0:8, :]
    delta = jnp.concatenate([part[h : h + 1] for h in range(HEADS)], axis=1)
    totals = [log_total[:, h * block_rows : (h + 1) * block_rows] for h in range(HEADS)]
    spare = jnp.zeros((8 - HEADS, block_rows), F32)
    own_span = block_span(own_shard)
    all_stats_ref[0:8, own_span] = jnp.concatenate(totals + [spare], axis=0)
    all_stats_ref[8:16, own_span] = part
    grads_ref[own_rows, :] = pack_columns(mixed_grad, rows_dev).astype(BF16)
    grads_gather.start()

    row = put_tiles(mlp_part_ref, 0, dot_tn(second_low, pre_low))
    row = put_tiles(mlp_part_ref, row, dot_tn(branch_low, hidden_low))
    row = put_tiles(mlp_part_ref, row, dot_tn(item_low, second_grad_low))
    put_zeros(mlp_part_ref, row)
    mlp_sum.scatter_start(0)
    first_block, second_block = third_out[:rows_dev], third_out[rows_dev:]
    layer_half_ref[...] = jnp.where(quad.side == 0, second_block, first_block).astype(BF16)
    own_layer = jnp.where(quad.side == 0, first_block, second_block)

    grad_blocks_ref[...] = head_blocks(mixed_grad, head_dim)
    turned_ref[...] = jnp.zeros(turned_ref.shape, F32)
    key_steps = key_total // block_rows

    @pl.loop(0, key_steps)
    def _(step):
        @pl.when(step == key_steps - 2)
        def _():
            grads_gather.forward(1)

        @pl.when(step == key_steps - 1)
        def _():
            grads_gather.forward(2)

        span = block_span(step)
        keys = keys_ref[span, :]
        attend_now = jnp.exp2(masked_scores(keys, step // 2, step % 2) - log_total)
        dots = dot_nt(values_ref[span, :], grad_blocks_ref[...])
        score_grad = (attend_now * (dots - delta)).astype(BF16)
        turned_ref[...] += dot_nn(keys_turned_ref[:, span], score_grad)

    query_grad = gather_heads_turned(turned_ref[...], block_rows, head_dim) * scaling

    blocks_ref[...] = head_blocks(own_keys, head_dim)
    grad_blocks_ref[...] = head_blocks(own_values, head_dim)
    total_ref[...] = jnp.zeros(total_ref.shape, F32)
    value_total_ref[...] = jnp.zeros(value_total_ref.shape, F32)

    def answer(shard_depth, shard_core):
        shard = shard_depth * 2 + shard_core
        span = block_span(shard)
        asked = dot_nn(hidden_of(shard), item_w[0]).astype(BF16)
        rows = pl.ds(pl.multiple_of(shard * rows_dev, rows_dev), rows_dev)
        grads = stack_columns(grads_ref[rows, :].astype(F32), width).astype(BF16)
        scores = dot_nt(blocks_ref[...], asked) * to_log2
        dots = dot_nt(grad_blocks_ref[...], grads)
        attends, score_grads = [], []
        for head in range(HEADS):
            part = slice(head * block_rows, (head + 1) * block_rows)
            attend_now = jnp.exp2(scores[part] - all_stats_ref[head : head + 1, span])
            attends.append(attend_now.astype(BF16))
            score_grads.append(
                (attend_now * (dots[part] - all_stats_ref[8 + head : 9 + head, span])).astype(BF16)
            )
        total_ref[...] += dot_nn(jnp.concatenate(score_grads, axis=0), asked)
        value_total_ref[...] += dot_nn(jnp.concatenate(attends, axis=0), grads)

    grads_gather.run(answer, 2)
    layer_copy = quad.across(layer_half_ref, layer_land_ref, side_sem.at[2])
    layer_copy.start()
    mlp_sum.scatter_finish(0)
    mlp_sum.scatter_start(1)

    own_open = open_rows((block_rows, width), depth, core)
    key_grad = gather_heads(total_ref[...], block_rows, head_dim) * scaling
    value_grad = gather_heads(value_total_ref[...], block_rows, head_dim)
    item_grads = [
        query_grad.astype(BF16),
        jnp.where(own_open, key_grad, 0.0).astype(BF16),
        jnp.where(own_open, value_grad, 0.0).astype(BF16),
    ]
    first_grad = second_grad
    for n in range(3):
        first_grad = first_grad + dot_nt(item_grads[n], item_w[n])
    first_in_grad, gain_one, shift_one = norm_back(
        unit_one, root_one, gains_ref[0:1, :], first_grad
    )
    branch_ref[...] = pack_columns(first_in_grad, rows_dev).astype(BF16)
    branch_copies = quad.spread(branch_ref, quad_branch_ref, quad_sem.at[1])
    for copy in branch_copies:
        copy.start()

    own_branch = first_in_grad.astype(BF16)
    row = put_tiles(
        item_part_ref,
        0,
        jnp.concatenate([dot_tn(first_low, item_grads[n]) for n in range(2)], axis=1),
    )
    row = put_tiles(
        item_part_ref,
        row,
        jnp.concatenate(
            [dot_tn(first_low, item_grads[2]), dot_tn(feat_mixed, own_branch)], axis=1
        ),
    )
    pairs = [
        jnp.concatenate(pair, axis=1)
        for pair in ((gain_one, shift_one), (gain_two, shift_two), (gain_three, shift_three))
    ]
    row = put_tiles(
        item_part_ref, row, jnp.concatenate(pairs + [jnp.zeros((13, 2 * width), F32)], axis=0)
    )
    put_zeros(item_part_ref, row)
    item_sum.scatter_start(0)

    other_query = dot_nn(all_low[block_rows:], feat_w[0]).astype(BF16).astype(F32)
    others = slots - 1
    other_weights = feature_weights(other_query, key_list, open_list, others, table, scaling)
    own_feat_grad = dot_nt(own_branch, feat_out_w).astype(BF16).astype(F32)

    def minus_mean(weights, dots):
        row_delta = None
        for weight, dot in zip(weights, dots):
            added = weight * dot
            row_delta = added if row_delta is None else row_delta + added
        return [dot - row_delta for dot in dots]

    own_dots = minus_mean(
        own_weights, [head_sums(own_feat_grad * part, table) for part in value_list]
    )
    own_score_grads = [
        (weight * dot).astype(BF16) for weight, dot in zip(own_weights, own_dots)
    ]
    feat_query_grad = None
    for score_grad, part in zip(own_score_grads, key_list):
        added = dot_nn(score_grad, wide) * part
        feat_query_grad = added if feat_query_grad is None else feat_query_grad + added
    mlp_sum.scatter_finish(1)
    mlp_sum.share_start()
    item_sum.scatter_finish(0)
    item_sum.scatter_start(1)
    for k in range(rows_count // 4):
        banks_gather.across_side(k)
    for copy in branch_copies:
        copy.wait()
    other_branch = jnp.concatenate(
        [
            stack_columns(quad_branch_ref[quad.number(pattern)].astype(F32), width)
            for pattern in range(1, 4)
        ],
        axis=0,
    ).astype(BF16)
    other_feat_grad = dot_nt(other_branch, feat_out_w).astype(BF16).astype(F32)
    other_dots = minus_mean(
        other_weights,
        [head_sums(other_feat_grad * tile_rows(part, others), table) for part in value_list],
    )
    other_score_grad = (other_weights[0] * other_dots[0]).astype(BF16)

    def own_and_others(own_part, other_part):
        total = own_part
        for n in range(others):
            total = total + other_part[n * block_rows : (n + 1) * block_rows]
        return total

    feat_key_grad = own_and_others(
        dot_nn(own_score_grads[0], wide) * own_query, dot_nn(other_score_grad, wide) * other_query
    )
    feat_value_grad = own_and_others(
        dot_nn(own_weights[0].astype(BF16), wide) * own_feat_grad,
        dot_nn(other_weights[0].astype(BF16), wide) * other_feat_grad,
    )
    feat_grads = [
        (feat_query_grad * scaling).astype(BF16),
        (feat_key_grad * scaling).astype(BF16),
        feat_value_grad.astype(BF16),
    ]
    row = put_tiles(
        feat_part_ref,
        0,
        jnp.concatenate([dot_tn(own_low, feat_grads[n]) for n in range(2)], axis=1),
    )
    row = put_tiles(feat_part_ref, row, dot_tn(own_low, feat_grads[2]))
    put_zeros(feat_part_ref, row)
    feat_sum.scatter_start(0)
    mlp_sum.share_finish()
    mlp_sum.gather_start(1)
    item_sum.scatter_finish(1)
    item_sum.share_start()
    feat_sum.scatter_finish(0)
    feat_sum.scatter_start(1)
    inner = None
    for n in range(3):
        added = dot_nt(feat_grads[n], feat_w[n])
        inner = added if inner is None else inner + added
    cells_grad = first_in_grad + inner.astype(BF16).astype(F32)
    first_block, second_block = cells_grad[:rows_dev], cells_grad[rows_dev:]
    grad_half_ref[...] = jnp.where(quad.side == 0, second_block, first_block)
    own_cells_grad = jnp.where(quad.side == 0, first_block, second_block)
    grad_copy = quad.across(grad_half_ref, grad_land_ref, side_sem.at[3])
    layer_copy.wait()
    layer_ref[...] = quad.joined(own_layer, layer_land_ref[...].astype(F32)).astype(BF16)
    results = [mover.start(layer_ref, layer_out)]
    mlp_sum.gather_finish(1)
    mlp_sum.gather_start(0)
    item_sum.share_finish()
    item_sum.gather_start(1)
    feat_sum.scatter_finish(1)
    feat_sum.share_start()
    grad_copy.start()
    for k in range(rows_count // 4):
        banks_gather.from_core(k, 0)
        banks_gather.from_core(k, 1)
    sort_rows = sorted_ref.shape[0]
    sort_block = math.gcd(sort_rows, 256)
    owner = owner_ref[...].reshape(1, sort_rows)

    def sort_some(first, last):
        @pl.loop(first, last)
        def _(step):
            start = pl.multiple_of(step * sort_block, sort_block)
            row = start + lax.broadcasted_iota(jnp.int32, (sort_block, sort_rows), 0)
            chosen = jnp.where(owner == row, 1.0, 0.0).astype(BF16)
            sorted_ref[pl.ds(start, sort_block), :] = dot_nn(chosen, banks_ref[...]).astype(BF16)

    thirds = sort_rows // sort_block // 3
    sort_some(0, thirds)
    mlp_sum.gather_finish(0)
    item_sum.gather_finish(1)
    item_sum.gather_start(0)
    feat_sum.share_finish()
    feat_sum.gather_start(1)
    sort_some(thirds, 2 * thirds)
    feat_sum.gather_finish(1)
    feat_sum.gather_start(0)
    grad_copy.wait()
    cells_grad_ref[...] = quad.joined(own_cells_grad, grad_land_ref[...])
    results.append(mover.start(cells_grad_ref, cells_grad_out))
    sort_some(2 * thirds, sort_rows // sort_block)
    results.append(mover.start(sorted_ref, sorted_out))
    item_sum.gather_finish(0)
    for gather in (hidden_gather, grads_gather, banks_gather):
        gather.wait_sent()
    for result in results:
        result.wait()
    feat_sum.gather_finish(0)


def moment_rule(gradient, first_old, second_old):
    first_new = BETA_ONE * first_old + (1.0 - BETA_ONE) * gradient
    second_new = BETA_TWO * second_old + (1.0 - BETA_TWO) * gradient * gradient
    first_hat = first_new * (1.0 / (1.0 - BETA_ONE**STEP))
    second_hat = second_new * (1.0 / (1.0 - BETA_TWO**STEP))
    return first_new, second_new, first_hat / (jnp.sqrt(second_hat) + EPSILON)


def root_mean(value):
    count = value.shape[0] * value.shape[1]
    square = jnp.sum(jnp.sum(value * value, axis=1, keepdims=True), axis=0, keepdims=True)
    return jnp.sqrt(square * (1.0 / count) + 1e-06)


def update_kernel(
    owner_ref,
    mlp_sum_ref,
    item_sum_ref,
    feat_sum_ref,
    gains_ref,
    shifts_ref,
    norm_first_ref,
    norm_second_ref,
    first_ref,
    second_ref,
    small_in,
    big_in,
    sorted_in,
    proj_in,
    feat_out_in,
    item_out_in,
    mlp_in_in,
    mlp_out_in,
    layer_in,
    cells_grad_in,
    layer_out,
    cells_grad_out,
    square_grad_out,
    in_grad_out,
    out_grad_out,
    norm_grad_ref,
    clip_ref,
    first_new_ref,
    second_new_ref,
    square_new_out,
    in_new_out,
    out_new_out,
    square_low_out,
    in_low_out,
    out_low_out,
    norm_new_ref,
    norm_first_new_ref,
    norm_second_new_ref,
    small_ref,
    big_ref,
    sorted_ref,
    olds_ref,
    mlp_in_ref,
    mlp_out_ref,
    square_grad_ref,
    in_grad_ref,
    out_grad_ref,
    square_new_ref,
    in_new_ref,
    out_new_ref,
    square_low_ref,
    in_low_ref,
    out_low_ref,
    rotated_ref,
    own_ref,
    move_sem,
):
    width, ff_width = mlp_in_ref.shape
    slots = first_ref.shape[0]
    squares = square_grad_ref.shape[0]
    mover = Mover(move_sem)
    small_loads = [
        (
            mover.start(small_in.at[n], small_ref.at[n]),
            mover.start(small_in.at[squares + n], small_ref.at[squares + n]),
        )
        for n in range(squares)
    ]
    last_loads = [
        mover.start(small_in.at[2 * squares], small_ref.at[2 * squares]),
        mover.start(small_in.at[2 * squares + 1], small_ref.at[2 * squares + 1]),
        mover.start(big_in, big_ref),
    ]
    sorted_load = mover.start(sorted_in, sorted_ref)
    old_loads = [
        mover.start(proj_in, olds_ref.at[0 : squares - 2]),
        mover.start(feat_out_in, olds_ref.at[squares - 2]),
        mover.start(item_out_in, olds_ref.at[squares - 1]),
    ]
    mlp_loads = [mover.start(mlp_in_in, mlp_in_ref), mover.start(mlp_out_in, mlp_out_ref)]
    results = [mover.start(layer_in, layer_out), mover.start(cells_grad_in, cells_grad_out)]

    square = None
    for part_ref in (mlp_sum_ref, item_sum_ref, feat_sum_ref):
        part = part_ref[...].astype(F32)
        added = jnp.sum(jnp.sum(part * part, axis=1, keepdims=True), axis=0, keepdims=True)
        square = added if square is None else square + added
    grad_norm = jnp.sqrt(square)
    factor = jnp.minimum(1.0, CLIP_NORM / grad_norm)
    clip_ref[0] = grad_norm[0, 0]
    both_width = 2 * width
    both_tiles = both_width // LANES * width
    feat_pair = take_tiles(feat_sum_ref, 0, width, both_width) * factor
    item_pair = take_tiles(item_sum_ref, 0, width, both_width) * factor
    mixed_pair = take_tiles(item_sum_ref, both_tiles, width, both_width) * factor
    parts = [
        feat_pair[:, :width],
        feat_pair[:, width:],
        take_tiles(feat_sum_ref, both_tiles, width, width) * factor,
        item_pair[:, :width],
        item_pair[:, width:],
        mixed_pair[:, :width],
        mixed_pair[:, width:],
        take_tiles(mlp_sum_ref, 2 * both_tiles, width, width) * factor,
    ]
    for n, clipped in enumerate(parts):
        square_grad_ref[n] = clipped
        for load in small_loads[n]:
            load.wait()
        turned = dot_low(dot_nn, clipped, small_ref[squares + n])
        rotated_ref[n * width : (n + 1) * width, :] = dot_low(dot_tn, small_ref[n], turned)
    results.append(mover.start(square_grad_ref, square_grad_out))
    start = squares * width
    middle = start + ff_width
    for load in last_loads:
        load.wait()
    clipped = take_tiles(mlp_sum_ref, 0, width, ff_width) * factor
    in_grad_ref[...] = clipped
    results.append(mover.start(in_grad_ref, in_grad_out))
    turned = dot_low(dot_tn, clipped, small_ref[2 * squares])
    rotated_ref[start:middle, :] = dot_low(dot_tn, big_ref[0], turned)
    clipped = take_tiles(mlp_sum_ref, both_tiles, width, ff_width) * factor
    out_grad_ref[...] = clipped
    results.append(mover.start(out_grad_ref, out_grad_out))
    turned = dot_low(dot_tn, clipped, small_ref[2 * squares + 1])
    rotated_ref[middle : middle + ff_width, :] = dot_low(dot_tn, big_ref[1], turned)

    def step_of(first_row, count):
        rows = slice(first_row, first_row + count)
        banks = sorted_ref[rows, :].astype(F32)
        return moment_rule(rotated_ref[rows, :], banks[:, :width], banks[:, width:])[2]

    sorted_load.wait()
    for load in old_loads:
        load.wait()
    for n in range(squares):
        turned = dot_low(dot_nt, step_of(n * width, width), small_ref[squares + n])
        update = dot_low(dot_nn, small_ref[n], turned)
        old = olds_ref[n]
        new = old - LEARN_RATE * root_mean(old) * update
        square_new_ref[n] = new
        square_low_ref[n] = new.astype(BF16)
        results.append(mover.start(square_new_ref.at[n], square_new_out.at[n]))
    results.append(mover.start(square_low_ref, square_low_out))
    for load in mlp_loads:
        load.wait()
    turned = dot_low(dot_nn, big_ref[0], step_of(start, ff_width))
    update = dot_low(dot_nt, small_ref[2 * squares], turned)
    new = mlp_in_ref[...] - LEARN_RATE * root_mean(mlp_in_ref[...]) * update
    in_new_ref[...] = new
    in_low_ref[...] = new.astype(BF16)
    results.append(mover.start(in_new_ref, in_new_out))
    results.append(mover.start(in_low_ref, in_low_out))
    turned = dot_low(dot_nn, big_ref[1], step_of(middle, ff_width))
    update = dot_low(dot_nt, small_ref[2 * squares + 1], turned)
    new = mlp_out_ref[...] - LEARN_RATE * root_mean(mlp_out_ref[...]) * update
    out_new_ref[...] = new
    out_low_ref[...] = new.astype(BF16)
    results.append(mover.start(out_new_ref, out_new_out))
    results.append(mover.start(out_low_ref, out_low_out))

    base = lax.axis_index("rows") * slots

    @pl.loop(0, slots // 8)
    def _(step):
        for n in range(8):
            row = owner_ref[base + step * 8 + n]
            own_ref[pl.ds(step * 8 + n, 1), :] = rotated_ref[pl.ds(row, 1), :]

    first_new, second_new, _ = moment_rule(own_ref[...], first_ref[...], second_ref[...])
    first_new_ref[...] = first_new
    second_new_ref[...] = second_new

    norm_pairs = take_tiles(item_sum_ref, 2 * both_tiles, 16, both_width) * factor
    for n in range(3):
        pair = norm_pairs[n : n + 1]
        both = jnp.concatenate([pair[:, :width], pair[:, width:]], axis=0)
        norm_grad_ref[n] = both
        first_new, second_new, change = moment_rule(both, norm_first_ref[n], norm_second_ref[n])
        norm_first_new_ref[n] = first_new
        norm_second_new_ref[n] = second_new
        old = jnp.concatenate([gains_ref[n : n + 1, :], shifts_ref[n : n + 1, :]], axis=0)
        size = jnp.sqrt(jnp.sum(old * old, axis=1, keepdims=True) * (1.0 / width) + 1e-06)
        norm_new_ref[n] = old - LEARN_RATE * size * change
    for result in results:
        result.wait()


def in_vmem():
    return pl.BlockSpec(memory_space=pltpu.VMEM)


def anywhere():
    return pl.BlockSpec(memory_space=pl.ANY)


def in_smem():
    return pl.BlockSpec(memory_space=pltpu.SMEM)


def fast_device(
    cells,
    feat_mask,
    train_rows,
    cotangent,
    proj_weights,
    feat_out_w,
    item_out_w,
    mlp_in,
    mlp_out,
    norm_gains,
    norm_shifts,
    bases_small,
    bases_big,
    owner_rows,
    bank_first,
    bank_second,
    norm_first,
    norm_second,
):
    rows_count, cols_count = lax.axis_size("rows"), lax.axis_size("cols")
    rows_dev, width_dev = cells.shape
    width = proj_weights.shape[-1]
    ff_width = mlp_in.shape[1]
    rows_all = rows_dev * rows_count
    key_total = rows_all // 4 * 3
    head_rows = HEADS * 2 * rows_dev
    dma = pltpu.SemaphoreType.DMA
    shape = jax.ShapeDtypeStruct
    sizes = {"z": rows_count // 4, "x": 2, "k": 2, "y": cols_count}

    mask_rows = feat_mask.T
    mlp_out_turned = mlp_out.T
    norm_first_turned = jnp.transpose(norm_first, (1, 0, 2))
    norm_second_turned = jnp.transpose(norm_second, (1, 0, 2))
    bank_rows = owner_rows.shape[0]

    def block_rows(rows):
        unit = 16 * math.prod(members(stage, sizes) for stage in STAGES[:-1])
        return -(-rows // unit) * unit

    def landings(rows):
        found = []
        for stage in STAGES[:-1]:
            count = members(stage, sizes)
            rows //= count
            found.append(pltpu.VMEM((count - 1, rows, LANES), BF16))
        return found + [pltpu.VMEM((members(STAGES[-1], sizes), rows, LANES), BF16)]

    both_tiles = 2 * width // LANES * width
    half_tiles = -(-width // LANES) * width
    sum_rows = [
        block_rows(2 * (ff_width // LANES) * width + half_tiles),
        block_rows(2 * both_tiles + 2 * width // LANES * 16),
        block_rows(both_tiles + half_tiles),
    ]
    widest = max(members(stage, sizes) for stage in STAGES) - 1
    layer_part, cells_part, mlp_total, item_total, feat_total, sorted_banks = pl.pallas_call(
        functools.partial(layer_kernel, rows_count, cols_count),
        name="layer_and_gradients",
        out_shape=(
            shape((rows_dev, width_dev), BF16),
            shape((rows_dev, width_dev), F32),
            *[shape((rows, LANES), BF16) for rows in sum_rows],
            shape((bank_rows, 2 * width), BF16),
        ),
        in_specs=[in_smem()] + [in_vmem()] * 5 + [anywhere()] * 8,
        out_specs=[anywhere()] * 2 + [in_vmem()] * 3 + [anywhere()],
        scratch_shapes=[
            pltpu.VMEM(proj_weights.shape, F32),
            pltpu.VMEM(feat_out_w.shape, F32),
            pltpu.VMEM(bank_first.shape, F32),
            pltpu.VMEM(bank_first.shape, F32),
            pltpu.VMEM(item_out_w.shape, F32),
            pltpu.VMEM(mlp_in.shape, F32),
            pltpu.VMEM(mlp_in.shape, F32),
            pltpu.VMEM((rows_dev, width_dev), BF16),
            pltpu.VMEM((rows_dev, width_dev), BF16),
            pltpu.VMEM((rows_dev, width_dev), F32),
            pltpu.VMEM((bank_rows, 2 * width), BF16),
            pltpu.VMEM((4, rows_dev, width_dev), BF16),
            pltpu.VMEM((2,) + mask_rows.shape, jnp.int32),
            pltpu.VMEM((rows_dev, width), BF16),
            pltpu.VMEM((rows_dev, width), BF16),
            pltpu.VMEM((rows_dev, width), BF16),
            pltpu.VMEM((rows_dev, width), BF16),
            pltpu.VMEM((rows_dev, width), F32),
            pltpu.VMEM((rows_dev, width), F32),
            pltpu.VMEM((rows_all // 2, width_dev), BF16),
            pltpu.VMEM((key_total, width), BF16),
            pltpu.VMEM((width, key_total), BF16),
            pltpu.VMEM((key_total, width), BF16),
            pltpu.VMEM((rows_all // 2, width_dev), BF16),
            pltpu.VMEM((16, rows_all), F32),
            pltpu.VMEM((bank_rows, 2 * width), BF16),
            pltpu.VMEM((head_rows, width), BF16),
            pltpu.VMEM((head_rows, width), BF16),
            pltpu.VMEM((1, head_rows), F32),
            pltpu.VMEM((1, head_rows), F32),
            pltpu.VMEM((width, head_rows), F32),
            pltpu.VMEM((head_rows, width), F32),
            pltpu.VMEM((head_rows, width), F32),
            pltpu.VMEM((rows_dev, width_dev), BF16),
            pltpu.VMEM((4, rows_dev, width_dev), BF16),
        ]
        + [pltpu.VMEM((rows, LANES), BF16) for rows in sum_rows]
        + [landing for rows in sum_rows for landing in landings(rows)]
        + [
            dma((2, 2, 3)),
            dma((4, 2)),
            dma((2, 1, DepthGather.slots(rows_count))),
            dma((2, 2, DepthGather.slots(rows_count))),
            dma((2, 1, RowGather.slots(rows_count))),
        ]
        + [dma((4, len(STAGES), widest))] * len(sum_rows)
        + [dma((11,))],
        compiler_params=pltpu.CompilerParams(
            collective_id=0, has_side_effects=True, vmem_limit_bytes=VMEM_BYTES
        ),
    )(
        train_rows,
        owner_rows,
        cells,
        mask_rows,
        norm_gains,
        norm_shifts,
        proj_weights,
        feat_out_w,
        bank_first,
        bank_second,
        item_out_w,
        mlp_in,
        mlp_out_turned,
        cotangent,
    )

    slots_dev = bank_first.shape[0]
    square = (8, width, width)
    (
        layer_out,
        cells_grad,
        square_grads,
        in_grad,
        out_grad,
        norm_grads,
        clip_norm,
        first_new,
        second_new,
        square_new,
        in_new,
        out_new,
        square_low,
        in_low,
        out_low,
        norm_new,
        norm_first_new,
        norm_second_new,
    ) = pl.pallas_call(
        update_kernel,
        name="rotated_update",
        out_shape=(
            shape(layer_part.shape, BF16),
            shape(cells_part.shape, F32),
            shape(square, F32),
            shape(mlp_in.shape, F32),
            shape(mlp_in.shape, F32),
            shape(norm_first_turned.shape, F32),
            shape((1,), F32),
            shape(bank_first.shape, F32),
            shape(bank_first.shape, F32),
            shape(square, F32),
            shape(mlp_in.shape, F32),
            shape(mlp_in.shape, F32),
            shape(square, BF16),
            shape(mlp_in.shape, BF16),
            shape(mlp_in.shape, BF16),
            shape(norm_first_turned.shape, F32),
            shape(norm_first_turned.shape, F32),
            shape(norm_first_turned.shape, F32),
        ),
        in_specs=[in_smem()] + [in_vmem()] * 9 + [anywhere()] * 10,
        out_specs=[anywhere()] * 5
        + [in_vmem(), in_smem(), in_vmem(), in_vmem()]
        + [anywhere()] * 6
        + [in_vmem()] * 3,
        scratch_shapes=[
            pltpu.VMEM(bases_small.shape, F32),
            pltpu.VMEM(bases_big.shape, F32),
            pltpu.VMEM(sorted_banks.shape, BF16),
            pltpu.VMEM(square, F32),
            pltpu.VMEM(mlp_in.shape, F32),
            pltpu.VMEM(mlp_in.shape, F32),
            pltpu.VMEM(square, F32),
            pltpu.VMEM(mlp_in.shape, F32),
            pltpu.VMEM(mlp_in.shape, F32),
            pltpu.VMEM(square, F32),
            pltpu.VMEM(mlp_in.shape, F32),
            pltpu.VMEM(mlp_in.shape, F32),
            pltpu.VMEM(square, BF16),
            pltpu.VMEM(mlp_in.shape, BF16),
            pltpu.VMEM(mlp_in.shape, BF16),
            pltpu.VMEM((bank_rows, width), F32),
            pltpu.VMEM((slots_dev, width), F32),
            dma((48,)),
        ],
        compiler_params=pltpu.CompilerParams(vmem_limit_bytes=VMEM_BYTES),
    )(
        owner_rows,
        mlp_total,
        item_total,
        feat_total,
        norm_gains,
        norm_shifts,
        norm_first_turned,
        norm_second_turned,
        bank_first,
        bank_second,
        bases_small,
        bases_big,
        sorted_banks,
        proj_weights,
        feat_out_w,
        item_out_w,
        mlp_in,
        mlp_out_turned,
        layer_part,
        cells_part,
    )
    return (
        layer_out,
        cells_grad,
        square_grads,
        in_grad,
        out_grad.T,
        jnp.transpose(norm_grads, (1, 0, 2)),
        clip_norm,
        first_new,
        second_new,
        square_new,
        in_new,
        out_new.T,
        square_low,
        in_low,
        out_low.T,
        jnp.transpose(norm_new, (1, 0, 2)),
        jnp.transpose(norm_first_new, (1, 0, 2)),
        jnp.transpose(norm_second_new, (1, 0, 2)),
    )


def solution(mesh):
    in_specs = (
        P("rows", "cols"),
        P("rows", None),
        P(),
        P("rows", "cols"),
        P(),
        P(),
        P(),
        P(),
        P(),
        P(),
        P(),
        P(),
        P(),
        P(),
        P("rows", None),
        P("rows", None),
        P(),
        P(),
    )
    out_specs = (
        P("rows", "cols"),
        P("rows", "cols"),
        P(),
        P(),
        P(),
        P(),
        P(),
        P("rows", None),
        P("rows", None),
        P(),
        P(),
        P(),
        P(),
        P(),
        P(),
        P(),
        P(),
        P(),
    )
    small = mesh.shape["rows"] == 16 and mesh.shape["cols"] == 2
    return jax.shard_map(
        fast_device if small else per_device, mesh=mesh, in_specs=in_specs, out_specs=out_specs, check_vma=False
    )
```

```python
import functools
import math

import jax
import jax.numpy as jnp
from jax import lax
from jax.experimental import pallas as pl
from jax.experimental.pallas import tpu as pltpu
from jax.sharding import PartitionSpec as P

HEADS = 6
STEP = 10


HIGHEST = lax.Precision.HIGHEST
NEGATIVE = -1e30
CLIP_NORM = 1.0
BETA_ONE = 0.9
BETA_TWO = 0.95
EPSILON = 1e-08
LEARN_RATE = 1.0


def layer_norm(hidden, gain_row, shift_row):
    center = jnp.mean(hidden, axis=-1, keepdims=True)
    centered = hidden - center
    spread = jnp.mean(centered * centered, axis=-1, keepdims=True)
    return centered * lax.rsqrt(spread + 1e-05) * gain_row + shift_row


def gelu_exact(hidden):
    return jax.nn.gelu(hidden, approximate=False)


def product(left_side, right_side):
    return jnp.dot(left_side, right_side, preferred_element_type=jnp.float32)


def product_left(left_side, right_side):
    return lax.dot_general(
        left_side, right_side, (((0,), (0,)), ((), ())), preferred_element_type=jnp.float32
    )


def product_right(left_side, right_side):
    return lax.dot_general(
        left_side, right_side, (((1,), (1,)), ((), ())), preferred_element_type=jnp.float32
    )


def feature_forward(queries, key_rows, value_rows, key_open):
    scaling = queries.shape[-1] ** (-0.5)
    scores = (
        jnp.einsum("nqhe,nkhe->nhqk", queries, key_rows, preferred_element_type=jnp.float32)
        * scaling
    )
    scores = jnp.where(key_open[:, None, None, :], scores, NEGATIVE)
    attend = jax.nn.softmax(scores, axis=-1)
    attend_low = attend.astype(jnp.bfloat16)
    mixed = jnp.einsum(
        "nhqk,nkhe->nqhe", attend_low, value_rows, preferred_element_type=jnp.float32
    )
    return (attend, attend_low, mixed.astype(jnp.bfloat16))


def feature_backward(queries, key_rows, value_rows, attend, attend_low, mixed_grad):
    scaling = queries.shape[-1] ** (-0.5)
    value_dots = jnp.einsum(
        "nqhe,nkhe->nhqk", mixed_grad, value_rows, preferred_element_type=jnp.float32
    )
    row_delta = jnp.sum(attend * value_dots, axis=-1, keepdims=True)
    score_grad = (attend * (value_dots - row_delta)).astype(jnp.bfloat16)
    query_grad = (
        jnp.einsum("nhqk,nkhe->nqhe", score_grad, key_rows, preferred_element_type=jnp.float32)
        * scaling
    )
    key_grad = (
        jnp.einsum("nhqk,nqhe->nkhe", score_grad, queries, preferred_element_type=jnp.float32)
        * scaling
    )
    value_grad = jnp.einsum(
        "nhqk,nqhe->nkhe", attend_low, mixed_grad, preferred_element_type=jnp.float32
    )
    return (
        query_grad.astype(jnp.bfloat16),
        key_grad.astype(jnp.bfloat16),
        value_grad.astype(jnp.bfloat16),
    )


def key_blocks_of(key_rows, value_rows):
    key_total = key_rows.shape[0]
    block_size = math.gcd(key_total, 1024)
    block_count = key_total // block_size
    tail_shape = key_rows.shape[1:]
    starts = jnp.arange(block_count, dtype=jnp.int32) * block_size
    return (
        key_rows.reshape((block_count, block_size) + tail_shape),
        value_rows.reshape((block_count, block_size) + tail_shape),
        starts,
    )


def block_scores(queries, key_block, start_row, train_count):
    scaling = queries.shape[-1] ** (-0.5)
    scores = (
        jnp.einsum("qche,kche->chqk", queries, key_block, preferred_element_type=jnp.float32)
        * scaling
    )
    open_keys = start_row + jnp.arange(key_block.shape[0], dtype=jnp.int32) < train_count
    return jnp.where(open_keys[None, None, None, :], scores, NEGATIVE)


def item_forward(queries, key_rows, value_rows, train_count):
    key_split, value_split, starts = key_blocks_of(key_rows, value_rows)
    stat_shape = (queries.shape[1], queries.shape[2], queries.shape[0])

    def max_pass(carried, packed):
        running_max, running_sum = carried
        key_block, start_row = packed
        scores = block_scores(queries, key_block, start_row, train_count)
        new_max = jnp.maximum(running_max, jnp.max(scores, axis=-1))
        running_sum = running_sum * jnp.exp(running_max - new_max) + jnp.sum(
            jnp.exp(scores - new_max[..., None]), axis=-1
        )
        return ((new_max, running_sum), None)

    start_max = jnp.full(stat_shape, NEGATIVE, jnp.float32)
    (row_max, row_sum), _ = lax.scan(
        max_pass, (start_max, jnp.zeros(stat_shape, jnp.float32)), (key_split, starts)
    )
    log_total = row_max + jnp.log(row_sum)

    def value_pass(carried, packed):
        key_block, value_block, start_row = packed
        attend = jnp.exp(
            block_scores(queries, key_block, start_row, train_count) - log_total[..., None]
        )
        added = jnp.einsum(
            "chqk,kche->qche",
            attend.astype(jnp.bfloat16),
            value_block,
            preferred_element_type=jnp.float32,
        )
        return (carried + added, None)

    item_full, _ = lax.scan(
        value_pass, jnp.zeros(queries.shape, jnp.float32), (key_split, value_split, starts)
    )
    return (log_total, item_full)


def delta_of(mixed_grad, item_full):
    return jnp.transpose(jnp.sum(mixed_grad.astype(jnp.float32) * item_full, axis=-1), (1, 2, 0))


def item_backward(queries, key_rows, value_rows, train_count, log_total, mixed_grad, item_full):
    key_split, value_split, starts = key_blocks_of(key_rows, value_rows)
    scaling = queries.shape[-1] ** (-0.5)
    row_delta = delta_of(mixed_grad, item_full)

    def back_pass(carried, packed):
        key_block, value_block, start_row = packed
        attend = jnp.exp(
            block_scores(queries, key_block, start_row, train_count) - log_total[..., None]
        )
        value_dots = jnp.einsum(
            "qche,kche->chqk", mixed_grad, value_block, preferred_element_type=jnp.float32
        )
        score_grad = (attend * (value_dots - row_delta[..., None])).astype(jnp.bfloat16)
        carried = carried + jnp.einsum(
            "chqk,kche->qche", score_grad, key_block, preferred_element_type=jnp.float32
        )
        key_grad = (
            jnp.einsum("chqk,qche->kche", score_grad, queries, preferred_element_type=jnp.float32)
            * scaling
        )
        value_grad = jnp.einsum(
            "chqk,qche->kche",
            attend.astype(jnp.bfloat16),
            mixed_grad,
            preferred_element_type=jnp.float32,
        )
        return (carried, (key_grad, value_grad))

    query_sum, (key_grads, value_grads) = lax.scan(
        back_pass, jnp.zeros(queries.shape, jnp.float32), (key_split, value_split, starts)
    )
    key_total = key_rows.shape[0]
    flat_width = queries.shape[1] * queries.shape[2] * queries.shape[3]
    return (
        query_sum * scaling,
        key_grads.reshape(key_total, flat_width),
        value_grads.reshape(key_total, flat_width),
    )


def clip_all(gradients):
    total_sq = jnp.sum(gradients[0] * gradients[0])
    for extra in gradients[1:]:
        total_sq = total_sq + jnp.sum(extra * extra)
    grad_norm = jnp.sqrt(total_sq)
    factor = jnp.minimum(1.0, CLIP_NORM / grad_norm)
    return ([gradient * factor for gradient in gradients], grad_norm)


def rotate_bank(square_grad, in_grad, out_grad, bases_small, bases_big):
    model_width = in_grad.shape[0]
    left_bases = bases_small[0:8]
    right_bases = bases_small[8:16]
    rot_square = jnp.matmul(
        jnp.swapaxes(left_bases, 1, 2),
        jnp.matmul(square_grad, right_bases, precision=HIGHEST),
        precision=HIGHEST,
    )
    rot_in = jnp.dot(
        bases_small[16].T, jnp.dot(in_grad, bases_big[0], precision=HIGHEST), precision=HIGHEST
    )
    rot_out = jnp.dot(
        bases_big[1].T, jnp.dot(out_grad, bases_small[17], precision=HIGHEST), precision=HIGHEST
    )
    return jnp.concatenate(
        [rot_square.reshape(8 * model_width, model_width), rot_in.T, rot_out], axis=0
    )


def rotate_back(step_bank, bases_small, bases_big):
    model_width = step_bank.shape[1]
    ff_width = (step_bank.shape[0] - 8 * model_width) // 2
    step_square = step_bank[: 8 * model_width].reshape(8, model_width, model_width)
    step_in = step_bank[8 * model_width : 8 * model_width + ff_width].T
    step_out = step_bank[8 * model_width + ff_width :]
    up_square = jnp.matmul(
        bases_small[0:8],
        jnp.matmul(step_square, jnp.swapaxes(bases_small[8:16], 1, 2), precision=HIGHEST),
        precision=HIGHEST,
    )
    up_in = jnp.dot(
        bases_small[16], jnp.dot(step_in, bases_big[0].T, precision=HIGHEST), precision=HIGHEST
    )
    up_out = jnp.dot(
        bases_big[1], jnp.dot(step_out, bases_small[17].T, precision=HIGHEST), precision=HIGHEST
    )
    return (up_square, up_in, up_out)


def adam_rows(gradient, first_old, second_old, step_float):
    first_new = BETA_ONE * first_old + (1.0 - BETA_ONE) * gradient
    second_new = BETA_TWO * second_old + (1.0 - BETA_TWO) * gradient * gradient
    first_hat = first_new / (1.0 - jnp.power(BETA_ONE, step_float))
    second_hat = second_new / (1.0 - jnp.power(BETA_TWO, step_float))
    return (first_new, second_new, first_hat / (jnp.sqrt(second_hat) + EPSILON))


def trusted(weight, update, over_axes):
    scaling = jnp.sqrt(jnp.mean(weight * weight, axis=over_axes, keepdims=True) + 1e-06)
    return weight - LEARN_RATE * scaling * update


def per_device(
    cells,
    feat_mask,
    train_rows,
    cotangent,
    proj_weights,
    feat_out_w,
    item_out_w,
    mlp_in,
    mlp_out,
    norm_gains,
    norm_shifts,
    bases_small,
    bases_big,
    owner_rows,
    bank_first,
    bank_second,
    norm_first,
    norm_second,
):
    rows_dev, width_dev = cells.shape
    model_width = proj_weights.shape[-1]
    head_count = HEADS
    head_dim = model_width // head_count
    cols_dev = width_dev // model_width
    col_count = lax.axis_size("cols")
    all_cols = cols_dev * col_count
    half_rows = rows_dev // col_count
    cell_count = rows_dev * cols_dev
    proj_low = proj_weights.astype(jnp.bfloat16)
    feat_qkv = jnp.concatenate([proj_low[0], proj_low[1], proj_low[2]], axis=1)
    item_qkv = jnp.concatenate([proj_low[3], proj_low[4], proj_low[5]], axis=1)
    feat_out_low = feat_out_w.astype(jnp.bfloat16)
    item_out_low = item_out_w.astype(jnp.bfloat16)
    mlp_in_cast = mlp_in.astype(jnp.bfloat16)
    mlp_out_cast = mlp_out.astype(jnp.bfloat16)
    train_count = train_rows[0]
    column_cells = lax.all_to_all(cells, "cols", split_axis=0, concat_axis=1, tiled=True)
    column_flat = column_cells.reshape(half_rows * all_cols, model_width)
    row_mask = (
        lax.dynamic_slice_in_dim(feat_mask, lax.axis_index("cols") * half_rows, half_rows, 0) > 0
    )
    feat_proj = (
        product(column_flat, feat_qkv)
        .astype(jnp.bfloat16)
        .reshape(half_rows, all_cols, 3, head_count, head_dim)
    )
    feat_query = feat_proj[:, :, 0]
    feat_key = feat_proj[:, :, 1]
    feat_value = feat_proj[:, :, 2]
    feat_attend, feat_attend_low, feat_mixed = feature_forward(
        feat_query, feat_key, feat_value, row_mask
    )
    feat_mixed_flat = feat_mixed.reshape(half_rows * all_cols, model_width)
    feat_branch = (
        product(feat_mixed_flat, feat_out_low)
        .astype(jnp.bfloat16)
        .reshape(half_rows, all_cols * model_width)
    )
    feat_back = lax.all_to_all(feat_branch, "cols", split_axis=1, concat_axis=0, tiled=True)
    inputs_flat = cells.astype(jnp.float32).reshape(cell_count, model_width)
    first_sum = inputs_flat + feat_back.astype(jnp.float32).reshape(cell_count, model_width)
    first_out, first_pull = jax.vjp(layer_norm, first_sum, norm_gains[0], norm_shifts[0])
    first_low = first_out.astype(jnp.bfloat16)
    item_proj = product(first_low, item_qkv).astype(jnp.bfloat16)
    item_query = item_proj[:, :model_width].reshape(rows_dev, cols_dev, head_count, head_dim)
    item_key = item_proj[:, model_width : 2 * model_width].reshape(rows_dev, width_dev)
    item_value = item_proj[:, 2 * model_width :].reshape(rows_dev, width_dev)
    key_rows, value_rows = (
        lax.all_gather(item_key, "rows", axis=0, tiled=True),
        lax.all_gather(item_value, "rows", axis=0, tiled=True),
    )
    key_total = key_rows.shape[0]
    key_rows = key_rows.reshape(key_total, cols_dev, head_count, head_dim)
    value_rows = value_rows.reshape(key_total, cols_dev, head_count, head_dim)
    log_total, item_full = item_forward(item_query, key_rows, value_rows, train_count)
    item_low = item_full.astype(jnp.bfloat16).reshape(cell_count, model_width)
    item_branch = product(item_low, item_out_low)
    second_sum = first_out + item_branch
    second_out, second_pull = jax.vjp(layer_norm, second_sum, norm_gains[1], norm_shifts[1])
    second_low = second_out.astype(jnp.bfloat16)
    hidden_pre = product(second_low, mlp_in_cast)
    hidden_act, gelu_pull = jax.vjp(gelu_exact, hidden_pre)
    hidden_low = hidden_act.astype(jnp.bfloat16)
    mlp_branch = product(hidden_low, mlp_out_cast)
    third_sum = second_out + mlp_branch
    third_out, third_pull = jax.vjp(layer_norm, third_sum, norm_gains[2], norm_shifts[2])
    layer_out = third_out.astype(jnp.bfloat16).reshape(rows_dev, width_dev)
    third_grad, gain_three, shift_three = third_pull(
        cotangent.astype(jnp.float32).reshape(cell_count, model_width)
    )
    branch_low = third_grad.astype(jnp.bfloat16)
    mlp_out_grad = product_left(hidden_low, branch_low)
    hidden_grad = product_right(branch_low, mlp_out_cast)
    (pre_grad,) = gelu_pull(hidden_grad)
    pre_low = pre_grad.astype(jnp.bfloat16)
    mlp_in_grad = product_left(second_low, pre_low)
    second_grad = third_grad + product_right(pre_low, mlp_in_cast)
    second_in_grad, gain_two, shift_two = second_pull(second_grad)
    item_branch_low = second_in_grad.astype(jnp.bfloat16)
    item_out_grad = product_left(item_low, item_branch_low)
    item_mixed_grad = (
        product_right(item_branch_low, item_out_low)
        .astype(jnp.bfloat16)
        .reshape(rows_dev, cols_dev, head_count, head_dim)
    )
    key_again, value_again = (
        lax.all_gather(item_key, "rows", axis=0, tiled=True),
        lax.all_gather(item_value, "rows", axis=0, tiled=True),
    )
    key_rows = key_again.reshape(key_total, cols_dev, head_count, head_dim)
    value_rows = value_again.reshape(key_total, cols_dev, head_count, head_dim)
    query_sum, key_grads, value_grads = item_backward(
        item_query, key_rows, value_rows, train_count, log_total, item_mixed_grad, item_full
    )
    key_sum, value_sum = (
        lax.psum_scatter(key_grads, "rows", scatter_dimension=0, tiled=True),
        lax.psum_scatter(value_grads, "rows", scatter_dimension=0, tiled=True),
    )
    item_grad_low = jnp.concatenate(
        [
            query_sum.astype(jnp.bfloat16).reshape(cell_count, model_width),
            key_sum.astype(jnp.bfloat16).reshape(cell_count, model_width),
            value_sum.astype(jnp.bfloat16).reshape(cell_count, model_width),
        ],
        axis=1,
    )
    item_qkv_grad = product_left(first_low, item_grad_low)
    first_grad = second_in_grad + product_right(item_grad_low, item_qkv)
    first_in_grad, gain_one, shift_one = first_pull(first_grad)
    feat_branch_grad = first_in_grad.astype(jnp.bfloat16).reshape(rows_dev, width_dev)
    column_grad = lax.all_to_all(
        feat_branch_grad, "cols", split_axis=0, concat_axis=1, tiled=True
    ).reshape(half_rows * all_cols, model_width)
    feat_out_grad = product_left(feat_mixed_flat, column_grad)
    feat_mixed_grad = (
        product_right(column_grad, feat_out_low)
        .astype(jnp.bfloat16)
        .reshape(half_rows, all_cols, head_count, head_dim)
    )
    feat_query_grad, feat_key_grad, feat_value_grad = feature_backward(
        feat_query, feat_key, feat_value, feat_attend, feat_attend_low, feat_mixed_grad
    )
    feat_grad_low = jnp.concatenate(
        [
            feat_query_grad.reshape(half_rows * all_cols, model_width),
            feat_key_grad.reshape(half_rows * all_cols, model_width),
            feat_value_grad.reshape(half_rows * all_cols, model_width),
        ],
        axis=1,
    )
    feat_qkv_grad = product_left(column_flat, feat_grad_low)
    column_in_grad = (
        product_right(feat_grad_low, feat_qkv)
        .astype(jnp.bfloat16)
        .reshape(half_rows, all_cols * model_width)
    )
    row_in_grad = lax.all_to_all(column_in_grad, "cols", split_axis=1, concat_axis=0, tiled=True)
    cells_grad = first_in_grad.reshape(rows_dev, width_dev) + row_in_grad.astype(jnp.float32)
    proj_grad = jnp.stack(
        [
            feat_qkv_grad[:, :model_width],
            feat_qkv_grad[:, model_width : 2 * model_width],
            feat_qkv_grad[:, 2 * model_width :],
            item_qkv_grad[:, :model_width],
            item_qkv_grad[:, model_width : 2 * model_width],
            item_qkv_grad[:, 2 * model_width :],
        ]
    )
    norm_grad = jnp.stack(
        [
            jnp.stack([gain_one, gain_two, gain_three]),
            jnp.stack([shift_one, shift_two, shift_three]),
        ]
    )
    proj_total, feat_total, item_total, in_total, out_total, norm_total = lax.psum(
        (proj_grad, feat_out_grad, item_out_grad, mlp_in_grad, mlp_out_grad, norm_grad),
        ("rows", "cols"),
    )
    square_grad = jnp.concatenate([proj_total, feat_total[None], item_total[None]], axis=0)
    clipped, grad_norm = clip_all([square_grad, in_total, out_total, norm_total])
    square_clip, in_clip, out_clip, norm_clip = clipped
    rot_bank = rotate_bank(square_clip, in_clip, out_clip, bases_small, bases_big)
    step_float = jnp.asarray(STEP, jnp.float32)
    slot_count = bank_first.shape[0]
    my_slots = lax.dynamic_slice_in_dim(
        owner_rows, lax.axis_index("rows") * slot_count, slot_count, 0
    )
    first_new, second_new, slot_steps = adam_rows(
        jnp.take(rot_bank, my_slots, axis=0), bank_first, bank_second, step_float
    )
    all_steps = lax.all_gather(slot_steps, "rows", axis=0, tiled=True)
    full_steps = jnp.take(all_steps, jnp.argsort(owner_rows), axis=0)
    up_square, up_in, up_out = rotate_back(full_steps, bases_small, bases_big)
    square_old = jnp.concatenate([proj_weights, feat_out_w[None], item_out_w[None]], axis=0)
    square_new = trusted(square_old, up_square, (1, 2))
    in_new = trusted(mlp_in, up_in, (0, 1))
    out_new = trusted(mlp_out, up_out, (0, 1))
    norm_old = jnp.stack([norm_gains, norm_shifts])
    norm_first_new, norm_second_new, norm_steps = adam_rows(
        norm_clip, norm_first, norm_second, step_float
    )
    norm_new = trusted(norm_old, norm_steps, (2,))
    return (
        layer_out,
        cells_grad,
        square_clip,
        in_clip,
        out_clip,
        norm_clip,
        grad_norm.reshape(1),
        first_new,
        second_new,
        square_new,
        in_new,
        out_new,
        square_new.astype(jnp.bfloat16),
        in_new.astype(jnp.bfloat16),
        out_new.astype(jnp.bfloat16),
        norm_new,
        norm_first_new,
        norm_second_new,
    )


F32 = jnp.float32
BF16 = jnp.bfloat16
MESH = pl.DeviceIdType.MESH
VMEM_BYTES = 56 * 1024 * 1024
LANES = 128


def dot_nn(left, right):
    return jnp.dot(left, right, preferred_element_type=F32)


def dot_nt(left, right):
    return lax.dot_general(left, right, (((1,), (1,)), ((), ())), preferred_element_type=F32)


def dot_tn(left, right):
    return lax.dot_general(left, right, (((0,), (0,)), ((), ())), preferred_element_type=F32)


def split_two(value):
    high = value.astype(BF16)
    return high, (value - high.astype(F32)).astype(BF16)


def dot_low(dot, left, right):
    return dot(left.astype(BF16), right.astype(BF16))


def stack_columns(packed, width):
    count = packed.shape[1] // width
    return jnp.concatenate([packed[:, n * width : (n + 1) * width] for n in range(count)], axis=0)


def pack_columns(stacked, rows):
    count = stacked.shape[0] // rows
    return jnp.concatenate([stacked[n * rows : (n + 1) * rows] for n in range(count)], axis=1)


def norm_parts(hidden):
    width = hidden.shape[1]
    center = jnp.sum(hidden, axis=1, keepdims=True) * (1.0 / width)
    centered = hidden - center
    spread = jnp.sum(centered * centered, axis=1, keepdims=True) * (1.0 / width)
    root = lax.rsqrt(spread + 1e-05)
    return centered * root, root


def norm_back(unit, root, gain, incoming):
    width = unit.shape[1]
    scaled = incoming * gain
    mean_one = jnp.sum(scaled, axis=1, keepdims=True) * (1.0 / width)
    mean_two = jnp.sum(scaled * unit, axis=1, keepdims=True) * (1.0 / width)
    gain_grad = jnp.sum(incoming * unit, axis=0, keepdims=True)
    shift_grad = jnp.sum(incoming, axis=0, keepdims=True)
    return root * (scaled - mean_one - unit * mean_two), gain_grad, shift_grad


def head_table(width, head_dim):
    feature = lax.broadcasted_iota(jnp.int32, (width, LANES), 0)
    head = lax.broadcasted_iota(jnp.int32, (width, LANES), 1)
    inside = (feature >= head * head_dim) & (feature < (head + 1) * head_dim)
    return jnp.where(inside, 1.0, 0.0).astype(BF16)


def spread_table(width, head_dim):
    head = lax.broadcasted_iota(jnp.int32, (LANES, width), 0)
    feature = lax.broadcasted_iota(jnp.int32, (LANES, width), 1)
    inside = (feature >= head * head_dim) & (feature < (head + 1) * head_dim)
    return jnp.where(inside, 1.0, 0.0).astype(BF16)


def head_rows_of(value, wide):
    high, low = split_two(value)
    return dot_nt(wide, high) + dot_nt(wide, low)


def head_sums(value, table):
    high, low = split_two(value)
    return dot_nn(high, table) + dot_nn(low, table)


def head_sums_low(value, table):
    return dot_nn(value.astype(BF16), table)


def head_mask(rows, width, head_dim, head):
    feature = lax.broadcasted_iota(jnp.int32, (rows, width), 1)
    return (feature >= head * head_dim) & (feature < (head + 1) * head_dim)


def tile_rows(value, count):
    return jnp.concatenate([value] * count, axis=0)


def feature_scores(queries, keys, is_open, repeat, table, scaling):
    raw = head_sums(queries * tile_rows(keys, repeat), table) * scaling
    return jnp.where(tile_rows(is_open, repeat), raw, NEGATIVE)


def softmax_of(scores):
    top = scores[0]
    for extra in scores[1:]:
        top = jnp.maximum(top, extra)
    grown = [jnp.exp(score - top) for score in scores]
    total = grown[0]
    for extra in grown[1:]:
        total = total + extra
    inverse = 1.0 / total
    return [part * inverse for part in grown]


def flip(value, pattern, size):
    out, step = 0, 1
    while step < size:
        out = out + step * (((value // step) % 2 + (pattern // step) % 2) % 2)
        step *= 2
    return out


class RowGather:
    def __init__(self, pieces, send_sem, recv_sem, rows_count):
        self.pieces, self.send_sem, self.recv_sem = pieces, send_sem, recv_sem
        self.deep = rows_count // 4
        me = lax.axis_index("rows")
        self.core, self.side, self.depth = me % 2, (me // 2) % 2, me // 4

    @staticmethod
    def slots(rows_count):
        return rows_count - 1

    def place(self, depth, side, core):
        return (depth * 2 + side) * 2 + core

    def source(self, k):
        return flip(self.depth, k, self.deep)

    def side_peer(self):
        return self.place(self.depth, 1 - self.side, self.core)

    def core_peer(self):
        return self.place(self.depth, self.side, 1 - self.core)

    def copies(self, shard, target, slot):
        return [
            pltpu.make_async_remote_copy(
                src_ref=piece(shard),
                dst_ref=piece(shard),
                send_sem=self.send_sem.at[n, slot],
                recv_sem=self.recv_sem.at[n, slot],
                device_id={"rows": target},
                device_id_type=MESH,
            )
            for n, piece in enumerate(self.pieces)
        ]

    def push(self, shard, target, slot):
        for copy in self.copies(shard, target, slot):
            copy.start()

    def arrive(self, shard, source, slot):
        for copy in self.copies(shard, source, slot):
            copy.wait_recv()

    def start_depth(self):
        own = self.place(self.depth, self.side, self.core)
        for k in range(1, self.deep):
            self.push(own, self.place(self.source(k), self.side, self.core), k - 1)

    def start_near(self):
        own = self.place(self.depth, self.side, self.core)
        self.push(own, self.core_peer(), 2 * self.deep - 1)
        self.push(own, self.side_peer(), self.deep - 1)

    def along_depth(self, k):
        shard = self.place(self.source(k), self.side, self.core)
        self.arrive(shard, shard, k - 1)
        self.push(shard, self.side_peer(), self.deep - 1 + k)
        self.push(shard, self.core_peer(), 2 * self.deep - 1 + k)

    def across_side(self, k):
        shard = self.place(self.source(k), 1 - self.side, self.core)
        self.arrive(shard, self.side_peer(), self.deep - 1 + k)
        self.push(shard, self.core_peer(), 3 * self.deep - 1 + k)

    def from_core(self, k, other_side):
        side = self.side + other_side - 2 * self.side * other_side
        shard = self.place(self.source(k), side, 1 - self.core)
        self.arrive(shard, self.core_peer(), (2 + other_side) * self.deep - 1 + k)

    def forward(self, k):
        self.across_side(k)

        @pl.when(k + 1 < self.deep)
        def _():
            self.along_depth(k + 1)

    def run(self, use, forwarded):
        @pl.loop(0, 2 * self.deep)
        def _(turn):
            k, other = turn // 2, turn % 2
            if forwarded:

                @pl.when((other == 0) & (k > 0) & (k + forwarded - 1 < self.deep))
                def _():
                    self.forward(k + forwarded - 1)

            else:

                @pl.when((turn == 1) | ((other == 0) & (k > 0)))
                def _():
                    self.forward(k)

            self.from_core(k, other)
            use(self.source(k), self.side + other - 2 * self.side * other)

    def wait_sent(self):
        own = self.place(self.depth, self.side, self.core)

        @pl.loop(0, 4 * self.deep - 1)
        def _(slot):
            for copy in self.copies(own, self.core_peer(), slot):
                copy.wait_send()


class DepthGather:
    def __init__(self, pieces, send_sem, recv_sem, rows_count):
        self.pieces, self.send_sem, self.recv_sem = pieces, send_sem, recv_sem
        self.deep = rows_count // 4
        me = lax.axis_index("rows")
        self.core, self.side, self.depth = me % 2, (me // 2) % 2, me // 4

    @staticmethod
    def slots(rows_count):
        return rows_count // 2 - 1

    def row(self, depth, core):
        return (depth * 2 + self.side) * 2 + core

    def source(self, k):
        return flip(self.depth, k, self.deep)

    def copies(self, shard, target, slot):
        return [
            pltpu.make_async_remote_copy(
                src_ref=piece(shard),
                dst_ref=piece(shard),
                send_sem=self.send_sem.at[n, slot],
                recv_sem=self.recv_sem.at[n, slot],
                device_id={"rows": target},
                device_id_type=MESH,
            )
            for n, piece in enumerate(self.pieces)
        ]

    def start(self):
        own = self.depth * 2 + self.core
        for copy in self.copies(own, self.row(self.depth, 1 - self.core), self.deep - 1):
            copy.start()
        for k in range(1, self.deep):
            for copy in self.copies(own, self.row(self.source(k), self.core), k - 1):
                copy.start()

    def forward(self, k):
        shard = self.source(k) * 2 + self.core
        for copy in self.copies(shard, self.row(self.source(k), self.core), k - 1):
            copy.wait_recv()
        twin = self.row(self.depth, 1 - self.core)
        for copy in self.copies(shard, twin, self.deep - 1 + k):
            copy.start()

    def run(self, use, forwarded):
        twin = self.row(self.depth, 1 - self.core)

        @pl.loop(0, 2 * self.deep)
        def _(turn):
            k, other = turn // 2, turn % 2

            @pl.when((other == 0) & (k > forwarded))
            def _():
                self.forward(k)

            @pl.when(other == 1)
            def _():
                shard = self.source(k) * 2 + 1 - self.core
                for copy in self.copies(shard, twin, self.deep - 1 + k):
                    copy.wait_recv()

            use(self.source(k), self.core + other - 2 * self.core * other)

    def wait_sent(self):
        own = self.depth * 2 + self.core

        @pl.loop(0, 2 * self.deep - 1)
        def _(slot):
            for copy in self.copies(own, self.row(self.depth, 1 - self.core), slot):
                copy.wait_send()


class Quad:
    def __init__(self):
        row = lax.axis_index("rows")
        self.side, self.col = (row // 2) % 2, lax.axis_index("cols")
        self.row = row
        self.own = self.side * 2 + self.col

    def device(self, pattern):
        side_flip, col_flip = pattern % 2, pattern // 2
        side = self.side + side_flip - 2 * self.side * side_flip
        col = self.col + col_flip - 2 * self.col * col_flip
        return {"rows": self.row + 2 * (side - self.side), "cols": col}

    def number(self, pattern):
        side_flip, col_flip = pattern % 2, pattern // 2
        side = self.side + side_flip - 2 * self.side * side_flip
        return side * 2 + self.col + col_flip - 2 * self.col * col_flip

    def spread(self, source, landing, sem):
        return [
            pltpu.make_async_remote_copy(
                src_ref=source,
                dst_ref=landing.at[self.own],
                send_sem=sem.at[0, pattern - 1],
                recv_sem=sem.at[1, pattern - 1],
                device_id=self.device(pattern),
                device_id_type=MESH,
            )
            for pattern in range(1, 4)
        ]

    def across(self, source, landing, sem):
        return pltpu.make_async_remote_copy(
            src_ref=source,
            dst_ref=landing,
            send_sem=sem.at[0],
            recv_sem=sem.at[1],
            device_id=self.device(1),
            device_id_type=MESH,
        )

    def pick(self, packed, width, other):
        left, right = packed[:, :width], packed[:, width:]
        return jnp.where(self.side == other, left, right)

    def joined(self, own, other):
        return jnp.concatenate(
            [jnp.where(self.side == 0, own, other), jnp.where(self.side == 0, other, own)], axis=1
        )

    def columns(self, landing, width, col_flip):
        col = self.col + col_flip - 2 * self.col * col_flip
        blocks = [landing[side * 2 + col].astype(F32) for side in range(2)]
        return [
            jnp.concatenate([self.pick(block, width, other) for block in blocks], axis=0)
            for other in range(2)
        ]


class StagedSum:
    def __init__(self, stages, sizes, part_ref, total_ref, landing, sems):
        self.stages, self.sizes = stages, sizes
        self.part_ref, self.total_ref, self.landing, self.sems = part_ref, total_ref, landing, sems
        row = lax.axis_index("rows")
        self.me = {"z": row // 4, "x": (row // 2) % 2, "k": row % 2, "y": lax.axis_index("cols")}
        self.spans, base, size = [], 0, part_ref.shape[0]
        for stage in stages[:-1]:
            size = size // members(stage, sizes)
            self.spans.append((base, size))
            base = base + self.number(self.me, stage) * size
        self.base, self.size = base, size
        self.unit = size

    def number(self, place, stage):
        out, scale = 0, 1
        for axis in stage:
            out = out + place[axis] * scale
            scale *= self.sizes[axis]
        return out

    def partner(self, stage, pattern):
        place = dict(self.me)
        for axis in stage:
            place[axis] = flip(self.me[axis], pattern % self.sizes[axis], self.sizes[axis])
            pattern //= self.sizes[axis]
        return place

    def device(self, place):
        return {"rows": (place["z"] * 2 + place["x"]) * 2 + place["k"], "cols": place["y"]}

    def rows_at(self, base, size):
        return pl.ds(pl.multiple_of(base, self.unit), size)

    def scatter(self, s):
        stage, (base, size) = self.stages[s], self.spans[s]
        found = []
        for j in range(1, members(stage, self.sizes)):
            place = self.partner(stage, j)
            rows = self.rows_at(base + self.number(place, stage) * size, size)
            found.append(
                pltpu.make_async_remote_copy(
                    src_ref=self.part_ref.at[rows, :],
                    dst_ref=self.landing[s].at[j - 1],
                    send_sem=self.sems.at[0, s, j - 1],
                    recv_sem=self.sems.at[1, s, j - 1],
                    device_id=self.device(place),
                    device_id_type=MESH,
                )
            )
        return found

    def scatter_start(self, s):
        for copy in self.scatter(s):
            copy.start()

    def scatter_finish(self, s):
        stage, (base, size) = self.stages[s], self.spans[s]
        rows = self.rows_at(base + self.number(self.me, stage) * size, size)
        total = self.part_ref[rows, :].astype(F32)
        copies = self.scatter(s)
        for j, copy in enumerate(copies):
            copy.wait_recv()
            total = total + self.landing[s][j].astype(F32)
        for copy in copies:
            copy.wait_send()
        self.part_ref[rows, :] = total.astype(BF16)

    def share(self):
        last = len(self.stages) - 1
        stage, landing = self.stages[last], self.landing[last]
        rows = self.rows_at(self.base, self.size)
        own = self.number(self.me, stage)
        found = []
        for j in range(1, members(stage, self.sizes)):
            found.append(
                pltpu.make_async_remote_copy(
                    src_ref=self.part_ref.at[rows, :],
                    dst_ref=landing.at[own],
                    send_sem=self.sems.at[0, last, j - 1],
                    recv_sem=self.sems.at[1, last, j - 1],
                    device_id=self.device(self.partner(stage, j)),
                    device_id_type=MESH,
                )
            )
        return found

    def share_start(self):
        for copy in self.share():
            copy.start()
        own = self.number(self.me, self.stages[-1])
        self.landing[-1][own] = self.part_ref[self.rows_at(self.base, self.size), :]

    def share_finish(self):
        copies = self.share()
        for copy in copies:
            copy.wait_recv()
        total = self.landing[-1][0].astype(F32)
        for n in range(1, members(self.stages[-1], self.sizes)):
            total = total + self.landing[-1][n].astype(F32)
        for copy in copies:
            copy.wait_send()
        self.total_ref[self.rows_at(self.base, self.size), :] = total.astype(BF16)

    def gather(self, s, own):
        stage, (base, size) = self.stages[s], self.spans[s]
        found = []
        for j in range(1, members(stage, self.sizes)):
            place = self.partner(stage, j)
            holder = self.me if own else place
            rows = self.rows_at(base + self.number(holder, stage) * size, size)
            found.append(
                pltpu.make_async_remote_copy(
                    src_ref=self.total_ref.at[rows, :],
                    dst_ref=self.total_ref.at[rows, :],
                    send_sem=self.sems.at[2, s, j - 1],
                    recv_sem=self.sems.at[3, s, j - 1],
                    device_id=self.device(place),
                    device_id_type=MESH,
                )
            )
        return found

    def gather_start(self, s):
        for copy in self.gather(s, True):
            copy.start()

    def gather_finish(self, s):
        for copy in self.gather(s, False):
            copy.wait_recv()
        for copy in self.gather(s, True):
            copy.wait_send()


class Mover:
    def __init__(self, sem):
        self.sem, self.count = sem, 0

    def start(self, source, target):
        copy = pltpu.make_async_copy(source, target, self.sem.at[self.count])
        copy.start()
        self.count += 1
        return copy


def put_tiles(ref, row, value):
    rows, lanes = value.shape
    if lanes % LANES:
        value = jnp.concatenate([value, jnp.zeros((rows, LANES - lanes % LANES), F32)], axis=1)
    for n in range(value.shape[1] // LANES):
        ref[row : row + rows, :] = value[:, n * LANES : (n + 1) * LANES].astype(ref.dtype)
        row += rows
    return row


def put_zeros(ref, row):
    if row < ref.shape[0]:
        ref[row:, :] = jnp.zeros((ref.shape[0] - row, ref.shape[1]), ref.dtype)


def take_tiles(ref, row, rows, lanes):
    count = -(-lanes // LANES)
    tiles = [ref[row + n * rows : row + (n + 1) * rows, :].astype(F32) for n in range(count)]
    value = jnp.concatenate(tiles, axis=1)
    return value if lanes % LANES == 0 else value[:, :lanes]


def members(stage, sizes):
    return math.prod(sizes[axis] for axis in stage)


def meet(targets):
    barrier = pltpu.get_barrier_semaphore()
    for target in targets:
        pl.semaphore_signal(barrier, inc=1, device_id=target, device_id_type=MESH)
    pl.semaphore_wait(barrier, len(targets))


def head_blocks(value, head_dim):
    rows, width = value.shape
    blocks = [
        jnp.where(head_mask(rows, width, head_dim, head), value, 0.0).astype(BF16)
        for head in range(HEADS)
    ]
    return jnp.concatenate(blocks, axis=0)


def gather_heads_turned(value, rows, head_dim):
    blocks = [
        value[head * head_dim : (head + 1) * head_dim, head * rows : (head + 1) * rows]
        for head in range(HEADS)
    ]
    return jnp.transpose(jnp.concatenate(blocks, axis=0))


def gather_heads(value, rows, head_dim):
    total = None
    for head in range(HEADS):
        block = value[head * rows : (head + 1) * rows]
        kept = jnp.where(head_mask(rows, value.shape[1], head_dim, head), block, 0.0)
        total = kept if total is None else total + kept
    return total


STAGES = ("k", "xy", "z")


def layer_kernel(
    rows_count,
    cols_count,
    train_ref,
    owner_ref,
    cells_ref,
    mask_ref,
    gains_ref,
    shifts_ref,
    proj_in,
    feat_out_in,
    bank_first_in,
    bank_second_in,
    item_out_in,
    mlp_in_in,
    mlp_out_in,
    cotangent_in,
    layer_out,
    cells_grad_out,
    mlp_total_ref,
    item_total_ref,
    feat_total_ref,
    sorted_out,
    proj_ref,
    feat_out_ref,
    bank_first_ref,
    bank_second_ref,
    item_out_ref,
    mlp_in_ref,
    mlp_out_ref,
    cotangent_ref,
    layer_ref,
    cells_grad_ref,
    sorted_ref,
    quad_ref,
    masks_ref,
    half_ref,
    cotangent_half_ref,
    layer_half_ref,
    layer_land_ref,
    grad_half_ref,
    grad_land_ref,
    gathered_ref,
    keys_turned_ref,
    values_ref,
    grads_ref,
    all_stats_ref,
    banks_ref,
    blocks_ref,
    grad_blocks_ref,
    scores_ref,
    top_ref,
    sum_ref,
    turned_ref,
    total_ref,
    value_total_ref,
    branch_ref,
    quad_branch_ref,
    mlp_part_ref,
    item_part_ref,
    feat_part_ref,
    mlp_land_k,
    mlp_land_xy,
    mlp_land_z,
    item_land_k,
    item_land_xy,
    item_land_z,
    feat_land_k,
    feat_land_xy,
    feat_land_z,
    quad_sem,
    side_sem,
    gather_sem,
    grads_sem,
    banks_sem,
    mlp_sem,
    item_sem,
    feat_sem,
    move_sem,
):
    mover = Mover(move_sem)
    proj_load = mover.start(proj_in, proj_ref)
    feat_out_load = mover.start(feat_out_in, feat_out_ref)
    cotangent_load = mover.start(cotangent_in, cotangent_ref)
    bank_loads = [
        mover.start(bank_first_in, bank_first_ref),
        mover.start(bank_second_in, bank_second_ref),
    ]
    later_loads = [
        mover.start(source, target)
        for source, target in (
            (item_out_in, item_out_ref),
            (mlp_in_in, mlp_in_ref),
            (mlp_out_in, mlp_out_ref),
        )
    ]
    rows_dev = cells_ref.shape[0]
    width = feat_out_ref.shape[0]
    head_dim = width // HEADS
    scaling = head_dim ** (-0.5)
    to_log2 = scaling * math.log2(math.e)
    key_total = values_ref.shape[0]
    block_rows = 2 * rows_dev
    bank_slots = bank_first_ref.shape[0]
    train_count = train_ref[0]
    me = lax.axis_index("rows")
    quad = Quad()
    sizes = {"z": rows_count // 4, "x": 2, "k": 2, "y": cols_count}

    def shard_of(ref, rows):
        return lambda shard: ref.at[pl.ds(pl.multiple_of(shard * rows, rows), rows), :]

    def stats_shard(shard):
        return all_stats_ref.at[:, block_span(shard)]

    def block_span(shard):
        return pl.ds(pl.multiple_of(shard * block_rows, block_rows), block_rows)

    hidden_gather = DepthGather(
        [shard_of(gathered_ref, rows_dev)], gather_sem.at[0], gather_sem.at[1], rows_count
    )
    grads_gather = DepthGather(
        [shard_of(grads_ref, rows_dev), stats_shard], grads_sem.at[0], grads_sem.at[1], rows_count
    )
    banks_gather = RowGather(
        [shard_of(banks_ref, bank_slots)], banks_sem.at[0], banks_sem.at[1], rows_count
    )
    mlp_sum = StagedSum(
        STAGES,
        sizes,
        mlp_part_ref,
        mlp_total_ref,
        (mlp_land_k, mlp_land_xy, mlp_land_z),
        mlp_sem,
    )
    item_sum = StagedSum(
        STAGES,
        sizes,
        item_part_ref,
        item_total_ref,
        (item_land_k, item_land_xy, item_land_z),
        item_sem,
    )
    feat_sum = StagedSum(
        STAGES,
        sizes,
        feat_part_ref,
        feat_total_ref,
        (feat_land_k, feat_land_xy, feat_land_z),
        feat_sem,
    )
    depth, core = hidden_gather.depth, hidden_gather.core
    own_shard = depth * 2 + core
    own_rows = pl.ds(pl.multiple_of(own_shard * rows_dev, rows_dev), rows_dev)
    meet(
        [
            mlp_sum.device(mlp_sum.partner(stage, j))
            for stage in STAGES
            for j in range(1, members(stage, sizes))
        ]
    )

    cell_copies = quad.spread(cells_ref, quad_ref, quad_sem.at[0])
    for copy in cell_copies:
        copy.start()
    mask_copy = quad.across(mask_ref, masks_ref.at[quad.side], side_sem.at[0])
    mask_copy.start()
    quad_ref[quad.own] = cells_ref[...]
    masks_ref[quad.side] = mask_ref[...]
    for load in bank_loads:
        load.wait()
    banks_ref[pl.ds(pl.multiple_of(me * bank_slots, bank_slots), bank_slots), :] = jnp.concatenate(
        [bank_first_ref[...], bank_second_ref[...]], axis=1
    ).astype(BF16)
    banks_gather.start_depth()
    cotangent_load.wait()
    cotangent = cotangent_ref[...].astype(F32)
    half_ref[...] = quad.pick(cotangent, width, 1).astype(BF16)
    cotangent_copy = quad.across(half_ref, cotangent_half_ref, side_sem.at[1])

    table = head_table(width, head_dim)
    wide = spread_table(width, head_dim)
    proj_load.wait()
    feat_w = [proj_ref[n].astype(BF16) for n in range(3)]
    slots = 4
    mask_blocks = []
    cell_copies[0].wait()
    mask_copy.wait()
    for side in range(2):
        rows = [
            masks_ref[
                side,
                pl.ds(
                    2 * (quad.col + col_flip - 2 * quad.col * col_flip)
                    + quad.side
                    + other
                    - 2 * quad.side * other,
                    1,
                ),
                :,
            ]
            for col_flip in range(2)
            for other in range(2)
        ]
        rows.append(jnp.zeros((8 - slots, rows_dev), jnp.int32))
        mask_blocks.append(jnp.transpose(jnp.concatenate(rows, axis=0).astype(F32)))
    masks = jnp.concatenate(mask_blocks, axis=0)
    open_list = [masks[:, n : n + 1] > 0.0 for n in range(slots)]
    columns, key_list, value_list, scores = [], [], [], []
    for col_flip in range(2):
        if col_flip == 1:
            cell_copies[1].wait()
            cell_copies[2].wait()
        columns += quad.columns(quad_ref, width, col_flip)
        if col_flip == 0:
            own = columns[0]
            own_low = own.astype(BF16)
            own_query = dot_nn(own_low, feat_w[0]).astype(BF16).astype(F32)
        pair = jnp.concatenate(columns[-2:], axis=0).astype(BF16)
        pair_keys = dot_nn(pair, feat_w[1]).astype(BF16).astype(F32)
        pair_values = dot_nn(pair, feat_w[2]).astype(BF16).astype(F32)
        for n in range(2):
            rows = slice(n * block_rows, (n + 1) * block_rows)
            key_list.append(pair_keys[rows])
            value_list.append(pair_values[rows])
            scores.append(
                feature_scores(own_query, pair_keys[rows], open_list[len(scores)], 1, table, scaling)
            )
    cotangent_copy.start()
    banks_gather.start_near()
    all_low = jnp.concatenate(columns, axis=0).astype(BF16)
    own_weights = softmax_of(scores)
    mixed = None
    for weight, column_values in zip(own_weights, value_list):
        added = dot_nn(weight.astype(BF16), wide) * column_values
        mixed = added if mixed is None else mixed + added
    feat_mixed = mixed.astype(BF16)
    feat_out_load.wait()
    feat_out_w = feat_out_ref[...].astype(BF16)
    first_sum = own + dot_nn(feat_mixed, feat_out_w).astype(BF16).astype(F32)
    unit_one, root_one = norm_parts(first_sum)
    first_out = unit_one * gains_ref[0:1, :] + shifts_ref[0:1, :]
    first_low = first_out.astype(BF16)
    gathered_ref[own_rows, :] = pack_columns(first_out, rows_dev).astype(BF16)
    hidden_gather.start()

    item_w = [proj_ref[3 + n].astype(BF16) for n in range(3)]
    turned_w = [jnp.transpose(proj_ref[4 + n]).astype(BF16) for n in range(2)]
    queries, own_keys, own_values = [
        dot_nn(first_low, weight).astype(BF16).astype(F32) for weight in item_w
    ]
    blocks_ref[...] = head_blocks(queries, head_dim)
    top_ref[...] = jnp.full(top_ref.shape, NEGATIVE, F32)
    sum_ref[...] = jnp.zeros(sum_ref.shape, F32)
    turned_ref[...] = jnp.zeros(turned_ref.shape, F32)

    def hidden_of(shard):
        rows = pl.ds(pl.multiple_of(shard * rows_dev, rows_dev), rows_dev)
        return stack_columns(gathered_ref[rows, :].astype(F32), width).astype(BF16)

    def open_rows(shape, shard_depth, shard_core):
        row = lax.broadcasted_iota(jnp.int32, shape, 0)
        row = row + jnp.where(row >= rows_dev, rows_dev, 0)
        return row < train_count - (shard_depth * 4 + shard_core) * rows_dev

    def masked_scores(keys, shard_depth, shard_core):
        raw = dot_nt(keys, blocks_ref[...]) * to_log2
        return jnp.where(open_rows(raw.shape, shard_depth, shard_core), raw, NEGATIVE)

    def attend(shard_depth, shard_core):
        @pl.when(shard_depth * 2 * block_rows < key_total)
        def _():
            shard = shard_depth * 2 + shard_core
            span = block_span(shard)
            hidden = hidden_of(shard)
            keys = dot_nn(hidden, item_w[1]).astype(BF16)
            values_ref[span, :] = dot_nn(hidden, item_w[2]).astype(BF16)
            keys_turned_ref[:, span] = dot_nt(turned_w[0], hidden).astype(BF16)
            values_turned = dot_nt(turned_w[1], hidden).astype(BF16)
            scores = masked_scores(keys, shard_depth, shard_core)
            scores_ref[span, :] = scores
            top_old = top_ref[...]
            top_new = jnp.maximum(top_old, jnp.max(scores, axis=0, keepdims=True))
            grown = jnp.exp2(scores - top_new)
            fade = jnp.exp2(top_old - top_new)
            top_ref[...] = top_new
            sum_ref[...] = sum_ref[...] * fade + jnp.sum(grown, axis=0, keepdims=True)
            turned_ref[...] = turned_ref[...] * fade + dot_nn(values_turned, grown.astype(BF16))

    hidden_gather.run(attend, 0)
    for k in range(1, rows_count // 4):
        banks_gather.along_depth(k)
    full = gather_heads_turned(turned_ref[...] / sum_ref[...], block_rows, head_dim)
    log_total = top_ref[...] + jnp.log2(sum_ref[...])

    item_low = full.astype(BF16)
    for load in later_loads:
        load.wait()
    item_out_w = item_out_ref[...].astype(BF16)
    mlp_in_w = mlp_in_ref[...].astype(BF16)
    mlp_out_w = mlp_out_ref[...].astype(BF16)
    unit_two, root_two = norm_parts(first_out + dot_nn(item_low, item_out_w))
    second_out = unit_two * gains_ref[1:2, :] + shifts_ref[1:2, :]
    second_low = second_out.astype(BF16)
    hidden_pre = dot_nn(second_low, mlp_in_w)
    normal = 0.5 + 0.5 * lax.erf(hidden_pre * (0.5**0.5))
    hidden_low = (hidden_pre * normal).astype(BF16)
    unit_three, root_three = norm_parts(second_out + dot_nt(hidden_low, mlp_out_w))
    third_out = unit_three * gains_ref[2:3, :] + shifts_ref[2:3, :]
    cotangent_copy.wait()
    own_part = quad.pick(cotangent, width, 0)
    other_part = cotangent_half_ref[...].astype(F32)
    incoming = jnp.concatenate(
        [
            jnp.where(quad.side == 0, own_part, other_part),
            jnp.where(quad.side == 0, other_part, own_part),
        ],
        axis=0,
    )
    third_grad, gain_three, shift_three = norm_back(
        unit_three, root_three, gains_ref[2:3, :], incoming
    )
    branch_low = third_grad.astype(BF16)
    density = jnp.exp(-0.5 * hidden_pre * hidden_pre) * (1.0 / math.sqrt(2.0 * math.pi))
    pre_low = (dot_nn(branch_low, mlp_out_w) * (normal + hidden_pre * density)).astype(BF16)
    second_grad, gain_two, shift_two = norm_back(
        unit_two, root_two, gains_ref[1:2, :], third_grad + dot_nt(pre_low, mlp_in_w)
    )
    second_grad_low = second_grad.astype(BF16)
    mixed_grad = dot_nt(second_grad_low, item_out_w).astype(BF16).astype(F32)
    part = head_rows_of(mixed_grad * full, wide)[0:8, :]
    delta = jnp.concatenate([part[h : h + 1] for h in range(HEADS)], axis=1)
    totals = [log_total[:, h * block_rows : (h + 1) * block_rows] for h in range(HEADS)]
    spare = jnp.zeros((8 - HEADS, block_rows), F32)
    own_span = block_span(own_shard)
    all_stats_ref[0:8, own_span] = jnp.concatenate(totals + [spare], axis=0)
    all_stats_ref[8:16, own_span] = part
    grads_ref[own_rows, :] = pack_columns(mixed_grad, rows_dev).astype(BF16)
    grads_gather.start()

    row = put_tiles(mlp_part_ref, 0, dot_tn(second_low, pre_low))
    row = put_tiles(mlp_part_ref, row, dot_tn(branch_low, hidden_low))
    row = put_tiles(mlp_part_ref, row, dot_tn(item_low, second_grad_low))
    put_zeros(mlp_part_ref, row)
    mlp_sum.scatter_start(0)
    first_block, second_block = third_out[:rows_dev], third_out[rows_dev:]
    layer_half_ref[...] = jnp.where(quad.side == 0, second_block, first_block).astype(BF16)
    own_layer = jnp.where(quad.side == 0, first_block, second_block)

    grad_blocks_ref[...] = head_blocks(mixed_grad, head_dim)
    turned_ref[...] = jnp.zeros(turned_ref.shape, F32)
    key_steps = key_total // block_rows

    @pl.loop(0, key_steps)
    def _(step):
        span = block_span(step)
        attend_now = jnp.exp2(scores_ref[span, :] - log_total)
        dots = dot_nt(values_ref[span, :], grad_blocks_ref[...])
        score_grad = (attend_now * (dots - delta)).astype(BF16)
        turned_ref[...] += dot_nn(keys_turned_ref[:, span], score_grad)

    mlp_sum.scatter_finish(0)
    mlp_sum.scatter_start(1)
    query_grad = gather_heads_turned(turned_ref[...], block_rows, head_dim) * scaling

    blocks_ref[...] = head_blocks(own_keys, head_dim)
    grad_blocks_ref[...] = head_blocks(own_values, head_dim)
    total_ref[...] = jnp.zeros(total_ref.shape, F32)
    value_total_ref[...] = jnp.zeros(value_total_ref.shape, F32)

    def answer(shard_depth, shard_core):
        shard = shard_depth * 2 + shard_core
        span = block_span(shard)
        asked = dot_nn(hidden_of(shard), item_w[0]).astype(BF16)
        rows = pl.ds(pl.multiple_of(shard * rows_dev, rows_dev), rows_dev)
        grads = stack_columns(grads_ref[rows, :].astype(F32), width).astype(BF16)
        scores = dot_nt(blocks_ref[...], asked) * to_log2
        dots = dot_nt(grad_blocks_ref[...], grads)
        attends, score_grads = [], []
        for head in range(HEADS):
            part = slice(head * block_rows, (head + 1) * block_rows)
            attend_now = jnp.exp2(scores[part] - all_stats_ref[head : head + 1, span])
            attends.append(attend_now.astype(BF16))
            score_grads.append(
                (attend_now * (dots[part] - all_stats_ref[8 + head : 9 + head, span])).astype(BF16)
            )
        total_ref[...] += dot_nn(jnp.concatenate(score_grads, axis=0), asked)
        value_total_ref[...] += dot_nn(jnp.concatenate(attends, axis=0), grads)

    grads_gather.run(answer, 0)
    layer_copy = quad.across(layer_half_ref, layer_land_ref, side_sem.at[2])
    layer_copy.start()
    mlp_sum.scatter_finish(1)
    mlp_sum.share_start()

    own_open = open_rows((block_rows, width), depth, core)
    key_grad = gather_heads(total_ref[...], block_rows, head_dim) * scaling
    value_grad = gather_heads(value_total_ref[...], block_rows, head_dim)
    item_grads = [
        query_grad.astype(BF16),
        jnp.where(own_open, key_grad, 0.0).astype(BF16),
        jnp.where(own_open, value_grad, 0.0).astype(BF16),
    ]
    first_grad = second_grad
    for n in range(3):
        first_grad = first_grad + dot_nt(item_grads[n], item_w[n])
    first_in_grad, gain_one, shift_one = norm_back(
        unit_one, root_one, gains_ref[0:1, :], first_grad
    )
    branch_ref[...] = pack_columns(first_in_grad, rows_dev).astype(BF16)
    branch_copies = quad.spread(branch_ref, quad_branch_ref, quad_sem.at[1])
    for copy in branch_copies:
        copy.start()

    own_branch = first_in_grad.astype(BF16)
    row = put_tiles(
        item_part_ref,
        0,
        jnp.concatenate([dot_tn(first_low, item_grads[n]) for n in range(2)], axis=1),
    )
    row = put_tiles(
        item_part_ref,
        row,
        jnp.concatenate(
            [dot_tn(first_low, item_grads[2]), dot_tn(feat_mixed, own_branch)], axis=1
        ),
    )
    pairs = [
        jnp.concatenate(pair, axis=1)
        for pair in ((gain_one, shift_one), (gain_two, shift_two), (gain_three, shift_three))
    ]
    row = put_tiles(
        item_part_ref, row, jnp.concatenate(pairs + [jnp.zeros((13, 2 * width), F32)], axis=0)
    )
    put_zeros(item_part_ref, row)
    item_sum.scatter_start(0)

    other_query = dot_nn(all_low[block_rows:], feat_w[0]).astype(BF16).astype(F32)
    others = slots - 1
    other_weights = softmax_of(
        [
            feature_scores(other_query, keys, is_open, others, table, scaling)
            for keys, is_open in zip(key_list, open_list)
        ]
    )
    own_feat_grad = dot_nt(own_branch, feat_out_w).astype(BF16).astype(F32)

    def minus_mean(weights, dots):
        row_delta = None
        for weight, dot in zip(weights, dots):
            added = weight * dot
            row_delta = added if row_delta is None else row_delta + added
        return [dot - row_delta for dot in dots]

    own_dots = minus_mean(
        own_weights, [head_sums(own_feat_grad * part, table) for part in value_list]
    )
    own_score_grads = [
        (weight * dot).astype(BF16) for weight, dot in zip(own_weights, own_dots)
    ]
    feat_query_grad = None
    for score_grad, part in zip(own_score_grads, key_list):
        added = dot_nn(score_grad, wide) * part
        feat_query_grad = added if feat_query_grad is None else feat_query_grad + added
    item_sum.scatter_finish(0)
    item_sum.scatter_start(1)
    mlp_sum.share_finish()
    mlp_sum.gather_start(1)
    feat_key_grad = dot_nn(own_score_grads[0], wide) * own_query
    feat_value_grad = dot_nn(own_weights[0].astype(BF16), wide) * own_feat_grad
    for n, pattern in enumerate((1, 2, 3)):
        branch_copies[pattern - 1].wait()
        rows = slice(n * block_rows, (n + 1) * block_rows)
        branch = stack_columns(quad_branch_ref[quad.number(pattern)].astype(F32), width)
        grad = dot_nt(branch.astype(BF16), feat_out_w).astype(BF16).astype(F32)
        part_weights = [weight[rows] for weight in other_weights]
        part_dots = minus_mean(part_weights, [head_sums(grad * part, table) for part in value_list])
        score_grad = (part_weights[0] * part_dots[0]).astype(BF16)
        feat_key_grad = feat_key_grad + dot_nn(score_grad, wide) * other_query[rows]
        feat_value_grad = feat_value_grad + dot_nn(part_weights[0].astype(BF16), wide) * grad
    feat_grads = [
        (feat_query_grad * scaling).astype(BF16),
        (feat_key_grad * scaling).astype(BF16),
        feat_value_grad.astype(BF16),
    ]
    row = put_tiles(
        feat_part_ref,
        0,
        jnp.concatenate([dot_tn(own_low, feat_grads[n]) for n in range(2)], axis=1),
    )
    row = put_tiles(feat_part_ref, row, dot_tn(own_low, feat_grads[2]))
    put_zeros(feat_part_ref, row)
    feat_sum.scatter_start(0)
    item_sum.scatter_finish(1)
    item_sum.share_start()
    feat_sum.scatter_finish(0)
    feat_sum.scatter_start(1)
    mlp_sum.gather_finish(1)
    mlp_sum.gather_start(0)
    for k in range(rows_count // 4):
        banks_gather.across_side(k)
    inner = None
    for n in range(3):
        added = dot_nt(feat_grads[n], feat_w[n])
        inner = added if inner is None else inner + added
    cells_grad = first_in_grad + inner.astype(BF16).astype(F32)
    first_block, second_block = cells_grad[:rows_dev], cells_grad[rows_dev:]
    grad_half_ref[...] = jnp.where(quad.side == 0, second_block, first_block)
    own_cells_grad = jnp.where(quad.side == 0, first_block, second_block)
    grad_copy = quad.across(grad_half_ref, grad_land_ref, side_sem.at[3])
    layer_copy.wait()
    layer_ref[...] = quad.joined(own_layer, layer_land_ref[...].astype(F32)).astype(BF16)
    results = [mover.start(layer_ref, layer_out)]
    feat_sum.scatter_finish(1)
    feat_sum.share_start()
    item_sum.share_finish()
    item_sum.gather_start(1)
    grad_copy.start()
    for k in range(rows_count // 4):
        banks_gather.from_core(k, 0)
        banks_gather.from_core(k, 1)
    sort_rows = sorted_ref.shape[0]
    sort_block = math.gcd(sort_rows, 256)
    owner = owner_ref[...].reshape(1, sort_rows)

    def sort_some(first, last):
        @pl.loop(first, last)
        def _(step):
            start = pl.multiple_of(step * sort_block, sort_block)
            row = start + lax.broadcasted_iota(jnp.int32, (sort_block, sort_rows), 0)
            chosen = jnp.where(owner == row, 1.0, 0.0).astype(BF16)
            sorted_ref[pl.ds(start, sort_block), :] = dot_nn(chosen, banks_ref[...]).astype(BF16)

    thirds = sort_rows // sort_block // 3
    sort_some(0, thirds)
    feat_sum.share_finish()
    feat_sum.gather_start(1)
    item_sum.gather_finish(1)
    item_sum.gather_start(0)
    sort_some(thirds, 2 * thirds)
    feat_sum.gather_finish(1)
    feat_sum.gather_start(0)
    grad_copy.wait()
    cells_grad_ref[...] = quad.joined(own_cells_grad, grad_land_ref[...])
    results.append(mover.start(cells_grad_ref, cells_grad_out))
    sort_some(2 * thirds, sort_rows // sort_block)
    results.append(mover.start(sorted_ref, sorted_out))
    mlp_sum.gather_finish(0)
    item_sum.gather_finish(0)
    for gather in (hidden_gather, grads_gather, banks_gather):
        gather.wait_sent()
    for result in results:
        result.wait()
    feat_sum.gather_finish(0)


def moment_rule(gradient, first_old, second_old):
    first_new = BETA_ONE * first_old + (1.0 - BETA_ONE) * gradient
    second_new = BETA_TWO * second_old + (1.0 - BETA_TWO) * gradient * gradient
    first_hat = first_new * (1.0 / (1.0 - BETA_ONE**STEP))
    second_hat = second_new * (1.0 / (1.0 - BETA_TWO**STEP))
    return first_new, second_new, first_hat / (jnp.sqrt(second_hat) + EPSILON)


def root_mean(value):
    count = value.shape[0] * value.shape[1]
    square = jnp.sum(jnp.sum(value * value, axis=1, keepdims=True), axis=0, keepdims=True)
    return jnp.sqrt(square * (1.0 / count) + 1e-06)


def update_kernel(
    owner_ref,
    mlp_sum_ref,
    item_sum_ref,
    feat_sum_ref,
    gains_ref,
    shifts_ref,
    norm_first_ref,
    norm_second_ref,
    first_ref,
    second_ref,
    layer_in,
    cells_grad_in,
    small_in,
    big_in,
    sorted_in,
    proj_in,
    feat_out_in,
    item_out_in,
    mlp_in_in,
    mlp_out_in,
    layer_out,
    cells_grad_out,
    square_grad_out,
    in_grad_out,
    out_grad_out,
    norm_grad_ref,
    clip_ref,
    first_new_ref,
    second_new_ref,
    square_new_out,
    in_new_out,
    out_new_out,
    square_low_out,
    in_low_out,
    out_low_out,
    norm_new_ref,
    norm_first_new_ref,
    norm_second_new_ref,
    small_ref,
    big_ref,
    sorted_ref,
    olds_ref,
    mlp_in_ref,
    mlp_out_ref,
    square_grad_ref,
    in_grad_ref,
    out_grad_ref,
    square_new_ref,
    in_new_ref,
    out_new_ref,
    square_low_ref,
    in_low_ref,
    out_low_ref,
    rotated_ref,
    own_ref,
    move_sem,
):
    width, ff_width = mlp_in_ref.shape
    slots = first_ref.shape[0]
    squares = square_grad_ref.shape[0]
    mover = Mover(move_sem)
    small_loads = [
        (
            mover.start(small_in.at[n], small_ref.at[n]),
            mover.start(small_in.at[squares + n], small_ref.at[squares + n]),
        )
        for n in range(squares)
    ]
    last_loads = [
        mover.start(small_in.at[2 * squares], small_ref.at[2 * squares]),
        mover.start(small_in.at[2 * squares + 1], small_ref.at[2 * squares + 1]),
        mover.start(big_in, big_ref),
    ]
    sorted_load = mover.start(sorted_in, sorted_ref)
    old_loads = [
        mover.start(proj_in, olds_ref.at[0 : squares - 2]),
        mover.start(feat_out_in, olds_ref.at[squares - 2]),
        mover.start(item_out_in, olds_ref.at[squares - 1]),
    ]
    mlp_loads = [mover.start(mlp_in_in, mlp_in_ref), mover.start(mlp_out_in, mlp_out_ref)]
    results = [mover.start(layer_in, layer_out), mover.start(cells_grad_in, cells_grad_out)]

    square = None
    for part_ref in (mlp_sum_ref, item_sum_ref, feat_sum_ref):
        part = part_ref[...].astype(F32)
        added = jnp.sum(jnp.sum(part * part, axis=1, keepdims=True), axis=0, keepdims=True)
        square = added if square is None else square + added
    grad_norm = jnp.sqrt(square)
    factor = jnp.minimum(1.0, CLIP_NORM / grad_norm)
    clip_ref[0] = grad_norm[0, 0]
    both_width = 2 * width
    both_tiles = both_width // LANES * width
    feat_pair = take_tiles(feat_sum_ref, 0, width, both_width) * factor
    item_pair = take_tiles(item_sum_ref, 0, width, both_width) * factor
    mixed_pair = take_tiles(item_sum_ref, both_tiles, width, both_width) * factor
    parts = [
        feat_pair[:, :width],
        feat_pair[:, width:],
        take_tiles(feat_sum_ref, both_tiles, width, width) * factor,
        item_pair[:, :width],
        item_pair[:, width:],
        mixed_pair[:, :width],
        mixed_pair[:, width:],
        take_tiles(mlp_sum_ref, 2 * both_tiles, width, width) * factor,
    ]
    for n, clipped in enumerate(parts):
        square_grad_ref[n] = clipped
        for load in small_loads[n]:
            load.wait()
        turned = dot_low(dot_nn, clipped, small_ref[squares + n])
        rotated_ref[n * width : (n + 1) * width, :] = dot_low(dot_tn, small_ref[n], turned)
    results.append(mover.start(square_grad_ref, square_grad_out))
    start = squares * width
    middle = start + ff_width
    for load in last_loads:
        load.wait()
    clipped = take_tiles(mlp_sum_ref, 0, width, ff_width) * factor
    in_grad_ref[...] = clipped
    results.append(mover.start(in_grad_ref, in_grad_out))
    turned = dot_low(dot_tn, clipped, small_ref[2 * squares])
    rotated_ref[start:middle, :] = dot_low(dot_tn, big_ref[0], turned)
    clipped = take_tiles(mlp_sum_ref, both_tiles, width, ff_width) * factor
    out_grad_ref[...] = clipped
    results.append(mover.start(out_grad_ref, out_grad_out))
    turned = dot_low(dot_tn, clipped, small_ref[2 * squares + 1])
    rotated_ref[middle : middle + ff_width, :] = dot_low(dot_tn, big_ref[1], turned)

    def step_of(first_row, count):
        rows = slice(first_row, first_row + count)
        banks = sorted_ref[rows, :].astype(F32)
        return moment_rule(rotated_ref[rows, :], banks[:, :width], banks[:, width:])[2]

    sorted_load.wait()
    for load in old_loads:
        load.wait()
    for n in range(squares):
        turned = dot_low(dot_nt, step_of(n * width, width), small_ref[squares + n])
        update = dot_low(dot_nn, small_ref[n], turned)
        old = olds_ref[n]
        new = old - LEARN_RATE * root_mean(old) * update
        square_new_ref[n] = new
        square_low_ref[n] = new.astype(BF16)
        results.append(mover.start(square_new_ref.at[n], square_new_out.at[n]))
    results.append(mover.start(square_low_ref, square_low_out))
    for load in mlp_loads:
        load.wait()
    turned = dot_low(dot_nn, big_ref[0], step_of(start, ff_width))
    update = dot_low(dot_nt, small_ref[2 * squares], turned)
    new = mlp_in_ref[...] - LEARN_RATE * root_mean(mlp_in_ref[...]) * update
    in_new_ref[...] = new
    in_low_ref[...] = new.astype(BF16)
    results.append(mover.start(in_new_ref, in_new_out))
    results.append(mover.start(in_low_ref, in_low_out))
    turned = dot_low(dot_nn, big_ref[1], step_of(middle, ff_width))
    update = dot_low(dot_nt, small_ref[2 * squares + 1], turned)
    new = mlp_out_ref[...] - LEARN_RATE * root_mean(mlp_out_ref[...]) * update
    out_new_ref[...] = new
    out_low_ref[...] = new.astype(BF16)
    results.append(mover.start(out_new_ref, out_new_out))
    results.append(mover.start(out_low_ref, out_low_out))

    base = lax.axis_index("rows") * slots

    @pl.loop(0, slots // 8)
    def _(step):
        for n in range(8):
            row = owner_ref[base + step * 8 + n]
            own_ref[pl.ds(step * 8 + n, 1), :] = rotated_ref[pl.ds(row, 1), :]

    first_new, second_new, _ = moment_rule(own_ref[...], first_ref[...], second_ref[...])
    first_new_ref[...] = first_new
    second_new_ref[...] = second_new

    norm_pairs = take_tiles(item_sum_ref, 2 * both_tiles, 16, both_width) * factor
    for n in range(3):
        pair = norm_pairs[n : n + 1]
        both = jnp.concatenate([pair[:, :width], pair[:, width:]], axis=0)
        norm_grad_ref[n] = both
        first_new, second_new, change = moment_rule(both, norm_first_ref[n], norm_second_ref[n])
        norm_first_new_ref[n] = first_new
        norm_second_new_ref[n] = second_new
        old = jnp.concatenate([gains_ref[n : n + 1, :], shifts_ref[n : n + 1, :]], axis=0)
        size = jnp.sqrt(jnp.sum(old * old, axis=1, keepdims=True) * (1.0 / width) + 1e-06)
        norm_new_ref[n] = old - LEARN_RATE * size * change
    for result in results:
        result.wait()


def in_vmem():
    return pl.BlockSpec(memory_space=pltpu.VMEM)


def anywhere():
    return pl.BlockSpec(memory_space=pl.ANY)


def in_smem():
    return pl.BlockSpec(memory_space=pltpu.SMEM)


def fast_device(
    cells,
    feat_mask,
    train_rows,
    cotangent,
    proj_weights,
    feat_out_w,
    item_out_w,
    mlp_in,
    mlp_out,
    norm_gains,
    norm_shifts,
    bases_small,
    bases_big,
    owner_rows,
    bank_first,
    bank_second,
    norm_first,
    norm_second,
):
    rows_count, cols_count = lax.axis_size("rows"), lax.axis_size("cols")
    rows_dev, width_dev = cells.shape
    width = proj_weights.shape[-1]
    ff_width = mlp_in.shape[1]
    rows_all = rows_dev * rows_count
    key_total = rows_all // 4 * 3
    head_rows = HEADS * 2 * rows_dev
    dma = pltpu.SemaphoreType.DMA
    shape = jax.ShapeDtypeStruct
    sizes = {"z": rows_count // 4, "x": 2, "k": 2, "y": cols_count}

    mask_rows = feat_mask.T
    mlp_out_turned = mlp_out.T
    norm_first_turned = jnp.transpose(norm_first, (1, 0, 2))
    norm_second_turned = jnp.transpose(norm_second, (1, 0, 2))
    bank_rows = owner_rows.shape[0]

    def block_rows(rows):
        unit = 16 * math.prod(members(stage, sizes) for stage in STAGES[:-1])
        return -(-rows // unit) * unit

    def landings(rows):
        found = []
        for stage in STAGES[:-1]:
            count = members(stage, sizes)
            rows //= count
            found.append(pltpu.VMEM((count - 1, rows, LANES), BF16))
        return found + [pltpu.VMEM((members(STAGES[-1], sizes), rows, LANES), BF16)]

    both_tiles = 2 * width // LANES * width
    half_tiles = -(-width // LANES) * width
    sum_rows = [
        block_rows(2 * (ff_width // LANES) * width + half_tiles),
        block_rows(2 * both_tiles + 2 * width // LANES * 16),
        block_rows(both_tiles + half_tiles),
    ]
    widest = max(members(stage, sizes) for stage in STAGES) - 1
    layer_part, cells_part, mlp_total, item_total, feat_total, sorted_banks = pl.pallas_call(
        functools.partial(layer_kernel, rows_count, cols_count),
        name="layer_and_gradients",
        out_shape=(
            shape((rows_dev, width_dev), BF16),
            shape((rows_dev, width_dev), F32),
            *[shape((rows, LANES), BF16) for rows in sum_rows],
            shape((bank_rows, 2 * width), BF16),
        ),
        in_specs=[in_smem()] + [in_vmem()] * 5 + [anywhere()] * 8,
        out_specs=[anywhere()] * 2 + [in_vmem()] * 3 + [anywhere()],
        scratch_shapes=[
            pltpu.VMEM(proj_weights.shape, F32),
            pltpu.VMEM(feat_out_w.shape, F32),
            pltpu.VMEM(bank_first.shape, F32),
            pltpu.VMEM(bank_first.shape, F32),
            pltpu.VMEM(item_out_w.shape, F32),
            pltpu.VMEM(mlp_in.shape, F32),
            pltpu.VMEM(mlp_in.shape, F32),
            pltpu.VMEM((rows_dev, width_dev), BF16),
            pltpu.VMEM((rows_dev, width_dev), BF16),
            pltpu.VMEM((rows_dev, width_dev), F32),
            pltpu.VMEM((bank_rows, 2 * width), BF16),
            pltpu.VMEM((4, rows_dev, width_dev), BF16),
            pltpu.VMEM((2,) + mask_rows.shape, jnp.int32),
            pltpu.VMEM((rows_dev, width), BF16),
            pltpu.VMEM((rows_dev, width), BF16),
            pltpu.VMEM((rows_dev, width), BF16),
            pltpu.VMEM((rows_dev, width), BF16),
            pltpu.VMEM((rows_dev, width), F32),
            pltpu.VMEM((rows_dev, width), F32),
            pltpu.VMEM((rows_all // 2, width_dev), BF16),
            pltpu.VMEM((width, key_total), BF16),
            pltpu.VMEM((key_total, width), BF16),
            pltpu.VMEM((rows_all // 2, width_dev), BF16),
            pltpu.VMEM((16, rows_all), F32),
            pltpu.VMEM((bank_rows, 2 * width), BF16),
            pltpu.VMEM((head_rows, width), BF16),
            pltpu.VMEM((head_rows, width), BF16),
            pltpu.VMEM((key_total, head_rows), F32),
            pltpu.VMEM((1, head_rows), F32),
            pltpu.VMEM((1, head_rows), F32),
            pltpu.VMEM((width, head_rows), F32),
            pltpu.VMEM((head_rows, width), F32),
            pltpu.VMEM((head_rows, width), F32),
            pltpu.VMEM((rows_dev, width_dev), BF16),
            pltpu.VMEM((4, rows_dev, width_dev), BF16),
        ]
        + [pltpu.VMEM((rows, LANES), BF16) for rows in sum_rows]
        + [landing for rows in sum_rows for landing in landings(rows)]
        + [
            dma((2, 2, 3)),
            dma((4, 2)),
            dma((2, 1, DepthGather.slots(rows_count))),
            dma((2, 2, DepthGather.slots(rows_count))),
            dma((2, 1, RowGather.slots(rows_count))),
        ]
        + [dma((4, len(STAGES), widest))] * len(sum_rows)
        + [dma((11,))],
        compiler_params=pltpu.CompilerParams(
            collective_id=0, has_side_effects=True, vmem_limit_bytes=VMEM_BYTES
        ),
    )(
        train_rows,
        owner_rows,
        cells,
        mask_rows,
        norm_gains,
        norm_shifts,
        proj_weights,
        feat_out_w,
        bank_first,
        bank_second,
        item_out_w,
        mlp_in,
        mlp_out_turned,
        cotangent,
    )

    slots_dev = bank_first.shape[0]
    square = (8, width, width)
    (
        layer_out,
        cells_grad,
        square_grads,
        in_grad,
        out_grad,
        norm_grads,
        clip_norm,
        first_new,
        second_new,
        square_new,
        in_new,
        out_new,
        square_low,
        in_low,
        out_low,
        norm_new,
        norm_first_new,
        norm_second_new,
    ) = pl.pallas_call(
        update_kernel,
        name="rotated_update",
        out_shape=(
            shape(layer_part.shape, BF16),
            shape(cells_part.shape, F32),
            shape(square, F32),
            shape(mlp_in.shape, F32),
            shape(mlp_in.shape, F32),
            shape(norm_first_turned.shape, F32),
            shape((1,), F32),
            shape(bank_first.shape, F32),
            shape(bank_first.shape, F32),
            shape(square, F32),
            shape(mlp_in.shape, F32),
            shape(mlp_in.shape, F32),
            shape(square, BF16),
            shape(mlp_in.shape, BF16),
            shape(mlp_in.shape, BF16),
            shape(norm_first_turned.shape, F32),
            shape(norm_first_turned.shape, F32),
            shape(norm_first_turned.shape, F32),
        ),
        in_specs=[in_smem()] + [in_vmem()] * 11 + [anywhere()] * 8,
        out_specs=[anywhere()] * 5
        + [in_vmem(), in_smem(), in_vmem(), in_vmem()]
        + [anywhere()] * 6
        + [in_vmem()] * 3,
        scratch_shapes=[
            pltpu.VMEM(bases_small.shape, F32),
            pltpu.VMEM(bases_big.shape, F32),
            pltpu.VMEM(sorted_banks.shape, BF16),
            pltpu.VMEM(square, F32),
            pltpu.VMEM(mlp_in.shape, F32),
            pltpu.VMEM(mlp_in.shape, F32),
            pltpu.VMEM(square, F32),
            pltpu.VMEM(mlp_in.shape, F32),
            pltpu.VMEM(mlp_in.shape, F32),
            pltpu.VMEM(square, F32),
            pltpu.VMEM(mlp_in.shape, F32),
            pltpu.VMEM(mlp_in.shape, F32),
            pltpu.VMEM(square, BF16),
            pltpu.VMEM(mlp_in.shape, BF16),
            pltpu.VMEM(mlp_in.shape, BF16),
            pltpu.VMEM((bank_rows, width), F32),
            pltpu.VMEM((slots_dev, width), F32),
            dma((48,)),
        ],
        compiler_params=pltpu.CompilerParams(vmem_limit_bytes=VMEM_BYTES),
    )(
        owner_rows,
        mlp_total,
        item_total,
        feat_total,
        norm_gains,
        norm_shifts,
        norm_first_turned,
        norm_second_turned,
        bank_first,
        bank_second,
        layer_part,
        cells_part,
        bases_small,
        bases_big,
        sorted_banks,
        proj_weights,
        feat_out_w,
        item_out_w,
        mlp_in,
        mlp_out_turned,
    )
    return (
        layer_out,
        cells_grad,
        square_grads,
        in_grad,
        out_grad.T,
        jnp.transpose(norm_grads, (1, 0, 2)),
        clip_norm,
        first_new,
        second_new,
        square_new,
        in_new,
        out_new.T,
        square_low,
        in_low,
        out_low.T,
        jnp.transpose(norm_new, (1, 0, 2)),
        jnp.transpose(norm_first_new, (1, 0, 2)),
        jnp.transpose(norm_second_new, (1, 0, 2)),
    )


def solution(mesh):
    in_specs = (
        P("rows", "cols"),
        P("rows", None),
        P(),
        P("rows", "cols"),
        P(),
        P(),
        P(),
        P(),
        P(),
        P(),
        P(),
        P(),
        P(),
        P(),
        P("rows", None),
        P("rows", None),
        P(),
        P(),
    )
    out_specs = (
        P("rows", "cols"),
        P("rows", "cols"),
        P(),
        P(),
        P(),
        P(),
        P(),
        P("rows", None),
        P("rows", None),
        P(),
        P(),
        P(),
        P(),
        P(),
        P(),
        P(),
        P(),
        P(),
    )
    small = mesh.shape["rows"] == 16 and mesh.shape["cols"] == 2
    return jax.shard_map(
        fast_device if small else per_device, mesh=mesh, in_specs=in_specs, out_specs=out_specs, check_vma=False
    )
```

```python
import functools
import math

import jax
import jax.numpy as jnp
from jax import lax
from jax.experimental import pallas as pl
from jax.experimental.pallas import tpu as pltpu
from jax.sharding import PartitionSpec as P

HEADS = 6
STEP = 10


HIGHEST = lax.Precision.HIGHEST
NEGATIVE = -1e30
CLIP_NORM = 1.0
BETA_ONE = 0.9
BETA_TWO = 0.95
EPSILON = 1e-08
LEARN_RATE = 1.0


def layer_norm(hidden, gain_row, shift_row):
    center = jnp.mean(hidden, axis=-1, keepdims=True)
    centered = hidden - center
    spread = jnp.mean(centered * centered, axis=-1, keepdims=True)
    return centered * lax.rsqrt(spread + 1e-05) * gain_row + shift_row


def gelu_exact(hidden):
    return jax.nn.gelu(hidden, approximate=False)


def product(left_side, right_side):
    return jnp.dot(left_side, right_side, preferred_element_type=jnp.float32)


def product_left(left_side, right_side):
    return lax.dot_general(
        left_side, right_side, (((0,), (0,)), ((), ())), preferred_element_type=jnp.float32
    )


def product_right(left_side, right_side):
    return lax.dot_general(
        left_side, right_side, (((1,), (1,)), ((), ())), preferred_element_type=jnp.float32
    )


def feature_forward(queries, key_rows, value_rows, key_open):
    scaling = queries.shape[-1] ** (-0.5)
    scores = (
        jnp.einsum("nqhe,nkhe->nhqk", queries, key_rows, preferred_element_type=jnp.float32)
        * scaling
    )
    scores = jnp.where(key_open[:, None, None, :], scores, NEGATIVE)
    attend = jax.nn.softmax(scores, axis=-1)
    attend_low = attend.astype(jnp.bfloat16)
    mixed = jnp.einsum(
        "nhqk,nkhe->nqhe", attend_low, value_rows, preferred_element_type=jnp.float32
    )
    return (attend, attend_low, mixed.astype(jnp.bfloat16))


def feature_backward(queries, key_rows, value_rows, attend, attend_low, mixed_grad):
    scaling = queries.shape[-1] ** (-0.5)
    value_dots = jnp.einsum(
        "nqhe,nkhe->nhqk", mixed_grad, value_rows, preferred_element_type=jnp.float32
    )
    row_delta = jnp.sum(attend * value_dots, axis=-1, keepdims=True)
    score_grad = (attend * (value_dots - row_delta)).astype(jnp.bfloat16)
    query_grad = (
        jnp.einsum("nhqk,nkhe->nqhe", score_grad, key_rows, preferred_element_type=jnp.float32)
        * scaling
    )
    key_grad = (
        jnp.einsum("nhqk,nqhe->nkhe", score_grad, queries, preferred_element_type=jnp.float32)
        * scaling
    )
    value_grad = jnp.einsum(
        "nhqk,nqhe->nkhe", attend_low, mixed_grad, preferred_element_type=jnp.float32
    )
    return (
        query_grad.astype(jnp.bfloat16),
        key_grad.astype(jnp.bfloat16),
        value_grad.astype(jnp.bfloat16),
    )


def key_blocks_of(key_rows, value_rows):
    key_total = key_rows.shape[0]
    block_size = math.gcd(key_total, 1024)
    block_count = key_total // block_size
    tail_shape = key_rows.shape[1:]
    starts = jnp.arange(block_count, dtype=jnp.int32) * block_size
    return (
        key_rows.reshape((block_count, block_size) + tail_shape),
        value_rows.reshape((block_count, block_size) + tail_shape),
        starts,
    )


def block_scores(queries, key_block, start_row, train_count):
    scaling = queries.shape[-1] ** (-0.5)
    scores = (
        jnp.einsum("qche,kche->chqk", queries, key_block, preferred_element_type=jnp.float32)
        * scaling
    )
    open_keys = start_row + jnp.arange(key_block.shape[0], dtype=jnp.int32) < train_count
    return jnp.where(open_keys[None, None, None, :], scores, NEGATIVE)


def item_forward(queries, key_rows, value_rows, train_count):
    key_split, value_split, starts = key_blocks_of(key_rows, value_rows)
    stat_shape = (queries.shape[1], queries.shape[2], queries.shape[0])

    def max_pass(carried, packed):
        running_max, running_sum = carried
        key_block, start_row = packed
        scores = block_scores(queries, key_block, start_row, train_count)
        new_max = jnp.maximum(running_max, jnp.max(scores, axis=-1))
        running_sum = running_sum * jnp.exp(running_max - new_max) + jnp.sum(
            jnp.exp(scores - new_max[..., None]), axis=-1
        )
        return ((new_max, running_sum), None)

    start_max = jnp.full(stat_shape, NEGATIVE, jnp.float32)
    (row_max, row_sum), _ = lax.scan(
        max_pass, (start_max, jnp.zeros(stat_shape, jnp.float32)), (key_split, starts)
    )
    log_total = row_max + jnp.log(row_sum)

    def value_pass(carried, packed):
        key_block, value_block, start_row = packed
        attend = jnp.exp(
            block_scores(queries, key_block, start_row, train_count) - log_total[..., None]
        )
        added = jnp.einsum(
            "chqk,kche->qche",
            attend.astype(jnp.bfloat16),
            value_block,
            preferred_element_type=jnp.float32,
        )
        return (carried + added, None)

    item_full, _ = lax.scan(
        value_pass, jnp.zeros(queries.shape, jnp.float32), (key_split, value_split, starts)
    )
    return (log_total, item_full)


def delta_of(mixed_grad, item_full):
    return jnp.transpose(jnp.sum(mixed_grad.astype(jnp.float32) * item_full, axis=-1), (1, 2, 0))


def item_backward(queries, key_rows, value_rows, train_count, log_total, mixed_grad, item_full):
    key_split, value_split, starts = key_blocks_of(key_rows, value_rows)
    scaling = queries.shape[-1] ** (-0.5)
    row_delta = delta_of(mixed_grad, item_full)

    def back_pass(carried, packed):
        key_block, value_block, start_row = packed
        attend = jnp.exp(
            block_scores(queries, key_block, start_row, train_count) - log_total[..., None]
        )
        value_dots = jnp.einsum(
            "qche,kche->chqk", mixed_grad, value_block, preferred_element_type=jnp.float32
        )
        score_grad = (attend * (value_dots - row_delta[..., None])).astype(jnp.bfloat16)
        carried = carried + jnp.einsum(
            "chqk,kche->qche", score_grad, key_block, preferred_element_type=jnp.float32
        )
        key_grad = (
            jnp.einsum("chqk,qche->kche", score_grad, queries, preferred_element_type=jnp.float32)
            * scaling
        )
        value_grad = jnp.einsum(
            "chqk,qche->kche",
            attend.astype(jnp.bfloat16),
            mixed_grad,
            preferred_element_type=jnp.float32,
        )
        return (carried, (key_grad, value_grad))

    query_sum, (key_grads, value_grads) = lax.scan(
        back_pass, jnp.zeros(queries.shape, jnp.float32), (key_split, value_split, starts)
    )
    key_total = key_rows.shape[0]
    flat_width = queries.shape[1] * queries.shape[2] * queries.shape[3]
    return (
        query_sum * scaling,
        key_grads.reshape(key_total, flat_width),
        value_grads.reshape(key_total, flat_width),
    )


def clip_all(gradients):
    total_sq = jnp.sum(gradients[0] * gradients[0])
    for extra in gradients[1:]:
        total_sq = total_sq + jnp.sum(extra * extra)
    grad_norm = jnp.sqrt(total_sq)
    factor = jnp.minimum(1.0, CLIP_NORM / grad_norm)
    return ([gradient * factor for gradient in gradients], grad_norm)


def rotate_bank(square_grad, in_grad, out_grad, bases_small, bases_big):
    model_width = in_grad.shape[0]
    left_bases = bases_small[0:8]
    right_bases = bases_small[8:16]
    rot_square = jnp.matmul(
        jnp.swapaxes(left_bases, 1, 2),
        jnp.matmul(square_grad, right_bases, precision=HIGHEST),
        precision=HIGHEST,
    )
    rot_in = jnp.dot(
        bases_small[16].T, jnp.dot(in_grad, bases_big[0], precision=HIGHEST), precision=HIGHEST
    )
    rot_out = jnp.dot(
        bases_big[1].T, jnp.dot(out_grad, bases_small[17], precision=HIGHEST), precision=HIGHEST
    )
    return jnp.concatenate(
        [rot_square.reshape(8 * model_width, model_width), rot_in.T, rot_out], axis=0
    )


def rotate_back(step_bank, bases_small, bases_big):
    model_width = step_bank.shape[1]
    ff_width = (step_bank.shape[0] - 8 * model_width) // 2
    step_square = step_bank[: 8 * model_width].reshape(8, model_width, model_width)
    step_in = step_bank[8 * model_width : 8 * model_width + ff_width].T
    step_out = step_bank[8 * model_width + ff_width :]
    up_square = jnp.matmul(
        bases_small[0:8],
        jnp.matmul(step_square, jnp.swapaxes(bases_small[8:16], 1, 2), precision=HIGHEST),
        precision=HIGHEST,
    )
    up_in = jnp.dot(
        bases_small[16], jnp.dot(step_in, bases_big[0].T, precision=HIGHEST), precision=HIGHEST
    )
    up_out = jnp.dot(
        bases_big[1], jnp.dot(step_out, bases_small[17].T, precision=HIGHEST), precision=HIGHEST
    )
    return (up_square, up_in, up_out)


def adam_rows(gradient, first_old, second_old, step_float):
    first_new = BETA_ONE * first_old + (1.0 - BETA_ONE) * gradient
    second_new = BETA_TWO * second_old + (1.0 - BETA_TWO) * gradient * gradient
    first_hat = first_new / (1.0 - jnp.power(BETA_ONE, step_float))
    second_hat = second_new / (1.0 - jnp.power(BETA_TWO, step_float))
    return (first_new, second_new, first_hat / (jnp.sqrt(second_hat) + EPSILON))


def trusted(weight, update, over_axes):
    scaling = jnp.sqrt(jnp.mean(weight * weight, axis=over_axes, keepdims=True) + 1e-06)
    return weight - LEARN_RATE * scaling * update


def per_device(
    cells,
    feat_mask,
    train_rows,
    cotangent,
    proj_weights,
    feat_out_w,
    item_out_w,
    mlp_in,
    mlp_out,
    norm_gains,
    norm_shifts,
    bases_small,
    bases_big,
    owner_rows,
    bank_first,
    bank_second,
    norm_first,
    norm_second,
):
    rows_dev, width_dev = cells.shape
    model_width = proj_weights.shape[-1]
    head_count = HEADS
    head_dim = model_width // head_count
    cols_dev = width_dev // model_width
    col_count = lax.axis_size("cols")
    all_cols = cols_dev * col_count
    half_rows = rows_dev // col_count
    cell_count = rows_dev * cols_dev
    proj_low = proj_weights.astype(jnp.bfloat16)
    feat_qkv = jnp.concatenate([proj_low[0], proj_low[1], proj_low[2]], axis=1)
    item_qkv = jnp.concatenate([proj_low[3], proj_low[4], proj_low[5]], axis=1)
    feat_out_low = feat_out_w.astype(jnp.bfloat16)
    item_out_low = item_out_w.astype(jnp.bfloat16)
    mlp_in_cast = mlp_in.astype(jnp.bfloat16)
    mlp_out_cast = mlp_out.astype(jnp.bfloat16)
    train_count = train_rows[0]
    column_cells = lax.all_to_all(cells, "cols", split_axis=0, concat_axis=1, tiled=True)
    column_flat = column_cells.reshape(half_rows * all_cols, model_width)
    row_mask = (
        lax.dynamic_slice_in_dim(feat_mask, lax.axis_index("cols") * half_rows, half_rows, 0) > 0
    )
    feat_proj = (
        product(column_flat, feat_qkv)
        .astype(jnp.bfloat16)
        .reshape(half_rows, all_cols, 3, head_count, head_dim)
    )
    feat_query = feat_proj[:, :, 0]
    feat_key = feat_proj[:, :, 1]
    feat_value = feat_proj[:, :, 2]
    feat_attend, feat_attend_low, feat_mixed = feature_forward(
        feat_query, feat_key, feat_value, row_mask
    )
    feat_mixed_flat = feat_mixed.reshape(half_rows * all_cols, model_width)
    feat_branch = (
        product(feat_mixed_flat, feat_out_low)
        .astype(jnp.bfloat16)
        .reshape(half_rows, all_cols * model_width)
    )
    feat_back = lax.all_to_all(feat_branch, "cols", split_axis=1, concat_axis=0, tiled=True)
    inputs_flat = cells.astype(jnp.float32).reshape(cell_count, model_width)
    first_sum = inputs_flat + feat_back.astype(jnp.float32).reshape(cell_count, model_width)
    first_out, first_pull = jax.vjp(layer_norm, first_sum, norm_gains[0], norm_shifts[0])
    first_low = first_out.astype(jnp.bfloat16)
    item_proj = product(first_low, item_qkv).astype(jnp.bfloat16)
    item_query = item_proj[:, :model_width].reshape(rows_dev, cols_dev, head_count, head_dim)
    item_key = item_proj[:, model_width : 2 * model_width].reshape(rows_dev, width_dev)
    item_value = item_proj[:, 2 * model_width :].reshape(rows_dev, width_dev)
    key_rows, value_rows = (
        lax.all_gather(item_key, "rows", axis=0, tiled=True),
        lax.all_gather(item_value, "rows", axis=0, tiled=True),
    )
    key_total = key_rows.shape[0]
    key_rows = key_rows.reshape(key_total, cols_dev, head_count, head_dim)
    value_rows = value_rows.reshape(key_total, cols_dev, head_count, head_dim)
    log_total, item_full = item_forward(item_query, key_rows, value_rows, train_count)
    item_low = item_full.astype(jnp.bfloat16).reshape(cell_count, model_width)
    item_branch = product(item_low, item_out_low)
    second_sum = first_out + item_branch
    second_out, second_pull = jax.vjp(layer_norm, second_sum, norm_gains[1], norm_shifts[1])
    second_low = second_out.astype(jnp.bfloat16)
    hidden_pre = product(second_low, mlp_in_cast)
    hidden_act, gelu_pull = jax.vjp(gelu_exact, hidden_pre)
    hidden_low = hidden_act.astype(jnp.bfloat16)
    mlp_branch = product(hidden_low, mlp_out_cast)
    third_sum = second_out + mlp_branch
    third_out, third_pull = jax.vjp(layer_norm, third_sum, norm_gains[2], norm_shifts[2])
    layer_out = third_out.astype(jnp.bfloat16).reshape(rows_dev, width_dev)
    third_grad, gain_three, shift_three = third_pull(
        cotangent.astype(jnp.float32).reshape(cell_count, model_width)
    )
    branch_low = third_grad.astype(jnp.bfloat16)
    mlp_out_grad = product_left(hidden_low, branch_low)
    hidden_grad = product_right(branch_low, mlp_out_cast)
    (pre_grad,) = gelu_pull(hidden_grad)
    pre_low = pre_grad.astype(jnp.bfloat16)
    mlp_in_grad = product_left(second_low, pre_low)
    second_grad = third_grad + product_right(pre_low, mlp_in_cast)
    second_in_grad, gain_two, shift_two = second_pull(second_grad)
    item_branch_low = second_in_grad.astype(jnp.bfloat16)
    item_out_grad = product_left(item_low, item_branch_low)
    item_mixed_grad = (
        product_right(item_branch_low, item_out_low)
        .astype(jnp.bfloat16)
        .reshape(rows_dev, cols_dev, head_count, head_dim)
    )
    key_again, value_again = (
        lax.all_gather(item_key, "rows", axis=0, tiled=True),
        lax.all_gather(item_value, "rows", axis=0, tiled=True),
    )
    key_rows = key_again.reshape(key_total, cols_dev, head_count, head_dim)
    value_rows = value_again.reshape(key_total, cols_dev, head_count, head_dim)
    query_sum, key_grads, value_grads = item_backward(
        item_query, key_rows, value_rows, train_count, log_total, item_mixed_grad, item_full
    )
    key_sum, value_sum = (
        lax.psum_scatter(key_grads, "rows", scatter_dimension=0, tiled=True),
        lax.psum_scatter(value_grads, "rows", scatter_dimension=0, tiled=True),
    )
    item_grad_low = jnp.concatenate(
        [
            query_sum.astype(jnp.bfloat16).reshape(cell_count, model_width),
            key_sum.astype(jnp.bfloat16).reshape(cell_count, model_width),
            value_sum.astype(jnp.bfloat16).reshape(cell_count, model_width),
        ],
        axis=1,
    )
    item_qkv_grad = product_left(first_low, item_grad_low)
    first_grad = second_in_grad + product_right(item_grad_low, item_qkv)
    first_in_grad, gain_one, shift_one = first_pull(first_grad)
    feat_branch_grad = first_in_grad.astype(jnp.bfloat16).reshape(rows_dev, width_dev)
    column_grad = lax.all_to_all(
        feat_branch_grad, "cols", split_axis=0, concat_axis=1, tiled=True
    ).reshape(half_rows * all_cols, model_width)
    feat_out_grad = product_left(feat_mixed_flat, column_grad)
    feat_mixed_grad = (
        product_right(column_grad, feat_out_low)
        .astype(jnp.bfloat16)
        .reshape(half_rows, all_cols, head_count, head_dim)
    )
    feat_query_grad, feat_key_grad, feat_value_grad = feature_backward(
        feat_query, feat_key, feat_value, feat_attend, feat_attend_low, feat_mixed_grad
    )
    feat_grad_low = jnp.concatenate(
        [
            feat_query_grad.reshape(half_rows * all_cols, model_width),
            feat_key_grad.reshape(half_rows * all_cols, model_width),
            feat_value_grad.reshape(half_rows * all_cols, model_width),
        ],
        axis=1,
    )
    feat_qkv_grad = product_left(column_flat, feat_grad_low)
    column_in_grad = (
        product_right(feat_grad_low, feat_qkv)
        .astype(jnp.bfloat16)
        .reshape(half_rows, all_cols * model_width)
    )
    row_in_grad = lax.all_to_all(column_in_grad, "cols", split_axis=1, concat_axis=0, tiled=True)
    cells_grad = first_in_grad.reshape(rows_dev, width_dev) + row_in_grad.astype(jnp.float32)
    proj_grad = jnp.stack(
        [
            feat_qkv_grad[:, :model_width],
            feat_qkv_grad[:, model_width : 2 * model_width],
            feat_qkv_grad[:, 2 * model_width :],
            item_qkv_grad[:, :model_width],
            item_qkv_grad[:, model_width : 2 * model_width],
            item_qkv_grad[:, 2 * model_width :],
        ]
    )
    norm_grad = jnp.stack(
        [
            jnp.stack([gain_one, gain_two, gain_three]),
            jnp.stack([shift_one, shift_two, shift_three]),
        ]
    )
    proj_total, feat_total, item_total, in_total, out_total, norm_total = lax.psum(
        (proj_grad, feat_out_grad, item_out_grad, mlp_in_grad, mlp_out_grad, norm_grad),
        ("rows", "cols"),
    )
    square_grad = jnp.concatenate([proj_total, feat_total[None], item_total[None]], axis=0)
    clipped, grad_norm = clip_all([square_grad, in_total, out_total, norm_total])
    square_clip, in_clip, out_clip, norm_clip = clipped
    rot_bank = rotate_bank(square_clip, in_clip, out_clip, bases_small, bases_big)
    step_float = jnp.asarray(STEP, jnp.float32)
    slot_count = bank_first.shape[0]
    my_slots = lax.dynamic_slice_in_dim(
        owner_rows, lax.axis_index("rows") * slot_count, slot_count, 0
    )
    first_new, second_new, slot_steps = adam_rows(
        jnp.take(rot_bank, my_slots, axis=0), bank_first, bank_second, step_float
    )
    all_steps = lax.all_gather(slot_steps, "rows", axis=0, tiled=True)
    full_steps = jnp.take(all_steps, jnp.argsort(owner_rows), axis=0)
    up_square, up_in, up_out = rotate_back(full_steps, bases_small, bases_big)
    square_old = jnp.concatenate([proj_weights, feat_out_w[None], item_out_w[None]], axis=0)
    square_new = trusted(square_old, up_square, (1, 2))
    in_new = trusted(mlp_in, up_in, (0, 1))
    out_new = trusted(mlp_out, up_out, (0, 1))
    norm_old = jnp.stack([norm_gains, norm_shifts])
    norm_first_new, norm_second_new, norm_steps = adam_rows(
        norm_clip, norm_first, norm_second, step_float
    )
    norm_new = trusted(norm_old, norm_steps, (2,))
    return (
        layer_out,
        cells_grad,
        square_clip,
        in_clip,
        out_clip,
        norm_clip,
        grad_norm.reshape(1),
        first_new,
        second_new,
        square_new,
        in_new,
        out_new,
        square_new.astype(jnp.bfloat16),
        in_new.astype(jnp.bfloat16),
        out_new.astype(jnp.bfloat16),
        norm_new,
        norm_first_new,
        norm_second_new,
    )


F32 = jnp.float32
BF16 = jnp.bfloat16
MESH = pl.DeviceIdType.MESH
VMEM_BYTES = 56 * 1024 * 1024
LANES = 128


def dot_nn(left, right):
    return jnp.dot(left, right, preferred_element_type=F32)


def dot_nt(left, right):
    return lax.dot_general(left, right, (((1,), (1,)), ((), ())), preferred_element_type=F32)


def dot_tn(left, right):
    return lax.dot_general(left, right, (((0,), (0,)), ((), ())), preferred_element_type=F32)


def split_two(value):
    high = value.astype(BF16)
    return high, (value - high.astype(F32)).astype(BF16)


def dot_low(dot, left, right):
    return dot(left.astype(BF16), right.astype(BF16))


def stack_columns(packed, width):
    count = packed.shape[1] // width
    return jnp.concatenate([packed[:, n * width : (n + 1) * width] for n in range(count)], axis=0)


def pack_columns(stacked, rows):
    count = stacked.shape[0] // rows
    return jnp.concatenate([stacked[n * rows : (n + 1) * rows] for n in range(count)], axis=1)


def norm_parts(hidden):
    width = hidden.shape[1]
    center = jnp.sum(hidden, axis=1, keepdims=True) * (1.0 / width)
    centered = hidden - center
    spread = jnp.sum(centered * centered, axis=1, keepdims=True) * (1.0 / width)
    root = lax.rsqrt(spread + 1e-05)
    return centered * root, root


def norm_back(unit, root, gain, incoming):
    width = unit.shape[1]
    scaled = incoming * gain
    mean_one = jnp.sum(scaled, axis=1, keepdims=True) * (1.0 / width)
    mean_two = jnp.sum(scaled * unit, axis=1, keepdims=True) * (1.0 / width)
    gain_grad = jnp.sum(incoming * unit, axis=0, keepdims=True)
    shift_grad = jnp.sum(incoming, axis=0, keepdims=True)
    return root * (scaled - mean_one - unit * mean_two), gain_grad, shift_grad


def head_table(width, head_dim):
    feature = lax.broadcasted_iota(jnp.int32, (width, LANES), 0)
    head = lax.broadcasted_iota(jnp.int32, (width, LANES), 1)
    inside = (feature >= head * head_dim) & (feature < (head + 1) * head_dim)
    return jnp.where(inside, 1.0, 0.0).astype(BF16)


def spread_table(width, head_dim):
    head = lax.broadcasted_iota(jnp.int32, (LANES, width), 0)
    feature = lax.broadcasted_iota(jnp.int32, (LANES, width), 1)
    inside = (feature >= head * head_dim) & (feature < (head + 1) * head_dim)
    return jnp.where(inside, 1.0, 0.0).astype(BF16)


def head_rows_of(value, wide):
    high, low = split_two(value)
    return dot_nt(wide, high) + dot_nt(wide, low)


def head_sums(value, table):
    high, low = split_two(value)
    return dot_nn(high, table) + dot_nn(low, table)


def head_sums_low(value, table):
    return dot_nn(value.astype(BF16), table)


def head_mask(rows, width, head_dim, head):
    feature = lax.broadcasted_iota(jnp.int32, (rows, width), 1)
    return (feature >= head * head_dim) & (feature < (head + 1) * head_dim)


def tile_rows(value, count):
    return jnp.concatenate([value] * count, axis=0)


def feature_scores(queries, keys, is_open, repeat, table, scaling):
    raw = head_sums(queries * tile_rows(keys, repeat), table) * scaling
    return jnp.where(tile_rows(is_open, repeat), raw, NEGATIVE)


def softmax_of(scores):
    top = scores[0]
    for extra in scores[1:]:
        top = jnp.maximum(top, extra)
    grown = [jnp.exp(score - top) for score in scores]
    total = grown[0]
    for extra in grown[1:]:
        total = total + extra
    inverse = 1.0 / total
    return [part * inverse for part in grown]


def flip(value, pattern, size):
    out, step = 0, 1
    while step < size:
        out = out + step * (((value // step) % 2 + (pattern // step) % 2) % 2)
        step *= 2
    return out


class RowGather:
    def __init__(self, pieces, send_sem, recv_sem, rows_count):
        self.pieces, self.send_sem, self.recv_sem = pieces, send_sem, recv_sem
        self.deep = rows_count // 4
        me = lax.axis_index("rows")
        self.core, self.side, self.depth = me % 2, (me // 2) % 2, me // 4

    @staticmethod
    def slots(rows_count):
        return rows_count - 1

    def place(self, depth, side, core):
        return (depth * 2 + side) * 2 + core

    def source(self, k):
        return flip(self.depth, k, self.deep)

    def side_peer(self):
        return self.place(self.depth, 1 - self.side, self.core)

    def core_peer(self):
        return self.place(self.depth, self.side, 1 - self.core)

    def copies(self, shard, target, slot):
        return [
            pltpu.make_async_remote_copy(
                src_ref=piece(shard),
                dst_ref=piece(shard),
                send_sem=self.send_sem.at[n, slot],
                recv_sem=self.recv_sem.at[n, slot],
                device_id={"rows": target},
                device_id_type=MESH,
            )
            for n, piece in enumerate(self.pieces)
        ]

    def push(self, shard, target, slot):
        for copy in self.copies(shard, target, slot):
            copy.start()

    def arrive(self, shard, source, slot):
        for copy in self.copies(shard, source, slot):
            copy.wait_recv()

    def start_depth(self):
        own = self.place(self.depth, self.side, self.core)
        for k in range(1, self.deep):
            self.push(own, self.place(self.source(k), self.side, self.core), k - 1)

    def start_near(self):
        own = self.place(self.depth, self.side, self.core)
        self.push(own, self.core_peer(), 2 * self.deep - 1)
        self.push(own, self.side_peer(), self.deep - 1)

    def along_depth(self, k):
        shard = self.place(self.source(k), self.side, self.core)
        self.arrive(shard, shard, k - 1)
        self.push(shard, self.side_peer(), self.deep - 1 + k)
        self.push(shard, self.core_peer(), 2 * self.deep - 1 + k)

    def across_side(self, k):
        shard = self.place(self.source(k), 1 - self.side, self.core)
        self.arrive(shard, self.side_peer(), self.deep - 1 + k)
        self.push(shard, self.core_peer(), 3 * self.deep - 1 + k)

    def from_core(self, k, other_side):
        side = self.side + other_side - 2 * self.side * other_side
        shard = self.place(self.source(k), side, 1 - self.core)
        self.arrive(shard, self.core_peer(), (2 + other_side) * self.deep - 1 + k)

    def forward(self, k):
        self.across_side(k)

        @pl.when(k + 1 < self.deep)
        def _():
            self.along_depth(k + 1)

    def run(self, use, forwarded):
        @pl.loop(0, 2 * self.deep)
        def _(turn):
            k, other = turn // 2, turn % 2
            if forwarded:

                @pl.when((other == 0) & (k > 0) & (k + forwarded - 1 < self.deep))
                def _():
                    self.forward(k + forwarded - 1)

            else:

                @pl.when((turn == 1) | ((other == 0) & (k > 0)))
                def _():
                    self.forward(k)

            self.from_core(k, other)
            use(self.source(k), self.side + other - 2 * self.side * other)

    def wait_sent(self):
        own = self.place(self.depth, self.side, self.core)

        @pl.loop(0, 4 * self.deep - 1)
        def _(slot):
            for copy in self.copies(own, self.core_peer(), slot):
                copy.wait_send()


class DepthGather:
    def __init__(self, pieces, send_sem, recv_sem, rows_count):
        self.pieces, self.send_sem, self.recv_sem = pieces, send_sem, recv_sem
        self.deep = rows_count // 4
        me = lax.axis_index("rows")
        self.core, self.side, self.depth = me % 2, (me // 2) % 2, me // 4

    @staticmethod
    def slots(rows_count):
        return rows_count // 2 - 1

    def row(self, depth, core):
        return (depth * 2 + self.side) * 2 + core

    def source(self, k):
        return flip(self.depth, k, self.deep)

    def copies(self, shard, target, slot):
        return [
            pltpu.make_async_remote_copy(
                src_ref=piece(shard),
                dst_ref=piece(shard),
                send_sem=self.send_sem.at[n, slot],
                recv_sem=self.recv_sem.at[n, slot],
                device_id={"rows": target},
                device_id_type=MESH,
            )
            for n, piece in enumerate(self.pieces)
        ]

    def start(self):
        own = self.depth * 2 + self.core
        for copy in self.copies(own, self.row(self.depth, 1 - self.core), self.deep - 1):
            copy.start()
        for k in range(1, self.deep):
            for copy in self.copies(own, self.row(self.source(k), self.core), k - 1):
                copy.start()

    def forward(self, k):
        shard = self.source(k) * 2 + self.core
        for copy in self.copies(shard, self.row(self.source(k), self.core), k - 1):
            copy.wait_recv()
        twin = self.row(self.depth, 1 - self.core)
        for copy in self.copies(shard, twin, self.deep - 1 + k):
            copy.start()

    def run(self, use, forwarded):
        twin = self.row(self.depth, 1 - self.core)

        @pl.loop(0, 2 * self.deep)
        def _(turn):
            k, other = turn // 2, turn % 2

            @pl.when((other == 0) & (k > forwarded))
            def _():
                self.forward(k)

            @pl.when(other == 1)
            def _():
                shard = self.source(k) * 2 + 1 - self.core
                for copy in self.copies(shard, twin, self.deep - 1 + k):
                    copy.wait_recv()

            use(self.source(k), self.core + other - 2 * self.core * other)

    def wait_sent(self):
        own = self.depth * 2 + self.core

        @pl.loop(0, 2 * self.deep - 1)
        def _(slot):
            for copy in self.copies(own, self.row(self.depth, 1 - self.core), slot):
                copy.wait_send()


class Quad:
    def __init__(self):
        row = lax.axis_index("rows")
        self.side, self.col = (row // 2) % 2, lax.axis_index("cols")
        self.row = row
        self.own = self.side * 2 + self.col

    def device(self, pattern):
        side_flip, col_flip = pattern % 2, pattern // 2
        side = self.side + side_flip - 2 * self.side * side_flip
        col = self.col + col_flip - 2 * self.col * col_flip
        return {"rows": self.row + 2 * (side - self.side), "cols": col}

    def number(self, pattern):
        side_flip, col_flip = pattern % 2, pattern // 2
        side = self.side + side_flip - 2 * self.side * side_flip
        return side * 2 + self.col + col_flip - 2 * self.col * col_flip

    def spread(self, source, landing, sem):
        return [
            pltpu.make_async_remote_copy(
                src_ref=source,
                dst_ref=landing.at[self.own],
                send_sem=sem.at[0, pattern - 1],
                recv_sem=sem.at[1, pattern - 1],
                device_id=self.device(pattern),
                device_id_type=MESH,
            )
            for pattern in range(1, 4)
        ]

    def across(self, source, landing, sem):
        return pltpu.make_async_remote_copy(
            src_ref=source,
            dst_ref=landing,
            send_sem=sem.at[0],
            recv_sem=sem.at[1],
            device_id=self.device(1),
            device_id_type=MESH,
        )

    def pick(self, packed, width, other):
        left, right = packed[:, :width], packed[:, width:]
        return jnp.where(self.side == other, left, right)

    def joined(self, own, other):
        return jnp.concatenate(
            [jnp.where(self.side == 0, own, other), jnp.where(self.side == 0, other, own)], axis=1
        )

    def columns(self, landing, width, col_flip):
        col = self.col + col_flip - 2 * self.col * col_flip
        blocks = [landing[side * 2 + col].astype(F32) for side in range(2)]
        return [
            jnp.concatenate([self.pick(block, width, other) for block in blocks], axis=0)
            for other in range(2)
        ]


class StagedSum:
    def __init__(self, stages, sizes, part_ref, total_ref, landing, sems):
        self.stages, self.sizes = stages, sizes
        self.part_ref, self.total_ref, self.landing, self.sems = part_ref, total_ref, landing, sems
        row = lax.axis_index("rows")
        self.me = {"z": row // 4, "x": (row // 2) % 2, "k": row % 2, "y": lax.axis_index("cols")}
        self.spans, base, size = [], 0, part_ref.shape[0]
        for stage in stages[:-1]:
            size = size // members(stage, sizes)
            self.spans.append((base, size))
            base = base + self.number(self.me, stage) * size
        self.base, self.size = base, size
        self.unit = size

    def number(self, place, stage):
        out, scale = 0, 1
        for axis in stage:
            out = out + place[axis] * scale
            scale *= self.sizes[axis]
        return out

    def partner(self, stage, pattern):
        place = dict(self.me)
        for axis in stage:
            place[axis] = flip(self.me[axis], pattern % self.sizes[axis], self.sizes[axis])
            pattern //= self.sizes[axis]
        return place

    def device(self, place):
        return {"rows": (place["z"] * 2 + place["x"]) * 2 + place["k"], "cols": place["y"]}

    def rows_at(self, base, size):
        return pl.ds(pl.multiple_of(base, self.unit), size)

    def scatter(self, s):
        stage, (base, size) = self.stages[s], self.spans[s]
        found = []
        for j in range(1, members(stage, self.sizes)):
            place = self.partner(stage, j)
            rows = self.rows_at(base + self.number(place, stage) * size, size)
            found.append(
                pltpu.make_async_remote_copy(
                    src_ref=self.part_ref.at[rows, :],
                    dst_ref=self.landing[s].at[j - 1],
                    send_sem=self.sems.at[0, s, j - 1],
                    recv_sem=self.sems.at[1, s, j - 1],
                    device_id=self.device(place),
                    device_id_type=MESH,
                )
            )
        return found

    def scatter_start(self, s):
        for copy in self.scatter(s):
            copy.start()

    def scatter_finish(self, s):
        stage, (base, size) = self.stages[s], self.spans[s]
        rows = self.rows_at(base + self.number(self.me, stage) * size, size)
        total = self.part_ref[rows, :].astype(F32)
        copies = self.scatter(s)
        for j, copy in enumerate(copies):
            copy.wait_recv()
            total = total + self.landing[s][j].astype(F32)
        for copy in copies:
            copy.wait_send()
        self.part_ref[rows, :] = total.astype(BF16)

    def share(self):
        last = len(self.stages) - 1
        stage, landing = self.stages[last], self.landing[last]
        rows = self.rows_at(self.base, self.size)
        own = self.number(self.me, stage)
        found = []
        for j in range(1, members(stage, self.sizes)):
            found.append(
                pltpu.make_async_remote_copy(
                    src_ref=self.part_ref.at[rows, :],
                    dst_ref=landing.at[own],
                    send_sem=self.sems.at[0, last, j - 1],
                    recv_sem=self.sems.at[1, last, j - 1],
                    device_id=self.device(self.partner(stage, j)),
                    device_id_type=MESH,
                )
            )
        return found

    def share_start(self):
        for copy in self.share():
            copy.start()
        own = self.number(self.me, self.stages[-1])
        self.landing[-1][own] = self.part_ref[self.rows_at(self.base, self.size), :]

    def share_finish(self):
        copies = self.share()
        for copy in copies:
            copy.wait_recv()
        total = self.landing[-1][0].astype(F32)
        for n in range(1, members(self.stages[-1], self.sizes)):
            total = total + self.landing[-1][n].astype(F32)
        for copy in copies:
            copy.wait_send()
        self.total_ref[self.rows_at(self.base, self.size), :] = total.astype(BF16)

    def gather(self, s, own):
        stage, (base, size) = self.stages[s], self.spans[s]
        found = []
        for j in range(1, members(stage, self.sizes)):
            place = self.partner(stage, j)
            holder = self.me if own else place
            rows = self.rows_at(base + self.number(holder, stage) * size, size)
            found.append(
                pltpu.make_async_remote_copy(
                    src_ref=self.total_ref.at[rows, :],
                    dst_ref=self.total_ref.at[rows, :],
                    send_sem=self.sems.at[2, s, j - 1],
                    recv_sem=self.sems.at[3, s, j - 1],
                    device_id=self.device(place),
                    device_id_type=MESH,
                )
            )
        return found

    def gather_start(self, s):
        for copy in self.gather(s, True):
            copy.start()

    def gather_finish(self, s):
        for copy in self.gather(s, False):
            copy.wait_recv()
        for copy in self.gather(s, True):
            copy.wait_send()


class Mover:
    def __init__(self, sem):
        self.sem, self.count = sem, 0

    def start(self, source, target):
        copy = pltpu.make_async_copy(source, target, self.sem.at[self.count])
        copy.start()
        self.count += 1
        return copy


def put_tiles(ref, row, value):
    rows, lanes = value.shape
    if lanes % LANES:
        value = jnp.concatenate([value, jnp.zeros((rows, LANES - lanes % LANES), F32)], axis=1)
    for n in range(value.shape[1] // LANES):
        ref[row : row + rows, :] = value[:, n * LANES : (n + 1) * LANES].astype(ref.dtype)
        row += rows
    return row


def put_zeros(ref, row):
    if row < ref.shape[0]:
        ref[row:, :] = jnp.zeros((ref.shape[0] - row, ref.shape[1]), ref.dtype)


def take_tiles(ref, row, rows, lanes):
    count = -(-lanes // LANES)
    tiles = [ref[row + n * rows : row + (n + 1) * rows, :].astype(F32) for n in range(count)]
    value = jnp.concatenate(tiles, axis=1)
    return value if lanes % LANES == 0 else value[:, :lanes]


def members(stage, sizes):
    return math.prod(sizes[axis] for axis in stage)


def meet(targets):
    barrier = pltpu.get_barrier_semaphore()
    for target in targets:
        pl.semaphore_signal(barrier, inc=1, device_id=target, device_id_type=MESH)
    pl.semaphore_wait(barrier, len(targets))


def head_blocks(value, head_dim):
    rows, width = value.shape
    blocks = [
        jnp.where(head_mask(rows, width, head_dim, head), value, 0.0).astype(BF16)
        for head in range(HEADS)
    ]
    return jnp.concatenate(blocks, axis=0)


def gather_heads_turned(value, rows, head_dim):
    blocks = [
        value[head * head_dim : (head + 1) * head_dim, head * rows : (head + 1) * rows]
        for head in range(HEADS)
    ]
    return jnp.transpose(jnp.concatenate(blocks, axis=0))


def gather_heads(value, rows, head_dim):
    total = None
    for head in range(HEADS):
        block = value[head * rows : (head + 1) * rows]
        kept = jnp.where(head_mask(rows, value.shape[1], head_dim, head), block, 0.0)
        total = kept if total is None else total + kept
    return total


STAGES = ("k", "xy", "z")


def layer_kernel(
    rows_count,
    cols_count,
    train_ref,
    owner_ref,
    cells_ref,
    mask_ref,
    gains_ref,
    shifts_ref,
    proj_in,
    feat_out_in,
    bank_first_in,
    bank_second_in,
    item_out_in,
    mlp_in_in,
    mlp_out_in,
    cotangent_in,
    layer_out,
    cells_grad_out,
    mlp_total_ref,
    item_total_ref,
    feat_total_ref,
    sorted_out,
    proj_ref,
    feat_out_ref,
    bank_first_ref,
    bank_second_ref,
    item_out_ref,
    mlp_in_ref,
    mlp_out_ref,
    cotangent_ref,
    layer_ref,
    cells_grad_ref,
    sorted_ref,
    quad_ref,
    masks_ref,
    half_ref,
    cotangent_half_ref,
    layer_half_ref,
    layer_land_ref,
    grad_half_ref,
    grad_land_ref,
    gathered_ref,
    keys_turned_ref,
    values_ref,
    grads_ref,
    all_stats_ref,
    banks_ref,
    blocks_ref,
    grad_blocks_ref,
    scores_ref,
    top_ref,
    sum_ref,
    turned_ref,
    total_ref,
    value_total_ref,
    branch_ref,
    quad_branch_ref,
    mlp_part_ref,
    item_part_ref,
    feat_part_ref,
    mlp_land_k,
    mlp_land_xy,
    mlp_land_z,
    item_land_k,
    item_land_xy,
    item_land_z,
    feat_land_k,
    feat_land_xy,
    feat_land_z,
    quad_sem,
    side_sem,
    gather_sem,
    grads_sem,
    banks_sem,
    mlp_sem,
    item_sem,
    feat_sem,
    move_sem,
):
    mover = Mover(move_sem)
    proj_load = mover.start(proj_in, proj_ref)
    feat_out_load = mover.start(feat_out_in, feat_out_ref)
    cotangent_load = mover.start(cotangent_in, cotangent_ref)
    bank_loads = [
        mover.start(bank_first_in, bank_first_ref),
        mover.start(bank_second_in, bank_second_ref),
    ]
    later_loads = [
        mover.start(source, target)
        for source, target in (
            (item_out_in, item_out_ref),
            (mlp_in_in, mlp_in_ref),
            (mlp_out_in, mlp_out_ref),
        )
    ]
    rows_dev = cells_ref.shape[0]
    width = feat_out_ref.shape[0]
    head_dim = width // HEADS
    scaling = head_dim ** (-0.5)
    to_log2 = scaling * math.log2(math.e)
    key_total = values_ref.shape[0]
    block_rows = 2 * rows_dev
    bank_slots = bank_first_ref.shape[0]
    train_count = train_ref[0]
    me = lax.axis_index("rows")
    quad = Quad()
    sizes = {"z": rows_count // 4, "x": 2, "k": 2, "y": cols_count}

    def shard_of(ref, rows):
        return lambda shard: ref.at[pl.ds(pl.multiple_of(shard * rows, rows), rows), :]

    def stats_shard(shard):
        return all_stats_ref.at[:, block_span(shard)]

    def block_span(shard):
        return pl.ds(pl.multiple_of(shard * block_rows, block_rows), block_rows)

    hidden_gather = DepthGather(
        [shard_of(gathered_ref, rows_dev)], gather_sem.at[0], gather_sem.at[1], rows_count
    )
    grads_gather = DepthGather(
        [shard_of(grads_ref, rows_dev), stats_shard], grads_sem.at[0], grads_sem.at[1], rows_count
    )
    banks_gather = RowGather(
        [shard_of(banks_ref, bank_slots)], banks_sem.at[0], banks_sem.at[1], rows_count
    )
    mlp_sum = StagedSum(
        STAGES,
        sizes,
        mlp_part_ref,
        mlp_total_ref,
        (mlp_land_k, mlp_land_xy, mlp_land_z),
        mlp_sem,
    )
    item_sum = StagedSum(
        STAGES,
        sizes,
        item_part_ref,
        item_total_ref,
        (item_land_k, item_land_xy, item_land_z),
        item_sem,
    )
    feat_sum = StagedSum(
        STAGES,
        sizes,
        feat_part_ref,
        feat_total_ref,
        (feat_land_k, feat_land_xy, feat_land_z),
        feat_sem,
    )
    depth, core = hidden_gather.depth, hidden_gather.core
    own_shard = depth * 2 + core
    own_rows = pl.ds(pl.multiple_of(own_shard * rows_dev, rows_dev), rows_dev)
    meet(
        [
            mlp_sum.device(mlp_sum.partner(stage, j))
            for stage in STAGES
            for j in range(1, members(stage, sizes))
        ]
    )

    cell_copies = quad.spread(cells_ref, quad_ref, quad_sem.at[0])
    for copy in cell_copies:
        copy.start()
    mask_copy = quad.across(mask_ref, masks_ref.at[quad.side], side_sem.at[0])
    mask_copy.start()
    quad_ref[quad.own] = cells_ref[...]
    masks_ref[quad.side] = mask_ref[...]
    for load in bank_loads:
        load.wait()
    banks_ref[pl.ds(pl.multiple_of(me * bank_slots, bank_slots), bank_slots), :] = jnp.concatenate(
        [bank_first_ref[...], bank_second_ref[...]], axis=1
    ).astype(BF16)
    banks_gather.start_depth()
    cotangent_load.wait()
    cotangent = cotangent_ref[...].astype(F32)
    half_ref[...] = quad.pick(cotangent, width, 1).astype(BF16)
    cotangent_copy = quad.across(half_ref, cotangent_half_ref, side_sem.at[1])

    table = head_table(width, head_dim)
    wide = spread_table(width, head_dim)
    proj_load.wait()
    feat_w = [proj_ref[n].astype(BF16) for n in range(3)]
    slots = 4
    mask_blocks = []
    cell_copies[0].wait()
    mask_copy.wait()
    for side in range(2):
        rows = [
            masks_ref[
                side,
                pl.ds(
                    2 * (quad.col + col_flip - 2 * quad.col * col_flip)
                    + quad.side
                    + other
                    - 2 * quad.side * other,
                    1,
                ),
                :,
            ]
            for col_flip in range(2)
            for other in range(2)
        ]
        rows.append(jnp.zeros((8 - slots, rows_dev), jnp.int32))
        mask_blocks.append(jnp.transpose(jnp.concatenate(rows, axis=0).astype(F32)))
    masks = jnp.concatenate(mask_blocks, axis=0)
    open_list = [masks[:, n : n + 1] > 0.0 for n in range(slots)]
    columns, key_list, value_list, scores = [], [], [], []
    for col_flip in range(2):
        if col_flip == 1:
            cell_copies[1].wait()
            cell_copies[2].wait()
        columns += quad.columns(quad_ref, width, col_flip)
        if col_flip == 0:
            own = columns[0]
            own_low = own.astype(BF16)
            own_query = dot_nn(own_low, feat_w[0]).astype(BF16).astype(F32)
        pair = jnp.concatenate(columns[-2:], axis=0).astype(BF16)
        pair_keys = dot_nn(pair, feat_w[1]).astype(BF16).astype(F32)
        pair_values = dot_nn(pair, feat_w[2]).astype(BF16).astype(F32)
        for n in range(2):
            rows = slice(n * block_rows, (n + 1) * block_rows)
            key_list.append(pair_keys[rows])
            value_list.append(pair_values[rows])
            scores.append(
                feature_scores(own_query, pair_keys[rows], open_list[len(scores)], 1, table, scaling)
            )
    cotangent_copy.start()
    banks_gather.start_near()
    all_low = jnp.concatenate(columns, axis=0).astype(BF16)
    own_weights = softmax_of(scores)
    mixed = None
    for weight, column_values in zip(own_weights, value_list):
        added = dot_nn(weight.astype(BF16), wide) * column_values
        mixed = added if mixed is None else mixed + added
    feat_mixed = mixed.astype(BF16)
    feat_out_load.wait()
    feat_out_w = feat_out_ref[...].astype(BF16)
    first_sum = own + dot_nn(feat_mixed, feat_out_w).astype(BF16).astype(F32)
    unit_one, root_one = norm_parts(first_sum)
    first_out = unit_one * gains_ref[0:1, :] + shifts_ref[0:1, :]
    first_low = first_out.astype(BF16)
    gathered_ref[own_rows, :] = pack_columns(first_out, rows_dev).astype(BF16)
    hidden_gather.start()

    item_w = [proj_ref[3 + n].astype(BF16) for n in range(3)]
    turned_w = [jnp.transpose(proj_ref[4 + n]).astype(BF16) for n in range(2)]
    queries, own_keys, own_values = [
        dot_nn(first_low, weight).astype(BF16).astype(F32) for weight in item_w
    ]
    blocks_ref[...] = head_blocks(queries, head_dim)
    top_ref[...] = jnp.full(top_ref.shape, NEGATIVE, F32)
    sum_ref[...] = jnp.zeros(sum_ref.shape, F32)
    turned_ref[...] = jnp.zeros(turned_ref.shape, F32)

    def hidden_of(shard):
        rows = pl.ds(pl.multiple_of(shard * rows_dev, rows_dev), rows_dev)
        return stack_columns(gathered_ref[rows, :].astype(F32), width).astype(BF16)

    def open_rows(shape, shard_depth, shard_core):
        row = lax.broadcasted_iota(jnp.int32, shape, 0)
        row = row + jnp.where(row >= rows_dev, rows_dev, 0)
        return row < train_count - (shard_depth * 4 + shard_core) * rows_dev

    def masked_scores(keys, shard_depth, shard_core):
        raw = dot_nt(keys, blocks_ref[...]) * to_log2
        return jnp.where(open_rows(raw.shape, shard_depth, shard_core), raw, NEGATIVE)

    def attend(shard_depth, shard_core):
        @pl.when(shard_depth * 2 * block_rows < key_total)
        def _():
            shard = shard_depth * 2 + shard_core
            span = block_span(shard)
            hidden = hidden_of(shard)
            keys = dot_nn(hidden, item_w[1]).astype(BF16)
            values_ref[span, :] = dot_nn(hidden, item_w[2]).astype(BF16)
            keys_turned_ref[:, span] = dot_nt(turned_w[0], hidden).astype(BF16)
            values_turned = dot_nt(turned_w[1], hidden).astype(BF16)
            scores = masked_scores(keys, shard_depth, shard_core)
            scores_ref[span, :] = scores
            top_old = top_ref[...]
            top_new = jnp.maximum(top_old, jnp.max(scores, axis=0, keepdims=True))
            grown = jnp.exp2(scores - top_new)
            fade = jnp.exp2(top_old - top_new)
            top_ref[...] = top_new
            sum_ref[...] = sum_ref[...] * fade + jnp.sum(grown, axis=0, keepdims=True)
            turned_ref[...] = turned_ref[...] * fade + dot_nn(values_turned, grown.astype(BF16))

    hidden_gather.run(attend, 0)
    for k in range(1, rows_count // 4):
        banks_gather.along_depth(k)
    full = gather_heads_turned(turned_ref[...] / sum_ref[...], block_rows, head_dim)
    log_total = top_ref[...] + jnp.log2(sum_ref[...])

    item_low = full.astype(BF16)
    for load in later_loads:
        load.wait()
    item_out_w = item_out_ref[...].astype(BF16)
    mlp_in_w = mlp_in_ref[...].astype(BF16)
    mlp_out_w = mlp_out_ref[...].astype(BF16)
    unit_two, root_two = norm_parts(first_out + dot_nn(item_low, item_out_w))
    second_out = unit_two * gains_ref[1:2, :] + shifts_ref[1:2, :]
    second_low = second_out.astype(BF16)
    hidden_pre = dot_nn(second_low, mlp_in_w)
    normal = 0.5 + 0.5 * lax.erf(hidden_pre * (0.5**0.5))
    hidden_low = (hidden_pre * normal).astype(BF16)
    unit_three, root_three = norm_parts(second_out + dot_nt(hidden_low, mlp_out_w))
    third_out = unit_three * gains_ref[2:3, :] + shifts_ref[2:3, :]
    cotangent_copy.wait()
    own_part = quad.pick(cotangent, width, 0)
    other_part = cotangent_half_ref[...].astype(F32)
    incoming = jnp.concatenate(
        [
            jnp.where(quad.side == 0, own_part, other_part),
            jnp.where(quad.side == 0, other_part, own_part),
        ],
        axis=0,
    )
    third_grad, gain_three, shift_three = norm_back(
        unit_three, root_three, gains_ref[2:3, :], incoming
    )
    branch_low = third_grad.astype(BF16)
    density = jnp.exp(-0.5 * hidden_pre * hidden_pre) * (1.0 / math.sqrt(2.0 * math.pi))
    pre_low = (dot_nn(branch_low, mlp_out_w) * (normal + hidden_pre * density)).astype(BF16)
    second_grad, gain_two, shift_two = norm_back(
        unit_two, root_two, gains_ref[1:2, :], third_grad + dot_nt(pre_low, mlp_in_w)
    )
    second_grad_low = second_grad.astype(BF16)
    mixed_grad = dot_nt(second_grad_low, item_out_w).astype(BF16).astype(F32)
    part = head_rows_of(mixed_grad * full, wide)[0:8, :]
    delta = jnp.concatenate([part[h : h + 1] for h in range(HEADS)], axis=1)
    totals = [log_total[:, h * block_rows : (h + 1) * block_rows] for h in range(HEADS)]
    spare = jnp.zeros((8 - HEADS, block_rows), F32)
    own_span = block_span(own_shard)
    all_stats_ref[0:8, own_span] = jnp.concatenate(totals + [spare], axis=0)
    all_stats_ref[8:16, own_span] = part
    grads_ref[own_rows, :] = pack_columns(mixed_grad, rows_dev).astype(BF16)
    grads_gather.start()

    row = put_tiles(mlp_part_ref, 0, dot_tn(second_low, pre_low))
    row = put_tiles(mlp_part_ref, row, dot_tn(branch_low, hidden_low))
    row = put_tiles(mlp_part_ref, row, dot_tn(item_low, second_grad_low))
    put_zeros(mlp_part_ref, row)
    mlp_sum.scatter_start(0)
    first_block, second_block = third_out[:rows_dev], third_out[rows_dev:]
    layer_half_ref[...] = jnp.where(quad.side == 0, second_block, first_block).astype(BF16)
    own_layer = jnp.where(quad.side == 0, first_block, second_block)

    grad_blocks_ref[...] = head_blocks(mixed_grad, head_dim)
    turned_ref[...] = jnp.zeros(turned_ref.shape, F32)
    key_steps = key_total // block_rows

    @pl.loop(0, key_steps, unroll=2)
    def _(step):
        span = block_span(step)
        attend_now = jnp.exp2(scores_ref[span, :] - log_total)
        dots = dot_nt(values_ref[span, :], grad_blocks_ref[...])
        score_grad = (attend_now * (dots - delta)).astype(BF16)
        turned_ref[...] += dot_nn(keys_turned_ref[:, span], score_grad)

    mlp_sum.scatter_finish(0)
    mlp_sum.scatter_start(1)
    query_grad = gather_heads_turned(turned_ref[...], block_rows, head_dim) * scaling

    blocks_ref[...] = head_blocks(own_keys, head_dim)
    grad_blocks_ref[...] = head_blocks(own_values, head_dim)
    total_ref[...] = jnp.zeros(total_ref.shape, F32)
    value_total_ref[...] = jnp.zeros(value_total_ref.shape, F32)

    def answer(shard_depth, shard_core):
        shard = shard_depth * 2 + shard_core
        span = block_span(shard)
        asked = dot_nn(hidden_of(shard), item_w[0]).astype(BF16)
        rows = pl.ds(pl.multiple_of(shard * rows_dev, rows_dev), rows_dev)
        grads = stack_columns(grads_ref[rows, :].astype(F32), width).astype(BF16)
        scores = dot_nt(blocks_ref[...], asked) * to_log2
        dots = dot_nt(grad_blocks_ref[...], grads)
        attends, score_grads = [], []
        for head in range(HEADS):
            part = slice(head * block_rows, (head + 1) * block_rows)
            attend_now = jnp.exp2(scores[part] - all_stats_ref[head : head + 1, span])
            attends.append(attend_now.astype(BF16))
            score_grads.append(
                (attend_now * (dots[part] - all_stats_ref[8 + head : 9 + head, span])).astype(BF16)
            )
        total_ref[...] += dot_nn(jnp.concatenate(score_grads, axis=0), asked)
        value_total_ref[...] += dot_nn(jnp.concatenate(attends, axis=0), grads)

    grads_gather.run(answer, 0)
    layer_copy = quad.across(layer_half_ref, layer_land_ref, side_sem.at[2])
    layer_copy.start()
    mlp_sum.scatter_finish(1)
    mlp_sum.share_start()

    own_open = open_rows((block_rows, width), depth, core)
    key_grad = gather_heads(total_ref[...], block_rows, head_dim) * scaling
    value_grad = gather_heads(value_total_ref[...], block_rows, head_dim)
    item_grads = [
        query_grad.astype(BF16),
        jnp.where(own_open, key_grad, 0.0).astype(BF16),
        jnp.where(own_open, value_grad, 0.0).astype(BF16),
    ]
    first_grad = second_grad
    for n in range(3):
        first_grad = first_grad + dot_nt(item_grads[n], item_w[n])
    first_in_grad, gain_one, shift_one = norm_back(
        unit_one, root_one, gains_ref[0:1, :], first_grad
    )
    branch_ref[...] = pack_columns(first_in_grad, rows_dev).astype(BF16)
    branch_copies = quad.spread(branch_ref, quad_branch_ref, quad_sem.at[1])
    for copy in branch_copies:
        copy.start()

    own_branch = first_in_grad.astype(BF16)
    row = put_tiles(
        item_part_ref,
        0,
        jnp.concatenate([dot_tn(first_low, item_grads[n]) for n in range(2)], axis=1),
    )
    row = put_tiles(
        item_part_ref,
        row,
        jnp.concatenate(
            [dot_tn(first_low, item_grads[2]), dot_tn(feat_mixed, own_branch)], axis=1
        ),
    )
    pairs = [
        jnp.concatenate(pair, axis=1)
        for pair in ((gain_one, shift_one), (gain_two, shift_two), (gain_three, shift_three))
    ]
    row = put_tiles(
        item_part_ref, row, jnp.concatenate(pairs + [jnp.zeros((13, 2 * width), F32)], axis=0)
    )
    put_zeros(item_part_ref, row)
    item_sum.scatter_start(0)

    other_query = dot_nn(all_low[block_rows:], feat_w[0]).astype(BF16).astype(F32)
    others = slots - 1
    other_weights = softmax_of(
        [
            feature_scores(other_query, keys, is_open, others, table, scaling)
            for keys, is_open in zip(key_list, open_list)
        ]
    )
    own_feat_grad = dot_nt(own_branch, feat_out_w).astype(BF16).astype(F32)

    def minus_mean(weights, dots):
        row_delta = None
        for weight, dot in zip(weights, dots):
            added = weight * dot
            row_delta = added if row_delta is None else row_delta + added
        return [dot - row_delta for dot in dots]

    own_dots = minus_mean(
        own_weights, [head_sums(own_feat_grad * part, table) for part in value_list]
    )
    own_score_grads = [
        (weight * dot).astype(BF16) for weight, dot in zip(own_weights, own_dots)
    ]
    feat_query_grad = None
    for score_grad, part in zip(own_score_grads, key_list):
        added = dot_nn(score_grad, wide) * part
        feat_query_grad = added if feat_query_grad is None else feat_query_grad + added
    item_sum.scatter_finish(0)
    item_sum.scatter_start(1)
    mlp_sum.share_finish()
    mlp_sum.gather_start(1)
    feat_key_grad = dot_nn(own_score_grads[0], wide) * own_query
    feat_value_grad = dot_nn(own_weights[0].astype(BF16), wide) * own_feat_grad
    for n, pattern in enumerate((1, 2, 3)):
        branch_copies[pattern - 1].wait()
        rows = slice(n * block_rows, (n + 1) * block_rows)
        branch = stack_columns(quad_branch_ref[quad.number(pattern)].astype(F32), width)
        grad = dot_nt(branch.astype(BF16), feat_out_w).astype(BF16).astype(F32)
        part_weights = [weight[rows] for weight in other_weights]
        part_dots = minus_mean(part_weights, [head_sums(grad * part, table) for part in value_list])
        score_grad = (part_weights[0] * part_dots[0]).astype(BF16)
        feat_key_grad = feat_key_grad + dot_nn(score_grad, wide) * other_query[rows]
        feat_value_grad = feat_value_grad + dot_nn(part_weights[0].astype(BF16), wide) * grad
    feat_grads = [
        (feat_query_grad * scaling).astype(BF16),
        (feat_key_grad * scaling).astype(BF16),
        feat_value_grad.astype(BF16),
    ]
    row = put_tiles(
        feat_part_ref,
        0,
        jnp.concatenate([dot_tn(own_low, feat_grads[n]) for n in range(2)], axis=1),
    )
    row = put_tiles(feat_part_ref, row, dot_tn(own_low, feat_grads[2]))
    put_zeros(feat_part_ref, row)
    feat_sum.scatter_start(0)
    item_sum.scatter_finish(1)
    item_sum.share_start()
    feat_sum.scatter_finish(0)
    feat_sum.scatter_start(1)
    mlp_sum.gather_finish(1)
    mlp_sum.gather_start(0)
    for k in range(rows_count // 4):
        banks_gather.across_side(k)
    inner = None
    for n in range(3):
        added = dot_nt(feat_grads[n], feat_w[n])
        inner = added if inner is None else inner + added
    cells_grad = first_in_grad + inner.astype(BF16).astype(F32)
    first_block, second_block = cells_grad[:rows_dev], cells_grad[rows_dev:]
    grad_half_ref[...] = jnp.where(quad.side == 0, second_block, first_block)
    own_cells_grad = jnp.where(quad.side == 0, first_block, second_block)
    grad_copy = quad.across(grad_half_ref, grad_land_ref, side_sem.at[3])
    layer_copy.wait()
    layer_ref[...] = quad.joined(own_layer, layer_land_ref[...].astype(F32)).astype(BF16)
    results = [mover.start(layer_ref, layer_out)]
    feat_sum.scatter_finish(1)
    feat_sum.share_start()
    item_sum.share_finish()
    item_sum.gather_start(1)
    grad_copy.start()
    for k in range(rows_count // 4):
        banks_gather.from_core(k, 0)
        banks_gather.from_core(k, 1)
    sort_rows = sorted_ref.shape[0]
    sort_block = math.gcd(sort_rows, 256)
    owner = owner_ref[...].reshape(1, sort_rows)

    def sort_some(first, last):
        @pl.loop(first, last)
        def _(step):
            start = pl.multiple_of(step * sort_block, sort_block)
            row = start + lax.broadcasted_iota(jnp.int32, (sort_block, sort_rows), 0)
            chosen = jnp.where(owner == row, 1.0, 0.0).astype(BF16)
            sorted_ref[pl.ds(start, sort_block), :] = dot_nn(chosen, banks_ref[...]).astype(BF16)

    sort_steps = sort_rows // sort_block
    most, nearly = 5 * sort_steps // 9, 8 * sort_steps // 9
    sort_some(0, most)
    feat_sum.share_finish()
    feat_sum.gather_start(1)
    item_sum.gather_finish(1)
    item_sum.gather_start(0)
    sort_some(most, nearly)
    feat_sum.gather_finish(1)
    feat_sum.gather_start(0)
    grad_copy.wait()
    cells_grad_ref[...] = quad.joined(own_cells_grad, grad_land_ref[...])
    results.append(mover.start(cells_grad_ref, cells_grad_out))
    sort_some(nearly, sort_steps)
    results.append(mover.start(sorted_ref, sorted_out))
    mlp_sum.gather_finish(0)
    item_sum.gather_finish(0)
    for gather in (hidden_gather, grads_gather, banks_gather):
        gather.wait_sent()
    for result in results:
        result.wait()
    feat_sum.gather_finish(0)


def moment_rule(gradient, first_old, second_old):
    first_new = BETA_ONE * first_old + (1.0 - BETA_ONE) * gradient
    second_new = BETA_TWO * second_old + (1.0 - BETA_TWO) * gradient * gradient
    first_hat = first_new * (1.0 / (1.0 - BETA_ONE**STEP))
    second_hat = second_new * (1.0 / (1.0 - BETA_TWO**STEP))
    return first_new, second_new, first_hat / (jnp.sqrt(second_hat) + EPSILON)


def root_mean(value):
    count = value.shape[0] * value.shape[1]
    square = jnp.sum(jnp.sum(value * value, axis=1, keepdims=True), axis=0, keepdims=True)
    return jnp.sqrt(square * (1.0 / count) + 1e-06)


def update_kernel(
    owner_ref,
    mlp_sum_ref,
    item_sum_ref,
    feat_sum_ref,
    gains_ref,
    shifts_ref,
    norm_first_ref,
    norm_second_ref,
    first_ref,
    second_ref,
    layer_in,
    cells_grad_in,
    small_in,
    big_in,
    sorted_in,
    proj_in,
    feat_out_in,
    item_out_in,
    mlp_in_in,
    mlp_out_in,
    layer_out,
    cells_grad_out,
    square_grad_out,
    in_grad_out,
    out_grad_out,
    norm_grad_ref,
    clip_ref,
    first_new_ref,
    second_new_ref,
    square_new_out,
    in_new_out,
    out_new_out,
    square_low_out,
    in_low_out,
    out_low_out,
    norm_new_ref,
    norm_first_new_ref,
    norm_second_new_ref,
    small_ref,
    big_ref,
    sorted_ref,
    olds_ref,
    mlp_in_ref,
    mlp_out_ref,
    square_grad_ref,
    in_grad_ref,
    out_grad_ref,
    square_new_ref,
    in_new_ref,
    out_new_ref,
    square_low_ref,
    in_low_ref,
    out_low_ref,
    rotated_ref,
    own_ref,
    move_sem,
):
    width, ff_width = mlp_in_ref.shape
    slots = first_ref.shape[0]
    squares = square_grad_ref.shape[0]
    mover = Mover(move_sem)
    small_loads = [
        (
            mover.start(small_in.at[n], small_ref.at[n]),
            mover.start(small_in.at[squares + n], small_ref.at[squares + n]),
        )
        for n in range(squares)
    ]
    last_loads = [
        mover.start(small_in.at[2 * squares], small_ref.at[2 * squares]),
        mover.start(small_in.at[2 * squares + 1], small_ref.at[2 * squares + 1]),
        mover.start(big_in, big_ref),
    ]
    sorted_load = mover.start(sorted_in, sorted_ref)
    old_loads = [
        mover.start(proj_in, olds_ref.at[0 : squares - 2]),
        mover.start(feat_out_in, olds_ref.at[squares - 2]),
        mover.start(item_out_in, olds_ref.at[squares - 1]),
    ]
    mlp_loads = [mover.start(mlp_in_in, mlp_in_ref), mover.start(mlp_out_in, mlp_out_ref)]
    results = [mover.start(layer_in, layer_out), mover.start(cells_grad_in, cells_grad_out)]

    square = None
    for part_ref in (mlp_sum_ref, item_sum_ref, feat_sum_ref):
        part = part_ref[...].astype(F32)
        added = jnp.sum(jnp.sum(part * part, axis=1, keepdims=True), axis=0, keepdims=True)
        square = added if square is None else square + added
    grad_norm = jnp.sqrt(square)
    factor = jnp.minimum(1.0, CLIP_NORM / grad_norm)
    clip_ref[0] = grad_norm[0, 0]
    both_width = 2 * width
    both_tiles = both_width // LANES * width
    feat_pair = take_tiles(feat_sum_ref, 0, width, both_width) * factor
    item_pair = take_tiles(item_sum_ref, 0, width, both_width) * factor
    mixed_pair = take_tiles(item_sum_ref, both_tiles, width, both_width) * factor
    parts = [
        feat_pair[:, :width],
        feat_pair[:, width:],
        take_tiles(feat_sum_ref, both_tiles, width, width) * factor,
        item_pair[:, :width],
        item_pair[:, width:],
        mixed_pair[:, :width],
        mixed_pair[:, width:],
        take_tiles(mlp_sum_ref, 2 * both_tiles, width, width) * factor,
    ]
    for n, clipped in enumerate(parts):
        square_grad_ref[n] = clipped
        for load in small_loads[n]:
            load.wait()
        turned = dot_low(dot_nn, clipped, small_ref[squares + n])
        rotated_ref[n * width : (n + 1) * width, :] = dot_low(dot_tn, small_ref[n], turned)
    results.append(mover.start(square_grad_ref, square_grad_out))
    start = squares * width
    middle = start + ff_width
    for load in last_loads:
        load.wait()
    clipped = take_tiles(mlp_sum_ref, 0, width, ff_width) * factor
    in_grad_ref[...] = clipped
    results.append(mover.start(in_grad_ref, in_grad_out))
    turned = dot_low(dot_tn, clipped, small_ref[2 * squares])
    rotated_ref[start:middle, :] = dot_low(dot_tn, big_ref[0], turned)
    clipped = take_tiles(mlp_sum_ref, both_tiles, width, ff_width) * factor
    out_grad_ref[...] = clipped
    results.append(mover.start(out_grad_ref, out_grad_out))
    turned = dot_low(dot_tn, clipped, small_ref[2 * squares + 1])
    rotated_ref[middle : middle + ff_width, :] = dot_low(dot_tn, big_ref[1], turned)

    def step_of(first_row, count):
        rows = slice(first_row, first_row + count)
        banks = sorted_ref[rows, :].astype(F32)
        return moment_rule(rotated_ref[rows, :], banks[:, :width], banks[:, width:])[2]

    sorted_load.wait()
    for load in old_loads:
        load.wait()
    for n in range(squares):
        turned = dot_low(dot_nt, step_of(n * width, width), small_ref[squares + n])
        update = dot_low(dot_nn, small_ref[n], turned)
        old = olds_ref[n]
        new = old - LEARN_RATE * root_mean(old) * update
        square_new_ref[n] = new
        square_low_ref[n] = new.astype(BF16)
        results.append(mover.start(square_new_ref.at[n], square_new_out.at[n]))
    results.append(mover.start(square_low_ref, square_low_out))
    for load in mlp_loads:
        load.wait()
    turned = dot_low(dot_nn, big_ref[0], step_of(start, ff_width))
    update = dot_low(dot_nt, small_ref[2 * squares], turned)
    new = mlp_in_ref[...] - LEARN_RATE * root_mean(mlp_in_ref[...]) * update
    in_new_ref[...] = new
    in_low_ref[...] = new.astype(BF16)
    results.append(mover.start(in_new_ref, in_new_out))
    results.append(mover.start(in_low_ref, in_low_out))
    turned = dot_low(dot_nn, big_ref[1], step_of(middle, ff_width))
    update = dot_low(dot_nt, small_ref[2 * squares + 1], turned)
    new = mlp_out_ref[...] - LEARN_RATE * root_mean(mlp_out_ref[...]) * update
    out_new_ref[...] = new
    out_low_ref[...] = new.astype(BF16)
    results.append(mover.start(out_new_ref, out_new_out))
    results.append(mover.start(out_low_ref, out_low_out))

    base = lax.axis_index("rows") * slots

    @pl.loop(0, slots // 8)
    def _(step):
        for n in range(8):
            row = owner_ref[base + step * 8 + n]
            own_ref[pl.ds(step * 8 + n, 1), :] = rotated_ref[pl.ds(row, 1), :]

    first_new, second_new, _ = moment_rule(own_ref[...], first_ref[...], second_ref[...])
    first_new_ref[...] = first_new
    second_new_ref[...] = second_new

    norm_pairs = take_tiles(item_sum_ref, 2 * both_tiles, 16, both_width) * factor
    for n in range(3):
        pair = norm_pairs[n : n + 1]
        both = jnp.concatenate([pair[:, :width], pair[:, width:]], axis=0)
        norm_grad_ref[n] = both
        first_new, second_new, change = moment_rule(both, norm_first_ref[n], norm_second_ref[n])
        norm_first_new_ref[n] = first_new
        norm_second_new_ref[n] = second_new
        old = jnp.concatenate([gains_ref[n : n + 1, :], shifts_ref[n : n + 1, :]], axis=0)
        size = jnp.sqrt(jnp.sum(old * old, axis=1, keepdims=True) * (1.0 / width) + 1e-06)
        norm_new_ref[n] = old - LEARN_RATE * size * change
    for result in results:
        result.wait()


def in_vmem():
    return pl.BlockSpec(memory_space=pltpu.VMEM)


def anywhere():
    return pl.BlockSpec(memory_space=pl.ANY)


def in_smem():
    return pl.BlockSpec(memory_space=pltpu.SMEM)


def fast_device(
    cells,
    feat_mask,
    train_rows,
    cotangent,
    proj_weights,
    feat_out_w,
    item_out_w,
    mlp_in,
    mlp_out,
    norm_gains,
    norm_shifts,
    bases_small,
    bases_big,
    owner_rows,
    bank_first,
    bank_second,
    norm_first,
    norm_second,
):
    rows_count, cols_count = lax.axis_size("rows"), lax.axis_size("cols")
    rows_dev, width_dev = cells.shape
    width = proj_weights.shape[-1]
    ff_width = mlp_in.shape[1]
    rows_all = rows_dev * rows_count
    key_total = rows_all // 4 * 3
    head_rows = HEADS * 2 * rows_dev
    dma = pltpu.SemaphoreType.DMA
    shape = jax.ShapeDtypeStruct
    sizes = {"z": rows_count // 4, "x": 2, "k": 2, "y": cols_count}

    mask_rows = feat_mask.T
    mlp_out_turned = mlp_out.T
    norm_first_turned = jnp.transpose(norm_first, (1, 0, 2))
    norm_second_turned = jnp.transpose(norm_second, (1, 0, 2))
    bank_rows = owner_rows.shape[0]

    def block_rows(rows):
        unit = 16 * math.prod(members(stage, sizes) for stage in STAGES[:-1])
        return -(-rows // unit) * unit

    def landings(rows):
        found = []
        for stage in STAGES[:-1]:
            count = members(stage, sizes)
            rows //= count
            found.append(pltpu.VMEM((count - 1, rows, LANES), BF16))
        return found + [pltpu.VMEM((members(STAGES[-1], sizes), rows, LANES), BF16)]

    both_tiles = 2 * width // LANES * width
    half_tiles = -(-width // LANES) * width
    sum_rows = [
        block_rows(2 * (ff_width // LANES) * width + half_tiles),
        block_rows(2 * both_tiles + 2 * width // LANES * 16),
        block_rows(both_tiles + half_tiles),
    ]
    widest = max(members(stage, sizes) for stage in STAGES) - 1
    layer_part, cells_part, mlp_total, item_total, feat_total, sorted_banks = pl.pallas_call(
        functools.partial(layer_kernel, rows_count, cols_count),
        name="layer_and_gradients",
        out_shape=(
            shape((rows_dev, width_dev), BF16),
            shape((rows_dev, width_dev), F32),
            *[shape((rows, LANES), BF16) for rows in sum_rows],
            shape((bank_rows, 2 * width), BF16),
        ),
        in_specs=[in_smem()] + [in_vmem()] * 5 + [anywhere()] * 8,
        out_specs=[anywhere()] * 2 + [in_vmem()] * 3 + [anywhere()],
        scratch_shapes=[
            pltpu.VMEM(proj_weights.shape, F32),
            pltpu.VMEM(feat_out_w.shape, F32),
            pltpu.VMEM(bank_first.shape, F32),
            pltpu.VMEM(bank_first.shape, F32),
            pltpu.VMEM(item_out_w.shape, F32),
            pltpu.VMEM(mlp_in.shape, F32),
            pltpu.VMEM(mlp_in.shape, F32),
            pltpu.VMEM((rows_dev, width_dev), BF16),
            pltpu.VMEM((rows_dev, width_dev), BF16),
            pltpu.VMEM((rows_dev, width_dev), F32),
            pltpu.VMEM((bank_rows, 2 * width), BF16),
            pltpu.VMEM((4, rows_dev, width_dev), BF16),
            pltpu.VMEM((2,) + mask_rows.shape, jnp.int32),
            pltpu.VMEM((rows_dev, width), BF16),
            pltpu.VMEM((rows_dev, width), BF16),
            pltpu.VMEM((rows_dev, width), BF16),
            pltpu.VMEM((rows_dev, width), BF16),
            pltpu.VMEM((rows_dev, width), F32),
            pltpu.VMEM((rows_dev, width), F32),
            pltpu.VMEM((rows_all // 2, width_dev), BF16),
            pltpu.VMEM((width, key_total), BF16),
            pltpu.VMEM((key_total, width), BF16),
            pltpu.VMEM((rows_all // 2, width_dev), BF16),
            pltpu.VMEM((16, rows_all), F32),
            pltpu.VMEM((bank_rows, 2 * width), BF16),
            pltpu.VMEM((head_rows, width), BF16),
            pltpu.VMEM((head_rows, width), BF16),
            pltpu.VMEM((key_total, head_rows), F32),
            pltpu.VMEM((1, head_rows), F32),
            pltpu.VMEM((1, head_rows), F32),
            pltpu.VMEM((width, head_rows), F32),
            pltpu.VMEM((head_rows, width), F32),
            pltpu.VMEM((head_rows, width), F32),
            pltpu.VMEM((rows_dev, width_dev), BF16),
            pltpu.VMEM((4, rows_dev, width_dev), BF16),
        ]
        + [pltpu.VMEM((rows, LANES), BF16) for rows in sum_rows]
        + [landing for rows in sum_rows for landing in landings(rows)]
        + [
            dma((2, 2, 3)),
            dma((4, 2)),
            dma((2, 1, DepthGather.slots(rows_count))),
            dma((2, 2, DepthGather.slots(rows_count))),
            dma((2, 1, RowGather.slots(rows_count))),
        ]
        + [dma((4, len(STAGES), widest))] * len(sum_rows)
        + [dma((11,))],
        compiler_params=pltpu.CompilerParams(
            collective_id=0, has_side_effects=True, vmem_limit_bytes=VMEM_BYTES
        ),
    )(
        train_rows,
        owner_rows,
        cells,
        mask_rows,
        norm_gains,
        norm_shifts,
        proj_weights,
        feat_out_w,
        bank_first,
        bank_second,
        item_out_w,
        mlp_in,
        mlp_out_turned,
        cotangent,
    )

    slots_dev = bank_first.shape[0]
    square = (8, width, width)
    (
        layer_out,
        cells_grad,
        square_grads,
        in_grad,
        out_grad,
        norm_grads,
        clip_norm,
        first_new,
        second_new,
        square_new,
        in_new,
        out_new,
        square_low,
        in_low,
        out_low,
        norm_new,
        norm_first_new,
        norm_second_new,
    ) = pl.pallas_call(
        update_kernel,
        name="rotated_update",
        out_shape=(
            shape(layer_part.shape, BF16),
            shape(cells_part.shape, F32),
            shape(square, F32),
            shape(mlp_in.shape, F32),
            shape(mlp_in.shape, F32),
            shape(norm_first_turned.shape, F32),
            shape((1,), F32),
            shape(bank_first.shape, F32),
            shape(bank_first.shape, F32),
            shape(square, F32),
            shape(mlp_in.shape, F32),
            shape(mlp_in.shape, F32),
            shape(square, BF16),
            shape(mlp_in.shape, BF16),
            shape(mlp_in.shape, BF16),
            shape(norm_first_turned.shape, F32),
            shape(norm_first_turned.shape, F32),
            shape(norm_first_turned.shape, F32),
        ),
        in_specs=[in_smem()] + [in_vmem()] * 11 + [anywhere()] * 8,
        out_specs=[anywhere()] * 5
        + [in_vmem(), in_smem(), in_vmem(), in_vmem()]
        + [anywhere()] * 6
        + [in_vmem()] * 3,
        scratch_shapes=[
            pltpu.VMEM(bases_small.shape, F32),
            pltpu.VMEM(bases_big.shape, F32),
            pltpu.VMEM(sorted_banks.shape, BF16),
            pltpu.VMEM(square, F32),
            pltpu.VMEM(mlp_in.shape, F32),
            pltpu.VMEM(mlp_in.shape, F32),
            pltpu.VMEM(square, F32),
            pltpu.VMEM(mlp_in.shape, F32),
            pltpu.VMEM(mlp_in.shape, F32),
            pltpu.VMEM(square, F32),
            pltpu.VMEM(mlp_in.shape, F32),
            pltpu.VMEM(mlp_in.shape, F32),
            pltpu.VMEM(square, BF16),
            pltpu.VMEM(mlp_in.shape, BF16),
            pltpu.VMEM(mlp_in.shape, BF16),
            pltpu.VMEM((bank_rows, width), F32),
            pltpu.VMEM((slots_dev, width), F32),
            dma((48,)),
        ],
        compiler_params=pltpu.CompilerParams(vmem_limit_bytes=VMEM_BYTES),
    )(
        owner_rows,
        mlp_total,
        item_total,
        feat_total,
        norm_gains,
        norm_shifts,
        norm_first_turned,
        norm_second_turned,
        bank_first,
        bank_second,
        layer_part,
        cells_part,
        bases_small,
        bases_big,
        sorted_banks,
        proj_weights,
        feat_out_w,
        item_out_w,
        mlp_in,
        mlp_out_turned,
    )
    return (
        layer_out,
        cells_grad,
        square_grads,
        in_grad,
        out_grad.T,
        jnp.transpose(norm_grads, (1, 0, 2)),
        clip_norm,
        first_new,
        second_new,
        square_new,
        in_new,
        out_new.T,
        square_low,
        in_low,
        out_low.T,
        jnp.transpose(norm_new, (1, 0, 2)),
        jnp.transpose(norm_first_new, (1, 0, 2)),
        jnp.transpose(norm_second_new, (1, 0, 2)),
    )


def solution(mesh):
    in_specs = (
        P("rows", "cols"),
        P("rows", None),
        P(),
        P("rows", "cols"),
        P(),
        P(),
        P(),
        P(),
        P(),
        P(),
        P(),
        P(),
        P(),
        P(),
        P("rows", None),
        P("rows", None),
        P(),
        P(),
    )
    out_specs = (
        P("rows", "cols"),
        P("rows", "cols"),
        P(),
        P(),
        P(),
        P(),
        P(),
        P("rows", None),
        P("rows", None),
        P(),
        P(),
        P(),
        P(),
        P(),
        P(),
        P(),
        P(),
        P(),
    )
    small = mesh.shape["rows"] == 16 and mesh.shape["cols"] == 2
    return jax.shard_map(
        fast_device if small else per_device, mesh=mesh, in_specs=in_specs, out_specs=out_specs, check_vma=False
    )
```

```python
import functools
import math

import jax
import jax.numpy as jnp
from jax import lax
from jax.experimental import pallas as pl
from jax.experimental.pallas import tpu as pltpu
from jax.sharding import PartitionSpec as P

HEADS = 6
STEP = 10


HIGHEST = lax.Precision.HIGHEST
NEGATIVE = -1e30
CLIP_NORM = 1.0
BETA_ONE = 0.9
BETA_TWO = 0.95
EPSILON = 1e-08
LEARN_RATE = 1.0


def layer_norm(hidden, gain_row, shift_row):
    center = jnp.mean(hidden, axis=-1, keepdims=True)
    centered = hidden - center
    spread = jnp.mean(centered * centered, axis=-1, keepdims=True)
    return centered * lax.rsqrt(spread + 1e-05) * gain_row + shift_row


def gelu_exact(hidden):
    return jax.nn.gelu(hidden, approximate=False)


def product(left_side, right_side):
    return jnp.dot(left_side, right_side, preferred_element_type=jnp.float32)


def product_left(left_side, right_side):
    return lax.dot_general(
        left_side, right_side, (((0,), (0,)), ((), ())), preferred_element_type=jnp.float32
    )


def product_right(left_side, right_side):
    return lax.dot_general(
        left_side, right_side, (((1,), (1,)), ((), ())), preferred_element_type=jnp.float32
    )


def feature_forward(queries, key_rows, value_rows, key_open):
    scaling = queries.shape[-1] ** (-0.5)
    scores = (
        jnp.einsum("nqhe,nkhe->nhqk", queries, key_rows, preferred_element_type=jnp.float32)
        * scaling
    )
    scores = jnp.where(key_open[:, None, None, :], scores, NEGATIVE)
    attend = jax.nn.softmax(scores, axis=-1)
    attend_low = attend.astype(jnp.bfloat16)
    mixed = jnp.einsum(
        "nhqk,nkhe->nqhe", attend_low, value_rows, preferred_element_type=jnp.float32
    )
    return (attend, attend_low, mixed.astype(jnp.bfloat16))


def feature_backward(queries, key_rows, value_rows, attend, attend_low, mixed_grad):
    scaling = queries.shape[-1] ** (-0.5)
    value_dots = jnp.einsum(
        "nqhe,nkhe->nhqk", mixed_grad, value_rows, preferred_element_type=jnp.float32
    )
    row_delta = jnp.sum(attend * value_dots, axis=-1, keepdims=True)
    score_grad = (attend * (value_dots - row_delta)).astype(jnp.bfloat16)
    query_grad = (
        jnp.einsum("nhqk,nkhe->nqhe", score_grad, key_rows, preferred_element_type=jnp.float32)
        * scaling
    )
    key_grad = (
        jnp.einsum("nhqk,nqhe->nkhe", score_grad, queries, preferred_element_type=jnp.float32)
        * scaling
    )
    value_grad = jnp.einsum(
        "nhqk,nqhe->nkhe", attend_low, mixed_grad, preferred_element_type=jnp.float32
    )
    return (
        query_grad.astype(jnp.bfloat16),
        key_grad.astype(jnp.bfloat16),
        value_grad.astype(jnp.bfloat16),
    )


def key_blocks_of(key_rows, value_rows):
    key_total = key_rows.shape[0]
    block_size = math.gcd(key_total, 1024)
    block_count = key_total // block_size
    tail_shape = key_rows.shape[1:]
    starts = jnp.arange(block_count, dtype=jnp.int32) * block_size
    return (
        key_rows.reshape((block_count, block_size) + tail_shape),
        value_rows.reshape((block_count, block_size) + tail_shape),
        starts,
    )


def block_scores(queries, key_block, start_row, train_count):
    scaling = queries.shape[-1] ** (-0.5)
    scores = (
        jnp.einsum("qche,kche->chqk", queries, key_block, preferred_element_type=jnp.float32)
        * scaling
    )
    open_keys = start_row + jnp.arange(key_block.shape[0], dtype=jnp.int32) < train_count
    return jnp.where(open_keys[None, None, None, :], scores, NEGATIVE)


def item_forward(queries, key_rows, value_rows, train_count):
    key_split, value_split, starts = key_blocks_of(key_rows, value_rows)
    stat_shape = (queries.shape[1], queries.shape[2], queries.shape[0])

    def max_pass(carried, packed):
        running_max, running_sum = carried
        key_block, start_row = packed
        scores = block_scores(queries, key_block, start_row, train_count)
        new_max = jnp.maximum(running_max, jnp.max(scores, axis=-1))
        running_sum = running_sum * jnp.exp(running_max - new_max) + jnp.sum(
            jnp.exp(scores - new_max[..., None]), axis=-1
        )
        return ((new_max, running_sum), None)

    start_max = jnp.full(stat_shape, NEGATIVE, jnp.float32)
    (row_max, row_sum), _ = lax.scan(
        max_pass, (start_max, jnp.zeros(stat_shape, jnp.float32)), (key_split, starts)
    )
    log_total = row_max + jnp.log(row_sum)

    def value_pass(carried, packed):
        key_block, value_block, start_row = packed
        attend = jnp.exp(
            block_scores(queries, key_block, start_row, train_count) - log_total[..., None]
        )
        added = jnp.einsum(
            "chqk,kche->qche",
            attend.astype(jnp.bfloat16),
            value_block,
            preferred_element_type=jnp.float32,
        )
        return (carried + added, None)

    item_full, _ = lax.scan(
        value_pass, jnp.zeros(queries.shape, jnp.float32), (key_split, value_split, starts)
    )
    return (log_total, item_full)


def delta_of(mixed_grad, item_full):
    return jnp.transpose(jnp.sum(mixed_grad.astype(jnp.float32) * item_full, axis=-1), (1, 2, 0))


def item_backward(queries, key_rows, value_rows, train_count, log_total, mixed_grad, item_full):
    key_split, value_split, starts = key_blocks_of(key_rows, value_rows)
    scaling = queries.shape[-1] ** (-0.5)
    row_delta = delta_of(mixed_grad, item_full)

    def back_pass(carried, packed):
        key_block, value_block, start_row = packed
        attend = jnp.exp(
            block_scores(queries, key_block, start_row, train_count) - log_total[..., None]
        )
        value_dots = jnp.einsum(
            "qche,kche->chqk", mixed_grad, value_block, preferred_element_type=jnp.float32
        )
        score_grad = (attend * (value_dots - row_delta[..., None])).astype(jnp.bfloat16)
        carried = carried + jnp.einsum(
            "chqk,kche->qche", score_grad, key_block, preferred_element_type=jnp.float32
        )
        key_grad = (
            jnp.einsum("chqk,qche->kche", score_grad, queries, preferred_element_type=jnp.float32)
            * scaling
        )
        value_grad = jnp.einsum(
            "chqk,qche->kche",
            attend.astype(jnp.bfloat16),
            mixed_grad,
            preferred_element_type=jnp.float32,
        )
        return (carried, (key_grad, value_grad))

    query_sum, (key_grads, value_grads) = lax.scan(
        back_pass, jnp.zeros(queries.shape, jnp.float32), (key_split, value_split, starts)
    )
    key_total = key_rows.shape[0]
    flat_width = queries.shape[1] * queries.shape[2] * queries.shape[3]
    return (
        query_sum * scaling,
        key_grads.reshape(key_total, flat_width),
        value_grads.reshape(key_total, flat_width),
    )


def clip_all(gradients):
    total_sq = jnp.sum(gradients[0] * gradients[0])
    for extra in gradients[1:]:
        total_sq = total_sq + jnp.sum(extra * extra)
    grad_norm = jnp.sqrt(total_sq)
    factor = jnp.minimum(1.0, CLIP_NORM / grad_norm)
    return ([gradient * factor for gradient in gradients], grad_norm)


def rotate_bank(square_grad, in_grad, out_grad, bases_small, bases_big):
    model_width = in_grad.shape[0]
    left_bases = bases_small[0:8]
    right_bases = bases_small[8:16]
    rot_square = jnp.matmul(
        jnp.swapaxes(left_bases, 1, 2),
        jnp.matmul(square_grad, right_bases, precision=HIGHEST),
        precision=HIGHEST,
    )
    rot_in = jnp.dot(
        bases_small[16].T, jnp.dot(in_grad, bases_big[0], precision=HIGHEST), precision=HIGHEST
    )
    rot_out = jnp.dot(
        bases_big[1].T, jnp.dot(out_grad, bases_small[17], precision=HIGHEST), precision=HIGHEST
    )
    return jnp.concatenate(
        [rot_square.reshape(8 * model_width, model_width), rot_in.T, rot_out], axis=0
    )


def rotate_back(step_bank, bases_small, bases_big):
    model_width = step_bank.shape[1]
    ff_width = (step_bank.shape[0] - 8 * model_width) // 2
    step_square = step_bank[: 8 * model_width].reshape(8, model_width, model_width)
    step_in = step_bank[8 * model_width : 8 * model_width + ff_width].T
    step_out = step_bank[8 * model_width + ff_width :]
    up_square = jnp.matmul(
        bases_small[0:8],
        jnp.matmul(step_square, jnp.swapaxes(bases_small[8:16], 1, 2), precision=HIGHEST),
        precision=HIGHEST,
    )
    up_in = jnp.dot(
        bases_small[16], jnp.dot(step_in, bases_big[0].T, precision=HIGHEST), precision=HIGHEST
    )
    up_out = jnp.dot(
        bases_big[1], jnp.dot(step_out, bases_small[17].T, precision=HIGHEST), precision=HIGHEST
    )
    return (up_square, up_in, up_out)


def adam_rows(gradient, first_old, second_old, step_float):
    first_new = BETA_ONE * first_old + (1.0 - BETA_ONE) * gradient
    second_new = BETA_TWO * second_old + (1.0 - BETA_TWO) * gradient * gradient
    first_hat = first_new / (1.0 - jnp.power(BETA_ONE, step_float))
    second_hat = second_new / (1.0 - jnp.power(BETA_TWO, step_float))
    return (first_new, second_new, first_hat / (jnp.sqrt(second_hat) + EPSILON))


def trusted(weight, update, over_axes):
    scaling = jnp.sqrt(jnp.mean(weight * weight, axis=over_axes, keepdims=True) + 1e-06)
    return weight - LEARN_RATE * scaling * update


def per_device(
    cells,
    feat_mask,
    train_rows,
    cotangent,
    proj_weights,
    feat_out_w,
    item_out_w,
    mlp_in,
    mlp_out,
    norm_gains,
    norm_shifts,
    bases_small,
    bases_big,
    owner_rows,
    bank_first,
    bank_second,
    norm_first,
    norm_second,
):
    rows_dev, width_dev = cells.shape
    model_width = proj_weights.shape[-1]
    head_count = HEADS
    head_dim = model_width // head_count
    cols_dev = width_dev // model_width
    col_count = lax.axis_size("cols")
    all_cols = cols_dev * col_count
    half_rows = rows_dev // col_count
    cell_count = rows_dev * cols_dev
    proj_low = proj_weights.astype(jnp.bfloat16)
    feat_qkv = jnp.concatenate([proj_low[0], proj_low[1], proj_low[2]], axis=1)
    item_qkv = jnp.concatenate([proj_low[3], proj_low[4], proj_low[5]], axis=1)
    feat_out_low = feat_out_w.astype(jnp.bfloat16)
    item_out_low = item_out_w.astype(jnp.bfloat16)
    mlp_in_cast = mlp_in.astype(jnp.bfloat16)
    mlp_out_cast = mlp_out.astype(jnp.bfloat16)
    train_count = train_rows[0]
    column_cells = lax.all_to_all(cells, "cols", split_axis=0, concat_axis=1, tiled=True)
    column_flat = column_cells.reshape(half_rows * all_cols, model_width)
    row_mask = (
        lax.dynamic_slice_in_dim(feat_mask, lax.axis_index("cols") * half_rows, half_rows, 0) > 0
    )
    feat_proj = (
        product(column_flat, feat_qkv)
        .astype(jnp.bfloat16)
        .reshape(half_rows, all_cols, 3, head_count, head_dim)
    )
    feat_query = feat_proj[:, :, 0]
    feat_key = feat_proj[:, :, 1]
    feat_value = feat_proj[:, :, 2]
    feat_attend, feat_attend_low, feat_mixed = feature_forward(
        feat_query, feat_key, feat_value, row_mask
    )
    feat_mixed_flat = feat_mixed.reshape(half_rows * all_cols, model_width)
    feat_branch = (
        product(feat_mixed_flat, feat_out_low)
        .astype(jnp.bfloat16)
        .reshape(half_rows, all_cols * model_width)
    )
    feat_back = lax.all_to_all(feat_branch, "cols", split_axis=1, concat_axis=0, tiled=True)
    inputs_flat = cells.astype(jnp.float32).reshape(cell_count, model_width)
    first_sum = inputs_flat + feat_back.astype(jnp.float32).reshape(cell_count, model_width)
    first_out, first_pull = jax.vjp(layer_norm, first_sum, norm_gains[0], norm_shifts[0])
    first_low = first_out.astype(jnp.bfloat16)
    item_proj = product(first_low, item_qkv).astype(jnp.bfloat16)
    item_query = item_proj[:, :model_width].reshape(rows_dev, cols_dev, head_count, head_dim)
    item_key = item_proj[:, model_width : 2 * model_width].reshape(rows_dev, width_dev)
    item_value = item_proj[:, 2 * model_width :].reshape(rows_dev, width_dev)
    key_rows, value_rows = (
        lax.all_gather(item_key, "rows", axis=0, tiled=True),
        lax.all_gather(item_value, "rows", axis=0, tiled=True),
    )
    key_total = key_rows.shape[0]
    key_rows = key_rows.reshape(key_total, cols_dev, head_count, head_dim)
    value_rows = value_rows.reshape(key_total, cols_dev, head_count, head_dim)
    log_total, item_full = item_forward(item_query, key_rows, value_rows, train_count)
    item_low = item_full.astype(jnp.bfloat16).reshape(cell_count, model_width)
    item_branch = product(item_low, item_out_low)
    second_sum = first_out + item_branch
    second_out, second_pull = jax.vjp(layer_norm, second_sum, norm_gains[1], norm_shifts[1])
    second_low = second_out.astype(jnp.bfloat16)
    hidden_pre = product(second_low, mlp_in_cast)
    hidden_act, gelu_pull = jax.vjp(gelu_exact, hidden_pre)
    hidden_low = hidden_act.astype(jnp.bfloat16)
    mlp_branch = product(hidden_low, mlp_out_cast)
    third_sum = second_out + mlp_branch
    third_out, third_pull = jax.vjp(layer_norm, third_sum, norm_gains[2], norm_shifts[2])
    layer_out = third_out.astype(jnp.bfloat16).reshape(rows_dev, width_dev)
    third_grad, gain_three, shift_three = third_pull(
        cotangent.astype(jnp.float32).reshape(cell_count, model_width)
    )
    branch_low = third_grad.astype(jnp.bfloat16)
    mlp_out_grad = product_left(hidden_low, branch_low)
    hidden_grad = product_right(branch_low, mlp_out_cast)
    (pre_grad,) = gelu_pull(hidden_grad)
    pre_low = pre_grad.astype(jnp.bfloat16)
    mlp_in_grad = product_left(second_low, pre_low)
    second_grad = third_grad + product_right(pre_low, mlp_in_cast)
    second_in_grad, gain_two, shift_two = second_pull(second_grad)
    item_branch_low = second_in_grad.astype(jnp.bfloat16)
    item_out_grad = product_left(item_low, item_branch_low)
    item_mixed_grad = (
        product_right(item_branch_low, item_out_low)
        .astype(jnp.bfloat16)
        .reshape(rows_dev, cols_dev, head_count, head_dim)
    )
    key_again, value_again = (
        lax.all_gather(item_key, "rows", axis=0, tiled=True),
        lax.all_gather(item_value, "rows", axis=0, tiled=True),
    )
    key_rows = key_again.reshape(key_total, cols_dev, head_count, head_dim)
    value_rows = value_again.reshape(key_total, cols_dev, head_count, head_dim)
    query_sum, key_grads, value_grads = item_backward(
        item_query, key_rows, value_rows, train_count, log_total, item_mixed_grad, item_full
    )
    key_sum, value_sum = (
        lax.psum_scatter(key_grads, "rows", scatter_dimension=0, tiled=True),
        lax.psum_scatter(value_grads, "rows", scatter_dimension=0, tiled=True),
    )
    item_grad_low = jnp.concatenate(
        [
            query_sum.astype(jnp.bfloat16).reshape(cell_count, model_width),
            key_sum.astype(jnp.bfloat16).reshape(cell_count, model_width),
            value_sum.astype(jnp.bfloat16).reshape(cell_count, model_width),
        ],
        axis=1,
    )
    item_qkv_grad = product_left(first_low, item_grad_low)
    first_grad = second_in_grad + product_right(item_grad_low, item_qkv)
    first_in_grad, gain_one, shift_one = first_pull(first_grad)
    feat_branch_grad = first_in_grad.astype(jnp.bfloat16).reshape(rows_dev, width_dev)
    column_grad = lax.all_to_all(
        feat_branch_grad, "cols", split_axis=0, concat_axis=1, tiled=True
    ).reshape(half_rows * all_cols, model_width)
    feat_out_grad = product_left(feat_mixed_flat, column_grad)
    feat_mixed_grad = (
        product_right(column_grad, feat_out_low)
        .astype(jnp.bfloat16)
        .reshape(half_rows, all_cols, head_count, head_dim)
    )
    feat_query_grad, feat_key_grad, feat_value_grad = feature_backward(
        feat_query, feat_key, feat_value, feat_attend, feat_attend_low, feat_mixed_grad
    )
    feat_grad_low = jnp.concatenate(
        [
            feat_query_grad.reshape(half_rows * all_cols, model_width),
            feat_key_grad.reshape(half_rows * all_cols, model_width),
            feat_value_grad.reshape(half_rows * all_cols, model_width),
        ],
        axis=1,
    )
    feat_qkv_grad = product_left(column_flat, feat_grad_low)
    column_in_grad = (
        product_right(feat_grad_low, feat_qkv)
        .astype(jnp.bfloat16)
        .reshape(half_rows, all_cols * model_width)
    )
    row_in_grad = lax.all_to_all(column_in_grad, "cols", split_axis=1, concat_axis=0, tiled=True)
    cells_grad = first_in_grad.reshape(rows_dev, width_dev) + row_in_grad.astype(jnp.float32)
    proj_grad = jnp.stack(
        [
            feat_qkv_grad[:, :model_width],
            feat_qkv_grad[:, model_width : 2 * model_width],
            feat_qkv_grad[:, 2 * model_width :],
            item_qkv_grad[:, :model_width],
            item_qkv_grad[:, model_width : 2 * model_width],
            item_qkv_grad[:, 2 * model_width :],
        ]
    )
    norm_grad = jnp.stack(
        [
            jnp.stack([gain_one, gain_two, gain_three]),
            jnp.stack([shift_one, shift_two, shift_three]),
        ]
    )
    proj_total, feat_total, item_total, in_total, out_total, norm_total = lax.psum(
        (proj_grad, feat_out_grad, item_out_grad, mlp_in_grad, mlp_out_grad, norm_grad),
        ("rows", "cols"),
    )
    square_grad = jnp.concatenate([proj_total, feat_total[None], item_total[None]], axis=0)
    clipped, grad_norm = clip_all([square_grad, in_total, out_total, norm_total])
    square_clip, in_clip, out_clip, norm_clip = clipped
    rot_bank = rotate_bank(square_clip, in_clip, out_clip, bases_small, bases_big)
    step_float = jnp.asarray(STEP, jnp.float32)
    slot_count = bank_first.shape[0]
    my_slots = lax.dynamic_slice_in_dim(
        owner_rows, lax.axis_index("rows") * slot_count, slot_count, 0
    )
    first_new, second_new, slot_steps = adam_rows(
        jnp.take(rot_bank, my_slots, axis=0), bank_first, bank_second, step_float
    )
    all_steps = lax.all_gather(slot_steps, "rows", axis=0, tiled=True)
    full_steps = jnp.take(all_steps, jnp.argsort(owner_rows), axis=0)
    up_square, up_in, up_out = rotate_back(full_steps, bases_small, bases_big)
    square_old = jnp.concatenate([proj_weights, feat_out_w[None], item_out_w[None]], axis=0)
    square_new = trusted(square_old, up_square, (1, 2))
    in_new = trusted(mlp_in, up_in, (0, 1))
    out_new = trusted(mlp_out, up_out, (0, 1))
    norm_old = jnp.stack([norm_gains, norm_shifts])
    norm_first_new, norm_second_new, norm_steps = adam_rows(
        norm_clip, norm_first, norm_second, step_float
    )
    norm_new = trusted(norm_old, norm_steps, (2,))
    return (
        layer_out,
        cells_grad,
        square_clip,
        in_clip,
        out_clip,
        norm_clip,
        grad_norm.reshape(1),
        first_new,
        second_new,
        square_new,
        in_new,
        out_new,
        square_new.astype(jnp.bfloat16),
        in_new.astype(jnp.bfloat16),
        out_new.astype(jnp.bfloat16),
        norm_new,
        norm_first_new,
        norm_second_new,
    )


F32 = jnp.float32
BF16 = jnp.bfloat16
MESH = pl.DeviceIdType.MESH
VMEM_BYTES = 56 * 1024 * 1024
LANES = 128


def dot_nn(left, right):
    return jnp.dot(left, right, preferred_element_type=F32)


def dot_nt(left, right):
    return lax.dot_general(left, right, (((1,), (1,)), ((), ())), preferred_element_type=F32)


def dot_tn(left, right):
    return lax.dot_general(left, right, (((0,), (0,)), ((), ())), preferred_element_type=F32)


def split_two(value):
    high = value.astype(BF16)
    return high, (value - high.astype(F32)).astype(BF16)


def dot_low(dot, left, right):
    return dot(left.astype(BF16), right.astype(BF16))


def stack_columns(packed, width):
    count = packed.shape[1] // width
    return jnp.concatenate([packed[:, n * width : (n + 1) * width] for n in range(count)], axis=0)


def pack_columns(stacked, rows):
    count = stacked.shape[0] // rows
    return jnp.concatenate([stacked[n * rows : (n + 1) * rows] for n in range(count)], axis=1)


def norm_parts(hidden):
    width = hidden.shape[1]
    center = jnp.sum(hidden, axis=1, keepdims=True) * (1.0 / width)
    centered = hidden - center
    spread = jnp.sum(centered * centered, axis=1, keepdims=True) * (1.0 / width)
    root = lax.rsqrt(spread + 1e-05)
    return centered * root, root


def norm_back(unit, root, gain, incoming):
    width = unit.shape[1]
    scaled = incoming * gain
    mean_one = jnp.sum(scaled, axis=1, keepdims=True) * (1.0 / width)
    mean_two = jnp.sum(scaled * unit, axis=1, keepdims=True) * (1.0 / width)
    gain_grad = jnp.sum(incoming * unit, axis=0, keepdims=True)
    shift_grad = jnp.sum(incoming, axis=0, keepdims=True)
    return root * (scaled - mean_one - unit * mean_two), gain_grad, shift_grad


def head_table(width, head_dim):
    feature = lax.broadcasted_iota(jnp.int32, (width, LANES), 0)
    head = lax.broadcasted_iota(jnp.int32, (width, LANES), 1)
    inside = (feature >= head * head_dim) & (feature < (head + 1) * head_dim)
    return jnp.where(inside, 1.0, 0.0).astype(BF16)


def spread_table(width, head_dim):
    head = lax.broadcasted_iota(jnp.int32, (LANES, width), 0)
    feature = lax.broadcasted_iota(jnp.int32, (LANES, width), 1)
    inside = (feature >= head * head_dim) & (feature < (head + 1) * head_dim)
    return jnp.where(inside, 1.0, 0.0).astype(BF16)


def head_rows_of(value, wide):
    high, low = split_two(value)
    return dot_nt(wide, high) + dot_nt(wide, low)


def head_sums(value, table):
    high, low = split_two(value)
    return dot_nn(high, table) + dot_nn(low, table)


def head_sums_low(value, table):
    return dot_nn(value.astype(BF16), table)


def head_mask(rows, width, head_dim, head):
    feature = lax.broadcasted_iota(jnp.int32, (rows, width), 1)
    return (feature >= head * head_dim) & (feature < (head + 1) * head_dim)


def tile_rows(value, count):
    return jnp.concatenate([value] * count, axis=0)


def feature_scores(queries, keys, is_open, repeat, table, scaling):
    raw = head_sums(queries * tile_rows(keys, repeat), table) * scaling
    return jnp.where(tile_rows(is_open, repeat), raw, NEGATIVE)


def softmax_of(scores):
    top = scores[0]
    for extra in scores[1:]:
        top = jnp.maximum(top, extra)
    grown = [jnp.exp(score - top) for score in scores]
    total = grown[0]
    for extra in grown[1:]:
        total = total + extra
    inverse = 1.0 / total
    return [part * inverse for part in grown]


def flip(value, pattern, size):
    out, step = 0, 1
    while step < size:
        out = out + step * (((value // step) % 2 + (pattern // step) % 2) % 2)
        step *= 2
    return out


class RowGather:
    def __init__(self, pieces, send_sem, recv_sem, rows_count):
        self.pieces, self.send_sem, self.recv_sem = pieces, send_sem, recv_sem
        self.deep = rows_count // 4
        me = lax.axis_index("rows")
        self.core, self.side, self.depth = me % 2, (me // 2) % 2, me // 4

    @staticmethod
    def slots(rows_count):
        return rows_count - 1

    def place(self, depth, side, core):
        return (depth * 2 + side) * 2 + core

    def source(self, k):
        return flip(self.depth, k, self.deep)

    def side_peer(self):
        return self.place(self.depth, 1 - self.side, self.core)

    def core_peer(self):
        return self.place(self.depth, self.side, 1 - self.core)

    def copies(self, shard, target, slot):
        return [
            pltpu.make_async_remote_copy(
                src_ref=piece(shard),
                dst_ref=piece(shard),
                send_sem=self.send_sem.at[n, slot],
                recv_sem=self.recv_sem.at[n, slot],
                device_id={"rows": target},
                device_id_type=MESH,
            )
            for n, piece in enumerate(self.pieces)
        ]

    def push(self, shard, target, slot):
        for copy in self.copies(shard, target, slot):
            copy.start()

    def arrive(self, shard, source, slot):
        for copy in self.copies(shard, source, slot):
            copy.wait_recv()

    def start_depth(self):
        own = self.place(self.depth, self.side, self.core)
        for k in range(1, self.deep):
            self.push(own, self.place(self.source(k), self.side, self.core), k - 1)

    def start_near(self):
        own = self.place(self.depth, self.side, self.core)
        self.push(own, self.core_peer(), 2 * self.deep - 1)
        self.push(own, self.side_peer(), self.deep - 1)

    def along_depth(self, k):
        shard = self.place(self.source(k), self.side, self.core)
        self.arrive(shard, shard, k - 1)
        self.push(shard, self.side_peer(), self.deep - 1 + k)
        self.push(shard, self.core_peer(), 2 * self.deep - 1 + k)

    def across_side(self, k):
        shard = self.place(self.source(k), 1 - self.side, self.core)
        self.arrive(shard, self.side_peer(), self.deep - 1 + k)
        self.push(shard, self.core_peer(), 3 * self.deep - 1 + k)

    def from_core(self, k, other_side):
        side = self.side + other_side - 2 * self.side * other_side
        shard = self.place(self.source(k), side, 1 - self.core)
        self.arrive(shard, self.core_peer(), (2 + other_side) * self.deep - 1 + k)

    def forward(self, k):
        self.across_side(k)

        @pl.when(k + 1 < self.deep)
        def _():
            self.along_depth(k + 1)

    def run(self, use, forwarded):
        @pl.loop(0, 2 * self.deep)
        def _(turn):
            k, other = turn // 2, turn % 2
            if forwarded:

                @pl.when((other == 0) & (k > 0) & (k + forwarded - 1 < self.deep))
                def _():
                    self.forward(k + forwarded - 1)

            else:

                @pl.when((turn == 1) | ((other == 0) & (k > 0)))
                def _():
                    self.forward(k)

            self.from_core(k, other)
            use(self.source(k), self.side + other - 2 * self.side * other)

    def wait_sent(self):
        own = self.place(self.depth, self.side, self.core)

        @pl.loop(0, 4 * self.deep - 1)
        def _(slot):
            for copy in self.copies(own, self.core_peer(), slot):
                copy.wait_send()


class DepthGather:
    def __init__(self, pieces, send_sem, recv_sem, rows_count):
        self.pieces, self.send_sem, self.recv_sem = pieces, send_sem, recv_sem
        self.deep = rows_count // 4
        me = lax.axis_index("rows")
        self.core, self.side, self.depth = me % 2, (me // 2) % 2, me // 4

    @staticmethod
    def slots(rows_count):
        return rows_count // 2 - 1

    def row(self, depth, core):
        return (depth * 2 + self.side) * 2 + core

    def source(self, k):
        return flip(self.depth, k, self.deep)

    def copies(self, shard, target, slot):
        return [
            pltpu.make_async_remote_copy(
                src_ref=piece(shard),
                dst_ref=piece(shard),
                send_sem=self.send_sem.at[n, slot],
                recv_sem=self.recv_sem.at[n, slot],
                device_id={"rows": target},
                device_id_type=MESH,
            )
            for n, piece in enumerate(self.pieces)
        ]

    def start(self):
        own = self.depth * 2 + self.core
        for copy in self.copies(own, self.row(self.depth, 1 - self.core), self.deep - 1):
            copy.start()
        for k in range(1, self.deep):
            for copy in self.copies(own, self.row(self.source(k), self.core), k - 1):
                copy.start()

    def forward(self, k):
        shard = self.source(k) * 2 + self.core
        for copy in self.copies(shard, self.row(self.source(k), self.core), k - 1):
            copy.wait_recv()
        twin = self.row(self.depth, 1 - self.core)
        for copy in self.copies(shard, twin, self.deep - 1 + k):
            copy.start()

    def run(self, use, forwarded):
        twin = self.row(self.depth, 1 - self.core)

        @pl.loop(0, 2 * self.deep)
        def _(turn):
            k, other = turn // 2, turn % 2

            @pl.when((other == 0) & (k > forwarded))
            def _():
                self.forward(k)

            @pl.when(other == 1)
            def _():
                shard = self.source(k) * 2 + 1 - self.core
                for copy in self.copies(shard, twin, self.deep - 1 + k):
                    copy.wait_recv()

            use(self.source(k), self.core + other - 2 * self.core * other)

    def wait_sent(self):
        own = self.depth * 2 + self.core

        @pl.loop(0, 2 * self.deep - 1)
        def _(slot):
            for copy in self.copies(own, self.row(self.depth, 1 - self.core), slot):
                copy.wait_send()


class Quad:
    def __init__(self):
        row = lax.axis_index("rows")
        self.side, self.col = (row // 2) % 2, lax.axis_index("cols")
        self.row = row
        self.own = self.side * 2 + self.col

    def device(self, pattern):
        side_flip, col_flip = pattern % 2, pattern // 2
        side = self.side + side_flip - 2 * self.side * side_flip
        col = self.col + col_flip - 2 * self.col * col_flip
        return {"rows": self.row + 2 * (side - self.side), "cols": col}

    def number(self, pattern):
        side_flip, col_flip = pattern % 2, pattern // 2
        side = self.side + side_flip - 2 * self.side * side_flip
        return side * 2 + self.col + col_flip - 2 * self.col * col_flip

    def spread(self, source, landing, sem):
        return [
            pltpu.make_async_remote_copy(
                src_ref=source,
                dst_ref=landing.at[self.own],
                send_sem=sem.at[0, pattern - 1],
                recv_sem=sem.at[1, pattern - 1],
                device_id=self.device(pattern),
                device_id_type=MESH,
            )
            for pattern in range(1, 4)
        ]

    def across(self, source, landing, sem):
        return pltpu.make_async_remote_copy(
            src_ref=source,
            dst_ref=landing,
            send_sem=sem.at[0],
            recv_sem=sem.at[1],
            device_id=self.device(1),
            device_id_type=MESH,
        )

    def pick(self, packed, width, other):
        left, right = packed[:, :width], packed[:, width:]
        return jnp.where(self.side == other, left, right)

    def joined(self, own, other):
        return jnp.concatenate(
            [jnp.where(self.side == 0, own, other), jnp.where(self.side == 0, other, own)], axis=1
        )

    def columns(self, landing, width, col_flip):
        col = self.col + col_flip - 2 * self.col * col_flip
        blocks = [landing[side * 2 + col].astype(F32) for side in range(2)]
        return [
            jnp.concatenate([self.pick(block, width, other) for block in blocks], axis=0)
            for other in range(2)
        ]


class StagedSum:
    def __init__(self, stages, sizes, part_ref, total_ref, landing, sems):
        self.stages, self.sizes = stages, sizes
        self.part_ref, self.total_ref, self.landing, self.sems = part_ref, total_ref, landing, sems
        row = lax.axis_index("rows")
        self.me = {"z": row // 4, "x": (row // 2) % 2, "k": row % 2, "y": lax.axis_index("cols")}
        self.spans, base, size = [], 0, part_ref.shape[0]
        for stage in stages[:-1]:
            size = size // members(stage, sizes)
            self.spans.append((base, size))
            base = base + self.number(self.me, stage) * size
        self.base, self.size = base, size
        self.unit = size

    def number(self, place, stage):
        out, scale = 0, 1
        for axis in stage:
            out = out + place[axis] * scale
            scale *= self.sizes[axis]
        return out

    def partner(self, stage, pattern):
        place = dict(self.me)
        for axis in stage:
            place[axis] = flip(self.me[axis], pattern % self.sizes[axis], self.sizes[axis])
            pattern //= self.sizes[axis]
        return place

    def device(self, place):
        return {"rows": (place["z"] * 2 + place["x"]) * 2 + place["k"], "cols": place["y"]}

    def rows_at(self, base, size):
        return pl.ds(pl.multiple_of(base, self.unit), size)

    def scatter(self, s):
        stage, (base, size) = self.stages[s], self.spans[s]
        found = []
        for j in range(1, members(stage, self.sizes)):
            place = self.partner(stage, j)
            rows = self.rows_at(base + self.number(place, stage) * size, size)
            found.append(
                pltpu.make_async_remote_copy(
                    src_ref=self.part_ref.at[rows, :],
                    dst_ref=self.landing[s].at[j - 1],
                    send_sem=self.sems.at[0, s, j - 1],
                    recv_sem=self.sems.at[1, s, j - 1],
                    device_id=self.device(place),
                    device_id_type=MESH,
                )
            )
        return found

    def scatter_start(self, s):
        for copy in self.scatter(s):
            copy.start()

    def scatter_finish(self, s):
        stage, (base, size) = self.stages[s], self.spans[s]
        rows = self.rows_at(base + self.number(self.me, stage) * size, size)
        total = self.part_ref[rows, :].astype(F32)
        copies = self.scatter(s)
        for j, copy in enumerate(copies):
            copy.wait_recv()
            total = total + self.landing[s][j].astype(F32)
        for copy in copies:
            copy.wait_send()
        self.part_ref[rows, :] = total.astype(BF16)

    def share(self):
        last = len(self.stages) - 1
        stage, landing = self.stages[last], self.landing[last]
        rows = self.rows_at(self.base, self.size)
        own = self.number(self.me, stage)
        found = []
        for j in range(1, members(stage, self.sizes)):
            found.append(
                pltpu.make_async_remote_copy(
                    src_ref=self.part_ref.at[rows, :],
                    dst_ref=landing.at[own],
                    send_sem=self.sems.at[0, last, j - 1],
                    recv_sem=self.sems.at[1, last, j - 1],
                    device_id=self.device(self.partner(stage, j)),
                    device_id_type=MESH,
                )
            )
        return found

    def share_start(self):
        for copy in self.share():
            copy.start()
        own = self.number(self.me, self.stages[-1])
        self.landing[-1][own] = self.part_ref[self.rows_at(self.base, self.size), :]

    def share_finish(self):
        copies = self.share()
        for copy in copies:
            copy.wait_recv()
        total = self.landing[-1][0].astype(F32)
        for n in range(1, members(self.stages[-1], self.sizes)):
            total = total + self.landing[-1][n].astype(F32)
        for copy in copies:
            copy.wait_send()
        self.total_ref[self.rows_at(self.base, self.size), :] = total.astype(BF16)

    def gather(self, s, own):
        stage, (base, size) = self.stages[s], self.spans[s]
        found = []
        for j in range(1, members(stage, self.sizes)):
            place = self.partner(stage, j)
            holder = self.me if own else place
            rows = self.rows_at(base + self.number(holder, stage) * size, size)
            found.append(
                pltpu.make_async_remote_copy(
                    src_ref=self.total_ref.at[rows, :],
                    dst_ref=self.total_ref.at[rows, :],
                    send_sem=self.sems.at[2, s, j - 1],
                    recv_sem=self.sems.at[3, s, j - 1],
                    device_id=self.device(place),
                    device_id_type=MESH,
                )
            )
        return found

    def gather_start(self, s):
        for copy in self.gather(s, True):
            copy.start()

    def gather_finish(self, s):
        for copy in self.gather(s, False):
            copy.wait_recv()
        for copy in self.gather(s, True):
            copy.wait_send()


class Mover:
    def __init__(self, sem):
        self.sem, self.count = sem, 0

    def start(self, source, target):
        copy = pltpu.make_async_copy(source, target, self.sem.at[self.count])
        copy.start()
        self.count += 1
        return copy


def put_tiles(ref, row, value):
    rows, lanes = value.shape
    if lanes % LANES:
        value = jnp.concatenate([value, jnp.zeros((rows, LANES - lanes % LANES), F32)], axis=1)
    for n in range(value.shape[1] // LANES):
        ref[row : row + rows, :] = value[:, n * LANES : (n + 1) * LANES].astype(ref.dtype)
        row += rows
    return row


def put_zeros(ref, row):
    if row < ref.shape[0]:
        ref[row:, :] = jnp.zeros((ref.shape[0] - row, ref.shape[1]), ref.dtype)


def take_tiles(ref, row, rows, lanes):
    count = -(-lanes // LANES)
    tiles = [ref[row + n * rows : row + (n + 1) * rows, :].astype(F32) for n in range(count)]
    value = jnp.concatenate(tiles, axis=1)
    return value if lanes % LANES == 0 else value[:, :lanes]


def members(stage, sizes):
    return math.prod(sizes[axis] for axis in stage)


def meet(targets):
    barrier = pltpu.get_barrier_semaphore()
    for target in targets:
        pl.semaphore_signal(barrier, inc=1, device_id=target, device_id_type=MESH)
    pl.semaphore_wait(barrier, len(targets))


def head_blocks(value, head_dim):
    rows, width = value.shape
    blocks = [
        jnp.where(head_mask(rows, width, head_dim, head), value, 0.0).astype(BF16)
        for head in range(HEADS)
    ]
    return jnp.concatenate(blocks, axis=0)


def gather_heads_turned(value, rows, head_dim):
    blocks = [
        value[head * head_dim : (head + 1) * head_dim, head * rows : (head + 1) * rows]
        for head in range(HEADS)
    ]
    return jnp.transpose(jnp.concatenate(blocks, axis=0))


def gather_heads(value, rows, head_dim):
    total = None
    for head in range(HEADS):
        block = value[head * rows : (head + 1) * rows]
        kept = jnp.where(head_mask(rows, value.shape[1], head_dim, head), block, 0.0)
        total = kept if total is None else total + kept
    return total


STAGES = ("k", "xy", "z")


def layer_kernel(
    rows_count,
    cols_count,
    train_ref,
    owner_ref,
    cells_ref,
    mask_ref,
    gains_ref,
    shifts_ref,
    proj_in,
    feat_out_in,
    bank_first_in,
    bank_second_in,
    item_out_in,
    mlp_in_in,
    mlp_out_in,
    cotangent_in,
    layer_out,
    cells_grad_out,
    mlp_total_ref,
    item_total_ref,
    feat_total_ref,
    sorted_out,
    proj_ref,
    feat_out_ref,
    bank_first_ref,
    bank_second_ref,
    item_out_ref,
    mlp_in_ref,
    mlp_out_ref,
    cotangent_ref,
    layer_ref,
    cells_grad_ref,
    sorted_ref,
    quad_ref,
    masks_ref,
    half_ref,
    cotangent_half_ref,
    layer_half_ref,
    layer_land_ref,
    grad_half_ref,
    grad_land_ref,
    gathered_ref,
    keys_turned_ref,
    values_ref,
    grads_ref,
    all_stats_ref,
    banks_ref,
    blocks_ref,
    grad_blocks_ref,
    scores_ref,
    top_ref,
    sum_ref,
    turned_ref,
    total_ref,
    value_total_ref,
    branch_ref,
    quad_branch_ref,
    mlp_part_ref,
    item_part_ref,
    feat_part_ref,
    mlp_land_k,
    mlp_land_xy,
    mlp_land_z,
    item_land_k,
    item_land_xy,
    item_land_z,
    feat_land_k,
    feat_land_xy,
    feat_land_z,
    quad_sem,
    side_sem,
    gather_sem,
    grads_sem,
    banks_sem,
    mlp_sem,
    item_sem,
    feat_sem,
    move_sem,
):
    mover = Mover(move_sem)
    proj_load = mover.start(proj_in, proj_ref)
    feat_out_load = mover.start(feat_out_in, feat_out_ref)
    cotangent_load = mover.start(cotangent_in, cotangent_ref)
    bank_loads = [
        mover.start(bank_first_in, bank_first_ref),
        mover.start(bank_second_in, bank_second_ref),
    ]
    later_loads = [
        mover.start(source, target)
        for source, target in (
            (item_out_in, item_out_ref),
            (mlp_in_in, mlp_in_ref),
            (mlp_out_in, mlp_out_ref),
        )
    ]
    rows_dev = cells_ref.shape[0]
    width = feat_out_ref.shape[0]
    head_dim = width // HEADS
    scaling = head_dim ** (-0.5)
    to_log2 = scaling * math.log2(math.e)
    key_total = values_ref.shape[0]
    block_rows = 2 * rows_dev
    bank_slots = bank_first_ref.shape[0]
    train_count = train_ref[0]
    me = lax.axis_index("rows")
    quad = Quad()
    sizes = {"z": rows_count // 4, "x": 2, "k": 2, "y": cols_count}

    def shard_of(ref, rows):
        return lambda shard: ref.at[pl.ds(pl.multiple_of(shard * rows, rows), rows), :]

    def stats_shard(shard):
        return all_stats_ref.at[:, block_span(shard)]

    def block_span(shard):
        return pl.ds(pl.multiple_of(shard * block_rows, block_rows), block_rows)

    hidden_gather = DepthGather(
        [shard_of(gathered_ref, rows_dev)], gather_sem.at[0], gather_sem.at[1], rows_count
    )
    grads_gather = DepthGather(
        [shard_of(grads_ref, rows_dev), stats_shard], grads_sem.at[0], grads_sem.at[1], rows_count
    )
    banks_gather = RowGather(
        [shard_of(banks_ref, bank_slots)], banks_sem.at[0], banks_sem.at[1], rows_count
    )
    mlp_sum = StagedSum(
        STAGES,
        sizes,
        mlp_part_ref,
        mlp_total_ref,
        (mlp_land_k, mlp_land_xy, mlp_land_z),
        mlp_sem,
    )
    item_sum = StagedSum(
        STAGES,
        sizes,
        item_part_ref,
        item_total_ref,
        (item_land_k, item_land_xy, item_land_z),
        item_sem,
    )
    feat_sum = StagedSum(
        STAGES,
        sizes,
        feat_part_ref,
        feat_total_ref,
        (feat_land_k, feat_land_xy, feat_land_z),
        feat_sem,
    )
    depth, core = hidden_gather.depth, hidden_gather.core
    own_shard = depth * 2 + core
    own_rows = pl.ds(pl.multiple_of(own_shard * rows_dev, rows_dev), rows_dev)
    meet(
        [
            mlp_sum.device(mlp_sum.partner(stage, j))
            for stage in STAGES
            for j in range(1, members(stage, sizes))
        ]
    )

    cell_copies = quad.spread(cells_ref, quad_ref, quad_sem.at[0])
    for copy in cell_copies:
        copy.start()
    mask_copy = quad.across(mask_ref, masks_ref.at[quad.side], side_sem.at[0])
    mask_copy.start()
    quad_ref[quad.own] = cells_ref[...]
    masks_ref[quad.side] = mask_ref[...]
    for load in bank_loads:
        load.wait()
    banks_ref[pl.ds(pl.multiple_of(me * bank_slots, bank_slots), bank_slots), :] = jnp.concatenate(
        [bank_first_ref[...], bank_second_ref[...]], axis=1
    ).astype(BF16)
    banks_gather.start_depth()
    cotangent_load.wait()
    cotangent = cotangent_ref[...].astype(F32)
    half_ref[...] = quad.pick(cotangent, width, 1).astype(BF16)
    cotangent_copy = quad.across(half_ref, cotangent_half_ref, side_sem.at[1])

    table = head_table(width, head_dim)
    wide = spread_table(width, head_dim)
    proj_load.wait()
    feat_w = [proj_ref[n].astype(BF16) for n in range(3)]
    slots = 4
    mask_blocks = []
    cell_copies[0].wait()
    mask_copy.wait()
    for side in range(2):
        rows = [
            masks_ref[
                side,
                pl.ds(
                    2 * (quad.col + col_flip - 2 * quad.col * col_flip)
                    + quad.side
                    + other
                    - 2 * quad.side * other,
                    1,
                ),
                :,
            ]
            for col_flip in range(2)
            for other in range(2)
        ]
        rows.append(jnp.zeros((8 - slots, rows_dev), jnp.int32))
        mask_blocks.append(jnp.transpose(jnp.concatenate(rows, axis=0).astype(F32)))
    masks = jnp.concatenate(mask_blocks, axis=0)
    open_list = [masks[:, n : n + 1] > 0.0 for n in range(slots)]
    columns, key_list, value_list, scores = [], [], [], []
    for col_flip in range(2):
        if col_flip == 1:
            cell_copies[1].wait()
            cell_copies[2].wait()
        columns += quad.columns(quad_ref, width, col_flip)
        if col_flip == 0:
            own = columns[0]
            own_low = own.astype(BF16)
            own_query = dot_nn(own_low, feat_w[0]).astype(BF16).astype(F32)
        pair = jnp.concatenate(columns[-2:], axis=0).astype(BF16)
        pair_keys = dot_nn(pair, feat_w[1]).astype(BF16).astype(F32)
        pair_values = dot_nn(pair, feat_w[2]).astype(BF16).astype(F32)
        for n in range(2):
            rows = slice(n * block_rows, (n + 1) * block_rows)
            key_list.append(pair_keys[rows])
            value_list.append(pair_values[rows])
            scores.append(
                feature_scores(own_query, pair_keys[rows], open_list[len(scores)], 1, table, scaling)
            )
    cotangent_copy.start()
    banks_gather.start_near()
    all_low = jnp.concatenate(columns, axis=0).astype(BF16)
    own_weights = softmax_of(scores)
    mixed = None
    for weight, column_values in zip(own_weights, value_list):
        added = dot_nn(weight.astype(BF16), wide) * column_values
        mixed = added if mixed is None else mixed + added
    feat_mixed = mixed.astype(BF16)
    feat_out_load.wait()
    feat_out_w = feat_out_ref[...].astype(BF16)
    first_sum = own + dot_nn(feat_mixed, feat_out_w).astype(BF16).astype(F32)
    unit_one, root_one = norm_parts(first_sum)
    first_out = unit_one * gains_ref[0:1, :] + shifts_ref[0:1, :]
    first_low = first_out.astype(BF16)
    gathered_ref[own_rows, :] = pack_columns(first_out, rows_dev).astype(BF16)
    hidden_gather.start()

    item_w = [proj_ref[3 + n].astype(BF16) for n in range(3)]
    turned_w = [jnp.transpose(proj_ref[4 + n]).astype(BF16) for n in range(2)]
    queries, own_keys, own_values = [
        dot_nn(first_low, weight).astype(BF16).astype(F32) for weight in item_w
    ]
    blocks_ref[...] = head_blocks(queries, head_dim)
    top_ref[...] = jnp.full(top_ref.shape, NEGATIVE, F32)
    sum_ref[...] = jnp.zeros(sum_ref.shape, F32)
    turned_ref[...] = jnp.zeros(turned_ref.shape, F32)

    def hidden_of(shard):
        rows = pl.ds(pl.multiple_of(shard * rows_dev, rows_dev), rows_dev)
        return stack_columns(gathered_ref[rows, :].astype(F32), width).astype(BF16)

    def open_rows(shape, shard_depth, shard_core):
        row = lax.broadcasted_iota(jnp.int32, shape, 0)
        row = row + jnp.where(row >= rows_dev, rows_dev, 0)
        return row < train_count - (shard_depth * 4 + shard_core) * rows_dev

    def masked_scores(keys, shard_depth, shard_core):
        raw = dot_nt(keys, blocks_ref[...]) * to_log2
        return jnp.where(open_rows(raw.shape, shard_depth, shard_core), raw, NEGATIVE)

    def attend(shard_depth, shard_core):
        @pl.when(shard_depth * 2 * block_rows < key_total)
        def _():
            shard = shard_depth * 2 + shard_core
            span = block_span(shard)
            hidden = hidden_of(shard)
            keys = dot_nn(hidden, item_w[1]).astype(BF16)
            values_ref[span, :] = dot_nn(hidden, item_w[2]).astype(BF16)
            keys_turned_ref[:, span] = dot_nt(turned_w[0], hidden).astype(BF16)
            values_turned = dot_nt(turned_w[1], hidden).astype(BF16)
            scores = masked_scores(keys, shard_depth, shard_core)
            scores_ref[span, :] = scores
            top_old = top_ref[...]
            top_new = jnp.maximum(top_old, jnp.max(scores, axis=0, keepdims=True))
            grown = jnp.exp2(scores - top_new)
            fade = jnp.exp2(top_old - top_new)
            top_ref[...] = top_new
            sum_ref[...] = sum_ref[...] * fade + jnp.sum(grown, axis=0, keepdims=True)
            turned_ref[...] = turned_ref[...] * fade + dot_nn(values_turned, grown.astype(BF16))

    hidden_gather.run(attend, 0)
    for k in range(1, rows_count // 4):
        banks_gather.along_depth(k)
    full = gather_heads_turned(turned_ref[...] / sum_ref[...], block_rows, head_dim)
    log_total = top_ref[...] + jnp.log2(sum_ref[...])

    item_low = full.astype(BF16)
    for load in later_loads:
        load.wait()
    item_out_w = item_out_ref[...].astype(BF16)
    mlp_in_w = mlp_in_ref[...].astype(BF16)
    mlp_out_w = mlp_out_ref[...].astype(BF16)
    unit_two, root_two = norm_parts(first_out + dot_nn(item_low, item_out_w))
    second_out = unit_two * gains_ref[1:2, :] + shifts_ref[1:2, :]
    second_low = second_out.astype(BF16)
    hidden_pre = dot_nn(second_low, mlp_in_w)
    normal = 0.5 + 0.5 * lax.erf(hidden_pre * (0.5**0.5))
    hidden_low = (hidden_pre * normal).astype(BF16)
    unit_three, root_three = norm_parts(second_out + dot_nt(hidden_low, mlp_out_w))
    third_out = unit_three * gains_ref[2:3, :] + shifts_ref[2:3, :]
    cotangent_copy.wait()
    own_part = quad.pick(cotangent, width, 0)
    other_part = cotangent_half_ref[...].astype(F32)
    incoming = jnp.concatenate(
        [
            jnp.where(quad.side == 0, own_part, other_part),
            jnp.where(quad.side == 0, other_part, own_part),
        ],
        axis=0,
    )
    third_grad, gain_three, shift_three = norm_back(
        unit_three, root_three, gains_ref[2:3, :], incoming
    )
    branch_low = third_grad.astype(BF16)
    density = jnp.exp(-0.5 * hidden_pre * hidden_pre) * (1.0 / math.sqrt(2.0 * math.pi))
    pre_low = (dot_nn(branch_low, mlp_out_w) * (normal + hidden_pre * density)).astype(BF16)
    second_grad, gain_two, shift_two = norm_back(
        unit_two, root_two, gains_ref[1:2, :], third_grad + dot_nt(pre_low, mlp_in_w)
    )
    second_grad_low = second_grad.astype(BF16)
    mixed_grad = dot_nt(second_grad_low, item_out_w).astype(BF16).astype(F32)
    part = head_rows_of(mixed_grad * full, wide)[0:8, :]
    delta = jnp.concatenate([part[h : h + 1] for h in range(HEADS)], axis=1)
    totals = [log_total[:, h * block_rows : (h + 1) * block_rows] for h in range(HEADS)]
    spare = jnp.zeros((8 - HEADS, block_rows), F32)
    own_span = block_span(own_shard)
    all_stats_ref[0:8, own_span] = jnp.concatenate(totals + [spare], axis=0)
    all_stats_ref[8:16, own_span] = part
    grads_ref[own_rows, :] = pack_columns(mixed_grad, rows_dev).astype(BF16)
    grads_gather.start()

    row = put_tiles(mlp_part_ref, 0, dot_tn(second_low, pre_low))
    row = put_tiles(mlp_part_ref, row, dot_tn(branch_low, hidden_low))
    row = put_tiles(mlp_part_ref, row, dot_tn(item_low, second_grad_low))
    put_zeros(mlp_part_ref, row)
    mlp_sum.scatter_start(0)
    first_block, second_block = third_out[:rows_dev], third_out[rows_dev:]
    layer_half_ref[...] = jnp.where(quad.side == 0, second_block, first_block).astype(BF16)
    own_layer = jnp.where(quad.side == 0, first_block, second_block)

    grad_blocks_ref[...] = head_blocks(mixed_grad, head_dim)
    turned_ref[...] = jnp.zeros(turned_ref.shape, F32)
    key_steps = key_total // block_rows

    @pl.loop(0, key_steps, unroll=2)
    def _(step):
        span = block_span(step)
        attend_now = jnp.exp2(scores_ref[span, :] - log_total)
        dots = dot_nt(values_ref[span, :], grad_blocks_ref[...])
        score_grad = (attend_now * (dots - delta)).astype(BF16)
        turned_ref[...] += dot_nn(keys_turned_ref[:, span], score_grad)

    mlp_sum.scatter_finish(0)
    mlp_sum.scatter_start(1)
    query_grad = gather_heads_turned(turned_ref[...], block_rows, head_dim) * scaling

    blocks_ref[...] = head_blocks(own_keys, head_dim)
    grad_blocks_ref[...] = head_blocks(own_values, head_dim)
    total_ref[...] = jnp.zeros(total_ref.shape, F32)
    value_total_ref[...] = jnp.zeros(value_total_ref.shape, F32)

    def answer(shard_depth, shard_core):
        shard = shard_depth * 2 + shard_core
        span = block_span(shard)
        asked = dot_nn(hidden_of(shard), item_w[0]).astype(BF16)
        rows = pl.ds(pl.multiple_of(shard * rows_dev, rows_dev), rows_dev)
        grads = stack_columns(grads_ref[rows, :].astype(F32), width).astype(BF16)
        scores = dot_nt(blocks_ref[...], asked) * to_log2
        dots = dot_nt(grad_blocks_ref[...], grads)
        attends, score_grads = [], []
        for head in range(HEADS):
            part = slice(head * block_rows, (head + 1) * block_rows)
            attend_now = jnp.exp2(scores[part] - all_stats_ref[head : head + 1, span])
            attends.append(attend_now.astype(BF16))
            score_grads.append(
                (attend_now * (dots[part] - all_stats_ref[8 + head : 9 + head, span])).astype(BF16)
            )
        total_ref[...] += dot_nn(jnp.concatenate(score_grads, axis=0), asked)
        value_total_ref[...] += dot_nn(jnp.concatenate(attends, axis=0), grads)

    grads_gather.run(answer, 0)
    layer_copy = quad.across(layer_half_ref, layer_land_ref, side_sem.at[2])
    layer_copy.start()
    mlp_sum.scatter_finish(1)
    mlp_sum.share_start()

    own_open = open_rows((block_rows, width), depth, core)
    key_grad = gather_heads(total_ref[...], block_rows, head_dim) * scaling
    value_grad = gather_heads(value_total_ref[...], block_rows, head_dim)
    item_grads = [
        query_grad.astype(BF16),
        jnp.where(own_open, key_grad, 0.0).astype(BF16),
        jnp.where(own_open, value_grad, 0.0).astype(BF16),
    ]
    first_grad = second_grad
    for n in range(3):
        first_grad = first_grad + dot_nt(item_grads[n], item_w[n])
    first_in_grad, gain_one, shift_one = norm_back(
        unit_one, root_one, gains_ref[0:1, :], first_grad
    )
    branch_ref[...] = pack_columns(first_in_grad, rows_dev).astype(BF16)
    branch_copies = quad.spread(branch_ref, quad_branch_ref, quad_sem.at[1])
    for copy in branch_copies:
        copy.start()

    own_branch = first_in_grad.astype(BF16)
    row = put_tiles(
        item_part_ref,
        0,
        jnp.concatenate([dot_tn(first_low, item_grads[n]) for n in range(2)], axis=1),
    )
    row = put_tiles(
        item_part_ref,
        row,
        jnp.concatenate(
            [dot_tn(first_low, item_grads[2]), dot_tn(feat_mixed, own_branch)], axis=1
        ),
    )
    pairs = [
        jnp.concatenate(pair, axis=1)
        for pair in ((gain_one, shift_one), (gain_two, shift_two), (gain_three, shift_three))
    ]
    row = put_tiles(
        item_part_ref, row, jnp.concatenate(pairs + [jnp.zeros((13, 2 * width), F32)], axis=0)
    )
    put_zeros(item_part_ref, row)
    item_sum.scatter_start(0)

    other_query = dot_nn(all_low[block_rows:], feat_w[0]).astype(BF16).astype(F32)
    others = slots - 1
    other_weights = softmax_of(
        [
            feature_scores(other_query, keys, is_open, others, table, scaling)
            for keys, is_open in zip(key_list, open_list)
        ]
    )
    own_feat_grad = dot_nt(own_branch, feat_out_w).astype(BF16).astype(F32)

    def minus_mean(weights, dots):
        row_delta = None
        for weight, dot in zip(weights, dots):
            added = weight * dot
            row_delta = added if row_delta is None else row_delta + added
        return [dot - row_delta for dot in dots]

    own_dots = minus_mean(
        own_weights, [head_sums_low(own_feat_grad * part, table) for part in value_list]
    )
    own_score_grads = [
        (weight * dot).astype(BF16) for weight, dot in zip(own_weights, own_dots)
    ]
    feat_query_grad = None
    for score_grad, part in zip(own_score_grads, key_list):
        added = dot_nn(score_grad, wide) * part
        feat_query_grad = added if feat_query_grad is None else feat_query_grad + added
    item_sum.scatter_finish(0)
    item_sum.scatter_start(1)
    mlp_sum.share_finish()
    mlp_sum.gather_start(1)
    feat_key_grad = dot_nn(own_score_grads[0], wide) * own_query
    feat_value_grad = dot_nn(own_weights[0].astype(BF16), wide) * own_feat_grad
    for n, pattern in enumerate((1, 2, 3)):
        branch_copies[pattern - 1].wait()
        rows = slice(n * block_rows, (n + 1) * block_rows)
        branch = stack_columns(quad_branch_ref[quad.number(pattern)].astype(F32), width)
        grad = dot_nt(branch.astype(BF16), feat_out_w).astype(BF16).astype(F32)
        part_weights = [weight[rows] for weight in other_weights]
        part_dots = minus_mean(part_weights, [head_sums_low(grad * part, table) for part in value_list])
        score_grad = (part_weights[0] * part_dots[0]).astype(BF16)
        feat_key_grad = feat_key_grad + dot_nn(score_grad, wide) * other_query[rows]
        feat_value_grad = feat_value_grad + dot_nn(part_weights[0].astype(BF16), wide) * grad
    feat_grads = [
        (feat_query_grad * scaling).astype(BF16),
        (feat_key_grad * scaling).astype(BF16),
        feat_value_grad.astype(BF16),
    ]
    row = put_tiles(
        feat_part_ref,
        0,
        jnp.concatenate([dot_tn(own_low, feat_grads[n]) for n in range(2)], axis=1),
    )
    row = put_tiles(feat_part_ref, row, dot_tn(own_low, feat_grads[2]))
    put_zeros(feat_part_ref, row)
    feat_sum.scatter_start(0)
    item_sum.scatter_finish(1)
    item_sum.share_start()
    feat_sum.scatter_finish(0)
    feat_sum.scatter_start(1)
    mlp_sum.gather_finish(1)
    mlp_sum.gather_start(0)
    for k in range(rows_count // 4):
        banks_gather.across_side(k)
    inner = None
    for n in range(3):
        added = dot_nt(feat_grads[n], feat_w[n])
        inner = added if inner is None else inner + added
    cells_grad = first_in_grad + inner.astype(BF16).astype(F32)
    first_block, second_block = cells_grad[:rows_dev], cells_grad[rows_dev:]
    grad_half_ref[...] = jnp.where(quad.side == 0, second_block, first_block)
    own_cells_grad = jnp.where(quad.side == 0, first_block, second_block)
    grad_copy = quad.across(grad_half_ref, grad_land_ref, side_sem.at[3])
    layer_copy.wait()
    layer_ref[...] = quad.joined(own_layer, layer_land_ref[...].astype(F32)).astype(BF16)
    results = [mover.start(layer_ref, layer_out)]
    feat_sum.scatter_finish(1)
    feat_sum.share_start()
    item_sum.share_finish()
    item_sum.gather_start(1)
    grad_copy.start()
    for k in range(rows_count // 4):
        banks_gather.from_core(k, 0)
        banks_gather.from_core(k, 1)
    sort_rows = sorted_ref.shape[0]
    sort_block = math.gcd(sort_rows, 256)
    owner = owner_ref[...].reshape(1, sort_rows)

    def sort_some(first, last):
        @pl.loop(first, last)
        def _(step):
            start = pl.multiple_of(step * sort_block, sort_block)
            row = start + lax.broadcasted_iota(jnp.int32, (sort_block, sort_rows), 0)
            chosen = jnp.where(owner == row, 1.0, 0.0).astype(BF16)
            sorted_ref[pl.ds(start, sort_block), :] = dot_nn(chosen, banks_ref[...]).astype(BF16)

    sort_steps = sort_rows // sort_block
    most, nearly = 5 * sort_steps // 9, 8 * sort_steps // 9
    sort_some(0, most)
    feat_sum.share_finish()
    feat_sum.gather_start(1)
    item_sum.gather_finish(1)
    item_sum.gather_start(0)
    sort_some(most, nearly)
    feat_sum.gather_finish(1)
    feat_sum.gather_start(0)
    grad_copy.wait()
    cells_grad_ref[...] = quad.joined(own_cells_grad, grad_land_ref[...])
    results.append(mover.start(cells_grad_ref, cells_grad_out))
    sort_some(nearly, sort_steps)
    results.append(mover.start(sorted_ref, sorted_out))
    mlp_sum.gather_finish(0)
    item_sum.gather_finish(0)
    for gather in (hidden_gather, grads_gather, banks_gather):
        gather.wait_sent()
    for result in results:
        result.wait()
    feat_sum.gather_finish(0)


def moment_rule(gradient, first_old, second_old):
    first_new = BETA_ONE * first_old + (1.0 - BETA_ONE) * gradient
    second_new = BETA_TWO * second_old + (1.0 - BETA_TWO) * gradient * gradient
    first_hat = first_new * (1.0 / (1.0 - BETA_ONE**STEP))
    second_hat = second_new * (1.0 / (1.0 - BETA_TWO**STEP))
    return first_new, second_new, first_hat / (jnp.sqrt(second_hat) + EPSILON)


def root_mean(value):
    count = value.shape[0] * value.shape[1]
    square = jnp.sum(jnp.sum(value * value, axis=1, keepdims=True), axis=0, keepdims=True)
    return jnp.sqrt(square * (1.0 / count) + 1e-06)


def update_kernel(
    owner_ref,
    mlp_sum_ref,
    item_sum_ref,
    feat_sum_ref,
    gains_ref,
    shifts_ref,
    norm_first_ref,
    norm_second_ref,
    first_ref,
    second_ref,
    layer_in,
    cells_grad_in,
    small_in,
    big_in,
    sorted_in,
    proj_in,
    feat_out_in,
    item_out_in,
    mlp_in_in,
    mlp_out_in,
    layer_out,
    cells_grad_out,
    square_grad_out,
    in_grad_out,
    out_grad_out,
    norm_grad_ref,
    clip_ref,
    first_new_ref,
    second_new_ref,
    square_new_out,
    in_new_out,
    out_new_out,
    square_low_out,
    in_low_out,
    out_low_out,
    norm_new_ref,
    norm_first_new_ref,
    norm_second_new_ref,
    small_ref,
    big_ref,
    sorted_ref,
    olds_ref,
    mlp_in_ref,
    mlp_out_ref,
    square_grad_ref,
    in_grad_ref,
    out_grad_ref,
    square_new_ref,
    in_new_ref,
    out_new_ref,
    square_low_ref,
    in_low_ref,
    out_low_ref,
    rotated_ref,
    own_ref,
    move_sem,
):
    width, ff_width = mlp_in_ref.shape
    slots = first_ref.shape[0]
    squares = square_grad_ref.shape[0]
    mover = Mover(move_sem)
    small_loads = [
        (
            mover.start(small_in.at[n], small_ref.at[n]),
            mover.start(small_in.at[squares + n], small_ref.at[squares + n]),
        )
        for n in range(squares)
    ]
    last_loads = [
        mover.start(small_in.at[2 * squares], small_ref.at[2 * squares]),
        mover.start(small_in.at[2 * squares + 1], small_ref.at[2 * squares + 1]),
        mover.start(big_in, big_ref),
    ]
    sorted_load = mover.start(sorted_in, sorted_ref)
    old_loads = [
        mover.start(proj_in, olds_ref.at[0 : squares - 2]),
        mover.start(feat_out_in, olds_ref.at[squares - 2]),
        mover.start(item_out_in, olds_ref.at[squares - 1]),
    ]
    mlp_loads = [mover.start(mlp_in_in, mlp_in_ref), mover.start(mlp_out_in, mlp_out_ref)]
    results = [mover.start(layer_in, layer_out), mover.start(cells_grad_in, cells_grad_out)]

    square = None
    for part_ref in (mlp_sum_ref, item_sum_ref, feat_sum_ref):
        part = part_ref[...].astype(F32)
        added = jnp.sum(jnp.sum(part * part, axis=1, keepdims=True), axis=0, keepdims=True)
        square = added if square is None else square + added
    grad_norm = jnp.sqrt(square)
    factor = jnp.minimum(1.0, CLIP_NORM / grad_norm)
    clip_ref[0] = grad_norm[0, 0]
    both_width = 2 * width
    both_tiles = both_width // LANES * width
    feat_pair = take_tiles(feat_sum_ref, 0, width, both_width) * factor
    item_pair = take_tiles(item_sum_ref, 0, width, both_width) * factor
    mixed_pair = take_tiles(item_sum_ref, both_tiles, width, both_width) * factor
    parts = [
        feat_pair[:, :width],
        feat_pair[:, width:],
        take_tiles(feat_sum_ref, both_tiles, width, width) * factor,
        item_pair[:, :width],
        item_pair[:, width:],
        mixed_pair[:, :width],
        mixed_pair[:, width:],
        take_tiles(mlp_sum_ref, 2 * both_tiles, width, width) * factor,
    ]
    for n, clipped in enumerate(parts):
        square_grad_ref[n] = clipped
        for load in small_loads[n]:
            load.wait()
        turned = dot_low(dot_nn, clipped, small_ref[squares + n])
        rotated_ref[n * width : (n + 1) * width, :] = dot_low(dot_tn, small_ref[n], turned)
    results.append(mover.start(square_grad_ref, square_grad_out))
    start = squares * width
    middle = start + ff_width
    for load in last_loads:
        load.wait()
    clipped = take_tiles(mlp_sum_ref, 0, width, ff_width) * factor
    in_grad_ref[...] = clipped
    results.append(mover.start(in_grad_ref, in_grad_out))
    turned = dot_low(dot_tn, clipped, small_ref[2 * squares])
    rotated_ref[start:middle, :] = dot_low(dot_tn, big_ref[0], turned)
    clipped = take_tiles(mlp_sum_ref, both_tiles, width, ff_width) * factor
    out_grad_ref[...] = clipped
    results.append(mover.start(out_grad_ref, out_grad_out))
    turned = dot_low(dot_tn, clipped, small_ref[2 * squares + 1])
    rotated_ref[middle : middle + ff_width, :] = dot_low(dot_tn, big_ref[1], turned)

    def step_of(first_row, count):
        rows = slice(first_row, first_row + count)
        banks = sorted_ref[rows, :].astype(F32)
        return moment_rule(rotated_ref[rows, :], banks[:, :width], banks[:, width:])[2]

    sorted_load.wait()
    for load in old_loads:
        load.wait()
    for n in range(squares):
        turned = dot_low(dot_nt, step_of(n * width, width), small_ref[squares + n])
        update = dot_low(dot_nn, small_ref[n], turned)
        old = olds_ref[n]
        new = old - LEARN_RATE * root_mean(old) * update
        square_new_ref[n] = new
        square_low_ref[n] = new.astype(BF16)
        results.append(mover.start(square_new_ref.at[n], square_new_out.at[n]))
    results.append(mover.start(square_low_ref, square_low_out))
    for load in mlp_loads:
        load.wait()
    turned = dot_low(dot_nn, big_ref[0], step_of(start, ff_width))
    update = dot_low(dot_nt, small_ref[2 * squares], turned)
    new = mlp_in_ref[...] - LEARN_RATE * root_mean(mlp_in_ref[...]) * update
    in_new_ref[...] = new
    in_low_ref[...] = new.astype(BF16)
    results.append(mover.start(in_new_ref, in_new_out))
    results.append(mover.start(in_low_ref, in_low_out))
    turned = dot_low(dot_nn, big_ref[1], step_of(middle, ff_width))
    update = dot_low(dot_nt, small_ref[2 * squares + 1], turned)
    new = mlp_out_ref[...] - LEARN_RATE * root_mean(mlp_out_ref[...]) * update
    out_new_ref[...] = new
    out_low_ref[...] = new.astype(BF16)
    results.append(mover.start(out_new_ref, out_new_out))
    results.append(mover.start(out_low_ref, out_low_out))

    base = lax.axis_index("rows") * slots

    @pl.loop(0, slots // 8)
    def _(step):
        for n in range(8):
            row = owner_ref[base + step * 8 + n]
            own_ref[pl.ds(step * 8 + n, 1), :] = rotated_ref[pl.ds(row, 1), :]

    first_new, second_new, _ = moment_rule(own_ref[...], first_ref[...], second_ref[...])
    first_new_ref[...] = first_new
    second_new_ref[...] = second_new

    norm_pairs = take_tiles(item_sum_ref, 2 * both_tiles, 16, both_width) * factor
    for n in range(3):
        pair = norm_pairs[n : n + 1]
        both = jnp.concatenate([pair[:, :width], pair[:, width:]], axis=0)
        norm_grad_ref[n] = both
        first_new, second_new, change = moment_rule(both, norm_first_ref[n], norm_second_ref[n])
        norm_first_new_ref[n] = first_new
        norm_second_new_ref[n] = second_new
        old = jnp.concatenate([gains_ref[n : n + 1, :], shifts_ref[n : n + 1, :]], axis=0)
        size = jnp.sqrt(jnp.sum(old * old, axis=1, keepdims=True) * (1.0 / width) + 1e-06)
        norm_new_ref[n] = old - LEARN_RATE * size * change
    for result in results:
        result.wait()


def in_vmem():
    return pl.BlockSpec(memory_space=pltpu.VMEM)


def anywhere():
    return pl.BlockSpec(memory_space=pl.ANY)


def in_smem():
    return pl.BlockSpec(memory_space=pltpu.SMEM)


def fast_device(
    cells,
    feat_mask,
    train_rows,
    cotangent,
    proj_weights,
    feat_out_w,
    item_out_w,
    mlp_in,
    mlp_out,
    norm_gains,
    norm_shifts,
    bases_small,
    bases_big,
    owner_rows,
    bank_first,
    bank_second,
    norm_first,
    norm_second,
):
    rows_count, cols_count = lax.axis_size("rows"), lax.axis_size("cols")
    rows_dev, width_dev = cells.shape
    width = proj_weights.shape[-1]
    ff_width = mlp_in.shape[1]
    rows_all = rows_dev * rows_count
    key_total = rows_all // 4 * 3
    head_rows = HEADS * 2 * rows_dev
    dma = pltpu.SemaphoreType.DMA
    shape = jax.ShapeDtypeStruct
    sizes = {"z": rows_count // 4, "x": 2, "k": 2, "y": cols_count}

    mask_rows = feat_mask.T
    mlp_out_turned = mlp_out.T
    norm_first_turned = jnp.transpose(norm_first, (1, 0, 2))
    norm_second_turned = jnp.transpose(norm_second, (1, 0, 2))
    bank_rows = owner_rows.shape[0]

    def block_rows(rows):
        unit = 16 * math.prod(members(stage, sizes) for stage in STAGES[:-1])
        return -(-rows // unit) * unit

    def landings(rows):
        found = []
        for stage in STAGES[:-1]:
            count = members(stage, sizes)
            rows //= count
            found.append(pltpu.VMEM((count - 1, rows, LANES), BF16))
        return found + [pltpu.VMEM((members(STAGES[-1], sizes), rows, LANES), BF16)]

    both_tiles = 2 * width // LANES * width
    half_tiles = -(-width // LANES) * width
    sum_rows = [
        block_rows(2 * (ff_width // LANES) * width + half_tiles),
        block_rows(2 * both_tiles + 2 * width // LANES * 16),
        block_rows(both_tiles + half_tiles),
    ]
    widest = max(members(stage, sizes) for stage in STAGES) - 1
    layer_part, cells_part, mlp_total, item_total, feat_total, sorted_banks = pl.pallas_call(
        functools.partial(layer_kernel, rows_count, cols_count),
        name="layer_and_gradients",
        out_shape=(
            shape((rows_dev, width_dev), BF16),
            shape((rows_dev, width_dev), F32),
            *[shape((rows, LANES), BF16) for rows in sum_rows],
            shape((bank_rows, 2 * width), BF16),
        ),
        in_specs=[in_smem()] + [in_vmem()] * 5 + [anywhere()] * 8,
        out_specs=[anywhere()] * 2 + [in_vmem()] * 3 + [anywhere()],
        scratch_shapes=[
            pltpu.VMEM(proj_weights.shape, F32),
            pltpu.VMEM(feat_out_w.shape, F32),
            pltpu.VMEM(bank_first.shape, F32),
            pltpu.VMEM(bank_first.shape, F32),
            pltpu.VMEM(item_out_w.shape, F32),
            pltpu.VMEM(mlp_in.shape, F32),
            pltpu.VMEM(mlp_in.shape, F32),
            pltpu.VMEM((rows_dev, width_dev), BF16),
            pltpu.VMEM((rows_dev, width_dev), BF16),
            pltpu.VMEM((rows_dev, width_dev), F32),
            pltpu.VMEM((bank_rows, 2 * width), BF16),
            pltpu.VMEM((4, rows_dev, width_dev), BF16),
            pltpu.VMEM((2,) + mask_rows.shape, jnp.int32),
            pltpu.VMEM((rows_dev, width), BF16),
            pltpu.VMEM((rows_dev, width), BF16),
            pltpu.VMEM((rows_dev, width), BF16),
            pltpu.VMEM((rows_dev, width), BF16),
            pltpu.VMEM((rows_dev, width), F32),
            pltpu.VMEM((rows_dev, width), F32),
            pltpu.VMEM((rows_all // 2, width_dev), BF16),
            pltpu.VMEM((width, key_total), BF16),
            pltpu.VMEM((key_total, width), BF16),
            pltpu.VMEM((rows_all // 2, width_dev), BF16),
            pltpu.VMEM((16, rows_all), F32),
            pltpu.VMEM((bank_rows, 2 * width), BF16),
            pltpu.VMEM((head_rows, width), BF16),
            pltpu.VMEM((head_rows, width), BF16),
            pltpu.VMEM((key_total, head_rows), F32),
            pltpu.VMEM((1, head_rows), F32),
            pltpu.VMEM((1, head_rows), F32),
            pltpu.VMEM((width, head_rows), F32),
            pltpu.VMEM((head_rows, width), F32),
            pltpu.VMEM((head_rows, width), F32),
            pltpu.VMEM((rows_dev, width_dev), BF16),
            pltpu.VMEM((4, rows_dev, width_dev), BF16),
        ]
        + [pltpu.VMEM((rows, LANES), BF16) for rows in sum_rows]
        + [landing for rows in sum_rows for landing in landings(rows)]
        + [
            dma((2, 2, 3)),
            dma((4, 2)),
            dma((2, 1, DepthGather.slots(rows_count))),
            dma((2, 2, DepthGather.slots(rows_count))),
            dma((2, 1, RowGather.slots(rows_count))),
        ]
        + [dma((4, len(STAGES), widest))] * len(sum_rows)
        + [dma((11,))],
        compiler_params=pltpu.CompilerParams(
            collective_id=0, has_side_effects=True, vmem_limit_bytes=VMEM_BYTES
        ),
    )(
        train_rows,
        owner_rows,
        cells,
        mask_rows,
        norm_gains,
        norm_shifts,
        proj_weights,
        feat_out_w,
        bank_first,
        bank_second,
        item_out_w,
        mlp_in,
        mlp_out_turned,
        cotangent,
    )

    slots_dev = bank_first.shape[0]
    square = (8, width, width)
    (
        layer_out,
        cells_grad,
        square_grads,
        in_grad,
        out_grad,
        norm_grads,
        clip_norm,
        first_new,
        second_new,
        square_new,
        in_new,
        out_new,
        square_low,
        in_low,
        out_low,
        norm_new,
        norm_first_new,
        norm_second_new,
    ) = pl.pallas_call(
        update_kernel,
        name="rotated_update",
        out_shape=(
            shape(layer_part.shape, BF16),
            shape(cells_part.shape, F32),
            shape(square, F32),
            shape(mlp_in.shape, F32),
            shape(mlp_in.shape, F32),
            shape(norm_first_turned.shape, F32),
            shape((1,), F32),
            shape(bank_first.shape, F32),
            shape(bank_first.shape, F32),
            shape(square, F32),
            shape(mlp_in.shape, F32),
            shape(mlp_in.shape, F32),
            shape(square, BF16),
            shape(mlp_in.shape, BF16),
            shape(mlp_in.shape, BF16),
            shape(norm_first_turned.shape, F32),
            shape(norm_first_turned.shape, F32),
            shape(norm_first_turned.shape, F32),
        ),
        in_specs=[in_smem()] + [in_vmem()] * 11 + [anywhere()] * 8,
        out_specs=[anywhere()] * 5
        + [in_vmem(), in_smem(), in_vmem(), in_vmem()]
        + [anywhere()] * 6
        + [in_vmem()] * 3,
        scratch_shapes=[
            pltpu.VMEM(bases_small.shape, F32),
            pltpu.VMEM(bases_big.shape, F32),
            pltpu.VMEM(sorted_banks.shape, BF16),
            pltpu.VMEM(square, F32),
            pltpu.VMEM(mlp_in.shape, F32),
            pltpu.VMEM(mlp_in.shape, F32),
            pltpu.VMEM(square, F32),
            pltpu.VMEM(mlp_in.shape, F32),
            pltpu.VMEM(mlp_in.shape, F32),
            pltpu.VMEM(square, F32),
            pltpu.VMEM(mlp_in.shape, F32),
            pltpu.VMEM(mlp_in.shape, F32),
            pltpu.VMEM(square, BF16),
            pltpu.VMEM(mlp_in.shape, BF16),
            pltpu.VMEM(mlp_in.shape, BF16),
            pltpu.VMEM((bank_rows, width), F32),
            pltpu.VMEM((slots_dev, width), F32),
            dma((48,)),
        ],
        compiler_params=pltpu.CompilerParams(vmem_limit_bytes=VMEM_BYTES),
    )(
        owner_rows,
        mlp_total,
        item_total,
        feat_total,
        norm_gains,
        norm_shifts,
        norm_first_turned,
        norm_second_turned,
        bank_first,
        bank_second,
        layer_part,
        cells_part,
        bases_small,
        bases_big,
        sorted_banks,
        proj_weights,
        feat_out_w,
        item_out_w,
        mlp_in,
        mlp_out_turned,
    )
    return (
        layer_out,
        cells_grad,
        square_grads,
        in_grad,
        out_grad.T,
        jnp.transpose(norm_grads, (1, 0, 2)),
        clip_norm,
        first_new,
        second_new,
        square_new,
        in_new,
        out_new.T,
        square_low,
        in_low,
        out_low.T,
        jnp.transpose(norm_new, (1, 0, 2)),
        jnp.transpose(norm_first_new, (1, 0, 2)),
        jnp.transpose(norm_second_new, (1, 0, 2)),
    )


def solution(mesh):
    in_specs = (
        P("rows", "cols"),
        P("rows", None),
        P(),
        P("rows", "cols"),
        P(),
        P(),
        P(),
        P(),
        P(),
        P(),
        P(),
        P(),
        P(),
        P(),
        P("rows", None),
        P("rows", None),
        P(),
        P(),
    )
    out_specs = (
        P("rows", "cols"),
        P("rows", "cols"),
        P(),
        P(),
        P(),
        P(),
        P(),
        P("rows", None),
        P("rows", None),
        P(),
        P(),
        P(),
        P(),
        P(),
        P(),
        P(),
        P(),
        P(),
    )
    small = mesh.shape["rows"] == 16 and mesh.shape["cols"] == 2
    return jax.shard_map(
        fast_device if small else per_device, mesh=mesh, in_specs=in_specs, out_specs=out_specs, check_vma=False
    )
```
